32 devices in a mesh: seq: 2 (over z_hi), fsdp: 8 (over y, x, core), dp: 2 (over z_lo).
Axes of the slice: x: 2, y: 2, z: 4 (z_hi: 2, z_lo: 2; z = z_hi * 2 + z_lo), core: 2. Of those that a mesh axis runs over, the one named last changes fastest.
Arguments:
- images: bfloat16 [48, 584, 1024], P(('fsdp', 'dp'), 'seq'), may hold values from -6 to 6
- key_mask: int32 [48, 584], P(('fsdp', 'dp')), may hold values from 0 to 1, as said below
- out_grad: bfloat16 [48, 584, 1024], P(('fsdp', 'dp'), 'seq'), may hold values from -6 to 6
- step_count: int32 [], replicated, may hold values from 2 to 20
- in_weights: float32 [1024, 3072], P(('seq', 'fsdp')), may hold values from -0.25 to 0.25
- out_weights: float32 [1024, 1024], P(('seq', 'fsdp')), may hold values from -0.375 to 0.375
- up_weights: float32 [4096, 1024], P(('seq', 'fsdp')), may hold values from -0.1875 to 0.1875
- down_weights: float32 [4096, 1024], P(('seq', 'fsdp')), may hold values from -0.09375 to 0.09375
- vectors: float32 [12288], P(('seq', 'fsdp')), may hold values from -0.4 to 1.4
- first_in: float32 [1024, 3072], P(('seq', 'fsdp')), may hold values from -1.5 to 1.5
- first_out: float32 [1024, 1024], P(('seq', 'fsdp')), may hold values from -0.9 to 0.9
- first_up: float32 [4096, 1024], P(('seq', 'fsdp')), may hold values from -2.2 to 2.2
- first_down: float32 [4096, 1024], P(('seq', 'fsdp')), may hold values from -4.5 to 4.5
- first_vectors: float32 [12288], P(('seq', 'fsdp')), may hold values from -4.5 to 4.5
- second_in: float32 [1024, 3072], P(('seq', 'fsdp')), may hold values from 0.03 to 0.25
- second_out: float32 [1024, 1024], P(('seq', 'fsdp')), may hold values from 0.012 to 0.09
- second_up: float32 [4096, 1024], P(('seq', 'fsdp')), may hold values from 0.07 to 0.55
- second_down: float32 [4096, 1024], P(('seq', 'fsdp')), may hold values from 0.28 to 2.2
- second_vectors: float32 [12288], P(('seq', 'fsdp')), may hold values from 0.28 to 2.2
Outputs:
- grad_norm: float32 [], replicated
- new_in: float32 [1024, 3072], P(('seq', 'fsdp'))
- new_out: float32 [1024, 1024], P(('seq', 'fsdp'))
- new_up: float32 [4096, 1024], P(('seq', 'fsdp'))
- new_down: float32 [4096, 1024], P(('seq', 'fsdp'))
- new_vectors: float32 [12288], P(('seq', 'fsdp'))
- first_in_new: float32 [1024, 3072], P(('seq', 'fsdp'))
- first_out_new: float32 [1024, 1024], P(('seq', 'fsdp'))
- first_up_new: float32 [4096, 1024], P(('seq', 'fsdp'))
- first_down_new: float32 [4096, 1024], P(('seq', 'fsdp'))
- first_vectors_new: float32 [12288], P(('seq', 'fsdp'))
- second_in_new: float32 [1024, 3072], P(('seq', 'fsdp'))
- second_out_new: float32 [1024, 1024], P(('seq', 'fsdp'))
- second_up_new: float32 [4096, 1024], P(('seq', 'fsdp'))
- second_down_new: float32 [4096, 1024], P(('seq', 'fsdp'))
- second_vectors_new: float32 [12288], P(('seq', 'fsdp'))
- copy_in: bfloat16 [1024, 3072], P(('seq', 'fsdp'))
- copy_out: bfloat16 [1024, 1024], P(('seq', 'fsdp'))
- copy_up: bfloat16 [4096, 1024], P(('seq', 'fsdp'))
- copy_down: bfloat16 [4096, 1024], P(('seq', 'fsdp'))
- copy_vectors: bfloat16 [12288], P(('seq', 'fsdp'))
- activations: float32 [48, 584, 1024], P(('fsdp', 'dp'), 'seq')
- input_grad: float32 [48, 584, 1024], P(('fsdp', 'dp'), 'seq')
The draws below stay inside these ranges and needn't reach their ends.
Inputs may be any that keep to these rules, and one draw needn't show every extreme that they name: `key_mask`: every image has exactly 577 ones; where its 7 zeros stand is drawn afresh for each image.
All inputs are finite; a program needn't handle non-finite values.
Results may differ from the reference program's by a relative error of at most 0.02.
The reference program's roundings to bfloat16 on the way count: a program that leaves them out, or rounds other values in their place, can miss the bound.
Values may be sent and summed in bfloat16 or wider, within the bound.
A program may use at most 256 MiB of HBM per device.

```python
import math
import jax
import jax.numpy as jnp
from jax import lax

D = 1024
HEADS = 16
HD = 64
FF = 4096
S = 584
PAD = 7
IMG_DEV = 3
IMAGES = 48
PVEC = 12288


def draw_key_mask(key, part):
    raw = jax.random.randint(key, (IMAGES, S), 0, 1 << 20)
    ranked = raw * S + jnp.arange(S, dtype=jnp.int32)[None, :]
    order = jnp.argsort(ranked, axis=1)
    placed = jnp.argsort(order, axis=1)
    return (placed >= PAD).astype(jnp.int32)


def draw_vectors(key, part):
    first_key, second_key, third_key, fourth_key = jax.random.split(key, 4)
    gain_one = jax.random.uniform(first_key, (D,), jnp.float32, 0.6, 1.4)
    shifts_one = jax.random.uniform(second_key, (4 * D,), jnp.float32, -0.4, 0.4)
    gain_two = jax.random.uniform(third_key, (D,), jnp.float32, 0.6, 1.4)
    shifts_two = jax.random.uniform(fourth_key, (6 * D,), jnp.float32, -0.4, 0.4)
    return jnp.concatenate([gain_one, shifts_one, gain_two, shifts_two])


def draw_up_weights(key, part):
    first_key, second_key = jax.random.split(jax.random.fold_in(key, 7))
    spread = jnp.float32(D) ** (-0.5)
    entries = jnp.clip(jax.random.normal(first_key, (FF, D), jnp.float32), -3.0, 3.0)
    offsets = jnp.clip(jax.random.normal(second_key, (FF, 1), jnp.float32), -3.0, 3.0)
    return (entries + offsets) * spread


def steps_of(key, shape, pieces, least, largest):
    def one(dim, parts):
        steps = jax.random.uniform(jax.random.fold_in(jax.random.fold_in(key, 6), dim), (parts,), jnp.float32, least / len(pieces), largest / len(pieces))
        return jnp.repeat(jnp.exp(steps), shape[dim] // parts).reshape((-1,) + (1,) * (len(shape) - dim - 1))

    level = one(*pieces[0])
    for cut in pieces[1:]:
        level = level * one(*cut)
    return level


def centred(key, extent, width, bound, shards=(), kind=jnp.bfloat16):
    values = jax.random.normal(key, extent, jnp.float32) * width
    if len(shards) > 0:
        values = steps_of(key, extent, shards, -0.22, 0.18) * values
    return jnp.clip(values, min=-bound, max=bound).astype(kind)


def setup_inputs(seed: int = 0) -> dict:
    streams_of = jax.random.split(jax.random.key(seed), 20)
    images = centred(streams_of[0], (IMAGES, S, D), 1.0, 6.0, ((0, 16), (1, 2)))
    key_mask = draw_key_mask(jax.random.fold_in(streams_of[19], 71), 0)
    out_grad = centred(streams_of[2], (IMAGES, S, D), 1.0, 6.0, ((0, 16), (1, 2)))
    step_count = jax.random.randint(streams_of[3], (), 2, 21).astype(jnp.int32)
    in_weights = centred(streams_of[4], (D, 3 * D), (D // 2) ** -0.5, 0.25, ((0, 16),), jnp.float32)
    out_weights = centred(streams_of[5], (D, D), (D // 4) ** -0.5, 0.375, ((0, 16),), jnp.float32)
    up_weights = draw_up_weights(jax.random.fold_in(streams_of[19], 71), 0)
    down_weights = centred(streams_of[7], (FF, D), FF ** -0.5, 0.09375, ((0, 16),), jnp.float32)
    vectors = draw_vectors(jax.random.fold_in(streams_of[19], 71), 0)
    first_in = centred(streams_of[9], (D, 3 * D), 0.25, 1.5, ((0, 16),), jnp.float32)
    first_out = centred(streams_of[10], (D, D), 0.15, 0.9, ((0, 16),), jnp.float32)
    first_up = centred(streams_of[11], (FF, D), 0.37, 2.2, ((0, 16),), jnp.float32)
    first_down = centred(streams_of[12], (FF, D), 0.75, 4.5, ((0, 16),), jnp.float32)
    first_vectors = centred(streams_of[13], (PVEC,), 0.75, 4.5, ((0, 16),), jnp.float32)
    second_in = jnp.clip(jnp.exp(math.log(0.25) - 2.1202636 * jax.random.uniform(streams_of[14], (D, 3 * D), jnp.float32) ** steps_of(streams_of[14], (D, 3 * D), ((0, 16),), -0.2, 0.2)), 0.03, 0.25)
    second_out = jnp.clip(jnp.exp(math.log(0.09) - 2.014903 * jax.random.uniform(streams_of[15], (D, D), jnp.float32) ** steps_of(streams_of[15], (D, D), ((0, 16),), -0.2, 0.2)), 0.012, 0.09)
    second_up = jnp.clip(jnp.exp(math.log(0.55) - 2.061423 * jax.random.uniform(streams_of[16], (FF, D), jnp.float32) ** steps_of(streams_of[16], (FF, D), ((0, 16),), -0.2, 0.2)), 0.07, 0.55)
    second_down = jnp.clip(jnp.exp(math.log(2.2) - 2.061423 * jax.random.uniform(streams_of[17], (FF, D), jnp.float32) ** steps_of(streams_of[17], (FF, D), ((0, 16),), -0.2, 0.2)), 0.28, 2.2)
    second_vectors = jnp.clip(jnp.exp(math.log(2.2) - 2.061423 * jax.random.uniform(streams_of[18], (PVEC,), jnp.float32) ** steps_of(streams_of[18], (PVEC,), ((0, 16),), -0.2, 0.2)), 0.28, 2.2)
    return {"images": images, "key_mask": key_mask, "out_grad": out_grad, "step_count": step_count, "in_weights": in_weights, "out_weights": out_weights, "up_weights": up_weights, "down_weights": down_weights, "vectors": vectors, "first_in": first_in, "first_out": first_out, "first_up": first_up, "first_down": first_down, "first_vectors": first_vectors, "second_in": second_in, "second_out": second_out, "second_up": second_up, "second_down": second_down, "second_vectors": second_vectors}


NEG_FILL = -1000000000.0
NORM_EPS = 1e-06
ADAM_EPS = 1e-08
WEIGHT_DECAY = 0.05
HIGH = lax.Precision.HIGHEST

@jax.custom_vjp
def low(v):
    return lax.optimization_barrier(v.astype(jnp.bfloat16)).astype(jnp.float32)

@jax.custom_vjp
def low_back(v):
    return v

def low_keep(v):
    return (low(v), None)

def low_pass(kept, grad):
    return (grad,)

def back_keep(v):
    return (v, None)

def back_low(kept, grad):
    return (low(grad),)
low.defvjp(low_keep, low_pass)
low_back.defvjp(back_keep, back_low)

def layer_norm(values, norm_gain, norm_shift):
    center = values - lax.optimization_barrier(jnp.mean(values, axis=-1, keepdims=True))
    spread = lax.optimization_barrier(jnp.mean(center * center, axis=-1, keepdims=True))
    return center * lax.rsqrt(spread + NORM_EPS) * norm_gain + norm_shift

def project(values, matrix):
    return jnp.einsum('gsd,de->gse', values, matrix, precision=HIGH)

def forward(inputs, weight_in, weight_out, weight_up, weight_down, weight_vec, valid_keys):
    features = inputs.shape[-1]
    image_count = inputs.shape[0]
    token_count = inputs.shape[1]
    vector_copy = low(weight_vec)
    matrix_in = low(weight_in)
    matrix_out = low(weight_out)
    matrix_up = low(weight_up)
    matrix_down = low(weight_down)
    gain_one = vector_copy[0:features]
    shift_one = vector_copy[features:2 * features]
    query_bias = vector_copy[2 * features:3 * features]
    value_bias = vector_copy[3 * features:4 * features]
    out_bias = vector_copy[4 * features:5 * features]
    gain_two = vector_copy[5 * features:6 * features]
    shift_two = vector_copy[6 * features:7 * features]
    down_bias = vector_copy[7 * features:8 * features]
    up_bias = vector_copy[8 * features:]
    in_bias = jnp.concatenate([query_bias, jnp.zeros_like(query_bias), value_bias])
    normed_one = low(layer_norm(inputs, gain_one, shift_one))
    packed = low_back(low(project(normed_one, matrix_in) + in_bias))
    heads_view = packed.reshape(image_count, token_count, 3, HEADS, HD)
    queries = heads_view[:, :, 0]
    key_rows = heads_view[:, :, 1]
    value_rows = heads_view[:, :, 2]
    scores = jnp.einsum('gqhd,gkhd->ghqk', queries, key_rows, precision=HIGH) * HD ** (-0.5)
    scores = low_back(scores)
    scores = jnp.where(valid_keys[:, None, None, :], scores, NEG_FILL)
    row_max = lax.optimization_barrier(jnp.max(scores, axis=-1, keepdims=True))
    exponent = jnp.exp(scores - row_max)
    attention = low(exponent / lax.optimization_barrier(jnp.sum(exponent, axis=-1, keepdims=True)))
    mixed = jnp.einsum('ghqk,gkhd->gqhd', attention, value_rows, precision=HIGH)
    mixed = low_back(low(mixed.reshape(image_count, token_count, features)))
    branch = low_back(project(mixed, matrix_out) + out_bias)
    middle = inputs + branch
    normed_two = low(layer_norm(middle, gain_two, shift_two))
    hidden_input = low_back(jnp.einsum('gsd,fd->gsf', normed_two, matrix_up, precision=HIGH) + up_bias)
    hidden = low(jax.nn.gelu(hidden_input, approximate=True))
    down_branch = low_back(project(hidden, matrix_down) + down_bias)
    return middle + down_branch

def adam_update(master, first_moment, second_moment, gradient, step_rate, bias_one, bias_two):
    first_new = 0.5 * first_moment + 0.5 * gradient
    second_new = 0.5 * second_moment + 0.5 * gradient * gradient
    update = first_new / bias_one / (jnp.sqrt(second_new / bias_two) + ADAM_EPS)
    master_new = master - step_rate * (update + WEIGHT_DECAY * master)
    return (master_new, first_new, second_new)

def reference(images, key_mask, out_grad, step_count, in_weights, out_weights, up_weights, down_weights, vectors, first_in, first_out, first_up, first_down, first_vectors, second_in, second_out, second_up, second_down, second_vectors):
    group_total = IMAGES // IMG_DEV
    image_groups = images.reshape(group_total, IMG_DEV, S, D)
    mask_groups = key_mask.reshape(group_total, IMG_DEV, S)
    grad_groups = out_grad.reshape(group_total, IMG_DEV, S, D)
    masters = (in_weights, out_weights, up_weights, down_weights, vectors)

    def one_group(totals, group_item):
        block_input, block_mask, block_grad = group_item
        valid_keys = block_mask > 0

        def forward_group(inputs, weight_in, weight_out, weight_up, weight_down, weight_vec):
            return forward(inputs, weight_in, weight_out, weight_up, weight_down, weight_vec, valid_keys)
        outputs, pullback = jax.vjp(forward_group, block_input.astype(jnp.float32), in_weights, out_weights, up_weights, down_weights, vectors)
        gradients = pullback(block_grad.astype(jnp.float32))
        new_totals = tuple((former + latter for former, latter in zip(totals, gradients[1:])))
        return (new_totals, (outputs, gradients[0]))
    zero_sums = tuple((jnp.zeros_like(master) for master in masters))
    totals, (outputs, input_grads) = lax.scan(one_group, zero_sums, (image_groups, mask_groups, grad_groups))
    square_sum = sum((jnp.sum(gradient * gradient) for gradient in totals))
    grad_norm = jnp.sqrt(square_sum)
    threshold = 0.5 * jnp.sqrt(jnp.float32(4 * D * D + 2 * D * FF + 12 * D))
    clip_factor = jnp.minimum(1.0, threshold / grad_norm)
    clipped = tuple((gradient * clip_factor for gradient in totals))
    decay_power = jnp.power(jnp.float32(0.5), step_count.astype(jnp.float32))
    bias_one = 1.0 - decay_power
    bias_two = 1.0 - decay_power
    rates = ((D // 2) ** (-0.5), (D // 4) ** (-0.5), D ** (-0.5), FF ** (-0.5), 0.2)
    firsts = (first_in, first_out, first_up, first_down, first_vectors)
    seconds = (second_in, second_out, second_up, second_down, second_vectors)
    results = [adam_update(masters[index], firsts[index], seconds[index], clipped[index], rates[index], bias_one, bias_two) for index in range(5)]
    new_masters = [entry[0] for entry in results]
    new_firsts = [entry[1] for entry in results]
    new_seconds = [entry[2] for entry in results]
    copies = [master.astype(jnp.bfloat16) for master in new_masters]
    activations = outputs.reshape(IMAGES, S, D)
    input_grad = input_grads.reshape(IMAGES, S, D)
    return (grad_norm, new_masters[0], new_masters[1], new_masters[2], new_masters[3], new_masters[4], new_firsts[0], new_firsts[1], new_firsts[2], new_firsts[3], new_firsts[4], new_seconds[0], new_seconds[1], new_seconds[2], new_seconds[3], new_seconds[4], copies[0], copies[1], copies[2], copies[3], copies[4], activations, input_grad)
```

```python
import functools
import math

import jax
import jax.numpy as jnp
import numpy as np
from jax import lax
from jax.experimental import pallas as pl
from jax.experimental.pallas import tpu as pltpu
from jax.sharding import Mesh
from jax.sharding import PartitionSpec as P

D = 1024
FF = 4096
PAD_ROWS = 16

NEG_FILL = -1000000000.0
ADAM_EPS = 1e-08
WEIGHT_DECAY = 0.05
AXES = ("seq", "y", "x", "core", "dp")
SHARD = ("seq", "y", "x", "core")

BF=jnp.bfloat16; F32=jnp.float32
def dot(a, b, dims=(((1,), (0,)), ((), ()))):
    return lax.dot_general(a, b, dims, preferred_element_type=F32)
NT=(((1,),(1,)),((),()))
TN=(((0,),(0,)),((),()))
ANY=pl.BlockSpec(memory_space=pl.ANY)
VM=pl.BlockSpec(memory_space=pltpu.VMEM)
SM=pl.BlockSpec(memory_space=pltpu.SMEM)

def gelu_both(u):
    c0=math.sqrt(2/math.pi)
    sq=u*u
    t=jnp.tanh(u*(c0+(c0*0.044715)*sq))
    half=0.5+0.5*t
    value=u*half
    slope=half+(0.5*u)*(1.0-t*t)*(c0+(3*c0*0.044715)*sq)
    return value,slope

def mlp_kernel(keys,*refs,gtile):
    nk=len(keys)
    at_ref,h2_ref,go_ref,gt_ref,bu_ref=refs[:5]
    pa,pb=refs[5:5+nk],refs[5+nk:5+2*nk]
    o=5+2*nk
    ga,gb=refs[o:o+nk],refs[o+nk:o+2*nk]
    yown_ref,yoth_ref,dh_ref,gbu_ref=refs[o+2*nk:o+2*nk+4]
    w,dd,a_all,du_all,y_acc,dh_acc,g_out,wsem,gsem=refs[o+2*nk+4:]
    images,half,feat=go_ref.shape
    hid=pa[0].shape[2]
    width=4*hid
    padded=h2_ref.shape[0]//(2*images)
    blocks=2*images

    def load(i,slot,go):
        for ki in range(nk):
            @pl.when(i==ki)
            def _():
                for kz in range(2):
                    for ud in range(2):
                        for ab,src in enumerate((pa[ki],pb[ki])):
                            cp=pltpu.make_async_copy(src.at[kz,ud],w.at[slot,ud,pl.ds((kz*2+ab)*hid,hid)],wsem.at[slot,kz*4+ud*2+ab])
                            cp.start() if go else cp.wait()
    def save(i,go):
        for ki in range(nk):
            @pl.when(i==ki)
            def _():
                for kz in range(2):
                    for ud in range(2):
                        for ab,dst in enumerate((ga[ki],gb[ki])):
                            cp=pltpu.make_async_copy(g_out.at[ud,pl.ds((kz*2+ab)*hid,hid)],dst.at[kz,ud],gsem.at[kz*4+ud*2+ab])
                            cp.start() if go else cp.wait()
    load(0,0,True)
    gbu_ref[...]=jnp.zeros_like(gbu_ref)
    for i in range(images):
        for s,src in enumerate((go_ref,gt_ref)):
            r=(2*i+s)*padded
            tail=padded-16
            dd[r+tail:r+padded,:]=jnp.zeros((16,feat),BF)
            dd[r:r+half,:]=src[i]
    def step(i,_):
        slot=lax.rem(i,2)
        load(i,slot,False)
        @pl.when(i+1<nk)
        def _(): load(i+1,1-slot,True)
        rows=[]
        for kz in range(2):
            for ab in range(2):
                row=jnp.int32(0)
                for ki,(ky,kx) in enumerate(keys):
                    z=lax.rem(at_ref[0]+kz,2); y=lax.rem(at_ref[1]+ky,at_ref[4]); x=lax.rem(at_ref[2]+kx,at_ref[5])
                    here=(((z*at_ref[4]+y)*at_ref[5]+x)*2+at_ref[3])*2+ab
                    row=jnp.where(i==ki,here,row)
                rows.append(row)
        bias=jnp.concatenate([bu_ref[pl.ds(r,1),:] for r in rows],axis=1)
        wu=w.at[slot,0]; wd=w.at[slot,1]
        def tokens(b,sums):
            r=pl.ds(pl.multiple_of(b*padded,16),padded)
            u=dot(h2_ref[r,:],wu[...],NT)+bias
            value,slope=gelu_both(u)
            a=value.astype(BF)
            a_all[r,:]=a
            dg=dot(dd[r,:],wd[...],NT)
            du=(dg*slope).astype(BF)
            du_all[r,:]=du
            ynew=dot(a,wd[...]); dnew=dot(du,wu[...])
            @pl.when(i==0)
            def _():
                y_acc[r,:]=ynew; dh_acc[r,:]=dnew
            @pl.when(i>0)
            def _():
                y_acc[r,:]+=ynew; dh_acc[r,:]+=dnew
            return sums+jnp.sum(du.astype(F32),axis=0,keepdims=True)
        sums=lax.fori_loop(0,blocks,tokens,jnp.zeros((1,width),F32))
        for q,row in enumerate(rows):
            gbu_ref[pl.ds(row,1),:]=sums[:,q*hid:(q+1)*hid]
        @pl.when(i>0)
        def _(): save(i-1,False)
        for t in range(0,width,gtile):
            g_out[1,t:t+gtile,:]=dot(a_all[:,t:t+gtile],dd[...],TN).astype(BF)
            g_out[0,t:t+gtile,:]=dot(du_all[:,t:t+gtile],h2_ref[...],TN).astype(BF)
        save(i,True)
        return 0
    lax.fori_loop(0,nk,step,0)
    for i in range(images):
        r=2*i*padded
        yown_ref[i]=y_acc[r:r+padded,:]
        yoth_ref[i]=y_acc[r+padded:r+2*padded,:].astype(BF)
    dh_ref[...]=dh_acc[...].astype(BF)
    save(nk-1,False)

def mlp(at,h2,g_own,g_oth,bu_rows,fa,fb,gtile=256):
    keys=sorted(fa); nk=len(keys)
    images,half,feat=g_own.shape
    tokens=h2.shape[0]; padded=tokens//(2*images)
    _,_,hid,_=fa[keys[0]].shape
    width=4*hid
    piece=jax.ShapeDtypeStruct(fa[keys[0]].shape,BF)
    out=pl.pallas_call(functools.partial(mlp_kernel,keys,gtile=min(gtile,width)),
        in_specs=[SM]+[VM]*4+[ANY]*(2*nk),
        out_specs=[ANY]*(2*nk)+[VM]*4,
        out_shape=[piece]*(2*nk)+[jax.ShapeDtypeStruct((images,padded,feat),F32),jax.ShapeDtypeStruct((images,padded,feat),BF),
            jax.ShapeDtypeStruct((tokens,feat),BF),jax.ShapeDtypeStruct(bu_rows.shape,F32)],
        scratch_shapes=[pltpu.VMEM((2,2,width,feat),BF),pltpu.VMEM((tokens,feat),BF),pltpu.VMEM((tokens,width),BF),pltpu.VMEM((tokens,width),BF),
            pltpu.VMEM((tokens,feat),F32),pltpu.VMEM((tokens,feat),F32),pltpu.VMEM((2,width,feat),BF),
            pltpu.SemaphoreType.DMA((2,8)),pltpu.SemaphoreType.DMA((8,))],
        name="feed_forward",
        compiler_params=pltpu.CompilerParams(vmem_limit_bytes=60<<20),
        cost_estimate=pl.CostEstimate(flops=nk*6*2*tokens*feat*width,bytes_accessed=40<<20,transcendentals=nk*tokens*width),
    )(at,h2,g_own,g_oth,bu_rows,*[fa[k] for k in keys],*[fb[k] for k in keys])
    return dict(zip(keys,out[:nk])),dict(zip(keys,out[nk:2*nk])),out[2*nk],out[2*nk+1],out[2*nk+2],out[2*nk+3]

HD=64; HALF_D=512

def head_operands(q_ref,k_ref,kb_ref,scale):
    q=q_ref[0].astype(F32)*scale; k=k_ref[0].astype(F32); kb=kb_ref[0].astype(F32)
    lane=lax.broadcasted_iota(jnp.int32,q.shape,1)
    low=lane<HD
    one=jnp.where((lane==0)|(lane==HD),1.0,0.0)
    qs=[jnp.where(low,q,one).astype(BF),jnp.where(low,one,q).astype(BF)]
    ks=[jnp.where(low,k,kb).astype(BF),jnp.where(low,kb,k).astype(BF)]
    return q,k,low,qs,ks

def attend_kernel(q_ref,k_ref,v_ref,kb_ref,o_ref,lse_ref):
    q,k,low,qs,ks=head_operands(q_ref,k_ref,kb_ref,HD**-0.5)
    vt=v_ref[0].astype(F32).T.astype(BF)
    outs=[]
    for j in range(2):
        s=dot(ks[j],qs[j],NT)
        m=jnp.max(s,axis=0,keepdims=True)
        e=jnp.exp(s-m)
        l=jnp.sum(e,axis=0,keepdims=True)
        o=dot(vt[j*HD:(j+1)*HD],e.astype(BF))
        outs.append(o*(1.0/l))
        lse_ref[0,0,j:j+1,:]=m+jnp.log(l)
    o_ref[0]=jnp.concatenate(outs,axis=0).T.astype(BF)

def attend(qkv,kbias):
    n,rows,w=qkv.shape; pairs=w//3//128
    blk=lambda off: pl.BlockSpec((1,rows,128),lambda i,p: (i,0,off+p))
    return pl.pallas_call(attend_kernel,grid=(n,pairs),
        in_specs=[blk(0),blk(pairs),blk(2*pairs),pl.BlockSpec((1,rows,128),lambda i,p:(i,0,0))],
        out_specs=[blk(0),pl.BlockSpec((1,1,8,rows),lambda i,p:(i,p,0,0))],
        out_shape=[jax.ShapeDtypeStruct((n,rows,w//3),BF),jax.ShapeDtypeStruct((n,pairs,8,rows),F32)],
        name="attend",
        compiler_params=pltpu.CompilerParams(vmem_limit_bytes=50<<20),
        cost_estimate=pl.CostEstimate(flops=n*pairs*8*rows*rows*128,bytes_accessed=n*rows*w*3,transcendentals=n*pairs*2*rows*rows),
    )(qkv,qkv,qkv,kbias)

def attend_back_kernel(q_ref,k_ref,v_ref,kb_ref,o_ref,g_ref,lse_ref,out_ref,sum_ref,*,pairs,chunk):
    p=pl.program_id(1)
    @pl.when((pl.program_id(0)==0)&(p==0))
    def _(): sum_ref[...]=jnp.zeros_like(sum_ref)
    scale=HD**-0.5
    q,k,low,qs,ks=head_operands(q_ref,k_ref,kb_ref,scale)
    qb=q.astype(BF)
    kt=k.T.astype(BF)
    g=g_ref[0]; gf=g.astype(F32)
    prod=(gf*o_ref[0].astype(F32)).T
    v=v_ref[0]
    rows=q.shape[0]
    dqs=[];dks=[];dvs=[]
    for j in range(2):
        gj=(jnp.where(low,gf,0.0) if j==0 else jnp.where(low,0.0,gf)).astype(BF)
        delta=jnp.sum(prod[j*HD:(j+1)*HD],axis=0,keepdims=True)
        lse=lse_ref[0,0,j:j+1,:]
        dq=None; dk=[]; dv=[]
        for r in range(0,rows,chunk):
            s=dot(ks[j][r:r+chunk],qs[j],NT)
            pr=jnp.exp(s-lse)
            dp=dot(v[r:r+chunk],gj,NT)
            ds=(pr*(dp-delta)).astype(BF)
            dv.append(dot(pr.astype(BF),g))
            dk.append(dot(ds,qb))
            t=dot(kt[j*HD:(j+1)*HD,r:r+chunk],ds) if chunk==rows else dot(k[r:r+chunk].astype(BF),ds,TN)[j*HD:(j+1)*HD]
            dq=t if dq is None else dq+t
        dqs.append(dq)
        dks.append(jnp.concatenate(dk,axis=0) if len(dk)>1 else dk[0]); dvs.append(jnp.concatenate(dv,axis=0) if len(dv)>1 else dv[0])
    parts=((jnp.concatenate(dqs,axis=0)*scale).T.astype(BF),jnp.where(low,dks[0],dks[1]).astype(BF),jnp.where(low,dvs[0],dvs[1]).astype(BF))
    for t,part in enumerate(parts):
        at=pl.ds(pl.multiple_of((t*pairs+p)*128,128),128)
        out_ref[0,:,at]=part
        sum_ref[0:1,at]+=jnp.sum(part.astype(F32),axis=0,keepdims=True)

def attend_back(qkv,kbias,mixed,grad,lse,chunk=None):
    n,rows,w=qkv.shape; pairs=w//3//128
    chunk=chunk or rows
    blk=lambda off: pl.BlockSpec((1,rows,128),lambda i,p: (i,0,off+p))
    return pl.pallas_call(functools.partial(attend_back_kernel,pairs=pairs,chunk=chunk),grid=(n,pairs),
        in_specs=[blk(0),blk(pairs),blk(2*pairs),pl.BlockSpec((1,rows,128),lambda i,p:(i,0,0)),blk(0),blk(0),pl.BlockSpec((1,1,8,rows),lambda i,p:(i,p,0,0))],
        out_specs=[pl.BlockSpec((1,rows,w),lambda i,p:(i,0,0)),pl.BlockSpec((8,w),lambda i,p:(0,0))],
        out_shape=[jax.ShapeDtypeStruct((n,rows,w),BF),jax.ShapeDtypeStruct((8,w),F32)],
        name="attend_back",
        compiler_params=pltpu.CompilerParams(vmem_limit_bytes=50<<20),
        cost_estimate=pl.CostEstimate(flops=n*pairs*20*rows*rows*128,bytes_accessed=n*rows*w*5,transcendentals=n*pairs*2*rows*rows),
    )(qkv,qkv,qkv,kbias,mixed,grad,lse)

NORM_EPS=1e-6
def norm_parts(values):
    center = values - jnp.mean(values, axis=-1, keepdims=True)
    inverse = lax.rsqrt(jnp.mean(center * center, axis=-1, keepdims=True) + NORM_EPS)
    return center * inverse, inverse

def norm_back(values, gain, grad):
    normed, inverse = norm_parts(values)
    scaled = grad * gain
    mean_one = jnp.mean(scaled, axis=-1, keepdims=True)
    mean_two = jnp.mean(scaled * normed, axis=-1, keepdims=True)
    return (scaled - mean_one - normed * mean_two) * inverse, grad * normed

def wide_rows(buf,block):
    n=block.shape[0]; total=buf.shape[0]
    buf[total-16:,:]=jnp.zeros((16,buf.shape[1]),F32)
    buf[0:n,:]=block.astype(F32)
    return buf[...]

def place(at_ref,keys,ka,size,pieces,buf,sem,gather):
    def both(go):
        n=0
        for ki,(ky,kx) in enumerate(keys):
            y=lax.rem(at_ref[1]+ky,at_ref[4]); x=lax.rem(at_ref[2]+kx,at_ref[5])
            for ab in range(2):
                for kz in range(ka):
                    z=lax.rem(at_ref[0]+kz,2) if ka==2 else 0
                    core=at_ref[3] if ab==0 else 1-at_ref[3]
                    if ka==1: core=at_ref[0] if ab==0 else 1-at_ref[0]
                    row=(((z*at_ref[4]+y)*at_ref[5]+x)*2+core)*size
                    inner=buf.at[pl.ds(pl.multiple_of(row,16),size)]
                    piece=pieces[ab*len(keys)+ki]
                    piece=piece.at[kz] if ka==2 else piece
                    cp=pltpu.make_async_copy(piece,inner,sem.at[n]) if gather else pltpu.make_async_copy(inner,piece,sem.at[n])
                    cp.start() if go else cp.wait()
                    n+=1
    both(True); both(False)

def project_kernel(keys,at_ref,own_ref,oth_ref,gain_ref,shift_ref,bias_ref,*refs):
    nk=len(keys)
    pieces=refs[:2*nk]; h_ref,qkv_ref,w,buf,sem=refs[2*nk:]
    @pl.when(pl.program_id(0)==0)
    def _(): place(at_ref,keys,2,pieces[0].shape[1],pieces,w,sem,True)
    for s,src in enumerate((own_ref,oth_ref)):
        v=wide_rows(buf.at[s],src[0])
        h=(norm_parts(v)[0]*gain_ref[...]+shift_ref[...]).astype(BF)
        h_ref[0,s]=h
        qkv_ref[0,s]=(dot(h,w[...])+bias_ref[...]).astype(BF)

def project(at,x_own,x_oth,gain,shift,bias,wa,wb,padded):
    keys=sorted(wa); nk=len(keys)
    n,half,feat=x_own.shape
    width=wa[keys[0]].shape[-1]
    tok=pl.BlockSpec((1,half,feat),lambda i:(i,0,0))
    row=lambda w: pl.BlockSpec((1,w),lambda i:(0,0))
    return pl.pallas_call(functools.partial(project_kernel,keys),grid=(n,),
        in_specs=[SM,tok,tok,row(feat),row(feat),row(width)]+[ANY]*(2*nk),
        out_specs=[pl.BlockSpec((1,2,padded,feat),lambda i:(i,0,0,0)),pl.BlockSpec((1,2,padded,width),lambda i:(i,0,0,0))],
        out_shape=[jax.ShapeDtypeStruct((n,2,padded,feat),BF),jax.ShapeDtypeStruct((n,2,padded,width),BF)],
        scratch_shapes=[pltpu.VMEM((feat,width),BF),pltpu.VMEM((2,padded,feat),F32),pltpu.SemaphoreType.DMA((4*nk,))],
        name="project",
        compiler_params=pltpu.CompilerParams(vmem_limit_bytes=50<<20),
        cost_estimate=pl.CostEstimate(flops=n*4*padded*feat*width,bytes_accessed=24<<20,transcendentals=0),
    )(at,x_own,x_oth,gain[None],shift[None],bias[None],*[wa[k] for k in keys],*[wb[k] for k in keys])

def gather_kernel(keys,at_ref,*refs):
    nk=len(keys)
    place(at_ref,keys,1,refs[0].shape[0],refs[:2*nk],refs[2*nk],refs[2*nk+1],True)

def gather_rows(at,pa,pb):
    keys=sorted(pa); nk=len(keys)
    rows,feat=pa[keys[0]].shape
    return pl.pallas_call(functools.partial(gather_kernel,keys),in_specs=[SM]+[ANY]*(2*nk),out_specs=ANY,
        out_shape=jax.ShapeDtypeStruct((2*nk*rows,feat),BF),scratch_shapes=[pltpu.SemaphoreType.DMA((2*nk,))],name="gather_rows",
    )(at,*[pa[k] for k in keys],*[pb[k] for k in keys])

def middle_kernel(own_ref,oth_ref,mo_ref,mt_ref,wo_ref,wt_ref,bias_ref,gain_ref,shift_ref,x2_ref,h2_ref,buf):
    for s,src in enumerate((own_ref,oth_ref)):
        v=wide_rows(buf.at[s],src[0])
        v=v+(dot(mo_ref[0,s],wo_ref[...])+dot(mt_ref[0,1-s],wt_ref[...]))+bias_ref[...]
        x2_ref[0,s]=v
        h2_ref[0,s]=(norm_parts(v)[0]*gain_ref[...]+shift_ref[...]).astype(BF)

def middle(x_own,x_oth,mixed,mixed_oth,w_own,w_oth,bias,gain,shift):
    n,half,feat=x_own.shape
    _,_,padded,width=mixed.shape
    tok=pl.BlockSpec((1,half,feat),lambda i:(i,0,0))
    mix=pl.BlockSpec((1,2,padded,width),lambda i:(i,0,0,0))
    swp=pl.BlockSpec((1,2,padded,width),lambda i:(i,0,0,0))
    full=pl.BlockSpec((width,feat),lambda i:(0,0))
    row=pl.BlockSpec((1,feat),lambda i:(0,0))
    out=pl.BlockSpec((1,2,padded,feat),lambda i:(i,0,0,0))
    return pl.pallas_call(middle_kernel,grid=(n,),in_specs=[tok,tok,mix,swp,full,full,row,row,row],out_specs=[out,out],
        out_shape=[jax.ShapeDtypeStruct((n,2,padded,feat),F32),jax.ShapeDtypeStruct((n,2,padded,feat),BF)],
        scratch_shapes=[pltpu.VMEM((2,padded,feat),F32)],name="middle",
        compiler_params=pltpu.CompilerParams(vmem_limit_bytes=50<<20),
        cost_estimate=pl.CostEstimate(flops=n*8*padded*feat*width,bytes_accessed=26<<20,transcendentals=0),
    )(x_own,x_oth,mixed,mixed_oth,w_own,w_oth,bias[None],gain[None],shift[None])

def middle_back_kernel(x2_ref,da_ref,db_ref,go_ref,gt_ref,mix_ref,w_ref,gain_ref,dx_ref,dat_ref,gw_ref,sum_ref,buf,acc):
    i=pl.program_id(0)
    @pl.when(i==0)
    def _():
        acc[...]=jnp.zeros_like(acc); sum_ref[...]=jnp.zeros_like(sum_ref)
    for s,src in enumerate((go_ref,gt_ref)):
        dd=wide_rows(buf.at[s],src[0])
        grad=da_ref[0,s].astype(F32)+db_ref[0,1-s].astype(F32)
        dx,gg=norm_back(x2_ref[0,s],gain_ref[...],grad)
        dx=dx+dd
        dob=dx.astype(BF)
        if s==0:
            dx_ref[0]=dx
            for r,t in enumerate((gg,grad,dob.astype(F32),dd)):
                sum_ref[r:r+1,:]+=jnp.sum(t,axis=0,keepdims=True)
        dat_ref[0,s]=dot(dob,w_ref[...],NT).astype(BF)
        acc[...]+=dot(mix_ref[0,s],dob,TN)
    @pl.when(i==pl.num_programs(0)-1)
    def _(): gw_ref[...]=acc[...].astype(BF)

def middle_back(x2,dh_own,dh_oth,g_own,g_oth,mixed,w_own,gain):
    n,half,feat=g_own.shape
    _,_,padded,width=mixed.shape
    tok=pl.BlockSpec((1,half,feat),lambda i:(i,0,0))
    mix=pl.BlockSpec((1,2,padded,width),lambda i:(i,0,0,0))
    big=pl.BlockSpec((1,2,padded,feat),lambda i:(i,0,0,0))
    full=pl.BlockSpec((width,feat),lambda i:(0,0))
    return pl.pallas_call(middle_back_kernel,grid=(n,),
        in_specs=[big,big,big,tok,tok,mix,full,pl.BlockSpec((1,feat),lambda i:(0,0))],
        out_specs=[pl.BlockSpec((1,padded,feat),lambda i:(i,0,0)),mix,full,pl.BlockSpec((8,feat),lambda i:(0,0))],
        out_shape=[jax.ShapeDtypeStruct((n,padded,feat),F32),jax.ShapeDtypeStruct(mixed.shape,BF),jax.ShapeDtypeStruct((width,feat),BF),jax.ShapeDtypeStruct((8,feat),F32)],
        scratch_shapes=[pltpu.VMEM((2,padded,feat),F32),pltpu.VMEM((width,feat),F32)],name="middle_back",
        compiler_params=pltpu.CompilerParams(vmem_limit_bytes=56<<20),
        cost_estimate=pl.CostEstimate(flops=n*8*padded*feat*width,bytes_accessed=30<<20,transcendentals=0),
    )(x2,dh_own,dh_oth,g_own,g_oth,mixed,w_own,gain[None])

def grad_in_kernel(keys,tile,at_ref,h_ref,d_ref,*refs):
    nk=len(keys)
    pieces=refs[:2*nk]; buf,sem=refs[2*nk:]
    for t in range(0,h_ref.shape[1],tile):
        buf[t:t+tile,:]=dot(h_ref[:,t:t+tile],d_ref[...],TN).astype(BF)
    place(at_ref,keys,2,pieces[0].shape[1],pieces,buf,sem,False)

def grad_in(at,h1,dqkv,keys,rows):
    tokens,feat=h1.shape; width=dqkv.shape[1]
    nk=len(keys)
    out=pl.pallas_call(functools.partial(grad_in_kernel,keys,256),in_specs=[SM,VM,VM],out_specs=[ANY]*(2*nk),
        out_shape=[jax.ShapeDtypeStruct((2,rows,width),BF)]*(2*nk),
        scratch_shapes=[pltpu.VMEM((feat,width),BF),pltpu.SemaphoreType.DMA((4*nk,))],name="grad_in",
        compiler_params=pltpu.CompilerParams(vmem_limit_bytes=50<<20),
        cost_estimate=pl.CostEstimate(flops=2*tokens*feat*width,bytes_accessed=14<<20,transcendentals=0),
    )(at,h1,dqkv)
    return dict(zip(keys,out[:nk])),dict(zip(keys,out[nk:]))

def project_back_kernel(keys,at_ref,d_ref,*refs):
    nk=len(keys)
    pieces=refs[:2*nk]; own_ref,oth_ref,w,sem=refs[2*nk:]
    @pl.when(pl.program_id(0)==0)
    def _(): place(at_ref,keys,2,pieces[0].shape[1],pieces,w,sem,True)
    own_ref[0]=dot(d_ref[0,0],w[...],NT)
    oth_ref[0]=dot(d_ref[0,1],w[...],NT).astype(BF)

def project_back(at,dqkv,wa,wb):
    keys=sorted(wa); nk=len(keys)
    n,_,padded,width=dqkv.shape
    feat=wa[keys[0]].shape[1]*4*nk
    out=pl.BlockSpec((1,padded,feat),lambda i:(i,0,0))
    return pl.pallas_call(functools.partial(project_back_kernel,keys),grid=(n,),
        in_specs=[SM,pl.BlockSpec((1,2,padded,width),lambda i:(i,0,0,0))]+[ANY]*(2*nk),out_specs=[out,out],
        out_shape=[jax.ShapeDtypeStruct((n,padded,feat),F32),jax.ShapeDtypeStruct((n,padded,feat),BF)],
        scratch_shapes=[pltpu.VMEM((feat,width),BF),pltpu.SemaphoreType.DMA((4*nk,))],name="project_back",
        compiler_params=pltpu.CompilerParams(vmem_limit_bytes=50<<20),
        cost_estimate=pl.CostEstimate(flops=n*4*padded*feat*width,bytes_accessed=18<<20,transcendentals=0),
    )(at,dqkv,*[wa[k] for k in keys],*[wb[k] for k in keys])

def input_back_kernel(x_ref,da_ref,db_ref,dx_ref,gain_ref,out_ref,sum_ref,buf):
    @pl.when(pl.program_id(0)==0)
    def _(): sum_ref[...]=jnp.zeros_like(sum_ref)
    half=x_ref.shape[1]
    v=wide_rows(buf,x_ref[0])
    grad=da_ref[0]+db_ref[0].astype(F32)
    dx,gg=norm_back(v,gain_ref[...],grad)
    out_ref[0]=(dx+dx_ref[0]).astype(BF)[:half]
    sum_ref[0:1,:]+=jnp.sum(gg,axis=0,keepdims=True)
    sum_ref[1:2,:]+=jnp.sum(grad,axis=0,keepdims=True)

def input_back(x_own,dh_own,dh_oth,dx2,gain):
    n,half,feat=x_own.shape
    padded=dx2.shape[1]
    tok=pl.BlockSpec((1,half,feat),lambda i:(i,0,0))
    big=pl.BlockSpec((1,padded,feat),lambda i:(i,0,0))
    return pl.pallas_call(input_back_kernel,grid=(n,),in_specs=[tok,big,big,big,pl.BlockSpec((1,feat),lambda i:(0,0))],
        out_specs=[tok,pl.BlockSpec((8,feat),lambda i:(0,0))],
        out_shape=[jax.ShapeDtypeStruct(x_own.shape,BF),jax.ShapeDtypeStruct((8,feat),F32)],
        scratch_shapes=[pltpu.VMEM((padded,feat),F32)],name="input_back",
        compiler_params=pltpu.CompilerParams(vmem_limit_bytes=40<<20),
        cost_estimate=pl.CostEstimate(flops=n*20*padded*feat,bytes_accessed=14<<20,transcendentals=0),
    )(x_own,dh_own,dh_oth,dx2,gain[None])


def shift(value, axis, up):
    n = lax.axis_size(axis)
    return lax.ppermute(value, axis, [(i, (i + up) % n) for i in range(n)])


def crossed(value):
    return lax.ppermute(value, ("seq", "core"), [(0, 0), (1, 2), (2, 1), (3, 3)])


def small_sum(value, axes):
    for axis in axes:
        n = lax.axis_size(axis)
        moved, total = value, value
        for _ in range(n - 1):
            moved = shift(moved, axis, 1)
            total = total + moved
        value = total
    return value


def gather_list(piece, axis):
    out = [piece]
    for _ in range(lax.axis_size(axis) - 1):
        out.append(shift(out[-1], axis, -1))
    return out


def gather_plane(piece, first, second):
    out = {}
    for i, one in enumerate(gather_list(piece, first)):
        for j, two in enumerate(gather_list(one, second)):
            out[(j, i) if first == "x" else (i, j)] = two
    return out


def reduce_list(pieces, axis):
    total = pieces[-1]
    for piece in pieces[-2::-1]:
        total = (shift(total, axis, 1).astype(F32) + piece.astype(F32)).astype(BF)
    return total


def reduce_plane(pieces, first, second):
    n_first, n_second = lax.axis_size(first), lax.axis_size(second)
    part = []
    for i in range(n_first):
        row = [pieces[(j, i) if first == "x" else (i, j)] for j in range(n_second)]
        part.append(reduce_list(row, second))
    return reduce_list(part, first)


def adam_update(master, first_moment, second_moment, gradient, step_rate, bias_one, bias_two):
    first_new = 0.5 * first_moment + 0.5 * gradient
    second_new = 0.5 * second_moment + 0.5 * gradient * gradient
    update = first_new / bias_one / (jnp.sqrt(second_new / bias_two) + ADAM_EPS)
    master_new = master - step_rate * (update + WEIGHT_DECAY * master)
    return (master_new, first_new, second_new)


def on_device(images, key_mask, out_grad, step_count, *params):
    masters, firsts, seconds = params[0:5], params[5:10], params[10:15]
    in_weights, out_weights, up_weights, down_weights, vectors = masters
    image_count, half, features = images.shape
    padded = -(-half // PAD_ROWS) * PAD_ROWS
    h, c = lax.axis_index("seq"), lax.axis_index("core")
    y, x = lax.axis_index("y"), lax.axis_index("x")
    ny, nx = lax.axis_size("y"), lax.axis_size("x")
    shards = 4 * ny * nx
    shard = ((h * ny + y) * nx + x) * 2 + c
    at = jnp.stack([h, y, x, c, jnp.int32(ny), jnp.int32(nx), jnp.int32(0), jnp.int32(0)]).astype(jnp.int32)

    placed = jnp.where(
        lax.broadcasted_iota(jnp.int32, (shards, 1), 0) == shard, vectors.astype(BF)[None, :], jnp.zeros((), BF)
    )
    full_vec = small_sum(placed, SHARD).reshape(-1).astype(F32)
    gain_one, shift_one, query_bias, value_bias, out_bias, gain_two, shift_two, down_bias = (
        full_vec[i * D : (i + 1) * D] for i in range(8)
    )
    up_bias = full_vec[8 * D :]

    rows_in = in_weights.shape[0]
    by_core = in_weights.astype(BF).reshape(rows_in, 3, 2, HALF_D)
    mine = jnp.where(c == 0, by_core[:, :, 0], by_core[:, :, 1]).reshape(rows_in, 3 * HALF_D)
    theirs = jnp.where(c == 0, by_core[:, :, 1], by_core[:, :, 0]).reshape(rows_in, 3 * HALF_D)
    in_a = jnp.stack(gather_list(mine, "seq"))
    in_b = jnp.stack(gather_list(shift(theirs, "core", 1), "seq"))
    in_a = gather_plane(in_a, "x", "y")
    in_b = gather_plane(in_b, "y", "x")
    keys = sorted(in_a)

    out_low = out_weights.astype(BF)
    rows_out = out_low.shape[0]
    out_a = gather_plane(crossed(out_low), "x", "y")
    out_b = gather_plane(crossed(shift(out_low, "core", 1)), "y", "x")
    my_out = gather_rows(at, out_a, out_b)
    other_out = shift(my_out, "core", 1)

    rows_ff = up_weights.shape[0]
    half_ff = rows_ff // 2
    updown = [jnp.stack([up_weights[r].astype(BF), down_weights[r].astype(BF)]) for r in (slice(0, half_ff), slice(half_ff, rows_ff))]
    ff_a = gather_plane(jnp.stack(gather_list(updown[0], "seq")), "x", "y")
    ff_b = gather_plane(jnp.stack(gather_list(updown[1], "seq")), "y", "x")

    x_own = crossed(images)
    x_oth = shift(x_own, "core", 1)
    g_own = crossed(out_grad)
    g_oth = shift(g_own, "core", 1)
    mask = key_mask.astype(F32)
    mask = jnp.where(h == c, mask, shift(mask, "core", 1)).reshape(image_count, 2, half)
    mask = jnp.where(c == 0, mask, mask[:, ::-1])
    mask = jnp.pad(mask, ((0, 0), (0, 0), (0, padded - half))).reshape(image_count, 2 * padded)
    key_fill = jnp.broadcast_to(jnp.where(mask > 0, 0.0, NEG_FILL)[..., None], mask.shape + (128,)).astype(BF)

    q_bias = lax.dynamic_slice(query_bias, (c * HALF_D,), (HALF_D,))
    v_bias = lax.dynamic_slice(value_bias, (c * HALF_D,), (HALF_D,))
    in_bias = jnp.concatenate([q_bias, jnp.zeros_like(q_bias), v_bias])
    h1, qkv = project(at, x_own, x_oth, gain_one, shift_one, in_bias, in_a, in_b, padded)
    tokens = image_count * 2 * padded
    qkv = qkv.reshape(image_count, 2 * padded, 3 * HALF_D)
    mixed, lse = attend(qkv, key_fill)
    halved = mixed.reshape(image_count, 2, padded, HALF_D)
    mixed_oth = shift(halved, "core", 1)
    x2, h2 = middle(x_own, x_oth, halved, mixed_oth, my_out, other_out, out_bias, gain_two, shift_two)

    grad_a, grad_b, y_own, y_oth, dh2, g_bu = mlp(
        at, h2.reshape(tokens, D), g_own, g_oth, up_bias.reshape(shards * 2, half_ff), ff_a, ff_b
    )
    share_ff = []
    for grads, order in ((grad_a, ("x", "y")), (grad_b, ("y", "x"))):
        total = reduce_plane(grads, *order)
        share_ff.append(reduce_list([total[0], total[1]], "seq"))
    share_ff = jnp.concatenate(share_ff, axis=1)
    result = y_own[:, :half] + shift(y_oth, "core", 1)[:, :half].astype(F32) + x2[:, 0, :half] + down_bias
    activations = crossed(result.astype(BF)).astype(F32)

    dh2 = dh2.reshape(image_count, 2, padded, D)
    dh2_oth = shift(dh2, "core", 1)
    dx2, dattn, g_out, sums_two = middle_back(x2, dh2, dh2_oth, g_own, g_oth, halved, my_out, gain_two)
    g_out = g_out.reshape(ny, nx, 2, rows_out, D)
    oa, ob = {}, {}
    for ky, kx in keys:
        spot = ((y + ky) % ny, (x + kx) % nx)
        oa[ky, kx] = lax.dynamic_slice(g_out, (*spot, h, 0, 0), (1, 1, 1, rows_out, D)).reshape(rows_out, D)
        ob[ky, kx] = lax.dynamic_slice(g_out, (*spot, 1 - h, 0, 0), (1, 1, 1, rows_out, D)).reshape(rows_out, D)
    keep = crossed(reduce_plane(oa, "x", "y"))
    give = crossed(reduce_plane(ob, "y", "x"))
    share_out = (keep.astype(F32) + shift(give, "core", 1).astype(F32)).astype(BF)

    dqkv, sums_qkv = attend_back(qkv, key_fill, mixed, dattn.reshape(mixed.shape), lse)
    ia, ib = grad_in(at, h1.reshape(tokens, D), dqkv.reshape(tokens, 3 * HALF_D), keys, rows_in)
    ia = reduce_plane(ia, "x", "y")
    ib = reduce_plane(ib, "y", "x")
    ia, ib = reduce_list([ia[0], ia[1]], "seq"), reduce_list([ib[0], ib[1]], "seq")
    ib = shift(ib, "core", 1)
    ia, ib = (t.reshape(rows_in, 3, 1, HALF_D) for t in (ia, ib))
    share_in = jnp.where(c == 0, jnp.concatenate([ia, ib], 2), jnp.concatenate([ib, ia], 2)).reshape(rows_in, 3 * D)

    dh_own, dh_oth = project_back(at, dqkv.reshape(image_count, 2, padded, 3 * HALF_D), in_a, in_b)
    input_grad, sums_one = input_back(x_own, dh_own, shift(dh_oth, "core", 1), dx2, gain_one)
    input_grad = crossed(input_grad).astype(F32)

    zero = jnp.zeros((D,), F32)
    grad_vec = jnp.concatenate(
        [
            sums_one[0],
            sums_one[1],
            lax.dynamic_update_slice(zero, sums_qkv[0, :HALF_D], (c * HALF_D,)),
            lax.dynamic_update_slice(zero, sums_qkv[0, 2 * HALF_D :], (c * HALF_D,)),
            sums_two[2],
            sums_two[0],
            sums_two[1],
            sums_two[3],
            g_bu.reshape(-1),
        ]
    ).reshape(shards, -1)
    grad_vec = small_sum(grad_vec, AXES)
    share_vec = lax.dynamic_slice(grad_vec, (shard, 0), (1, grad_vec.shape[1])).reshape(-1)

    def over_dp(share):
        return small_sum(share, ("dp",)).astype(F32)

    shares = (over_dp(share_in), over_dp(share_out), over_dp(share_ff[0]), over_dp(share_ff[1]), share_vec)
    square = sum(jnp.sum(s * s) for s in shares)
    square = small_sum(jnp.full((8, 128), square), SHARD)[0, 0]
    grad_norm = jnp.sqrt(square)
    threshold = 0.5 * math.sqrt(4 * D * D + 2 * D * FF + 12 * D)
    clip_factor = jnp.minimum(1.0, threshold / grad_norm)
    bias = 1.0 - jnp.power(F32(0.5), step_count.astype(F32))
    rates = ((D // 2) ** (-0.5), (D // 4) ** (-0.5), D ** (-0.5), FF ** (-0.5), 0.2)
    results = [
        adam_update(masters[i], firsts[i], seconds[i], shares[i] * clip_factor, rates[i], bias, bias) for i in range(5)
    ]
    return (
        grad_norm,
        *(r[0] for r in results),
        *(r[1] for r in results),
        *(r[2] for r in results),
        *(r[0].astype(BF) for r in results),
        activations,
        input_grad,
    )


def solution(mesh):
    seq_n, fsdp_n, dp_n = (mesh.shape[a] for a in ("seq", "fsdp", "dp"))
    nx = math.isqrt(fsdp_n // 2)
    ny = fsdp_n // 2 // nx
    grid = Mesh(np.asarray(mesh.devices).reshape(seq_n, ny, nx, 2, dp_n), AXES)
    tokens = P(("y", "x", "core", "dp"), "seq", None)
    matrix, vector = P(SHARD, None), P(SHARD)
    five = (matrix, matrix, matrix, matrix, vector)
    return jax.shard_map(
        on_device,
        mesh=grid,
        in_specs=(tokens, P(("y", "x", "core", "dp"), None), tokens, P()) + five * 3,
        out_specs=(P(),) + five * 4 + (tokens, tokens),
        check_vma=False,
    )
```

```python
import functools
import math

import jax
import jax.numpy as jnp
import numpy as np
from jax import lax
from jax.experimental import pallas as pl
from jax.experimental.pallas import tpu as pltpu
from jax.sharding import Mesh
from jax.sharding import PartitionSpec as P

D = 1024
FF = 4096
PAD_ROWS = 16

NEG_FILL = -1000000000.0
ADAM_EPS = 1e-08
WEIGHT_DECAY = 0.05
AXES = ("seq", "y", "x", "core", "dp")
SHARD = ("seq", "y", "x", "core")

BF=jnp.bfloat16; F32=jnp.float32
def dot(a, b, dims=(((1,), (0,)), ((), ()))):
    return lax.dot_general(a, b, dims, preferred_element_type=F32)
NT=(((1,),(1,)),((),()))
TN=(((0,),(0,)),((),()))
ANY=pl.BlockSpec(memory_space=pl.ANY)
VM=pl.BlockSpec(memory_space=pltpu.VMEM)
SM=pl.BlockSpec(memory_space=pltpu.SMEM)

def gelu_both(u):
    c0=math.sqrt(2/math.pi)
    sq=u*u
    t=jnp.tanh(u*(c0+(c0*0.044715)*sq))
    half=0.5+0.5*t
    value=u*half
    slope=half+(0.5*u)*(1.0-t*t)*(c0+(3*c0*0.044715)*sq)
    return value,slope

def mlp_kernel(keys,*refs,gtile):
    nk=len(keys)
    at_ref,h2_ref,go_ref,gt_ref,bu_ref=refs[:5]
    pa,pb=refs[5:5+nk],refs[5+nk:5+2*nk]
    o=5+2*nk
    ga,gb=refs[o:o+nk],refs[o+nk:o+2*nk]
    yown_ref,yoth_ref,dh_ref,gbu_ref=refs[o+2*nk:o+2*nk+4]
    w,dd,a_all,du_all,y_acc,dh_acc,g_out,wsem,gsem=refs[o+2*nk+4:]
    images,half,feat=go_ref.shape
    hid=pa[0].shape[2]
    width=4*hid
    padded=h2_ref.shape[0]//(2*images)
    blocks=2*images

    def load(i,slot,go):
        for ki in range(nk):
            @pl.when(i==ki)
            def _():
                for kz in range(2):
                    for ud in range(2):
                        for ab,src in enumerate((pa[ki],pb[ki])):
                            cp=pltpu.make_async_copy(src.at[kz,ud],w.at[slot,ud,pl.ds((kz*2+ab)*hid,hid)],wsem.at[slot,kz*4+ud*2+ab])
                            cp.start() if go else cp.wait()
    def save(i,go):
        for ki in range(nk):
            @pl.when(i==ki)
            def _():
                for kz in range(2):
                    for ud in range(2):
                        for ab,dst in enumerate((ga[ki],gb[ki])):
                            cp=pltpu.make_async_copy(g_out.at[ud,pl.ds((kz*2+ab)*hid,hid)],dst.at[kz,ud],gsem.at[kz*4+ud*2+ab])
                            cp.start() if go else cp.wait()
    load(0,0,True)
    gbu_ref[...]=jnp.zeros_like(gbu_ref)
    for i in range(images):
        for s,src in enumerate((go_ref,gt_ref)):
            r=(2*i+s)*padded
            tail=padded-16
            dd[r+tail:r+padded,:]=jnp.zeros((16,feat),BF)
            dd[r:r+half,:]=src[i]
    def step(i,_):
        slot=lax.rem(i,2)
        load(i,slot,False)
        @pl.when(i+1<nk)
        def _(): load(i+1,1-slot,True)
        rows=[]
        for kz in range(2):
            for ab in range(2):
                row=jnp.int32(0)
                for ki,(ky,kx) in enumerate(keys):
                    z=lax.rem(at_ref[0]+kz,2); y=lax.rem(at_ref[1]+ky,at_ref[4]); x=lax.rem(at_ref[2]+kx,at_ref[5])
                    here=(((z*at_ref[4]+y)*at_ref[5]+x)*2+at_ref[3])*2+ab
                    row=jnp.where(i==ki,here,row)
                rows.append(row)
        bias=jnp.concatenate([bu_ref[pl.ds(r,1),:] for r in rows],axis=1)
        wu=w.at[slot,0]; wd=w.at[slot,1]
        def tokens(b,sums):
            r=pl.ds(pl.multiple_of(b*padded,16),padded)
            u=dot(h2_ref[r,:],wu[...],NT)+bias
            value,slope=gelu_both(u)
            a=value.astype(BF)
            a_all[r,:]=a
            dg=dot(dd[r,:],wd[...],NT)
            du=(dg*slope).astype(BF)
            du_all[r,:]=du
            ynew=dot(a,wd[...]); dnew=dot(du,wu[...])
            @pl.when(i==0)
            def _():
                y_acc[r,:]=ynew; dh_acc[r,:]=dnew
            @pl.when(i>0)
            def _():
                y_acc[r,:]+=ynew; dh_acc[r,:]+=dnew
            return sums+jnp.sum(du.astype(F32),axis=0,keepdims=True)
        sums=lax.fori_loop(0,blocks,tokens,jnp.zeros((1,width),F32))
        for q,row in enumerate(rows):
            gbu_ref[pl.ds(row,1),:]=sums[:,q*hid:(q+1)*hid]
        @pl.when(i>0)
        def _(): save(i-1,False)
        for t in range(0,width,gtile):
            g_out[1,t:t+gtile,:]=dot(a_all[:,t:t+gtile],dd[...],TN).astype(BF)
            g_out[0,t:t+gtile,:]=dot(du_all[:,t:t+gtile],h2_ref[...],TN).astype(BF)
        save(i,True)
        return 0
    lax.fori_loop(0,nk,step,0)
    for i in range(images):
        r=2*i*padded
        yown_ref[i]=y_acc[r:r+padded,:]
        yoth_ref[i]=y_acc[r+padded:r+2*padded,:].astype(BF)
    dh_ref[...]=dh_acc[...].astype(BF)
    save(nk-1,False)

def mlp(at,h2,g_own,g_oth,bu_rows,fa,fb,gtile=256):
    keys=sorted(fa); nk=len(keys)
    images,half,feat=g_own.shape
    tokens=h2.shape[0]; padded=tokens//(2*images)
    _,_,hid,_=fa[keys[0]].shape
    width=4*hid
    piece=jax.ShapeDtypeStruct(fa[keys[0]].shape,BF)
    out=pl.pallas_call(functools.partial(mlp_kernel,keys,gtile=min(gtile,width)),
        in_specs=[SM]+[VM]*4+[ANY]*(2*nk),
        out_specs=[ANY]*(2*nk)+[VM]*4,
        out_shape=[piece]*(2*nk)+[jax.ShapeDtypeStruct((images,padded,feat),F32),jax.ShapeDtypeStruct((images,padded,feat),BF),
            jax.ShapeDtypeStruct((tokens,feat),BF),jax.ShapeDtypeStruct(bu_rows.shape,F32)],
        scratch_shapes=[pltpu.VMEM((2,2,width,feat),BF),pltpu.VMEM((tokens,feat),BF),pltpu.VMEM((tokens,width),BF),pltpu.VMEM((tokens,width),BF),
            pltpu.VMEM((tokens,feat),F32),pltpu.VMEM((tokens,feat),F32),pltpu.VMEM((2,width,feat),BF),
            pltpu.SemaphoreType.DMA((2,8)),pltpu.SemaphoreType.DMA((8,))],
        name="feed_forward",
        compiler_params=pltpu.CompilerParams(vmem_limit_bytes=60<<20),
        cost_estimate=pl.CostEstimate(flops=nk*6*2*tokens*feat*width,bytes_accessed=40<<20,transcendentals=nk*tokens*width),
    )(at,h2,g_own,g_oth,bu_rows,*[fa[k] for k in keys],*[fb[k] for k in keys])
    return dict(zip(keys,out[:nk])),dict(zip(keys,out[nk:2*nk])),out[2*nk],out[2*nk+1],out[2*nk+2],out[2*nk+3]

HD=64; HALF_D=512

def head_operands(q_ref,k_ref,kb_ref,scale):
    q=q_ref[0].astype(F32)*scale; k=k_ref[0].astype(F32); kb=kb_ref[0].astype(F32)
    lane=lax.broadcasted_iota(jnp.int32,q.shape,1)
    low=lane<HD
    one=jnp.where((lane==0)|(lane==HD),1.0,0.0)
    qs=[jnp.where(low,q,one).astype(BF),jnp.where(low,one,q).astype(BF)]
    ks=[jnp.where(low,k,kb).astype(BF),jnp.where(low,kb,k).astype(BF)]
    return q,k,low,qs,ks

def attend_kernel(q_ref,k_ref,v_ref,kb_ref,o_ref,lse_ref):
    q,k,low,qs,ks=head_operands(q_ref,k_ref,kb_ref,HD**-0.5)
    vt=v_ref[0].astype(F32).T.astype(BF)
    outs=[]
    for j in range(2):
        s=dot(ks[j],qs[j],NT)
        m=jnp.max(s,axis=0,keepdims=True)
        e=jnp.exp(s-m)
        l=jnp.sum(e,axis=0,keepdims=True)
        o=dot(vt[j*HD:(j+1)*HD],e.astype(BF))
        outs.append(o*(1.0/l))
        lse_ref[0,0,j:j+1,:]=m+jnp.log(l)
    o_ref[0]=jnp.concatenate(outs,axis=0).T.astype(BF)

def attend(qkv,kbias):
    n,rows,w=qkv.shape; pairs=w//3//128
    blk=lambda off: pl.BlockSpec((1,rows,128),lambda i,p: (i,0,off+p))
    return pl.pallas_call(attend_kernel,grid=(n,pairs),
        in_specs=[blk(0),blk(pairs),blk(2*pairs),pl.BlockSpec((1,rows,128),lambda i,p:(i,0,0))],
        out_specs=[blk(0),pl.BlockSpec((1,1,8,rows),lambda i,p:(i,p,0,0))],
        out_shape=[jax.ShapeDtypeStruct((n,rows,w//3),BF),jax.ShapeDtypeStruct((n,pairs,8,rows),F32)],
        name="attend",
        compiler_params=pltpu.CompilerParams(vmem_limit_bytes=50<<20),
        cost_estimate=pl.CostEstimate(flops=n*pairs*8*rows*rows*128,bytes_accessed=n*rows*w*3,transcendentals=n*pairs*2*rows*rows),
    )(qkv,qkv,qkv,kbias)

def attend_back_kernel(q_ref,k_ref,v_ref,kb_ref,o_ref,g_ref,lse_ref,out_ref,sum_ref,*,pairs,chunk):
    p=pl.program_id(1)
    @pl.when((pl.program_id(0)==0)&(p==0))
    def _(): sum_ref[...]=jnp.zeros_like(sum_ref)
    scale=HD**-0.5
    q,k,low,qs,ks=head_operands(q_ref,k_ref,kb_ref,scale)
    qb=q.astype(BF)
    kt=k.T.astype(BF)
    g=g_ref[0]; gf=g.astype(F32)
    prod=(gf*o_ref[0].astype(F32)).T
    v=v_ref[0]
    rows=q.shape[0]
    dqs=[];dks=[];dvs=[]
    for j in range(2):
        gj=(jnp.where(low,gf,0.0) if j==0 else jnp.where(low,0.0,gf)).astype(BF)
        delta=jnp.sum(prod[j*HD:(j+1)*HD],axis=0,keepdims=True)
        lse=lse_ref[0,0,j:j+1,:]
        dq=None; dk=[]; dv=[]
        for r in range(0,rows,chunk):
            s=dot(ks[j][r:r+chunk],qs[j],NT)
            pr=jnp.exp(s-lse)
            dp=dot(v[r:r+chunk],gj,NT)
            ds=(pr*(dp-delta)).astype(BF)
            dv.append(dot(pr.astype(BF),g))
            dk.append(dot(ds,qb))
            t=dot(kt[j*HD:(j+1)*HD,r:r+chunk],ds) if chunk==rows else dot(k[r:r+chunk].astype(BF),ds,TN)[j*HD:(j+1)*HD]
            dq=t if dq is None else dq+t
        dqs.append(dq)
        dks.append(jnp.concatenate(dk,axis=0) if len(dk)>1 else dk[0]); dvs.append(jnp.concatenate(dv,axis=0) if len(dv)>1 else dv[0])
    parts=((jnp.concatenate(dqs,axis=0)*scale).T.astype(BF),jnp.where(low,dks[0],dks[1]).astype(BF),jnp.where(low,dvs[0],dvs[1]).astype(BF))
    for t,part in enumerate(parts):
        at=pl.ds(pl.multiple_of((t*pairs+p)*128,128),128)
        out_ref[0,:,at]=part
        sum_ref[0:1,at]+=jnp.sum(part.astype(F32),axis=0,keepdims=True)

def attend_back(qkv,kbias,mixed,grad,lse,chunk=None):
    n,rows,w=qkv.shape; pairs=w//3//128
    chunk=chunk or rows
    blk=lambda off: pl.BlockSpec((1,rows,128),lambda i,p: (i,0,off+p))
    return pl.pallas_call(functools.partial(attend_back_kernel,pairs=pairs,chunk=chunk),grid=(n,pairs),
        in_specs=[blk(0),blk(pairs),blk(2*pairs),pl.BlockSpec((1,rows,128),lambda i,p:(i,0,0)),blk(0),blk(0),pl.BlockSpec((1,1,8,rows),lambda i,p:(i,p,0,0))],
        out_specs=[pl.BlockSpec((1,rows,w),lambda i,p:(i,0,0)),pl.BlockSpec((8,w),lambda i,p:(0,0))],
        out_shape=[jax.ShapeDtypeStruct((n,rows,w),BF),jax.ShapeDtypeStruct((8,w),F32)],
        name="attend_back",
        compiler_params=pltpu.CompilerParams(vmem_limit_bytes=50<<20),
        cost_estimate=pl.CostEstimate(flops=n*pairs*20*rows*rows*128,bytes_accessed=n*rows*w*5,transcendentals=n*pairs*2*rows*rows),
    )(qkv,qkv,qkv,kbias,mixed,grad,lse)

NORM_EPS=1e-6
def norm_parts(values):
    center = values - jnp.mean(values, axis=-1, keepdims=True)
    inverse = lax.rsqrt(jnp.mean(center * center, axis=-1, keepdims=True) + NORM_EPS)
    return center * inverse, inverse

def norm_back(values, gain, grad):
    normed, inverse = norm_parts(values)
    scaled = grad * gain
    mean_one = jnp.mean(scaled, axis=-1, keepdims=True)
    mean_two = jnp.mean(scaled * normed, axis=-1, keepdims=True)
    return (scaled - mean_one - normed * mean_two) * inverse, grad * normed

def wide_rows(buf,block):
    n=block.shape[0]; total=buf.shape[0]
    buf[total-16:,:]=jnp.zeros((16,buf.shape[1]),F32)
    buf[0:n,:]=block.astype(F32)
    return buf[...]

def place(at_ref,keys,ka,size,pieces,buf,sem,gather):
    def both(go):
        n=0
        for ki,(ky,kx) in enumerate(keys):
            y=lax.rem(at_ref[1]+ky,at_ref[4]); x=lax.rem(at_ref[2]+kx,at_ref[5])
            for ab in range(2):
                for kz in range(ka):
                    z=lax.rem(at_ref[0]+kz,2) if ka==2 else 0
                    core=at_ref[3] if ab==0 else 1-at_ref[3]
                    if ka==1: core=at_ref[0] if ab==0 else 1-at_ref[0]
                    row=(((z*at_ref[4]+y)*at_ref[5]+x)*2+core)*size
                    inner=buf.at[pl.ds(pl.multiple_of(row,16),size)]
                    piece=pieces[ab*len(keys)+ki]
                    piece=piece.at[kz] if ka==2 else piece
                    cp=pltpu.make_async_copy(piece,inner,sem.at[n]) if gather else pltpu.make_async_copy(inner,piece,sem.at[n])
                    cp.start() if go else cp.wait()
                    n+=1
    both(True); both(False)

def project_kernel(keys,at_ref,own_ref,oth_ref,gain_ref,shift_ref,bias_ref,*refs):
    nk=len(keys)
    pieces=refs[:2*nk]; h_ref,qkv_ref,w,buf,sem=refs[2*nk:]
    @pl.when(pl.program_id(0)==0)
    def _(): place(at_ref,keys,2,pieces[0].shape[1],pieces,w,sem,True)
    for s,src in enumerate((own_ref,oth_ref)):
        v=wide_rows(buf.at[s],src[0])
        h=(norm_parts(v)[0]*gain_ref[...]+shift_ref[...]).astype(BF)
        h_ref[0,s]=h
        qkv_ref[0,s]=(dot(h,w[...])+bias_ref[...]).astype(BF)

def project(at,x_own,x_oth,gain,shift,bias,wa,wb,padded):
    keys=sorted(wa); nk=len(keys)
    n,half,feat=x_own.shape
    width=wa[keys[0]].shape[-1]
    tok=pl.BlockSpec((1,half,feat),lambda i:(i,0,0))
    row=lambda w: pl.BlockSpec((1,w),lambda i:(0,0))
    return pl.pallas_call(functools.partial(project_kernel,keys),grid=(n,),
        in_specs=[SM,tok,tok,row(feat),row(feat),row(width)]+[ANY]*(2*nk),
        out_specs=[pl.BlockSpec((1,2,padded,feat),lambda i:(i,0,0,0)),pl.BlockSpec((1,2,padded,width),lambda i:(i,0,0,0))],
        out_shape=[jax.ShapeDtypeStruct((n,2,padded,feat),BF),jax.ShapeDtypeStruct((n,2,padded,width),BF)],
        scratch_shapes=[pltpu.VMEM((feat,width),BF),pltpu.VMEM((2,padded,feat),F32),pltpu.SemaphoreType.DMA((4*nk,))],
        name="project",
        compiler_params=pltpu.CompilerParams(vmem_limit_bytes=50<<20),
        cost_estimate=pl.CostEstimate(flops=n*4*padded*feat*width,bytes_accessed=24<<20,transcendentals=0),
    )(at,x_own,x_oth,gain[None],shift[None],bias[None],*[wa[k] for k in keys],*[wb[k] for k in keys])

def gather_kernel(keys,at_ref,*refs):
    nk=len(keys)
    place(at_ref,keys,1,refs[0].shape[0],refs[:2*nk],refs[2*nk],refs[2*nk+1],True)

def gather_rows(at,pa,pb):
    keys=sorted(pa); nk=len(keys)
    rows,feat=pa[keys[0]].shape
    return pl.pallas_call(functools.partial(gather_kernel,keys),in_specs=[SM]+[ANY]*(2*nk),out_specs=VM,
        out_shape=jax.ShapeDtypeStruct((2*nk*rows,feat),BF),scratch_shapes=[pltpu.SemaphoreType.DMA((2*nk,))],name="gather_rows",
    )(at,*[pa[k] for k in keys],*[pb[k] for k in keys])

def middle_kernel(own_ref,oth_ref,mo_ref,mt_ref,wo_ref,wt_ref,bias_ref,gain_ref,shift_ref,x2_ref,h2_ref,buf):
    for s,src in enumerate((own_ref,oth_ref)):
        v=wide_rows(buf.at[s],src[0])
        v=v+(dot(mo_ref[0,s],wo_ref[...])+dot(mt_ref[0,1-s],wt_ref[...]))+bias_ref[...]
        x2_ref[0,s]=v
        h2_ref[0,s]=(norm_parts(v)[0]*gain_ref[...]+shift_ref[...]).astype(BF)

def middle(x_own,x_oth,mixed,mixed_oth,w_own,w_oth,bias,gain,shift):
    n,half,feat=x_own.shape
    _,_,padded,width=mixed.shape
    tok=pl.BlockSpec((1,half,feat),lambda i:(i,0,0))
    mix=pl.BlockSpec((1,2,padded,width),lambda i:(i,0,0,0))
    swp=pl.BlockSpec((1,2,padded,width),lambda i:(i,0,0,0))
    full=pl.BlockSpec((width,feat),lambda i:(0,0))
    row=pl.BlockSpec((1,feat),lambda i:(0,0))
    out=pl.BlockSpec((1,2,padded,feat),lambda i:(i,0,0,0))
    return pl.pallas_call(middle_kernel,grid=(n,),in_specs=[tok,tok,mix,swp,full,full,row,row,row],out_specs=[out,out],
        out_shape=[jax.ShapeDtypeStruct((n,2,padded,feat),F32),jax.ShapeDtypeStruct((n,2,padded,feat),BF)],
        scratch_shapes=[pltpu.VMEM((2,padded,feat),F32)],name="middle",
        compiler_params=pltpu.CompilerParams(vmem_limit_bytes=50<<20),
        cost_estimate=pl.CostEstimate(flops=n*8*padded*feat*width,bytes_accessed=26<<20,transcendentals=0),
    )(x_own,x_oth,mixed,mixed_oth,w_own,w_oth,bias[None],gain[None],shift[None])

def middle_back_kernel(x2_ref,da_ref,db_ref,go_ref,gt_ref,mix_ref,w_ref,gain_ref,dx_ref,dat_ref,gw_ref,sum_ref,buf,acc):
    i=pl.program_id(0)
    @pl.when(i==0)
    def _():
        acc[...]=jnp.zeros_like(acc); sum_ref[...]=jnp.zeros_like(sum_ref)
    for s,src in enumerate((go_ref,gt_ref)):
        dd=wide_rows(buf.at[s],src[0])
        grad=da_ref[0,s].astype(F32)+db_ref[0,1-s].astype(F32)
        dx,gg=norm_back(x2_ref[0,s],gain_ref[...],grad)
        dx=dx+dd
        dob=dx.astype(BF)
        if s==0:
            dx_ref[0]=dx
            for r,t in enumerate((gg,grad,dob.astype(F32),dd)):
                sum_ref[r:r+1,:]+=jnp.sum(t,axis=0,keepdims=True)
        dat_ref[0,s]=dot(dob,w_ref[...],NT).astype(BF)
        acc[...]+=dot(mix_ref[0,s],dob,TN)
    @pl.when(i==pl.num_programs(0)-1)
    def _(): gw_ref[...]=acc[...].astype(BF)

def middle_back(x2,dh_own,dh_oth,g_own,g_oth,mixed,w_own,gain):
    n,half,feat=g_own.shape
    _,_,padded,width=mixed.shape
    tok=pl.BlockSpec((1,half,feat),lambda i:(i,0,0))
    mix=pl.BlockSpec((1,2,padded,width),lambda i:(i,0,0,0))
    big=pl.BlockSpec((1,2,padded,feat),lambda i:(i,0,0,0))
    full=pl.BlockSpec((width,feat),lambda i:(0,0))
    return pl.pallas_call(middle_back_kernel,grid=(n,),
        in_specs=[big,big,big,tok,tok,mix,full,pl.BlockSpec((1,feat),lambda i:(0,0))],
        out_specs=[pl.BlockSpec((1,padded,feat),lambda i:(i,0,0)),mix,full,pl.BlockSpec((8,feat),lambda i:(0,0))],
        out_shape=[jax.ShapeDtypeStruct((n,padded,feat),F32),jax.ShapeDtypeStruct(mixed.shape,BF),jax.ShapeDtypeStruct((width,feat),BF),jax.ShapeDtypeStruct((8,feat),F32)],
        scratch_shapes=[pltpu.VMEM((2,padded,feat),F32),pltpu.VMEM((width,feat),F32)],name="middle_back",
        compiler_params=pltpu.CompilerParams(vmem_limit_bytes=56<<20),
        cost_estimate=pl.CostEstimate(flops=n*8*padded*feat*width,bytes_accessed=30<<20,transcendentals=0),
    )(x2,dh_own,dh_oth,g_own,g_oth,mixed,w_own,gain[None])

def grad_in_kernel(keys,tile,at_ref,h_ref,d_ref,*refs):
    nk=len(keys)
    pieces=refs[:2*nk]; buf,sem=refs[2*nk:]
    for t in range(0,h_ref.shape[1],tile):
        buf[t:t+tile,:]=dot(h_ref[:,t:t+tile],d_ref[...],TN).astype(BF)
    place(at_ref,keys,2,pieces[0].shape[1],pieces,buf,sem,False)

def grad_in(at,h1,dqkv,keys,rows):
    tokens,feat=h1.shape; width=dqkv.shape[1]
    nk=len(keys)
    out=pl.pallas_call(functools.partial(grad_in_kernel,keys,256),in_specs=[SM,VM,VM],out_specs=[ANY]*(2*nk),
        out_shape=[jax.ShapeDtypeStruct((2,rows,width),BF)]*(2*nk),
        scratch_shapes=[pltpu.VMEM((feat,width),BF),pltpu.SemaphoreType.DMA((4*nk,))],name="grad_in",
        compiler_params=pltpu.CompilerParams(vmem_limit_bytes=50<<20),
        cost_estimate=pl.CostEstimate(flops=2*tokens*feat*width,bytes_accessed=14<<20,transcendentals=0),
    )(at,h1,dqkv)
    return dict(zip(keys,out[:nk])),dict(zip(keys,out[nk:]))

def project_back_kernel(keys,at_ref,d_ref,*refs):
    nk=len(keys)
    pieces=refs[:2*nk]; own_ref,oth_ref,w,sem=refs[2*nk:]
    @pl.when(pl.program_id(0)==0)
    def _(): place(at_ref,keys,2,pieces[0].shape[1],pieces,w,sem,True)
    own_ref[0]=dot(d_ref[0,0],w[...],NT)
    oth_ref[0]=dot(d_ref[0,1],w[...],NT).astype(BF)

def project_back(at,dqkv,wa,wb):
    keys=sorted(wa); nk=len(keys)
    n,_,padded,width=dqkv.shape
    feat=wa[keys[0]].shape[1]*4*nk
    out=pl.BlockSpec((1,padded,feat),lambda i:(i,0,0))
    return pl.pallas_call(functools.partial(project_back_kernel,keys),grid=(n,),
        in_specs=[SM,pl.BlockSpec((1,2,padded,width),lambda i:(i,0,0,0))]+[ANY]*(2*nk),out_specs=[out,out],
        out_shape=[jax.ShapeDtypeStruct((n,padded,feat),F32),jax.ShapeDtypeStruct((n,padded,feat),BF)],
        scratch_shapes=[pltpu.VMEM((feat,width),BF),pltpu.SemaphoreType.DMA((4*nk,))],name="project_back",
        compiler_params=pltpu.CompilerParams(vmem_limit_bytes=50<<20),
        cost_estimate=pl.CostEstimate(flops=n*4*padded*feat*width,bytes_accessed=18<<20,transcendentals=0),
    )(at,dqkv,*[wa[k] for k in keys],*[wb[k] for k in keys])

def input_back_kernel(x_ref,da_ref,db_ref,dx_ref,gain_ref,out_ref,sum_ref,buf):
    @pl.when(pl.program_id(0)==0)
    def _(): sum_ref[...]=jnp.zeros_like(sum_ref)
    half=x_ref.shape[1]
    v=wide_rows(buf,x_ref[0])
    grad=da_ref[0]+db_ref[0].astype(F32)
    dx,gg=norm_back(v,gain_ref[...],grad)
    out_ref[0]=(dx+dx_ref[0]).astype(BF)[:half]
    sum_ref[0:1,:]+=jnp.sum(gg,axis=0,keepdims=True)
    sum_ref[1:2,:]+=jnp.sum(grad,axis=0,keepdims=True)

def input_back(x_own,dh_own,dh_oth,dx2,gain):
    n,half,feat=x_own.shape
    padded=dx2.shape[1]
    tok=pl.BlockSpec((1,half,feat),lambda i:(i,0,0))
    big=pl.BlockSpec((1,padded,feat),lambda i:(i,0,0))
    return pl.pallas_call(input_back_kernel,grid=(n,),in_specs=[tok,big,big,big,pl.BlockSpec((1,feat),lambda i:(0,0))],
        out_specs=[tok,pl.BlockSpec((8,feat),lambda i:(0,0))],
        out_shape=[jax.ShapeDtypeStruct(x_own.shape,BF),jax.ShapeDtypeStruct((8,feat),F32)],
        scratch_shapes=[pltpu.VMEM((padded,feat),F32)],name="input_back",
        compiler_params=pltpu.CompilerParams(vmem_limit_bytes=40<<20),
        cost_estimate=pl.CostEstimate(flops=n*20*padded*feat,bytes_accessed=14<<20,transcendentals=0),
    )(x_own,dh_own,dh_oth,dx2,gain[None])


def shift(value, axis, up):
    n = lax.axis_size(axis)
    return lax.ppermute(value, axis, [(i, (i + up) % n) for i in range(n)])


def after(value, *others):
    return lax.optimization_barrier((value, others))[0]


def crossing(value):
    return lax.ppermute(value, ("seq", "core"), [(1, 2), (2, 1)])


def pick(own, received):
    return jnp.where(lax.axis_index("seq") == lax.axis_index("core"), own, received)


def crossed(value):
    return pick(value, crossing(value))


def small_sum(value, axes):
    for axis in axes:
        n = lax.axis_size(axis)
        moved, total = value, value
        for _ in range(n - 1):
            moved = shift(moved, axis, 1)
            total = total + moved
        value = total
    return value


def gather_list(piece, axis):
    out = [piece]
    for _ in range(lax.axis_size(axis) - 1):
        out.append(shift(out[-1], axis, -1))
    return out


def gather_plane(piece, first, second, dep=()):
    out = {}
    for i, one in enumerate(gather_list(piece, first)):
        one = after(one, dep) if i else one
        for j, two in enumerate(gather_list(one, second)):
            out[(j, i) if first == "x" else (i, j)] = two
    return out


def reduce_list(pieces, axis, dep):
    total = pieces[-1]
    for piece in pieces[-2::-1]:
        total = (after(shift(total, axis, 1), dep).astype(F32) + piece.astype(F32)).astype(BF)
    return total


def reduce_plane(pieces, first, second, dep_one, dep_two):
    n_first, n_second = lax.axis_size(first), lax.axis_size(second)
    part = []
    for i in range(n_first):
        row = [pieces[(j, i) if first == "x" else (i, j)] for j in range(n_second)]
        part.append(reduce_list(row, second, dep_one))
    return reduce_list(part, first, dep_two)


def adam_update(master, first_moment, second_moment, gradient, step_rate, bias_one, bias_two):
    first_new = 0.5 * first_moment + 0.5 * gradient
    second_new = 0.5 * second_moment + 0.5 * gradient * gradient
    update = first_new / bias_one / (jnp.sqrt(second_new / bias_two) + ADAM_EPS)
    master_new = master - step_rate * (update + WEIGHT_DECAY * master)
    return (master_new, first_new, second_new)


def on_device(images, key_mask, out_grad, step_count, *params):
    masters, firsts, seconds = params[0:5], params[5:10], params[10:15]
    in_weights, out_weights, up_weights, down_weights, vectors = masters
    image_count, half, features = images.shape
    padded = -(-half // PAD_ROWS) * PAD_ROWS
    h, c = lax.axis_index("seq"), lax.axis_index("core")
    y, x = lax.axis_index("y"), lax.axis_index("x")
    ny, nx = lax.axis_size("y"), lax.axis_size("x")
    shards = 4 * ny * nx
    shard = ((h * ny + y) * nx + x) * 2 + c
    at = jnp.stack([h, y, x, c, jnp.int32(ny), jnp.int32(nx), jnp.int32(0), jnp.int32(0)]).astype(jnp.int32)

    placed = jnp.where(
        lax.broadcasted_iota(jnp.int32, (shards, 1), 0) == shard, vectors.astype(BF)[None, :], jnp.zeros((), BF)
    )
    full_vec = small_sum(placed, SHARD).reshape(-1).astype(F32)
    gain_one, shift_one, query_bias, value_bias, out_bias, gain_two, shift_two, down_bias = (
        full_vec[i * D : (i + 1) * D] for i in range(8)
    )
    up_bias = full_vec[8 * D :]

    rows_in = in_weights.shape[0]
    by_core = in_weights.astype(BF).reshape(rows_in, 3, 2, HALF_D)
    mine = jnp.where(c == 0, by_core[:, :, 0], by_core[:, :, 1]).reshape(rows_in, 3 * HALF_D)
    theirs = jnp.where(c == 0, by_core[:, :, 1], by_core[:, :, 0]).reshape(rows_in, 3 * HALF_D)
    in_za = jnp.stack(gather_list(mine, "seq"))
    in_zb = jnp.stack(gather_list(shift(theirs, "core", 1), "seq"))
    in_a = gather_plane(in_za, "x", "y")
    in_b = gather_plane(in_zb, "y", "x")
    keys = sorted(in_a)

    x_got = crossing(images)
    x_own = pick(images, after(x_got, list(in_a.values()), list(in_b.values())))
    x_oth = shift(x_own, "core", 1)
    mask = key_mask.astype(F32)
    mask = jnp.where(h == c, mask, shift(mask, "core", 1)).reshape(image_count, 2, half)
    mask = jnp.where(c == 0, mask, mask[:, ::-1])
    mask = jnp.pad(mask, ((0, 0), (0, 0), (0, padded - half))).reshape(image_count, 2 * padded)
    key_fill = jnp.broadcast_to(jnp.where(mask > 0, 0.0, NEG_FILL)[..., None], mask.shape + (128,)).astype(BF)

    out_low = after(out_weights.astype(BF), in_za, in_zb)
    rows_out = out_low.shape[0]
    out_a = gather_plane(crossed(out_low), "x", "y")
    out_b = gather_plane(crossed(shift(out_low, "core", 1)), "y", "x")
    my_out = gather_rows(at, out_a, out_b)
    other_out = shift(my_out, "core", 1)

    rows_ff = up_weights.shape[0]
    half_ff = rows_ff // 2
    updown = [jnp.stack([up_weights[r].astype(BF), down_weights[r].astype(BF)]) for r in (slice(0, half_ff), slice(half_ff, rows_ff))]
    ff_za, ff_zb = (jnp.stack([t, after(shift(after(t, in_za, in_zb), "seq", -1), x_own)]) for t in updown)
    g_got = crossing(after(out_grad, x_got))

    q_bias = lax.dynamic_slice(query_bias, (c * HALF_D,), (HALF_D,))
    v_bias = lax.dynamic_slice(value_bias, (c * HALF_D,), (HALF_D,))
    in_bias = jnp.concatenate([q_bias, jnp.zeros_like(q_bias), v_bias])
    h1, qkv = project(at, x_own, x_oth, gain_one, shift_one, in_bias, in_a, in_b, padded)
    tokens = image_count * 2 * padded
    ff_a = gather_plane(ff_za, "x", "y", qkv)
    ff_b = gather_plane(ff_zb, "y", "x", qkv)
    qkv = qkv.reshape(image_count, 2 * padded, 3 * HALF_D)
    mixed, lse = attend(qkv, key_fill)
    halved = mixed.reshape(image_count, 2, padded, HALF_D)
    mixed_oth = shift(halved, "core", 1)
    g_own = pick(out_grad, after(g_got, mixed))
    g_oth = shift(g_own, "core", 1)
    x2, h2 = middle(x_own, x_oth, halved, mixed_oth, my_out, other_out, out_bias, gain_two, shift_two)

    grad_a, grad_b, y_own, y_oth, dh2, g_bu = mlp(
        at, h2.reshape(tokens, D), g_own, g_oth, up_bias.reshape(shards * 2, half_ff), ff_a, ff_b
    )
    result = y_own[:, :half] + shift(y_oth, "core", 1)[:, :half].astype(F32) + x2[:, 0, :half] + down_bias
    result = result.astype(BF)

    dh2 = dh2.reshape(image_count, 2, padded, D)
    dh2_oth = shift(dh2, "core", 1)
    dx2, dattn, g_out, sums_two = middle_back(x2, dh2, dh2_oth, g_own, g_oth, halved, my_out, gain_two)
    g_out = g_out.reshape(ny, nx, 2, rows_out, D)
    oa, ob = {}, {}
    for ky, kx in keys:
        spot = ((y + ky) % ny, (x + kx) % nx)
        oa[ky, kx] = lax.dynamic_slice(g_out, (*spot, h, 0, 0), (1, 1, 1, rows_out, D)).reshape(rows_out, D)
        ob[ky, kx] = lax.dynamic_slice(g_out, (*spot, 1 - h, 0, 0), (1, 1, 1, rows_out, D)).reshape(rows_out, D)
    result_got = crossing(after(result, dattn))
    dqkv, sums_qkv = attend_back(qkv, key_fill, mixed, dattn.reshape(mixed.shape), lse)
    ia, ib = grad_in(at, h1.reshape(tokens, D), dqkv.reshape(tokens, 3 * HALF_D), keys, rows_in)
    dh_own, dh_oth = project_back(at, dqkv.reshape(image_count, 2, padded, 3 * HALF_D), in_a, in_b)
    dh_got = shift(dh_oth, "core", 1)
    activations = pick(result, after(result_got, dh_own)).astype(F32)
    share_ff = []
    for grads, order in ((grad_a, ("x", "y")), (grad_b, ("y", "x"))):
        total = reduce_plane(grads, *order, dattn, dqkv)
        share_ff.append(reduce_list([total[0], total[1]], "seq", dh_own))
    share_ff = jnp.concatenate(share_ff, axis=1)
    keep = crossed(reduce_plane(oa, "x", "y", dqkv, dh_own))
    give = crossed(reduce_plane(ob, "y", "x", dqkv, dh_own))
    share_out = (keep.astype(F32) + shift(give, "core", 1).astype(F32)).astype(BF)
    ia = reduce_plane(ia, "x", "y", dh_own, dh_own)
    ib = reduce_plane(ib, "y", "x", dh_own, dh_own)
    ia, ib = reduce_list([ia[0], ia[1]], "seq", dh_own), reduce_list([ib[0], ib[1]], "seq", dh_own)
    ib = shift(ib, "core", 1)
    ia, ib = (t.reshape(rows_in, 3, 1, HALF_D) for t in (ia, ib))
    share_in = jnp.where(c == 0, jnp.concatenate([ia, ib], 2), jnp.concatenate([ib, ia], 2)).reshape(rows_in, 3 * D)

    input_grad, sums_one = input_back(x_own, dh_own, dh_got, dx2, gain_one)
    input_grad = crossed(input_grad).astype(F32)

    zero = jnp.zeros((D,), F32)
    grad_vec = jnp.concatenate(
        [
            sums_one[0],
            sums_one[1],
            lax.dynamic_update_slice(zero, sums_qkv[0, :HALF_D], (c * HALF_D,)),
            lax.dynamic_update_slice(zero, sums_qkv[0, 2 * HALF_D :], (c * HALF_D,)),
            sums_two[2],
            sums_two[0],
            sums_two[1],
            sums_two[3],
            g_bu.reshape(-1),
        ]
    ).reshape(shards, -1)
    grad_vec = small_sum(grad_vec, AXES)
    share_vec = lax.dynamic_slice(grad_vec, (shard, 0), (1, grad_vec.shape[1])).reshape(-1)

    def over_dp(share):
        return small_sum(share, ("dp",)).astype(F32)

    shares = (over_dp(share_in), over_dp(share_out), over_dp(share_ff[0]), over_dp(share_ff[1]), share_vec)
    square = sum(jnp.sum(s * s) for s in shares)
    square = small_sum(jnp.full((8, 128), square), SHARD)[0, 0]
    grad_norm = jnp.sqrt(square)
    threshold = 0.5 * math.sqrt(4 * D * D + 2 * D * FF + 12 * D)
    clip_factor = jnp.minimum(1.0, threshold / grad_norm)
    bias = 1.0 - jnp.power(F32(0.5), step_count.astype(F32))
    rates = ((D // 2) ** (-0.5), (D // 4) ** (-0.5), D ** (-0.5), FF ** (-0.5), 0.2)
    results = [
        adam_update(masters[i], firsts[i], seconds[i], shares[i] * clip_factor, rates[i], bias, bias) for i in range(5)
    ]
    return (
        grad_norm,
        *(r[0] for r in results),
        *(r[1] for r in results),
        *(r[2] for r in results),
        *(r[0].astype(BF) for r in results),
        activations,
        input_grad,
    )


def solution(mesh):
    seq_n, fsdp_n, dp_n = (mesh.shape[a] for a in ("seq", "fsdp", "dp"))
    nx = math.isqrt(fsdp_n // 2)
    ny = fsdp_n // 2 // nx
    grid = Mesh(np.asarray(mesh.devices).reshape(seq_n, ny, nx, 2, dp_n), AXES)
    tokens = P(("y", "x", "core", "dp"), "seq", None)
    matrix, vector = P(SHARD, None), P(SHARD)
    five = (matrix, matrix, matrix, matrix, vector)
    return jax.shard_map(
        on_device,
        mesh=grid,
        in_specs=(tokens, P(("y", "x", "core", "dp"), None), tokens, P()) + five * 3,
        out_specs=(P(),) + five * 4 + (tokens, tokens),
        check_vma=False,
    )
```

```python
import functools
import math

import jax
import jax.numpy as jnp
import numpy as np
from jax import lax
from jax.experimental import pallas as pl
from jax.experimental.pallas import tpu as pltpu
from jax.sharding import Mesh
from jax.sharding import PartitionSpec as P

D = 1024
FF = 4096
PAD_ROWS = 16

NEG_FILL = -1000000000.0
ADAM_EPS = 1e-08
WEIGHT_DECAY = 0.05
AXES = ("seq", "y", "x", "core", "dp")
SHARD = ("seq", "y", "x", "core")

BF=jnp.bfloat16; F32=jnp.float32
def dot(a, b, dims=(((1,), (0,)), ((), ()))):
    return lax.dot_general(a, b, dims, preferred_element_type=F32)
NT=(((1,),(1,)),((),()))
TN=(((0,),(0,)),((),()))
ANY=pl.BlockSpec(memory_space=pl.ANY)
VM=pl.BlockSpec(memory_space=pltpu.VMEM)
SM=pl.BlockSpec(memory_space=pltpu.SMEM)

def gelu_both(u):
    c0=math.sqrt(2/math.pi)
    sq=u*u
    t=jnp.tanh(u*(c0+(c0*0.044715)*sq))
    half=0.5+0.5*t
    value=u*half
    slope=half+(0.5*u)*(1.0-t*t)*(c0+(3*c0*0.044715)*sq)
    return value,slope

def mlp_kernel(keys,*refs,gtile):
    nk=len(keys)
    at_ref,h2_ref,go_ref,gt_ref,bu_ref=refs[:5]
    pa,pb=refs[5:5+nk],refs[5+nk:5+2*nk]
    o=5+2*nk
    ga,gb=refs[o:o+nk],refs[o+nk:o+2*nk]
    yown_ref,yoth_ref,dh_ref,gbu_ref=refs[o+2*nk:o+2*nk+4]
    w,dd,a_all,du_all,y_acc,dh_acc,g_out,wsem,gsem=refs[o+2*nk+4:]
    images,half,feat=go_ref.shape
    hid=pa[0].shape[2]
    width=4*hid
    padded=h2_ref.shape[0]//(2*images)
    blocks=2*images

    def load(i,slot,go):
        for ki in range(nk):
            @pl.when(i==ki)
            def _():
                for kz in range(2):
                    for ud in range(2):
                        for ab,src in enumerate((pa[ki],pb[ki])):
                            cp=pltpu.make_async_copy(src.at[kz,ud],w.at[slot,ud,pl.ds((kz*2+ab)*hid,hid)],wsem.at[slot,kz*4+ud*2+ab])
                            cp.start() if go else cp.wait()
    def save(i,go):
        for ki in range(nk):
            @pl.when(i==ki)
            def _():
                for kz in range(2):
                    for ud in range(2):
                        for ab,dst in enumerate((ga[ki],gb[ki])):
                            cp=pltpu.make_async_copy(g_out.at[ud,pl.ds((kz*2+ab)*hid,hid)],dst.at[kz,ud],gsem.at[kz*4+ud*2+ab])
                            cp.start() if go else cp.wait()
    load(0,0,True)
    gbu_ref[...]=jnp.zeros_like(gbu_ref)
    for i in range(images):
        for s,src in enumerate((go_ref,gt_ref)):
            r=(2*i+s)*padded
            tail=padded-16
            dd[r+tail:r+padded,:]=jnp.zeros((16,feat),BF)
            dd[r:r+half,:]=src[i]
    def step(i,_):
        slot=lax.rem(i,2)
        load(i,slot,False)
        @pl.when(i+1<nk)
        def _(): load(i+1,1-slot,True)
        rows=[]
        for kz in range(2):
            for ab in range(2):
                row=jnp.int32(0)
                for ki,(ky,kx) in enumerate(keys):
                    z=lax.rem(at_ref[0]+kz,2); y=lax.rem(at_ref[1]+ky,at_ref[4]); x=lax.rem(at_ref[2]+kx,at_ref[5])
                    here=(((z*at_ref[4]+y)*at_ref[5]+x)*2+at_ref[3])*2+ab
                    row=jnp.where(i==ki,here,row)
                rows.append(row)
        bias=jnp.concatenate([bu_ref[pl.ds(r,1),:] for r in rows],axis=1)
        wu=w.at[slot,0]; wd=w.at[slot,1]
        def tokens(b,sums):
            r=pl.ds(pl.multiple_of(b*padded,16),padded)
            u=dot(h2_ref[r,:],wu[...],NT)+bias
            value,slope=gelu_both(u)
            a=value.astype(BF)
            a_all[r,:]=a
            dg=dot(dd[r,:],wd[...],NT)
            du=(dg*slope).astype(BF)
            du_all[r,:]=du
            ynew=dot(a,wd[...]); dnew=dot(du,wu[...])
            @pl.when(i==0)
            def _():
                y_acc[r,:]=ynew; dh_acc[r,:]=dnew
            @pl.when(i>0)
            def _():
                y_acc[r,:]+=ynew; dh_acc[r,:]+=dnew
            return sums+jnp.sum(du.astype(F32),axis=0,keepdims=True)
        sums=lax.fori_loop(0,blocks,tokens,jnp.zeros((1,width),F32))
        for q,row in enumerate(rows):
            gbu_ref[pl.ds(row,1),:]=sums[:,q*hid:(q+1)*hid]
        @pl.when(i>0)
        def _(): save(i-1,False)
        for t in range(0,width,gtile):
            g_out[1,t:t+gtile,:]=dot(a_all[:,t:t+gtile],dd[...],TN).astype(BF)
            g_out[0,t:t+gtile,:]=dot(du_all[:,t:t+gtile],h2_ref[...],TN).astype(BF)
        save(i,True)
        return 0
    lax.fori_loop(0,nk,step,0)
    for i in range(images):
        r=2*i*padded
        yown_ref[i]=y_acc[r:r+padded,:]
        yoth_ref[i]=y_acc[r+padded:r+2*padded,:].astype(BF)
    dh_ref[...]=dh_acc[...].astype(BF)
    save(nk-1,False)

def mlp(at,h2,g_own,g_oth,bu_rows,fa,fb,gtile=256):
    keys=sorted(fa); nk=len(keys)
    images,half,feat=g_own.shape
    tokens=h2.shape[0]; padded=tokens//(2*images)
    _,_,hid,_=fa[keys[0]].shape
    width=4*hid
    piece=jax.ShapeDtypeStruct(fa[keys[0]].shape,BF)
    out=pl.pallas_call(functools.partial(mlp_kernel,keys,gtile=min(gtile,width)),
        in_specs=[SM]+[VM]*4+[ANY]*(2*nk),
        out_specs=[ANY]*(2*nk)+[VM]*4,
        out_shape=[piece]*(2*nk)+[jax.ShapeDtypeStruct((images,padded,feat),F32),jax.ShapeDtypeStruct((images,padded,feat),BF),
            jax.ShapeDtypeStruct((tokens,feat),BF),jax.ShapeDtypeStruct(bu_rows.shape,F32)],
        scratch_shapes=[pltpu.VMEM((2,2,width,feat),BF),pltpu.VMEM((tokens,feat),BF),pltpu.VMEM((tokens,width),BF),pltpu.VMEM((tokens,width),BF),
            pltpu.VMEM((tokens,feat),F32),pltpu.VMEM((tokens,feat),F32),pltpu.VMEM((2,width,feat),BF),
            pltpu.SemaphoreType.DMA((2,8)),pltpu.SemaphoreType.DMA((8,))],
        name="feed_forward",
        compiler_params=pltpu.CompilerParams(vmem_limit_bytes=60<<20),
        cost_estimate=pl.CostEstimate(flops=nk*6*2*tokens*feat*width,bytes_accessed=40<<20,transcendentals=nk*tokens*width),
    )(at,h2,g_own,g_oth,bu_rows,*[fa[k] for k in keys],*[fb[k] for k in keys])
    return dict(zip(keys,out[:nk])),dict(zip(keys,out[nk:2*nk])),out[2*nk],out[2*nk+1],out[2*nk+2],out[2*nk+3]

HD=64; HALF_D=512

def head_operands(q_ref,k_ref,kb_ref,scale):
    q=q_ref[0].astype(F32)*scale; k=k_ref[0].astype(F32); kb=kb_ref[0].astype(F32)
    lane=lax.broadcasted_iota(jnp.int32,q.shape,1)
    low=lane<HD
    one=jnp.where((lane==0)|(lane==HD),1.0,0.0)
    qs=[jnp.where(low,q,one).astype(BF),jnp.where(low,one,q).astype(BF)]
    ks=[jnp.where(low,k,kb).astype(BF),jnp.where(low,kb,k).astype(BF)]
    return q,k,low,qs,ks

def attend_kernel(q_ref,k_ref,v_ref,kb_ref,o_ref,lse_ref):
    q,k,low,qs,ks=head_operands(q_ref,k_ref,kb_ref,HD**-0.5)
    vt=v_ref[0].astype(F32).T.astype(BF)
    outs=[]
    for j in range(2):
        s=dot(ks[j],qs[j],NT)
        m=jnp.max(s,axis=0,keepdims=True)
        e=jnp.exp(s-m)
        l=jnp.sum(e,axis=0,keepdims=True)
        o=dot(vt[j*HD:(j+1)*HD],e.astype(BF))
        outs.append(o*(1.0/l))
        lse_ref[0,0,j:j+1,:]=m+jnp.log(l)
    o_ref[0]=jnp.concatenate(outs,axis=0).T.astype(BF)

def attend(qkv,kbias):
    n,rows,w=qkv.shape; pairs=w//3//128
    blk=lambda off: pl.BlockSpec((1,rows,128),lambda i,p: (i,0,off+p))
    return pl.pallas_call(attend_kernel,grid=(n,pairs),
        in_specs=[blk(0),blk(pairs),blk(2*pairs),pl.BlockSpec((1,rows,128),lambda i,p:(i,0,0))],
        out_specs=[blk(0),pl.BlockSpec((1,1,8,rows),lambda i,p:(i,p,0,0))],
        out_shape=[jax.ShapeDtypeStruct((n,rows,w//3),BF),jax.ShapeDtypeStruct((n,pairs,8,rows),F32)],
        name="attend",
        compiler_params=pltpu.CompilerParams(vmem_limit_bytes=50<<20),
        cost_estimate=pl.CostEstimate(flops=n*pairs*8*rows*rows*128,bytes_accessed=n*rows*w*3,transcendentals=n*pairs*2*rows*rows),
    )(qkv,qkv,qkv,kbias)

def attend_back_kernel(q_ref,k_ref,v_ref,kb_ref,o_ref,g_ref,lse_ref,out_ref,sum_ref,*,pairs,chunk):
    p=pl.program_id(1)
    @pl.when((pl.program_id(0)==0)&(p==0))
    def _(): sum_ref[...]=jnp.zeros_like(sum_ref)
    scale=HD**-0.5
    q,k,low,qs,ks=head_operands(q_ref,k_ref,kb_ref,scale)
    qb=q.astype(BF)
    kt=k.T.astype(BF)
    g=g_ref[0]; gf=g.astype(F32)
    prod=(gf*o_ref[0].astype(F32)).T
    v=v_ref[0]
    rows=q.shape[0]
    dqs=[];dks=[];dvs=[]
    for j in range(2):
        gj=(jnp.where(low,gf,0.0) if j==0 else jnp.where(low,0.0,gf)).astype(BF)
        delta=jnp.sum(prod[j*HD:(j+1)*HD],axis=0,keepdims=True)
        lse=lse_ref[0,0,j:j+1,:]
        dq=None; dk=[]; dv=[]
        for r in range(0,rows,chunk):
            s=dot(ks[j][r:r+chunk],qs[j],NT)
            pr=jnp.exp(s-lse)
            dp=dot(v[r:r+chunk],gj,NT)
            ds=(pr*(dp-delta)).astype(BF)
            dv.append(dot(pr.astype(BF),g))
            dk.append(dot(ds,qb))
            t=dot(kt[j*HD:(j+1)*HD,r:r+chunk],ds) if chunk==rows else dot(k[r:r+chunk].astype(BF),ds,TN)[j*HD:(j+1)*HD]
            dq=t if dq is None else dq+t
        dqs.append(dq)
        dks.append(jnp.concatenate(dk,axis=0) if len(dk)>1 else dk[0]); dvs.append(jnp.concatenate(dv,axis=0) if len(dv)>1 else dv[0])
    parts=((jnp.concatenate(dqs,axis=0)*scale).T.astype(BF),jnp.where(low,dks[0],dks[1]).astype(BF),jnp.where(low,dvs[0],dvs[1]).astype(BF))
    for t,part in enumerate(parts):
        at=pl.ds(pl.multiple_of((t*pairs+p)*128,128),128)
        out_ref[0,:,at]=part
        sum_ref[0:1,at]+=jnp.sum(part.astype(F32),axis=0,keepdims=True)

def attend_back(qkv,kbias,mixed,grad,lse,chunk=None):
    n,rows,w=qkv.shape; pairs=w//3//128
    chunk=chunk or rows
    blk=lambda off: pl.BlockSpec((1,rows,128),lambda i,p: (i,0,off+p))
    return pl.pallas_call(functools.partial(attend_back_kernel,pairs=pairs,chunk=chunk),grid=(n,pairs),
        in_specs=[blk(0),blk(pairs),blk(2*pairs),pl.BlockSpec((1,rows,128),lambda i,p:(i,0,0)),blk(0),blk(0),pl.BlockSpec((1,1,8,rows),lambda i,p:(i,p,0,0))],
        out_specs=[pl.BlockSpec((1,rows,w),lambda i,p:(i,0,0)),pl.BlockSpec((8,w),lambda i,p:(0,0))],
        out_shape=[jax.ShapeDtypeStruct((n,rows,w),BF),jax.ShapeDtypeStruct((8,w),F32)],
        name="attend_back",
        compiler_params=pltpu.CompilerParams(vmem_limit_bytes=50<<20),
        cost_estimate=pl.CostEstimate(flops=n*pairs*20*rows*rows*128,bytes_accessed=n*rows*w*5,transcendentals=n*pairs*2*rows*rows),
    )(qkv,qkv,qkv,kbias,mixed,grad,lse)

NORM_EPS=1e-6
def norm_parts(values):
    center = values - jnp.mean(values, axis=-1, keepdims=True)
    inverse = lax.rsqrt(jnp.mean(center * center, axis=-1, keepdims=True) + NORM_EPS)
    return center * inverse, inverse

def norm_back(values, gain, grad):
    normed, inverse = norm_parts(values)
    scaled = grad * gain
    mean_one = jnp.mean(scaled, axis=-1, keepdims=True)
    mean_two = jnp.mean(scaled * normed, axis=-1, keepdims=True)
    return (scaled - mean_one - normed * mean_two) * inverse, grad * normed

def wide_rows(buf,block):
    n=block.shape[0]; total=buf.shape[0]
    buf[total-16:,:]=jnp.zeros((16,buf.shape[1]),F32)
    buf[0:n,:]=block.astype(F32)
    return buf[...]

def place(at_ref,keys,ka,size,pieces,buf,sem,gather):
    def both(go):
        n=0
        for ki,(ky,kx) in enumerate(keys):
            y=lax.rem(at_ref[1]+ky,at_ref[4]); x=lax.rem(at_ref[2]+kx,at_ref[5])
            for ab in range(2):
                for kz in range(ka):
                    z=lax.rem(at_ref[0]+kz,2) if ka==2 else 0
                    core=at_ref[3] if ab==0 else 1-at_ref[3]
                    if ka==1: core=at_ref[0] if ab==0 else 1-at_ref[0]
                    row=(((z*at_ref[4]+y)*at_ref[5]+x)*2+core)*size
                    inner=buf.at[pl.ds(pl.multiple_of(row,16),size)]
                    piece=pieces[ab*len(keys)+ki]
                    piece=piece.at[kz] if ka==2 else piece
                    cp=pltpu.make_async_copy(piece,inner,sem.at[n]) if gather else pltpu.make_async_copy(inner,piece,sem.at[n])
                    cp.start() if go else cp.wait()
                    n+=1
    both(True); both(False)

def project_kernel(keys,at_ref,own_ref,oth_ref,gain_ref,shift_ref,bias_ref,*refs):
    nk=len(keys)
    pieces=refs[:2*nk]; h_ref,qkv_ref,w,buf,sem=refs[2*nk:]
    @pl.when(pl.program_id(0)==0)
    def _(): place(at_ref,keys,2,pieces[0].shape[1],pieces,w,sem,True)
    for s,src in enumerate((own_ref,oth_ref)):
        v=wide_rows(buf.at[s],src[0])
        h=(norm_parts(v)[0]*gain_ref[...]+shift_ref[...]).astype(BF)
        h_ref[0,s]=h
        qkv_ref[0,s]=(dot(h,w[...])+bias_ref[...]).astype(BF)

def project(at,x_own,x_oth,gain,shift,bias,wa,wb,padded):
    keys=sorted(wa); nk=len(keys)
    n,half,feat=x_own.shape
    width=wa[keys[0]].shape[-1]
    tok=pl.BlockSpec((1,half,feat),lambda i:(i,0,0))
    row=lambda w: pl.BlockSpec((1,w),lambda i:(0,0))
    return pl.pallas_call(functools.partial(project_kernel,keys),grid=(n,),
        in_specs=[SM,tok,tok,row(feat),row(feat),row(width)]+[ANY]*(2*nk),
        out_specs=[pl.BlockSpec((1,2,padded,feat),lambda i:(i,0,0,0)),pl.BlockSpec((1,2,padded,width),lambda i:(i,0,0,0))],
        out_shape=[jax.ShapeDtypeStruct((n,2,padded,feat),BF),jax.ShapeDtypeStruct((n,2,padded,width),BF)],
        scratch_shapes=[pltpu.VMEM((feat,width),BF),pltpu.VMEM((2,padded,feat),F32),pltpu.SemaphoreType.DMA((4*nk,))],
        name="project",
        compiler_params=pltpu.CompilerParams(vmem_limit_bytes=50<<20),
        cost_estimate=pl.CostEstimate(flops=n*4*padded*feat*width,bytes_accessed=24<<20,transcendentals=0),
    )(at,x_own,x_oth,gain[None],shift[None],bias[None],*[wa[k] for k in keys],*[wb[k] for k in keys])

def gather_kernel(keys,at_ref,*refs):
    nk=len(keys)
    place(at_ref,keys,1,refs[0].shape[0],refs[:2*nk],refs[2*nk],refs[2*nk+1],True)

def gather_rows(at,pa,pb):
    keys=sorted(pa); nk=len(keys)
    rows,feat=pa[keys[0]].shape
    return pl.pallas_call(functools.partial(gather_kernel,keys),in_specs=[SM]+[ANY]*(2*nk),out_specs=VM,
        out_shape=jax.ShapeDtypeStruct((2*nk*rows,feat),BF),scratch_shapes=[pltpu.SemaphoreType.DMA((2*nk,))],name="gather_rows",
    )(at,*[pa[k] for k in keys],*[pb[k] for k in keys])

def middle_kernel(own_ref,oth_ref,mo_ref,mt_ref,wo_ref,wt_ref,bias_ref,gain_ref,shift_ref,x2_ref,h2_ref,buf):
    for s,src in enumerate((own_ref,oth_ref)):
        v=wide_rows(buf.at[s],src[0])
        v=v+(dot(mo_ref[0,s],wo_ref[...])+dot(mt_ref[0,1-s],wt_ref[...]))+bias_ref[...]
        x2_ref[0,s]=v
        h2_ref[0,s]=(norm_parts(v)[0]*gain_ref[...]+shift_ref[...]).astype(BF)

def middle(x_own,x_oth,mixed,mixed_oth,w_own,w_oth,bias,gain,shift):
    n,half,feat=x_own.shape
    _,_,padded,width=mixed.shape
    tok=pl.BlockSpec((1,half,feat),lambda i:(i,0,0))
    mix=pl.BlockSpec((1,2,padded,width),lambda i:(i,0,0,0))
    swp=pl.BlockSpec((1,2,padded,width),lambda i:(i,0,0,0))
    full=pl.BlockSpec((width,feat),lambda i:(0,0))
    row=pl.BlockSpec((1,feat),lambda i:(0,0))
    out=pl.BlockSpec((1,2,padded,feat),lambda i:(i,0,0,0))
    return pl.pallas_call(middle_kernel,grid=(n,),in_specs=[tok,tok,mix,swp,full,full,row,row,row],out_specs=[out,out],
        out_shape=[jax.ShapeDtypeStruct((n,2,padded,feat),F32),jax.ShapeDtypeStruct((n,2,padded,feat),BF)],
        scratch_shapes=[pltpu.VMEM((2,padded,feat),F32)],name="middle",
        compiler_params=pltpu.CompilerParams(vmem_limit_bytes=50<<20),
        cost_estimate=pl.CostEstimate(flops=n*8*padded*feat*width,bytes_accessed=26<<20,transcendentals=0),
    )(x_own,x_oth,mixed,mixed_oth,w_own,w_oth,bias[None],gain[None],shift[None])

def middle_back_kernel(x2_ref,da_ref,db_ref,go_ref,gt_ref,mix_ref,w_ref,gain_ref,dx_ref,dat_ref,gw_ref,sum_ref,buf,acc):
    i=pl.program_id(0)
    @pl.when(i==0)
    def _():
        acc[...]=jnp.zeros_like(acc); sum_ref[...]=jnp.zeros_like(sum_ref)
    for s,src in enumerate((go_ref,gt_ref)):
        dd=wide_rows(buf.at[s],src[0])
        grad=da_ref[0,s].astype(F32)+db_ref[0,1-s].astype(F32)
        dx,gg=norm_back(x2_ref[0,s],gain_ref[...],grad)
        dx=dx+dd
        dob=dx.astype(BF)
        if s==0:
            dx_ref[0]=dx
            for r,t in enumerate((gg,grad,dob.astype(F32),dd)):
                sum_ref[r:r+1,:]+=jnp.sum(t,axis=0,keepdims=True)
        dat_ref[0,s]=dot(dob,w_ref[...],NT).astype(BF)
        acc[...]+=dot(mix_ref[0,s],dob,TN)
    @pl.when(i==pl.num_programs(0)-1)
    def _(): gw_ref[...]=acc[...].astype(BF)

def middle_back(x2,dh_own,dh_oth,g_own,g_oth,mixed,w_own,gain):
    n,half,feat=g_own.shape
    _,_,padded,width=mixed.shape
    tok=pl.BlockSpec((1,half,feat),lambda i:(i,0,0))
    mix=pl.BlockSpec((1,2,padded,width),lambda i:(i,0,0,0))
    big=pl.BlockSpec((1,2,padded,feat),lambda i:(i,0,0,0))
    full=pl.BlockSpec((width,feat),lambda i:(0,0))
    return pl.pallas_call(middle_back_kernel,grid=(n,),
        in_specs=[big,big,big,tok,tok,mix,full,pl.BlockSpec((1,feat),lambda i:(0,0))],
        out_specs=[pl.BlockSpec((1,padded,feat),lambda i:(i,0,0)),mix,full,pl.BlockSpec((8,feat),lambda i:(0,0))],
        out_shape=[jax.ShapeDtypeStruct((n,padded,feat),F32),jax.ShapeDtypeStruct(mixed.shape,BF),jax.ShapeDtypeStruct((width,feat),BF),jax.ShapeDtypeStruct((8,feat),F32)],
        scratch_shapes=[pltpu.VMEM((2,padded,feat),F32),pltpu.VMEM((width,feat),F32)],name="middle_back",
        compiler_params=pltpu.CompilerParams(vmem_limit_bytes=56<<20),
        cost_estimate=pl.CostEstimate(flops=n*8*padded*feat*width,bytes_accessed=30<<20,transcendentals=0),
    )(x2,dh_own,dh_oth,g_own,g_oth,mixed,w_own,gain[None])

def grad_in_kernel(keys,tile,at_ref,h_ref,d_ref,*refs):
    nk=len(keys)
    pieces=refs[:2*nk]; buf,sem=refs[2*nk:]
    for t in range(0,h_ref.shape[1],tile):
        buf[t:t+tile,:]=dot(h_ref[:,t:t+tile],d_ref[...],TN).astype(BF)
    place(at_ref,keys,2,pieces[0].shape[1],pieces,buf,sem,False)

def grad_in(at,h1,dqkv,keys,rows):
    tokens,feat=h1.shape; width=dqkv.shape[1]
    nk=len(keys)
    out=pl.pallas_call(functools.partial(grad_in_kernel,keys,256),in_specs=[SM,VM,VM],out_specs=[ANY]*(2*nk),
        out_shape=[jax.ShapeDtypeStruct((2,rows,width),BF)]*(2*nk),
        scratch_shapes=[pltpu.VMEM((feat,width),BF),pltpu.SemaphoreType.DMA((4*nk,))],name="grad_in",
        compiler_params=pltpu.CompilerParams(vmem_limit_bytes=50<<20),
        cost_estimate=pl.CostEstimate(flops=2*tokens*feat*width,bytes_accessed=14<<20,transcendentals=0),
    )(at,h1,dqkv)
    return dict(zip(keys,out[:nk])),dict(zip(keys,out[nk:]))

def project_back_kernel(keys,at_ref,d_ref,*refs):
    nk=len(keys)
    pieces=refs[:2*nk]; own_ref,oth_ref,w,sem=refs[2*nk:]
    @pl.when(pl.program_id(0)==0)
    def _(): place(at_ref,keys,2,pieces[0].shape[1],pieces,w,sem,True)
    own_ref[0]=dot(d_ref[0,0],w[...],NT)
    oth_ref[0]=dot(d_ref[0,1],w[...],NT).astype(BF)

def project_back(at,dqkv,wa,wb):
    keys=sorted(wa); nk=len(keys)
    n,_,padded,width=dqkv.shape
    feat=wa[keys[0]].shape[1]*4*nk
    out=pl.BlockSpec((1,padded,feat),lambda i:(i,0,0))
    return pl.pallas_call(functools.partial(project_back_kernel,keys),grid=(n,),
        in_specs=[SM,pl.BlockSpec((1,2,padded,width),lambda i:(i,0,0,0))]+[ANY]*(2*nk),out_specs=[out,out],
        out_shape=[jax.ShapeDtypeStruct((n,padded,feat),F32),jax.ShapeDtypeStruct((n,padded,feat),BF)],
        scratch_shapes=[pltpu.VMEM((feat,width),BF),pltpu.SemaphoreType.DMA((4*nk,))],name="project_back",
        compiler_params=pltpu.CompilerParams(vmem_limit_bytes=50<<20),
        cost_estimate=pl.CostEstimate(flops=n*4*padded*feat*width,bytes_accessed=18<<20,transcendentals=0),
    )(at,dqkv,*[wa[k] for k in keys],*[wb[k] for k in keys])

def input_back_kernel(x_ref,da_ref,db_ref,dx_ref,gain_ref,out_ref,sum_ref,buf):
    @pl.when(pl.program_id(0)==0)
    def _(): sum_ref[...]=jnp.zeros_like(sum_ref)
    half=x_ref.shape[1]
    v=wide_rows(buf,x_ref[0])
    grad=da_ref[0]+db_ref[0].astype(F32)
    dx,gg=norm_back(v,gain_ref[...],grad)
    out_ref[0]=(dx+dx_ref[0]).astype(BF)[:half]
    sum_ref[0:1,:]+=jnp.sum(gg,axis=0,keepdims=True)
    sum_ref[1:2,:]+=jnp.sum(grad,axis=0,keepdims=True)

def input_back(x_own,dh_own,dh_oth,dx2,gain):
    n,half,feat=x_own.shape
    padded=dx2.shape[1]
    tok=pl.BlockSpec((1,half,feat),lambda i:(i,0,0))
    big=pl.BlockSpec((1,padded,feat),lambda i:(i,0,0))
    return pl.pallas_call(input_back_kernel,grid=(n,),in_specs=[tok,big,big,big,pl.BlockSpec((1,feat),lambda i:(0,0))],
        out_specs=[tok,pl.BlockSpec((8,feat),lambda i:(0,0))],
        out_shape=[jax.ShapeDtypeStruct(x_own.shape,BF),jax.ShapeDtypeStruct((8,feat),F32)],
        scratch_shapes=[pltpu.VMEM((padded,feat),F32)],name="input_back",
        compiler_params=pltpu.CompilerParams(vmem_limit_bytes=40<<20),
        cost_estimate=pl.CostEstimate(flops=n*20*padded*feat,bytes_accessed=14<<20,transcendentals=0),
    )(x_own,dh_own,dh_oth,dx2,gain[None])

MESH_ID = pl.DeviceIdType.MESH


class Wires:
    def __init__(self, send_sem, recv_sem):
        self.send_sem, self.recv_sem, self.count, self.sent = send_sem, recv_sem, 0, []

    def make(self, src, dst, to):
        cp = pltpu.make_async_remote_copy(
            src_ref=src, dst_ref=dst, send_sem=self.send_sem.at[self.count], recv_sem=self.recv_sem.at[self.count],
            device_id=to, device_id_type=MESH_ID)
        self.count += 1
        return cp

    def send(self, src, dst, to):
        cp = self.make(src, dst, to)
        cp.start()
        self.sent.append(cp)
        return cp

    def finish(self):
        for cp in self.sent:
            cp.wait_send()


def greet(peers, crossing_peer, apart):
    barrier = pltpu.get_barrier_semaphore()
    for peer in peers:
        pl.semaphore_signal(barrier, inc=1, device_id=peer, device_id_type=MESH_ID)

    @pl.when(apart)
    def _():
        pl.semaphore_signal(barrier, inc=1, device_id=crossing_peer, device_id_type=MESH_ID)

    pl.semaphore_wait(barrier, len(peers) + jnp.where(apart, 1, 0))


def add_all(first, *others):
    total = first.astype(F32)
    for other in others:
        total = total + other.astype(F32)
    return total


def tail_kernel(keys, ny, nx, *refs):
    nk = len(keys)
    h1_ref, dqkv_ref, go_ref, x_ref, dx_ref, gain_ref, vec_ref = refs[:7]
    wa, wb = refs[7:7 + nk], refs[7 + nk:7 + 2 * nk]
    o = 7 + 2 * nk
    fa, fb = refs[o:o + nx], refs[o + nx:o + nx + ny]
    o += nx + ny
    mine_ref, theirs_ref, so_ref, sf_ref, ig_ref, vout_ref, norm_ref = refs[o:o + 7]
    (w, grad, ra1, ra2, rb1, rb2, sa, sb, oa1, oa2, ob1, ob2, ta, tb, osum, ocross, ocore, odp, ofin,
     rfa, rfb, fsum, fpart, frecv, fdp, isum, ipart, irecv, idp, ifin,
     buf, give, got, stage, vrecv, nrecv, nval, wsem, send_sem, recv_sem) = refs[o + 7:]
    h, y, x, c, l = (lax.axis_index(a) for a in AXES)
    images, half, feat = x_ref.shape
    padded = dx_ref.shape[1]
    rows = grad.shape[4]
    apart = h != c
    cross = {"seq": 1 - h, "core": 1 - c}
    to_core, to_seq, to_dp = {"core": 1 - c}, {"seq": 1 - h}, {"dp": 1 - l}
    to_x = [{"x": lax.rem(x + k, nx)} for k in range(nx)]
    to_y = [{"y": lax.rem(y + k, ny)} for k in range(ny)]
    yy = [lax.rem(y + k, ny) for k in range(ny)]
    xx = [lax.rem(x + k, nx) for k in range(nx)]
    zz = [h, 1 - h]
    wires = Wires(send_sem, recv_sem)
    loads = []
    for ki, (ky, kx) in enumerate(keys):
        for kz in range(2):
            for core, src in ((c, wa), (1 - c, wb)):
                row = (((zz[kz] * ny + yy[ky]) * nx + xx[kx]) * 2 + core) * rows
                cp = pltpu.make_async_copy(src[ki].at[kz], w.at[pl.ds(pl.multiple_of(row, 16), rows)], wsem.at[len(loads)])
                cp.start()
                loads.append(cp)
    greet([to_core, to_seq, to_dp] + to_x[1:] + to_y[1:], cross, apart)

    ff_got = [wires.send(fa[k], rfa.at[k - 1], to_x[k]) for k in range(1, nx)]
    ff_got += [wires.send(fb[k], rfb.at[k - 1], to_y[k]) for k in range(1, ny)]
    oa_got = [[wires.send(go_ref.at[yy[ky], xx[kx], h], oa1.at[ky - 1, kx], to_y[ky]) for kx in range(nx)] for ky in range(1, ny)]
    ob_got = [[wires.send(go_ref.at[yy[ky], xx[kx], 1 - h], ob1.at[kx - 1, ky], to_x[kx]) for ky in range(ny)] for kx in range(1, nx)]
    width = nx * 2 * rows
    ia_got, ib_got = [], []
    for ky in range(ny - 1, -1, -1):
        for kz in range(2):
            col = pl.multiple_of((zz[kz] * ny + yy[ky]) * width, 128)
            t = dot(h1_ref[:, pl.ds(col, width)], dqkv_ref[...], TN).astype(BF)
            for q in range(nx):
                for core in range(2):
                    r = (q * 2 + core) * rows
                    grad[zz[kz], yy[ky], q, core] = t[r:r + rows]
        if ky > 0:
            for kx in range(nx):
                for kz in range(2):
                    ia_got.append(wires.send(grad.at[zz[kz], yy[ky], xx[kx], c], ra1.at[ky - 1, kz, kx], to_y[ky]))
    for kx in range(1, nx):
        for ky in range(ny):
            for kz in range(2):
                ib_got.append(wires.send(grad.at[zz[kz], yy[ky], xx[kx], 1 - c], rb1.at[kx - 1, kz, ky], to_x[kx]))
    for cp in loads:
        cp.wait()
    dh_got = []
    for i in range(images):
        r = (2 * i + 1) * padded
        give[i] = dot(dqkv_ref[r:r + padded, :], w[...], NT).astype(BF)
        dh_got.append(wires.send(give.at[i], got.at[i], to_core))
    for cp in ff_got:
        cp.wait_recv()
    fsum[0] = add_all(fa[0][...], *(rfa[k] for k in range(nx - 1))).astype(BF)
    fsum[1] = add_all(fb[0][...], *(rfb[k] for k in range(ny - 1))).astype(BF)
    fd = wires.send(fsum.at[1 - l], fdp, to_dp)
    for row in oa_got + ob_got:
        for cp in row:
            cp.wait_recv()
    o_got = []
    for kx in range(1, nx):
        ta[kx - 1] = add_all(go_ref[y, xx[kx], h], *(oa1[k, kx] for k in range(ny - 1))).astype(BF)
        o_got.append(wires.send(ta.at[kx - 1], oa2.at[kx - 1], to_x[kx]))
    for ky in range(1, ny):
        tb[ky - 1] = add_all(go_ref[yy[ky], x, 1 - h], *(ob1[k, ky] for k in range(nx - 1))).astype(BF)
        o_got.append(wires.send(tb.at[ky - 1], ob2.at[ky - 1], to_y[ky]))

    sum_gain, sum_shift = jnp.zeros((1, feat), F32), jnp.zeros((1, feat), F32)
    crossing_copies = [wires.make(stage.at[i], ig_ref.at[i], cross) for i in range(images)]

    def input_back(i, sum_gain, sum_shift):
        r = 2 * i * padded
        own = dot(dqkv_ref[r:r + padded, :], w[...], NT)
        dh_got[i].wait_recv()
        g = own + got[i].astype(F32)
        dx, gg = norm_back(wide_rows(buf, x_ref[i]), gain_ref[...], g)
        stage[i] = (dx + dx_ref[i]).astype(BF)[:half]

        @pl.when(apart)
        def _():
            crossing_copies[i].start()

        @pl.when(jnp.logical_not(apart))
        def _():
            ig_ref[i] = stage[i]

        return sum_gain + jnp.sum(gg, axis=0, keepdims=True), sum_shift + jnp.sum(g, axis=0, keepdims=True)

    sum_gain, sum_shift = input_back(0, sum_gain, sum_shift)
    for cp in ia_got + ib_got:
        cp.wait_recv()
    i_got = []
    for kz in range(2):
        for kx in range(1, nx):
            sa[kx - 1, kz] = add_all(grad[zz[kz], y, xx[kx], c], *(ra1[k, kz, kx] for k in range(ny - 1))).astype(BF)
        for ky in range(1, ny):
            sb[ky - 1, kz] = add_all(grad[zz[kz], yy[ky], x, 1 - c], *(rb1[k, kz, ky] for k in range(nx - 1))).astype(BF)
    for kx in range(1, nx):
        i_got.append(wires.send(sa.at[kx - 1], ra2.at[kx - 1], to_x[kx]))
    for ky in range(1, ny):
        i_got.append(wires.send(sb.at[ky - 1], rb2.at[ky - 1], to_y[ky]))
    sum_gain, sum_shift = input_back(1, sum_gain, sum_shift)
    fd.wait_recv()
    fpart[...] = add_all(fsum[l], fdp[...]).astype(BF)
    fs = wires.send(fpart.at[1], frecv, to_seq)
    for i in range(2, images):
        sum_gain, sum_shift = input_back(i, sum_gain, sum_shift)
    vout_ref[...] = vec_ref[...]
    for q in range(feat // 128):
        vout_ref[q:q + 1, :] = sum_gain[:, q * 128:(q + 1) * 128]
        vout_ref[feat // 128 + q:feat // 128 + q + 1, :] = sum_shift[:, q * 128:(q + 1) * 128]
    rounds = [[to_core], to_x[1:], to_y[1:], [to_seq], [to_dp]]
    slot = [0]

    def start_round(value, landing, peers):
        first = slot[0]
        cps = [wires.send(value, landing.at[first + k], peer) for k, peer in enumerate(peers)]
        slot[0] += len(peers)
        return first, cps

    def end_round(value_ref, landing, started):
        first, cps = started
        for cp in cps:
            cp.wait_recv()
        for cp in cps:
            cp.wait_send()
        wires.sent = [cp for cp in wires.sent if all(cp is not other for other in cps)]
        value_ref[...] = add_all(value_ref[...], *(landing[first + k] for k in range(len(cps))))

    vec_round = start_round(vout_ref, vrecv, rounds[0])
    for cp in i_got:
        cp.wait_recv()
    for kz in range(2):
        isum[0, kz] = add_all(grad[zz[kz], y, x, c], *(ra1[k, kz, 0] for k in range(ny - 1)), *(ra2[k, kz] for k in range(nx - 1))).astype(BF)
        isum[1, kz] = add_all(grad[zz[kz], y, x, 1 - c], *(rb1[k, kz, 0] for k in range(nx - 1)), *(rb2[k, kz] for k in range(ny - 1))).astype(BF)
    idd = wires.send(isum.at[1 - l], idp, to_dp)
    for cp in o_got:
        cp.wait_recv()
    osum[0] = add_all(go_ref[y, x, h], *(oa1[k, 0] for k in range(ny - 1)), *(oa2[k] for k in range(nx - 1))).astype(BF)
    osum[1] = add_all(go_ref[y, x, 1 - h], *(ob1[k, 0] for k in range(nx - 1)), *(ob2[k] for k in range(ny - 1))).astype(BF)
    out_cross = wires.make(osum, ocross, cross)

    @pl.when(apart)
    def _():
        out_cross.start()

    @pl.when(jnp.logical_not(apart))
    def _():
        ocross[...] = osum[...]

    end_round(vout_ref, vrecv, vec_round)
    vec_round = start_round(vout_ref, vrecv, rounds[1])
    idd.wait_recv()
    ipart[...] = add_all(isum[l], idp[...]).astype(BF)
    is_ = wires.send(ipart.at[1], irecv, to_seq)
    end_round(vout_ref, vrecv, vec_round)
    vec_round = start_round(vout_ref, vrecv, rounds[2])

    @pl.when(apart)
    def _():
        out_cross.wait_recv()

    oc = wires.send(ocross.at[1], ocore, to_core)
    fs.wait_recv()
    sf_ref[l] = add_all(fpart[0], frecv[...]).astype(BF)
    ff_last = wires.send(sf_ref.at[l], sf_ref.at[l], to_dp)
    end_round(vout_ref, vrecv, vec_round)
    vec_round = start_round(vout_ref, vrecv, rounds[3])
    oc.wait_recv()
    ofin[...] = add_all(ocross[0], ocore[...]).astype(BF)
    od = wires.send(ofin, odp, to_dp)
    is_.wait_recv()
    ifin[l] = add_all(ipart[0], irecv[...]).astype(BF)
    in_last = wires.send(ifin.at[l], ifin.at[l], to_dp)
    end_round(vout_ref, vrecv, vec_round)
    vec_round = start_round(vout_ref, vrecv, rounds[4])
    in_last.wait_recv()
    ic = wires.send(ifin.at[1], theirs_ref, to_core)
    mine_ref[...] = ifin[0]
    od.wait_recv()
    so_ref[...] = add_all(ofin[...], odp[...]).astype(BF)
    end_round(vout_ref, vrecv, vec_round)
    ff_last.wait_recv()

    def squares(value):
        value = value.astype(F32)
        return jnp.sum(jnp.sum(value * value, axis=0, keepdims=True), axis=1, keepdims=True)

    shard = ((h * ny + y) * nx + x) * 2 + c
    v = vout_ref[...]
    place = lax.broadcasted_iota(jnp.int32, v.shape, 0) * 128 + lax.broadcasted_iota(jnp.int32, v.shape, 1)
    share = v.shape[0] * 128 // (4 * ny * nx)
    v = jnp.where((place >= shard * share) & (place < (shard + 1) * share), v, 0.0)
    total = squares(v) + squares(so_ref[...]) + squares(mine_ref[...])
    for ab in range(2):
        for ud in range(2):
            total = total + squares(sf_ref[ab, ud])
    ic.wait_recv()
    total = total + squares(theirs_ref[...])
    nval[...] = jnp.broadcast_to(total, nval.shape)
    slot[0] = 0
    for peers in rounds[:4]:
        end_round(nval, nrecv, start_round(nval, nrecv, peers))
    norm_ref[...] = jnp.sqrt(nval[...])

    @pl.when(apart)
    def _():
        for cp in crossing_copies:
            cp.wait_recv()
        for cp in crossing_copies:
            cp.wait_send()
        out_cross.wait_send()

    wires.finish()


def tail_stage(h1, dqkv, g_out, x_own, dx2, gain, vec, wa, wb, fa, fb, ny, nx):
    keys = sorted(wa)
    nk = len(keys)
    tokens, feat = h1.shape
    width = dqkv.shape[1]
    rows = wa[keys[0]].shape[1]
    rows_o = g_out.shape[3]
    images, half, _ = x_own.shape
    padded = dx2.shape[1]
    _, ud, hid, _ = fa[0].shape
    ma, mb = max(ny - 1, 1), max(nx - 1, 1)
    piece, out_piece, ff = (rows, width), (rows_o, feat), (ud, hid, feat)
    peers = 4 + nx - 1 + ny - 1
    many = 200 + 8 * nk * 4
    V = lambda *s: pltpu.VMEM(s, BF)
    scratch = [
        V(feat, width), V(2, ny, nx, 2, *piece),
        V(ny - 1, 2, nx, *piece), V(nx - 1, 2, *piece), V(nx - 1, 2, ny, *piece), V(ny - 1, 2, *piece),
        V(nx - 1, 2, *piece), V(ny - 1, 2, *piece),
        V(ny - 1, nx, *out_piece), V(nx - 1, *out_piece), V(nx - 1, ny, *out_piece), V(ny - 1, *out_piece),
        V(nx - 1, *out_piece), V(ny - 1, *out_piece),
        V(2, *out_piece), V(2, *out_piece), V(*out_piece), V(*out_piece), V(*out_piece),
        V(nx - 1, 2, *ff), V(ny - 1, 2, *ff), V(2, 2, *ff), V(2, *ff), V(*ff), V(2, *ff),
        V(2, 2, *piece), V(2, *piece), V(*piece), V(2, *piece), V(2, *piece),
        pltpu.VMEM((padded, feat), F32), V(images, padded, feat), V(images, padded, feat), V(images, half, feat),
        pltpu.VMEM((peers,) + vec.shape, F32), pltpu.VMEM((peers, 8, 128), F32), pltpu.VMEM((8, 128), F32),
        pltpu.SemaphoreType.DMA((4 * nk,)), pltpu.SemaphoreType.DMA((many,)), pltpu.SemaphoreType.DMA((many,)),
    ]
    return pl.pallas_call(
        functools.partial(tail_kernel, keys, ny, nx),
        in_specs=[VM] * 7 + [ANY] * (2 * nk) + [VM] * (nx + ny),
        out_specs=[VM] * 7,
        out_shape=[
            jax.ShapeDtypeStruct(piece, BF), jax.ShapeDtypeStruct(piece, BF), jax.ShapeDtypeStruct(out_piece, BF),
            jax.ShapeDtypeStruct((2,) + ff, BF), jax.ShapeDtypeStruct(x_own.shape, BF),
            jax.ShapeDtypeStruct(vec.shape, F32), jax.ShapeDtypeStruct((8, 128), F32),
        ],
        scratch_shapes=scratch,
        name="tail_stage",
        compiler_params=pltpu.CompilerParams(collective_id=1, has_side_effects=True, vmem_limit_bytes=62 << 20),
        cost_estimate=pl.CostEstimate(flops=4 * tokens * feat * width, bytes_accessed=40 << 20, transcendentals=0),
    )(h1, dqkv, g_out, x_own, dx2, gain[None], vec, *[wa[k] for k in keys], *[wb[k] for k in keys], *fa, *fb)


def shift(value, axis, up):
    n = lax.axis_size(axis)
    return lax.ppermute(value, axis, [(i, (i + up) % n) for i in range(n)])


def after(value, *others):
    return lax.optimization_barrier((value, others))[0]


def crossing(value):
    return lax.ppermute(value, ("seq", "core"), [(1, 2), (2, 1)])


def pick(own, received):
    return jnp.where(lax.axis_index("seq") == lax.axis_index("core"), own, received)


def crossed(value):
    return pick(value, crossing(value))


def small_sum(value, axes):
    for axis in axes:
        n = lax.axis_size(axis)
        moved, total = value, value
        for _ in range(n - 1):
            moved = shift(moved, axis, 1)
            total = total + moved
        value = total
    return value


def gather_list(piece, axis):
    out = [piece]
    for _ in range(lax.axis_size(axis) - 1):
        out.append(shift(out[-1], axis, -1))
    return out


def gather_plane(piece, first, second, dep=()):
    out = {}
    for i, one in enumerate(gather_list(piece, first)):
        one = after(one, dep) if i else one
        for j, two in enumerate(gather_list(one, second)):
            out[(j, i) if first == "x" else (i, j)] = two
    return out


def reduce_list(pieces, axis, dep):
    total = pieces[-1]
    for piece in pieces[-2::-1]:
        total = (after(shift(total, axis, 1), dep).astype(F32) + piece.astype(F32)).astype(BF)
    return total


def reduce_second(pieces, first, second, dep):
    n_first, n_second = lax.axis_size(first), lax.axis_size(second)
    part = []
    for i in range(n_first):
        row = [pieces[(j, i) if first == "x" else (i, j)] for j in range(n_second)]
        part.append(reduce_list(row, second, dep))
    return part


def adam_update(master, first_moment, second_moment, gradient, step_rate, bias_one, bias_two):
    first_new = 0.5 * first_moment + 0.5 * gradient
    second_new = 0.5 * second_moment + 0.5 * gradient * gradient
    update = first_new / bias_one / (jnp.sqrt(second_new / bias_two) + ADAM_EPS)
    master_new = master - step_rate * (update + WEIGHT_DECAY * master)
    return (master_new, first_new, second_new)


def on_device(images, key_mask, out_grad, step_count, *params):
    masters, firsts, seconds = params[0:5], params[5:10], params[10:15]
    in_weights, out_weights, up_weights, down_weights, vectors = masters
    image_count, half, features = images.shape
    padded = -(-half // PAD_ROWS) * PAD_ROWS
    h, c = lax.axis_index("seq"), lax.axis_index("core")
    y, x = lax.axis_index("y"), lax.axis_index("x")
    ny, nx = lax.axis_size("y"), lax.axis_size("x")
    shards = 4 * ny * nx
    shard = ((h * ny + y) * nx + x) * 2 + c
    at = jnp.stack([h, y, x, c, jnp.int32(ny), jnp.int32(nx), jnp.int32(0), jnp.int32(0)]).astype(jnp.int32)

    placed = jnp.where(
        lax.broadcasted_iota(jnp.int32, (shards, 1), 0) == shard, vectors.astype(BF)[None, :], jnp.zeros((), BF)
    )
    full_vec = small_sum(placed, SHARD).reshape(-1).astype(F32)
    gain_one, shift_one, query_bias, value_bias, out_bias, gain_two, shift_two, down_bias = (
        full_vec[i * D : (i + 1) * D] for i in range(8)
    )
    up_bias = full_vec[8 * D :]

    rows_in = in_weights.shape[0]
    by_core = in_weights.astype(BF).reshape(rows_in, 3, 2, HALF_D)
    mine = jnp.where(c == 0, by_core[:, :, 0], by_core[:, :, 1]).reshape(rows_in, 3 * HALF_D)
    theirs = jnp.where(c == 0, by_core[:, :, 1], by_core[:, :, 0]).reshape(rows_in, 3 * HALF_D)
    in_za = jnp.stack(gather_list(mine, "seq"))
    in_zb = jnp.stack(gather_list(shift(theirs, "core", 1), "seq"))
    in_a = gather_plane(in_za, "x", "y")
    in_b = gather_plane(in_zb, "y", "x")
    keys = sorted(in_a)

    x_got = crossing(images)
    x_own = pick(images, after(x_got, list(in_a.values()), list(in_b.values())))
    x_oth = shift(x_own, "core", 1)
    mask = key_mask.astype(F32)
    mask = jnp.where(h == c, mask, shift(mask, "core", 1)).reshape(image_count, 2, half)
    mask = jnp.where(c == 0, mask, mask[:, ::-1])
    mask = jnp.pad(mask, ((0, 0), (0, 0), (0, padded - half))).reshape(image_count, 2 * padded)
    key_fill = jnp.broadcast_to(jnp.where(mask > 0, 0.0, NEG_FILL)[..., None], mask.shape + (128,)).astype(BF)

    out_low = after(out_weights.astype(BF), in_za, in_zb)
    rows_out = out_low.shape[0]
    out_a = gather_plane(crossed(out_low), "x", "y")
    out_b = gather_plane(crossed(shift(out_low, "core", 1)), "y", "x")
    my_out = gather_rows(at, out_a, out_b)
    other_out = shift(my_out, "core", 1)

    rows_ff = up_weights.shape[0]
    half_ff = rows_ff // 2
    updown = [jnp.stack([up_weights[r].astype(BF), down_weights[r].astype(BF)]) for r in (slice(0, half_ff), slice(half_ff, rows_ff))]
    ff_za, ff_zb = (jnp.stack([t, after(shift(after(t, in_za, in_zb), "seq", -1), x_own)]) for t in updown)
    g_got = crossing(after(out_grad, x_got))

    q_bias = lax.dynamic_slice(query_bias, (c * HALF_D,), (HALF_D,))
    v_bias = lax.dynamic_slice(value_bias, (c * HALF_D,), (HALF_D,))
    in_bias = jnp.concatenate([q_bias, jnp.zeros_like(q_bias), v_bias])
    h1, qkv = project(at, x_own, x_oth, gain_one, shift_one, in_bias, in_a, in_b, padded)
    tokens = image_count * 2 * padded
    ff_a = gather_plane(ff_za, "x", "y", qkv)
    ff_b = gather_plane(ff_zb, "y", "x", qkv)
    qkv = qkv.reshape(image_count, 2 * padded, 3 * HALF_D)
    mixed, lse = attend(qkv, key_fill)
    halved = mixed.reshape(image_count, 2, padded, HALF_D)
    mixed_oth = shift(halved, "core", 1)
    g_own = pick(out_grad, after(g_got, mixed))
    g_oth = shift(g_own, "core", 1)
    x2, h2 = middle(x_own, x_oth, halved, mixed_oth, my_out, other_out, out_bias, gain_two, shift_two)

    grad_a, grad_b, y_own, y_oth, dh2, g_bu = mlp(
        at, h2.reshape(tokens, D), g_own, g_oth, up_bias.reshape(shards * 2, half_ff), ff_a, ff_b
    )
    result = y_own[:, :half] + shift(y_oth, "core", 1)[:, :half].astype(F32) + x2[:, 0, :half] + down_bias
    result = result.astype(BF)

    dh2 = dh2.reshape(image_count, 2, padded, D)
    dh2_oth = shift(dh2, "core", 1)
    dx2, dattn, g_out, sums_two = middle_back(x2, dh2, dh2_oth, g_own, g_oth, halved, my_out, gain_two)
    result_got = crossing(after(result, dattn))
    dqkv, sums_qkv = attend_back(qkv, key_fill, mixed, dattn.reshape(mixed.shape), lse)
    part_a = reduce_second(grad_a, "x", "y", dqkv)
    part_b = reduce_second(grad_b, "y", "x", dqkv)
    zero = jnp.zeros((D,), F32)
    vec = jnp.concatenate(
        [
            zero,
            zero,
            lax.dynamic_update_slice(zero, sums_qkv[0, :HALF_D], (c * HALF_D,)),
            lax.dynamic_update_slice(zero, sums_qkv[0, 2 * HALF_D :], (c * HALF_D,)),
            sums_two[2],
            sums_two[0],
            sums_two[1],
            sums_two[3],
            g_bu.reshape(-1),
        ]
    ).reshape(-1, 128)
    in_mine, in_theirs, share_out, share_ff, input_grad, vec, norm = tail_stage(
        h1.reshape(tokens, D),
        dqkv.reshape(tokens, 3 * HALF_D),
        g_out.reshape(ny, nx, 2, rows_out, D),
        x_own,
        dx2,
        gain_one,
        vec,
        in_a,
        in_b,
        part_a,
        part_b,
        ny,
        nx,
    )
    activations = pick(result, after(result_got, norm)).astype(F32)
    input_grad = input_grad.astype(F32)
    share_vec = lax.dynamic_slice(vec.reshape(shards, -1), (shard, 0), (1, vec.size // shards)).reshape(-1)
    in_mine, in_theirs = (s.reshape(rows_in, 3, 1, HALF_D) for s in (in_mine, in_theirs))
    share_in = jnp.where(
        c == 0, jnp.concatenate([in_mine, in_theirs], 2), jnp.concatenate([in_theirs, in_mine], 2)
    ).reshape(rows_in, 3 * D)
    share_up, share_down = (share_ff[:, i].reshape(rows_ff, D) for i in range(2))
    shares = tuple(s.astype(F32) for s in (share_in, share_out, share_up, share_down, share_vec))
    grad_norm = norm[0, 0]
    threshold = 0.5 * math.sqrt(4 * D * D + 2 * D * FF + 12 * D)
    clip_factor = jnp.minimum(1.0, threshold / grad_norm)
    bias = 1.0 - jnp.power(F32(0.5), step_count.astype(F32))
    rates = ((D // 2) ** (-0.5), (D // 4) ** (-0.5), D ** (-0.5), FF ** (-0.5), 0.2)
    results = [
        adam_update(masters[i], firsts[i], seconds[i], shares[i] * clip_factor, rates[i], bias, bias) for i in range(5)
    ]
    return (
        grad_norm,
        *(r[0] for r in results),
        *(r[1] for r in results),
        *(r[2] for r in results),
        *(r[0].astype(BF) for r in results),
        activations,
        input_grad,
    )


def solution(mesh):
    seq_n, fsdp_n, dp_n = (mesh.shape[a] for a in ("seq", "fsdp", "dp"))
    nx = math.isqrt(fsdp_n // 2)
    ny = fsdp_n // 2 // nx
    grid = Mesh(np.asarray(mesh.devices).reshape(seq_n, ny, nx, 2, dp_n), AXES)
    tokens = P(("y", "x", "core", "dp"), "seq", None)
    matrix, vector = P(SHARD, None), P(SHARD)
    five = (matrix, matrix, matrix, matrix, vector)
    return jax.shard_map(
        on_device,
        mesh=grid,
        in_specs=(tokens, P(("y", "x", "core", "dp"), None), tokens, P()) + five * 3,
        out_specs=(P(),) + five * 4 + (tokens, tokens),
        check_vma=False,
    )
```

```python
import functools
import math

import jax
import jax.numpy as jnp
import numpy as np
from jax import lax
from jax.experimental import pallas as pl
from jax.experimental.pallas import tpu as pltpu
from jax.sharding import Mesh
from jax.sharding import PartitionSpec as P

D = 1024
FF = 4096
PAD_ROWS = 16

NEG_FILL = -1000000000.0
ADAM_EPS = 1e-08
WEIGHT_DECAY = 0.05
AXES = ("seq", "y", "x", "core", "dp")
SHARD = ("seq", "y", "x", "core")

BF=jnp.bfloat16; F32=jnp.float32
def dot(a, b, dims=(((1,), (0,)), ((), ()))):
    return lax.dot_general(a, b, dims, preferred_element_type=F32)
NT=(((1,),(1,)),((),()))
TN=(((0,),(0,)),((),()))
ANY=pl.BlockSpec(memory_space=pl.ANY)
VM=pl.BlockSpec(memory_space=pltpu.VMEM)
SM=pl.BlockSpec(memory_space=pltpu.SMEM)

def gelu_both(u):
    c0=math.sqrt(2/math.pi)
    sq=u*u
    t=jnp.tanh(u*(c0+(c0*0.044715)*sq))
    half=0.5+0.5*t
    value=u*half
    slope=half+(0.5*u)*(1.0-t*t)*(c0+(3*c0*0.044715)*sq)
    return value,slope

def mlp_kernel(keys,*refs,gtile):
    nk=len(keys)
    at_ref,h2_ref,go_ref,gt_ref,bu_ref=refs[:5]
    own=refs[5:7]
    pa,pb=refs[7:7+nk],refs[7+nk:7+2*nk]
    o=7+2*nk
    ga,gb=refs[o:o+nk],refs[o+nk:o+2*nk]
    yown_ref,yoth_ref,dh_ref,gbu_ref=refs[o+2*nk:o+2*nk+4]
    w,dd,a_all,du_all,y_acc,dh_acc,g_out,wsem,gsem=refs[o+2*nk+4:]
    images,half,feat=go_ref.shape
    hid=pa[0].shape[1]
    width=4*hid
    padded=h2_ref.shape[0]//(2*images)
    blocks=2*images

    def load(i,slot,go):
        for ki in range(nk):
            @pl.when(i==ki)
            def _():
                for kz in range(2):
                    for ud in range(2):
                        for ab,src in enumerate((pa[ki],pb[ki])):
                            src=own[ab].at[keys[ki][0],keys[ki][1]] if kz==0 else src
                            cp=pltpu.make_async_copy(src.at[ud],w.at[slot,ud,pl.ds((kz*2+ab)*hid,hid)],wsem.at[slot,kz*4+ud*2+ab])
                            cp.start() if go else cp.wait()
    def save(i,go):
        for ki in range(nk):
            @pl.when(i==ki)
            def _():
                for kz in range(2):
                    for ud in range(2):
                        for ab,dst in enumerate((ga[ki],gb[ki])):
                            cp=pltpu.make_async_copy(g_out.at[ud,pl.ds((kz*2+ab)*hid,hid)],dst.at[kz,ud],gsem.at[kz*4+ud*2+ab])
                            cp.start() if go else cp.wait()
    load(0,0,True)
    gbu_ref[...]=jnp.zeros_like(gbu_ref)
    for i in range(images):
        for s,src in enumerate((go_ref,gt_ref)):
            r=(2*i+s)*padded
            tail=padded-16
            dd[r+tail:r+padded,:]=jnp.zeros((16,feat),BF)
            dd[r:r+half,:]=src[i]
    def step(i,_):
        slot=lax.rem(i,2)
        load(i,slot,False)
        @pl.when(i+1<nk)
        def _(): load(i+1,1-slot,True)
        rows=[]
        for kz in range(2):
            for ab in range(2):
                row=jnp.int32(0)
                for ki,(ky,kx) in enumerate(keys):
                    z=lax.rem(at_ref[0]+kz,2); y=lax.rem(at_ref[1]+ky,at_ref[4]); x=lax.rem(at_ref[2]+kx,at_ref[5])
                    here=(((z*at_ref[4]+y)*at_ref[5]+x)*2+at_ref[3])*2+ab
                    row=jnp.where(i==ki,here,row)
                rows.append(row)
        bias=jnp.concatenate([bu_ref[pl.ds(r,1),:] for r in rows],axis=1)
        wu=w.at[slot,0]; wd=w.at[slot,1]
        def tokens(b,sums):
            r=pl.ds(pl.multiple_of(b*padded,16),padded)
            u=dot(h2_ref[r,:],wu[...],NT)+bias
            value,slope=gelu_both(u)
            a=value.astype(BF)
            a_all[r,:]=a
            dg=dot(dd[r,:],wd[...],NT)
            du=(dg*slope).astype(BF)
            du_all[r,:]=du
            ynew=dot(a,wd[...]); dnew=dot(du,wu[...])
            @pl.when(i==0)
            def _():
                y_acc[r,:]=ynew; dh_acc[r,:]=dnew
            @pl.when(i>0)
            def _():
                y_acc[r,:]+=ynew; dh_acc[r,:]+=dnew
            return sums+jnp.sum(du.astype(F32),axis=0,keepdims=True)
        sums=lax.fori_loop(0,blocks,tokens,jnp.zeros((1,width),F32))
        for q,row in enumerate(rows):
            gbu_ref[pl.ds(row,1),:]=sums[:,q*hid:(q+1)*hid]
        @pl.when(i>0)
        def _(): save(i-1,False)
        for t in range(0,width,gtile):
            g_out[1,t:t+gtile,:]=dot(a_all[:,t:t+gtile],dd[...],TN).astype(BF)
            g_out[0,t:t+gtile,:]=dot(du_all[:,t:t+gtile],h2_ref[...],TN).astype(BF)
        save(i,True)
        return 0
    lax.fori_loop(0,nk,step,0)
    for i in range(images):
        r=2*i*padded
        yown_ref[i]=y_acc[r:r+padded,:]
        yoth_ref[i]=y_acc[r+padded:r+2*padded,:].astype(BF)
    dh_ref[...]=dh_acc[...].astype(BF)
    save(nk-1,False)

def mlp(at,h2,g_own,g_oth,bu_rows,own_a,own_b,fa,fb,gtile=256):
    keys=sorted(fa); nk=len(keys)
    images,half,feat=g_own.shape
    tokens=h2.shape[0]; padded=tokens//(2*images)
    ud,hid,_=fa[keys[0]].shape
    width=4*hid
    piece=jax.ShapeDtypeStruct((2,ud,hid,feat),BF)
    out=pl.pallas_call(functools.partial(mlp_kernel,keys,gtile=min(gtile,width)),
        in_specs=[SM]+[VM]*4+[ANY]*(2+2*nk),
        out_specs=[ANY]*(2*nk)+[VM]*4,
        out_shape=[piece]*(2*nk)+[jax.ShapeDtypeStruct((images,padded,feat),F32),jax.ShapeDtypeStruct((images,padded,feat),BF),
            jax.ShapeDtypeStruct((tokens,feat),BF),jax.ShapeDtypeStruct(bu_rows.shape,F32)],
        scratch_shapes=[pltpu.VMEM((2,2,width,feat),BF),pltpu.VMEM((tokens,feat),BF),pltpu.VMEM((tokens,width),BF),pltpu.VMEM((tokens,width),BF),
            pltpu.VMEM((tokens,feat),F32),pltpu.VMEM((tokens,feat),F32),pltpu.VMEM((2,width,feat),BF),
            pltpu.SemaphoreType.DMA((2,8)),pltpu.SemaphoreType.DMA((8,))],
        name="feed_forward",
        compiler_params=pltpu.CompilerParams(vmem_limit_bytes=60<<20),
        cost_estimate=pl.CostEstimate(flops=nk*6*2*tokens*feat*width,bytes_accessed=40<<20,transcendentals=nk*tokens*width),
    )(at,h2,g_own,g_oth,bu_rows,own_a,own_b,*[fa[k] for k in keys],*[fb[k] for k in keys])
    return dict(zip(keys,out[:nk])),dict(zip(keys,out[nk:2*nk])),out[2*nk],out[2*nk+1],out[2*nk+2],out[2*nk+3]

HD=64; HALF_D=512

def head_operands(q_ref,k_ref,kb_ref,scale):
    q=q_ref[0].astype(F32)*scale; k=k_ref[0].astype(F32); kb=kb_ref[0].astype(F32)
    lane=lax.broadcasted_iota(jnp.int32,q.shape,1)
    low=lane<HD
    one=jnp.where((lane==0)|(lane==HD),1.0,0.0)
    qs=[jnp.where(low,q,one).astype(BF),jnp.where(low,one,q).astype(BF)]
    ks=[jnp.where(low,k,kb).astype(BF),jnp.where(low,kb,k).astype(BF)]
    return q,k,low,qs,ks

def attend_kernel(q_ref,k_ref,v_ref,kb_ref,o_ref,lse_ref):
    q,k,low,qs,ks=head_operands(q_ref,k_ref,kb_ref,HD**-0.5)
    vt=v_ref[0].astype(F32).T.astype(BF)
    outs=[]
    for j in range(2):
        s=dot(ks[j],qs[j],NT)
        m=jnp.max(s,axis=0,keepdims=True)
        e=jnp.exp(s-m)
        l=jnp.sum(e,axis=0,keepdims=True)
        o=dot(vt[j*HD:(j+1)*HD],e.astype(BF))
        outs.append(o*(1.0/l))
        lse_ref[0,0,j:j+1,:]=m+jnp.log(l)
    o_ref[0]=jnp.concatenate(outs,axis=0).T.astype(BF)

def attend(qkv,kbias):
    n,rows,w=qkv.shape; pairs=w//3//128
    blk=lambda off: pl.BlockSpec((1,rows,128),lambda i,p: (i,0,off+p))
    return pl.pallas_call(attend_kernel,grid=(n,pairs),
        in_specs=[blk(0),blk(pairs),blk(2*pairs),pl.BlockSpec((1,rows,128),lambda i,p:(i,0,0))],
        out_specs=[blk(0),pl.BlockSpec((1,1,8,rows),lambda i,p:(i,p,0,0))],
        out_shape=[jax.ShapeDtypeStruct((n,rows,w//3),BF),jax.ShapeDtypeStruct((n,pairs,8,rows),F32)],
        name="attend",
        compiler_params=pltpu.CompilerParams(vmem_limit_bytes=50<<20),
        cost_estimate=pl.CostEstimate(flops=n*pairs*8*rows*rows*128,bytes_accessed=n*rows*w*3,transcendentals=n*pairs*2*rows*rows),
    )(qkv,qkv,qkv,kbias)

def attend_back_kernel(q_ref,k_ref,v_ref,kb_ref,o_ref,g_ref,lse_ref,out_ref,sum_ref,*,pairs,chunk):
    p=pl.program_id(1)
    @pl.when((pl.program_id(0)==0)&(p==0))
    def _(): sum_ref[...]=jnp.zeros_like(sum_ref)
    scale=HD**-0.5
    q,k,low,qs,ks=head_operands(q_ref,k_ref,kb_ref,scale)
    qb=q.astype(BF)
    kt=k.T.astype(BF)
    g=g_ref[0]; gf=g.astype(F32)
    prod=(gf*o_ref[0].astype(F32)).T
    v=v_ref[0]
    rows=q.shape[0]
    dqs=[];dks=[];dvs=[]
    for j in range(2):
        gj=(jnp.where(low,gf,0.0) if j==0 else jnp.where(low,0.0,gf)).astype(BF)
        delta=jnp.sum(prod[j*HD:(j+1)*HD],axis=0,keepdims=True)
        lse=lse_ref[0,0,j:j+1,:]
        dq=None; dk=[]; dv=[]
        for r in range(0,rows,chunk):
            s=dot(ks[j][r:r+chunk],qs[j],NT)
            pr=jnp.exp(s-lse)
            dp=dot(v[r:r+chunk],gj,NT)
            ds=(pr*(dp-delta)).astype(BF)
            dv.append(dot(pr.astype(BF),g))
            dk.append(dot(ds,qb))
            t=dot(kt[j*HD:(j+1)*HD,r:r+chunk],ds) if chunk==rows else dot(k[r:r+chunk].astype(BF),ds,TN)[j*HD:(j+1)*HD]
            dq=t if dq is None else dq+t
        dqs.append(dq)
        dks.append(jnp.concatenate(dk,axis=0) if len(dk)>1 else dk[0]); dvs.append(jnp.concatenate(dv,axis=0) if len(dv)>1 else dv[0])
    parts=((jnp.concatenate(dqs,axis=0)*scale).T.astype(BF),jnp.where(low,dks[0],dks[1]).astype(BF),jnp.where(low,dvs[0],dvs[1]).astype(BF))
    for t,part in enumerate(parts):
        at=pl.ds(pl.multiple_of((t*pairs+p)*128,128),128)
        out_ref[0,:,at]=part
        sum_ref[0:1,at]+=jnp.sum(part.astype(F32),axis=0,keepdims=True)

def attend_back(qkv,kbias,mixed,grad,lse,chunk=None):
    n,rows,w=qkv.shape; pairs=w//3//128
    chunk=chunk or rows
    blk=lambda off: pl.BlockSpec((1,rows,128),lambda i,p: (i,0,off+p))
    return pl.pallas_call(functools.partial(attend_back_kernel,pairs=pairs,chunk=chunk),grid=(n,pairs),
        in_specs=[blk(0),blk(pairs),blk(2*pairs),pl.BlockSpec((1,rows,128),lambda i,p:(i,0,0)),blk(0),blk(0),pl.BlockSpec((1,1,8,rows),lambda i,p:(i,p,0,0))],
        out_specs=[pl.BlockSpec((1,rows,w),lambda i,p:(i,0,0)),pl.BlockSpec((8,w),lambda i,p:(0,0))],
        out_shape=[jax.ShapeDtypeStruct((n,rows,w),BF),jax.ShapeDtypeStruct((8,w),F32)],
        name="attend_back",
        compiler_params=pltpu.CompilerParams(vmem_limit_bytes=50<<20),
        cost_estimate=pl.CostEstimate(flops=n*pairs*20*rows*rows*128,bytes_accessed=n*rows*w*5,transcendentals=n*pairs*2*rows*rows),
    )(qkv,qkv,qkv,kbias,mixed,grad,lse)

NORM_EPS=1e-6
def norm_parts(values):
    center = values - jnp.mean(values, axis=-1, keepdims=True)
    inverse = lax.rsqrt(jnp.mean(center * center, axis=-1, keepdims=True) + NORM_EPS)
    return center * inverse, inverse

def norm_back(values, gain, grad):
    normed, inverse = norm_parts(values)
    scaled = grad * gain
    mean_one = jnp.mean(scaled, axis=-1, keepdims=True)
    mean_two = jnp.mean(scaled * normed, axis=-1, keepdims=True)
    return (scaled - mean_one - normed * mean_two) * inverse, grad * normed

def wide_rows(buf,block):
    n=block.shape[0]; total=buf.shape[0]
    buf[total-16:,:]=jnp.zeros((16,buf.shape[1]),F32)
    buf[0:n,:]=block.astype(F32)
    return buf[...]

def place(at_ref,keys,ka,size,pieces,buf,sem,gather):
    def both(go):
        n=0
        for ki,(ky,kx) in enumerate(keys):
            y=lax.rem(at_ref[1]+ky,at_ref[4]); x=lax.rem(at_ref[2]+kx,at_ref[5])
            for ab in range(2):
                for kz in range(ka):
                    z=lax.rem(at_ref[0]+kz,2) if ka==2 else 0
                    core=at_ref[3] if ab==0 else 1-at_ref[3]
                    if ka==1: core=at_ref[0] if ab==0 else 1-at_ref[0]
                    row=(((z*at_ref[4]+y)*at_ref[5]+x)*2+core)*size
                    inner=buf.at[pl.ds(pl.multiple_of(row,16),size)]
                    piece=pieces[ab*len(keys)+ki]
                    piece=piece.at[kz] if ka==2 else piece
                    cp=pltpu.make_async_copy(piece,inner,sem.at[n]) if gather else pltpu.make_async_copy(inner,piece,sem.at[n])
                    cp.start() if go else cp.wait()
                    n+=1
    both(True); both(False)

def project_kernel(keys,at_ref,own_ref,oth_ref,gain_ref,shift_ref,bias_ref,*refs):
    nk=len(keys)
    pieces=refs[:2*nk]; h_ref,qkv_ref,w,buf,sem=refs[2*nk:]
    @pl.when(pl.program_id(0)==0)
    def _(): place(at_ref,keys,2,pieces[0].shape[1],pieces,w,sem,True)
    for s,src in enumerate((own_ref,oth_ref)):
        v=wide_rows(buf.at[s],src[0])
        h=(norm_parts(v)[0]*gain_ref[...]+shift_ref[...]).astype(BF)
        h_ref[0,s]=h
        qkv_ref[0,s]=(dot(h,w[...])+bias_ref[...]).astype(BF)

def project(at,x_own,x_oth,gain,shift,bias,wa,wb,padded):
    keys=sorted(wa); nk=len(keys)
    n,half,feat=x_own.shape
    width=wa[keys[0]].shape[-1]
    tok=pl.BlockSpec((1,half,feat),lambda i:(i,0,0))
    row=lambda w: pl.BlockSpec((1,w),lambda i:(0,0))
    return pl.pallas_call(functools.partial(project_kernel,keys),grid=(n,),
        in_specs=[SM,tok,tok,row(feat),row(feat),row(width)]+[ANY]*(2*nk),
        out_specs=[pl.BlockSpec((1,2,padded,feat),lambda i:(i,0,0,0)),pl.BlockSpec((1,2,padded,width),lambda i:(i,0,0,0))],
        out_shape=[jax.ShapeDtypeStruct((n,2,padded,feat),BF),jax.ShapeDtypeStruct((n,2,padded,width),BF)],
        scratch_shapes=[pltpu.VMEM((feat,width),BF),pltpu.VMEM((2,padded,feat),F32),pltpu.SemaphoreType.DMA((4*nk,))],
        name="project",
        compiler_params=pltpu.CompilerParams(vmem_limit_bytes=50<<20),
        cost_estimate=pl.CostEstimate(flops=n*4*padded*feat*width,bytes_accessed=24<<20,transcendentals=0),
    )(at,x_own,x_oth,gain[None],shift[None],bias[None],*[wa[k] for k in keys],*[wb[k] for k in keys])

def gather_kernel(keys,at_ref,*refs):
    nk=len(keys)
    place(at_ref,keys,1,refs[0].shape[0],refs[:2*nk],refs[2*nk],refs[2*nk+1],True)

def gather_rows(at,pa,pb):
    keys=sorted(pa); nk=len(keys)
    rows,feat=pa[keys[0]].shape
    return pl.pallas_call(functools.partial(gather_kernel,keys),in_specs=[SM]+[ANY]*(2*nk),out_specs=VM,
        out_shape=jax.ShapeDtypeStruct((2*nk*rows,feat),BF),scratch_shapes=[pltpu.SemaphoreType.DMA((2*nk,))],name="gather_rows",
    )(at,*[pa[k] for k in keys],*[pb[k] for k in keys])

def middle_kernel(own_ref,oth_ref,mo_ref,mt_ref,wo_ref,wt_ref,bias_ref,gain_ref,shift_ref,x2_ref,h2_ref,buf):
    for s,src in enumerate((own_ref,oth_ref)):
        v=wide_rows(buf.at[s],src[0])
        v=v+(dot(mo_ref[0,s],wo_ref[...])+dot(mt_ref[0,1-s],wt_ref[...]))+bias_ref[...]
        x2_ref[0,s]=v
        h2_ref[0,s]=(norm_parts(v)[0]*gain_ref[...]+shift_ref[...]).astype(BF)

def middle(x_own,x_oth,mixed,mixed_oth,w_own,w_oth,bias,gain,shift):
    n,half,feat=x_own.shape
    _,_,padded,width=mixed.shape
    tok=pl.BlockSpec((1,half,feat),lambda i:(i,0,0))
    mix=pl.BlockSpec((1,2,padded,width),lambda i:(i,0,0,0))
    swp=pl.BlockSpec((1,2,padded,width),lambda i:(i,0,0,0))
    full=pl.BlockSpec((width,feat),lambda i:(0,0))
    row=pl.BlockSpec((1,feat),lambda i:(0,0))
    out=pl.BlockSpec((1,2,padded,feat),lambda i:(i,0,0,0))
    return pl.pallas_call(middle_kernel,grid=(n,),in_specs=[tok,tok,mix,swp,full,full,row,row,row],out_specs=[out,out],
        out_shape=[jax.ShapeDtypeStruct((n,2,padded,feat),F32),jax.ShapeDtypeStruct((n,2,padded,feat),BF)],
        scratch_shapes=[pltpu.VMEM((2,padded,feat),F32)],name="middle",
        compiler_params=pltpu.CompilerParams(vmem_limit_bytes=50<<20),
        cost_estimate=pl.CostEstimate(flops=n*8*padded*feat*width,bytes_accessed=26<<20,transcendentals=0),
    )(x_own,x_oth,mixed,mixed_oth,w_own,w_oth,bias[None],gain[None],shift[None])

def middle_back_kernel(x2_ref,da_ref,db_ref,go_ref,gt_ref,mix_ref,w_ref,gain_ref,dx_ref,dat_ref,gw_ref,sum_ref,buf,acc):
    i=pl.program_id(0)
    @pl.when(i==0)
    def _():
        acc[...]=jnp.zeros_like(acc); sum_ref[...]=jnp.zeros_like(sum_ref)
    for s,src in enumerate((go_ref,gt_ref)):
        dd=wide_rows(buf.at[s],src[0])
        grad=da_ref[0,s].astype(F32)+db_ref[0,1-s].astype(F32)
        dx,gg=norm_back(x2_ref[0,s],gain_ref[...],grad)
        dx=dx+dd
        dob=dx.astype(BF)
        if s==0:
            dx_ref[0]=dx
            for r,t in enumerate((gg,grad,dob.astype(F32),dd)):
                sum_ref[r:r+1,:]+=jnp.sum(t,axis=0,keepdims=True)
        dat_ref[0,s]=dot(dob,w_ref[...],NT).astype(BF)
        acc[...]+=dot(mix_ref[0,s],dob,TN)
    @pl.when(i==pl.num_programs(0)-1)
    def _(): gw_ref[...]=acc[...].astype(BF)

def middle_back(x2,dh_own,dh_oth,g_own,g_oth,mixed,w_own,gain):
    n,half,feat=g_own.shape
    _,_,padded,width=mixed.shape
    tok=pl.BlockSpec((1,half,feat),lambda i:(i,0,0))
    mix=pl.BlockSpec((1,2,padded,width),lambda i:(i,0,0,0))
    big=pl.BlockSpec((1,2,padded,feat),lambda i:(i,0,0,0))
    full=pl.BlockSpec((width,feat),lambda i:(0,0))
    return pl.pallas_call(middle_back_kernel,grid=(n,),
        in_specs=[big,big,big,tok,tok,mix,full,pl.BlockSpec((1,feat),lambda i:(0,0))],
        out_specs=[pl.BlockSpec((1,padded,feat),lambda i:(i,0,0)),mix,full,pl.BlockSpec((8,feat),lambda i:(0,0))],
        out_shape=[jax.ShapeDtypeStruct((n,padded,feat),F32),jax.ShapeDtypeStruct(mixed.shape,BF),jax.ShapeDtypeStruct((width,feat),BF),jax.ShapeDtypeStruct((8,feat),F32)],
        scratch_shapes=[pltpu.VMEM((2,padded,feat),F32),pltpu.VMEM((width,feat),F32)],name="middle_back",
        compiler_params=pltpu.CompilerParams(vmem_limit_bytes=56<<20),
        cost_estimate=pl.CostEstimate(flops=n*8*padded*feat*width,bytes_accessed=30<<20,transcendentals=0),
    )(x2,dh_own,dh_oth,g_own,g_oth,mixed,w_own,gain[None])

def grad_in_kernel(keys,tile,at_ref,h_ref,d_ref,*refs):
    nk=len(keys)
    pieces=refs[:2*nk]; buf,sem=refs[2*nk:]
    for t in range(0,h_ref.shape[1],tile):
        buf[t:t+tile,:]=dot(h_ref[:,t:t+tile],d_ref[...],TN).astype(BF)
    place(at_ref,keys,2,pieces[0].shape[1],pieces,buf,sem,False)

def grad_in(at,h1,dqkv,keys,rows):
    tokens,feat=h1.shape; width=dqkv.shape[1]
    nk=len(keys)
    out=pl.pallas_call(functools.partial(grad_in_kernel,keys,256),in_specs=[SM,VM,VM],out_specs=[ANY]*(2*nk),
        out_shape=[jax.ShapeDtypeStruct((2,rows,width),BF)]*(2*nk),
        scratch_shapes=[pltpu.VMEM((feat,width),BF),pltpu.SemaphoreType.DMA((4*nk,))],name="grad_in",
        compiler_params=pltpu.CompilerParams(vmem_limit_bytes=50<<20),
        cost_estimate=pl.CostEstimate(flops=2*tokens*feat*width,bytes_accessed=14<<20,transcendentals=0),
    )(at,h1,dqkv)
    return dict(zip(keys,out[:nk])),dict(zip(keys,out[nk:]))

def project_back_kernel(keys,at_ref,d_ref,*refs):
    nk=len(keys)
    pieces=refs[:2*nk]; own_ref,oth_ref,w,sem=refs[2*nk:]
    @pl.when(pl.program_id(0)==0)
    def _(): place(at_ref,keys,2,pieces[0].shape[1],pieces,w,sem,True)
    own_ref[0]=dot(d_ref[0,0],w[...],NT)
    oth_ref[0]=dot(d_ref[0,1],w[...],NT).astype(BF)

def project_back(at,dqkv,wa,wb):
    keys=sorted(wa); nk=len(keys)
    n,_,padded,width=dqkv.shape
    feat=wa[keys[0]].shape[1]*4*nk
    out=pl.BlockSpec((1,padded,feat),lambda i:(i,0,0))
    return pl.pallas_call(functools.partial(project_back_kernel,keys),grid=(n,),
        in_specs=[SM,pl.BlockSpec((1,2,padded,width),lambda i:(i,0,0,0))]+[ANY]*(2*nk),out_specs=[out,out],
        out_shape=[jax.ShapeDtypeStruct((n,padded,feat),F32),jax.ShapeDtypeStruct((n,padded,feat),BF)],
        scratch_shapes=[pltpu.VMEM((feat,width),BF),pltpu.SemaphoreType.DMA((4*nk,))],name="project_back",
        compiler_params=pltpu.CompilerParams(vmem_limit_bytes=50<<20),
        cost_estimate=pl.CostEstimate(flops=n*4*padded*feat*width,bytes_accessed=18<<20,transcendentals=0),
    )(at,dqkv,*[wa[k] for k in keys],*[wb[k] for k in keys])

def input_back_kernel(x_ref,da_ref,db_ref,dx_ref,gain_ref,out_ref,sum_ref,buf):
    @pl.when(pl.program_id(0)==0)
    def _(): sum_ref[...]=jnp.zeros_like(sum_ref)
    half=x_ref.shape[1]
    v=wide_rows(buf,x_ref[0])
    grad=da_ref[0]+db_ref[0].astype(F32)
    dx,gg=norm_back(v,gain_ref[...],grad)
    out_ref[0]=(dx+dx_ref[0]).astype(BF)[:half]
    sum_ref[0:1,:]+=jnp.sum(gg,axis=0,keepdims=True)
    sum_ref[1:2,:]+=jnp.sum(grad,axis=0,keepdims=True)

def input_back(x_own,dh_own,dh_oth,dx2,gain):
    n,half,feat=x_own.shape
    padded=dx2.shape[1]
    tok=pl.BlockSpec((1,half,feat),lambda i:(i,0,0))
    big=pl.BlockSpec((1,padded,feat),lambda i:(i,0,0))
    return pl.pallas_call(input_back_kernel,grid=(n,),in_specs=[tok,big,big,big,pl.BlockSpec((1,feat),lambda i:(0,0))],
        out_specs=[tok,pl.BlockSpec((8,feat),lambda i:(0,0))],
        out_shape=[jax.ShapeDtypeStruct(x_own.shape,BF),jax.ShapeDtypeStruct((8,feat),F32)],
        scratch_shapes=[pltpu.VMEM((padded,feat),F32)],name="input_back",
        compiler_params=pltpu.CompilerParams(vmem_limit_bytes=40<<20),
        cost_estimate=pl.CostEstimate(flops=n*20*padded*feat,bytes_accessed=14<<20,transcendentals=0),
    )(x_own,dh_own,dh_oth,dx2,gain[None])

MESH_ID = pl.DeviceIdType.MESH


class Wires:
    def __init__(self, send_sem, recv_sem):
        self.send_sem, self.recv_sem, self.count, self.sent = send_sem, recv_sem, 0, []

    def make(self, src, dst, to):
        cp = pltpu.make_async_remote_copy(
            src_ref=src, dst_ref=dst, send_sem=self.send_sem.at[self.count], recv_sem=self.recv_sem.at[self.count],
            device_id=to, device_id_type=MESH_ID)
        self.count += 1
        return cp

    def send(self, src, dst, to):
        cp = self.make(src, dst, to)
        cp.start()
        self.sent.append(cp)
        return cp

    def finish(self):
        for cp in self.sent:
            cp.wait_send()


def greet(peers, crossing_peer, apart):
    barrier = pltpu.get_barrier_semaphore()
    for peer in peers:
        pl.semaphore_signal(barrier, inc=1, device_id=peer, device_id_type=MESH_ID)

    @pl.when(apart)
    def _():
        pl.semaphore_signal(barrier, inc=1, device_id=crossing_peer, device_id_type=MESH_ID)

    pl.semaphore_wait(barrier, len(peers) + jnp.where(apart, 1, 0))


def add_all(first, *others):
    total = first.astype(F32)
    for other in others:
        total = total + other.astype(F32)
    return total


def tail_kernel(ny, nx, *refs):
    h1_ref, dqkv_ref, go_ref, x_ref, dx_ref, gain_ref, vec_ref, w = refs[:8]
    o = 8
    fa, fb = refs[o:o + nx], refs[o + nx:o + nx + ny]
    o += nx + ny
    mine_ref, theirs_ref, so_ref, sf_ref, ig_ref, vout_ref, norm_ref = refs[o:o + 7]
    (grad, ra1, ra2, rb1, rb2, sa, sb, oa1, oa2, ob1, ob2, ta, tb, osum, ocross, ocore, odp, ofin,
     rfa, rfb, fsum, fpart, frecv, fdp, isum, ipart, irecv, idp, ifin,
     buf, give, got, stage, vrecv, nrecv, nval, send_sem, recv_sem) = refs[o + 7:]
    h, y, x, c, l = (lax.axis_index(a) for a in AXES)
    images, half, feat = x_ref.shape
    padded = dx_ref.shape[1]
    rows = grad.shape[4]
    apart = h != c
    cross = {"seq": 1 - h, "core": 1 - c}
    to_core, to_seq, to_dp = {"core": 1 - c}, {"seq": 1 - h}, {"dp": 1 - l}
    to_x = [{"x": lax.rem(x + k, nx)} for k in range(nx)]
    to_y = [{"y": lax.rem(y + k, ny)} for k in range(ny)]
    yy = [lax.rem(y + k, ny) for k in range(ny)]
    xx = [lax.rem(x + k, nx) for k in range(nx)]
    zz = [h, 1 - h]
    wires = Wires(send_sem, recv_sem)
    greet([to_core, to_seq, to_dp] + to_x[1:] + to_y[1:], cross, apart)

    ff_got = [wires.send(fa[k], rfa.at[k - 1], to_x[k]) for k in range(1, nx)]
    ff_got += [wires.send(fb[k], rfb.at[k - 1], to_y[k]) for k in range(1, ny)]
    oa_got = [[wires.send(go_ref.at[yy[ky], xx[kx], h], oa1.at[ky - 1, kx], to_y[ky]) for kx in range(nx)] for ky in range(1, ny)]
    ob_got = [[wires.send(go_ref.at[yy[ky], xx[kx], 1 - h], ob1.at[kx - 1, ky], to_x[kx]) for ky in range(ny)] for kx in range(1, nx)]
    width = nx * 2 * rows
    ia_got, ib_got = [], []
    for ky in range(ny - 1, -1, -1):
        for kz in range(2):
            col = pl.multiple_of((zz[kz] * ny + yy[ky]) * width, 128)
            t = dot(h1_ref[:, pl.ds(col, width)], dqkv_ref[...], TN).astype(BF)
            for q in range(nx):
                for core in range(2):
                    r = (q * 2 + core) * rows
                    grad[zz[kz], yy[ky], q, core] = t[r:r + rows]
        if ky > 0:
            for kx in range(nx):
                for kz in range(2):
                    ia_got.append(wires.send(grad.at[zz[kz], yy[ky], xx[kx], c], ra1.at[ky - 1, kz, kx], to_y[ky]))
    for kx in range(1, nx):
        for ky in range(ny):
            for kz in range(2):
                ib_got.append(wires.send(grad.at[zz[kz], yy[ky], xx[kx], 1 - c], rb1.at[kx - 1, kz, ky], to_x[kx]))
    dh_got = []
    for i in range(images):
        r = (2 * i + 1) * padded
        give[i] = dot(dqkv_ref[r:r + padded, :], w[...], NT).astype(BF)
        dh_got.append(wires.send(give.at[i], got.at[i], to_core))
    for cp in ff_got:
        cp.wait_recv()
    fsum[0] = add_all(fa[0][...], *(rfa[k] for k in range(nx - 1))).astype(BF)
    fsum[1] = add_all(fb[0][...], *(rfb[k] for k in range(ny - 1))).astype(BF)
    fd = wires.send(fsum.at[1 - l], fdp, to_dp)
    for row in oa_got + ob_got:
        for cp in row:
            cp.wait_recv()
    o_got = []
    for kx in range(1, nx):
        ta[kx - 1] = add_all(go_ref[y, xx[kx], h], *(oa1[k, kx] for k in range(ny - 1))).astype(BF)
        o_got.append(wires.send(ta.at[kx - 1], oa2.at[kx - 1], to_x[kx]))
    for ky in range(1, ny):
        tb[ky - 1] = add_all(go_ref[yy[ky], x, 1 - h], *(ob1[k, ky] for k in range(nx - 1))).astype(BF)
        o_got.append(wires.send(tb.at[ky - 1], ob2.at[ky - 1], to_y[ky]))

    sum_gain, sum_shift = jnp.zeros((1, feat), F32), jnp.zeros((1, feat), F32)
    crossing_copies = [wires.make(stage.at[i], ig_ref.at[i], cross) for i in range(images)]

    def input_back(i, sum_gain, sum_shift):
        r = 2 * i * padded
        own = dot(dqkv_ref[r:r + padded, :], w[...], NT)
        dh_got[i].wait_recv()
        g = own + got[i].astype(F32)
        dx, gg = norm_back(wide_rows(buf, x_ref[i]), gain_ref[...], g)
        stage[i] = (dx + dx_ref[i]).astype(BF)[:half]

        @pl.when(apart)
        def _():
            crossing_copies[i].start()

        @pl.when(jnp.logical_not(apart))
        def _():
            ig_ref[i] = stage[i]

        return sum_gain + jnp.sum(gg, axis=0, keepdims=True), sum_shift + jnp.sum(g, axis=0, keepdims=True)

    sum_gain, sum_shift = input_back(0, sum_gain, sum_shift)
    for cp in ia_got + ib_got:
        cp.wait_recv()
    i_got = []
    for kz in range(2):
        for kx in range(1, nx):
            sa[kx - 1, kz] = add_all(grad[zz[kz], y, xx[kx], c], *(ra1[k, kz, kx] for k in range(ny - 1))).astype(BF)
        for ky in range(1, ny):
            sb[ky - 1, kz] = add_all(grad[zz[kz], yy[ky], x, 1 - c], *(rb1[k, kz, ky] for k in range(nx - 1))).astype(BF)
    for kx in range(1, nx):
        i_got.append(wires.send(sa.at[kx - 1], ra2.at[kx - 1], to_x[kx]))
    for ky in range(1, ny):
        i_got.append(wires.send(sb.at[ky - 1], rb2.at[ky - 1], to_y[ky]))
    sum_gain, sum_shift = input_back(1, sum_gain, sum_shift)
    fd.wait_recv()
    fpart[...] = add_all(fsum[l], fdp[...]).astype(BF)
    fs = wires.send(fpart.at[1], frecv, to_seq)
    for i in range(2, images):
        sum_gain, sum_shift = input_back(i, sum_gain, sum_shift)
    vout_ref[...] = vec_ref[...]
    for q in range(feat // 128):
        vout_ref[q:q + 1, :] = sum_gain[:, q * 128:(q + 1) * 128]
        vout_ref[feat // 128 + q:feat // 128 + q + 1, :] = sum_shift[:, q * 128:(q + 1) * 128]
    rounds = [[to_core], to_x[1:], to_y[1:], [to_seq], [to_dp]]
    slot = [0]

    def start_round(value, landing, peers):
        first = slot[0]
        cps = [wires.send(value, landing.at[first + k], peer) for k, peer in enumerate(peers)]
        slot[0] += len(peers)
        return first, cps

    def end_round(value_ref, landing, started):
        first, cps = started
        for cp in cps:
            cp.wait_recv()
        for cp in cps:
            cp.wait_send()
        wires.sent = [cp for cp in wires.sent if all(cp is not other for other in cps)]
        value_ref[...] = add_all(value_ref[...], *(landing[first + k] for k in range(len(cps))))

    vec_round = start_round(vout_ref, vrecv, rounds[0])
    for cp in i_got:
        cp.wait_recv()
    for kz in range(2):
        isum[0, kz] = add_all(grad[zz[kz], y, x, c], *(ra1[k, kz, 0] for k in range(ny - 1)), *(ra2[k, kz] for k in range(nx - 1))).astype(BF)
        isum[1, kz] = add_all(grad[zz[kz], y, x, 1 - c], *(rb1[k, kz, 0] for k in range(nx - 1)), *(rb2[k, kz] for k in range(ny - 1))).astype(BF)
    idd = wires.send(isum.at[1 - l], idp, to_dp)
    for cp in o_got:
        cp.wait_recv()
    osum[0] = add_all(go_ref[y, x, h], *(oa1[k, 0] for k in range(ny - 1)), *(oa2[k] for k in range(nx - 1))).astype(BF)
    osum[1] = add_all(go_ref[y, x, 1 - h], *(ob1[k, 0] for k in range(nx - 1)), *(ob2[k] for k in range(ny - 1))).astype(BF)
    out_cross = wires.make(osum, ocross, cross)

    @pl.when(apart)
    def _():
        out_cross.start()

    @pl.when(jnp.logical_not(apart))
    def _():
        ocross[...] = osum[...]

    end_round(vout_ref, vrecv, vec_round)
    vec_round = start_round(vout_ref, vrecv, rounds[1])
    idd.wait_recv()
    ipart[...] = add_all(isum[l], idp[...]).astype(BF)
    is_ = wires.send(ipart.at[1], irecv, to_seq)
    end_round(vout_ref, vrecv, vec_round)
    vec_round = start_round(vout_ref, vrecv, rounds[2])

    @pl.when(apart)
    def _():
        out_cross.wait_recv()

    oc = wires.send(ocross.at[1], ocore, to_core)
    fs.wait_recv()
    sf_ref[l] = add_all(fpart[0], frecv[...]).astype(BF)
    ff_last = wires.send(sf_ref.at[l], sf_ref.at[l], to_dp)
    end_round(vout_ref, vrecv, vec_round)
    vec_round = start_round(vout_ref, vrecv, rounds[3])
    oc.wait_recv()
    ofin[...] = add_all(ocross[0], ocore[...]).astype(BF)
    od = wires.send(ofin, odp, to_dp)
    is_.wait_recv()
    ifin[l] = add_all(ipart[0], irecv[...]).astype(BF)
    in_last = wires.send(ifin.at[l], ifin.at[l], to_dp)
    end_round(vout_ref, vrecv, vec_round)
    vec_round = start_round(vout_ref, vrecv, rounds[4])
    in_last.wait_recv()
    ic = wires.send(ifin.at[1], theirs_ref, to_core)
    mine_ref[...] = ifin[0]
    od.wait_recv()
    so_ref[...] = add_all(ofin[...], odp[...]).astype(BF)
    end_round(vout_ref, vrecv, vec_round)
    ff_last.wait_recv()

    def squares(value):
        value = value.astype(F32)
        return jnp.sum(jnp.sum(value * value, axis=0, keepdims=True), axis=1, keepdims=True)

    shard = ((h * ny + y) * nx + x) * 2 + c
    v = vout_ref[...]
    place = lax.broadcasted_iota(jnp.int32, v.shape, 0) * 128 + lax.broadcasted_iota(jnp.int32, v.shape, 1)
    share = v.shape[0] * 128 // (4 * ny * nx)
    v = jnp.where((place >= shard * share) & (place < (shard + 1) * share), v, 0.0)
    total = squares(v) + squares(so_ref[...]) + squares(mine_ref[...])
    for ab in range(2):
        for ud in range(2):
            total = total + squares(sf_ref[ab, ud])
    ic.wait_recv()
    total = total + squares(theirs_ref[...])
    nval[...] = jnp.broadcast_to(total, nval.shape)
    slot[0] = 0
    for peers in rounds[:4]:
        end_round(nval, nrecv, start_round(nval, nrecv, peers))
    norm_ref[...] = jnp.sqrt(nval[...])

    @pl.when(apart)
    def _():
        for cp in crossing_copies:
            cp.wait_recv()
        for cp in crossing_copies:
            cp.wait_send()
        out_cross.wait_send()

    wires.finish()


def tail_stage(h1, dqkv, g_out, x_own, dx2, gain, vec, w, fa, fb, ny, nx):
    tokens, feat = h1.shape
    width = dqkv.shape[1]
    rows = feat // (4 * ny * nx)
    rows_o = g_out.shape[3]
    images, half, _ = x_own.shape
    padded = dx2.shape[1]
    _, ud, hid, _ = fa[0].shape
    ma, mb = max(ny - 1, 1), max(nx - 1, 1)
    piece, out_piece, ff = (rows, width), (rows_o, feat), (ud, hid, feat)
    peers = 4 + nx - 1 + ny - 1
    many = 200 + 32 * ny * nx
    V = lambda *s: pltpu.VMEM(s, BF)
    scratch = [
        V(2, ny, nx, 2, *piece),
        V(ny - 1, 2, nx, *piece), V(nx - 1, 2, *piece), V(nx - 1, 2, ny, *piece), V(ny - 1, 2, *piece),
        V(nx - 1, 2, *piece), V(ny - 1, 2, *piece),
        V(ny - 1, nx, *out_piece), V(nx - 1, *out_piece), V(nx - 1, ny, *out_piece), V(ny - 1, *out_piece),
        V(nx - 1, *out_piece), V(ny - 1, *out_piece),
        V(2, *out_piece), V(2, *out_piece), V(*out_piece), V(*out_piece), V(*out_piece),
        V(nx - 1, 2, *ff), V(ny - 1, 2, *ff), V(2, 2, *ff), V(2, *ff), V(*ff), V(2, *ff),
        V(2, 2, *piece), V(2, *piece), V(*piece), V(2, *piece), V(2, *piece),
        pltpu.VMEM((padded, feat), F32), V(images, padded, feat), V(images, padded, feat), V(images, half, feat),
        pltpu.VMEM((peers,) + vec.shape, F32), pltpu.VMEM((peers, 8, 128), F32), pltpu.VMEM((8, 128), F32),
        pltpu.SemaphoreType.DMA((many,)), pltpu.SemaphoreType.DMA((many,)),
    ]
    return pl.pallas_call(
        functools.partial(tail_kernel, ny, nx),
        in_specs=[VM] * (8 + nx + ny),
        out_specs=[VM] * 7,
        out_shape=[
            jax.ShapeDtypeStruct(piece, BF), jax.ShapeDtypeStruct(piece, BF), jax.ShapeDtypeStruct(out_piece, BF),
            jax.ShapeDtypeStruct((2,) + ff, BF), jax.ShapeDtypeStruct(x_own.shape, BF),
            jax.ShapeDtypeStruct(vec.shape, F32), jax.ShapeDtypeStruct((8, 128), F32),
        ],
        scratch_shapes=scratch,
        name="tail_stage",
        compiler_params=pltpu.CompilerParams(collective_id=1, has_side_effects=True, vmem_limit_bytes=62 << 20),
        cost_estimate=pl.CostEstimate(flops=4 * tokens * feat * width, bytes_accessed=40 << 20, transcendentals=0),
    )(h1, dqkv, g_out, x_own, dx2, gain[None], vec, w, *fa, *fb)

def head_kernel(ny, nx, *refs):
    (in_ref, out_ref, up_ref, down_ref, vec_ref, img_ref,
     h1_ref, qkv_ref, xb, w, my_out, other_out, fa, fb, cast_ref, vfull,
     theirs, o_own, o_core, tmp, buf, xsem, csem, send_sem, recv_sem) = refs
    h, y, x, c, _ = (lax.axis_index(a) for a in AXES)
    images, half, feat = img_ref.shape
    rows = in_ref.shape[0]
    width = w.shape[1]
    part = width // 3
    hid = up_ref.shape[0] // 2
    apart = h != c
    cross = {"seq": 1 - h, "core": 1 - c}
    to_core, to_seq = {"core": 1 - c}, {"seq": 1 - h}
    to_x = [{"x": lax.rem(x + nx - k, nx)} for k in range(nx)]
    to_y = [{"y": lax.rem(y + ny - k, ny)} for k in range(ny)]
    yy = [lax.rem(y + k, ny) for k in range(ny)]
    xx = [lax.rem(x + k, nx) for k in range(nx)]
    zz = [h, 1 - h]
    wires = Wires(send_sem, recv_sem)
    barrier = pltpu.get_barrier_semaphore()
    peers = [to_core, to_seq] + to_x[1:] + to_y[1:]
    for peer in peers:
        pl.semaphore_signal(barrier, inc=1, device_id=peer, device_id_type=MESH_ID)

    @pl.when(apart)
    def _():
        pl.semaphore_signal(barrier, inc=1, device_id=cross, device_id_type=MESH_ID)

    local_images = pltpu.make_async_copy(img_ref, xb.at[0], xsem)

    @pl.when(jnp.logical_not(apart))
    def _():
        local_images.start()

    def slot(z, yi, xi, core):
        return w.at[pl.ds(pl.multiple_of((((z * ny + yi) * nx + xi) * 2 + core) * rows, 16), rows)]

    mine = slot(h, y, x, c)
    for t in range(3):
        mine[:, t * part:(t + 1) * part] = in_ref[:, pl.ds(pl.multiple_of(t * 2 * part + c * part, 128), part)].astype(BF)
        theirs[:, t * part:(t + 1) * part] = in_ref[:, pl.ds(pl.multiple_of(t * 2 * part + (1 - c) * part, 128), part)].astype(BF)
    vfull[h, y, x, c] = vec_ref[...].astype(BF).astype(F32)
    o_own[...] = out_ref[...].astype(BF)
    pl.semaphore_wait(barrier, len(peers) + jnp.where(apart, 1, 0))

    def spread(piece_at, kz, first):
        got = {}
        for k in range(1, nx):
            got[0, k] = wires.send(piece_at(kz, 0, 0), piece_at(kz, 0, 0, k, "x"), to_x[k])
        for k in range(1, ny):
            got[k, 0] = wires.send(piece_at(kz, 0, 0), piece_at(kz, 0, 0, k, "y"), to_y[k])
        return got

    def forward(piece_at, kz, first, got):
        if first == "x":
            for kx in range(1, nx):
                got[0, kx].wait_recv()
                for ky in range(1, ny):
                    got[ky, kx] = wires.send(piece_at(kz, 0, kx), piece_at(kz, 0, kx, ky, "y"), to_y[ky])
            for ky in range(1, ny):
                got[ky, 0].wait_recv()
        else:
            for ky in range(1, ny):
                got[ky, 0].wait_recv()
                for kx in range(1, nx):
                    got[ky, kx] = wires.send(piece_at(kz, ky, 0), piece_at(kz, ky, 0, kx, "x"), to_x[kx])
            for kx in range(1, nx):
                got[0, kx].wait_recv()

    def settle(got):
        for (ky, kx), cp in got.items():
            if ky > 0 and kx > 0:
                cp.wait_recv()

    def in_a(kz, ky, kx, *_):
        return slot(zz[kz], yy[ky], xx[kx], c)

    def in_b(kz, ky, kx, *_):
        return slot(zz[kz], yy[ky], xx[kx], 1 - c)

    def out_a(kz, ky, kx, *_):
        return my_out.at[yy[ky], xx[kx], h]

    def out_b(kz, ky, kx, *_):
        return my_out.at[yy[ky], xx[kx], 1 - h]

    def by_offset(store, own):
        def piece_at(kz, ky, kx, k=0, axis=""):
            if k == 0 and ky == 0 and kx == 0:
                return own
            return store.at[ky + (k if axis == "y" else 0), kx + (k if axis == "x" else 0)]

        return piece_at

    ff_a, ff_b = by_offset(fa, tmp.at[0]), by_offset(fb, tmp.at[1])

    b_got = wires.send(theirs, slot(h, y, x, c), to_core)
    az = wires.send(mine, mine, to_seq)
    a0 = spread(in_a, 0, "x")
    vec_peers = [[to_core], to_x[1:], to_y[1:], [to_seq]]
    vec_at = [vfull.at[h, y, x, c], vfull.at[h, y, x], vfull.at[h, y], vfull.at[h]]

    def vec_send(r):
        return [wires.send(vec_at[r], vec_at[r], peer) for peer in vec_peers[r]]

    v = vec_send(0)
    oc = wires.send(o_own, o_core, to_core)
    xl = wires.make(img_ref, xb.at[1], to_core)

    @pl.when(jnp.logical_not(apart))
    def _():
        xl.start()

    b_got.wait_recv()
    bz = wires.send(in_b(0, 0, 0), in_b(0, 0, 0), to_seq)
    b0 = spread(in_b, 0, "y")
    for cp in v:
        cp.wait_recv()
    v = vec_send(1)
    for ab in range(2):
        tmp[ab, 0] = up_ref[ab * hid:(ab + 1) * hid, :].astype(BF)
        tmp[ab, 1] = down_ref[ab * hid:(ab + 1) * hid, :].astype(BF)
    keep = [
        pltpu.make_async_copy(tmp.at[0], fa.at[0, 0], csem.at[0]),
        pltpu.make_async_copy(tmp.at[1], fb.at[0, 0], csem.at[1]),
        pltpu.make_async_copy(tmp, cast_ref, csem.at[2]),
    ]
    for cp in keep:
        cp.start()
    for cp in v:
        cp.wait_recv()
    v = vec_send(2)
    forward(in_a, 0, "x", a0)
    forward(in_b, 0, "y", b0)
    az.wait_recv()
    a1 = spread(in_a, 1, "x")
    bz.wait_recv()
    b1 = spread(in_b, 1, "y")
    for cp in v:
        cp.wait_recv()
    v = vec_send(3)
    oc.wait_recv()
    x_cross = [wires.make(img_ref.at[i], xb.at[0, i], cross) for i in range(images)]
    o_cross = [wires.make(o_own, my_out.at[y, x, 1 - h], cross), wires.make(o_core, my_out.at[y, x, h], cross)]

    @pl.when(apart)
    def _():
        x_cross[0].start()
        for cp in o_cross:
            cp.start()
        for cp in x_cross[1:]:
            cp.start()

    @pl.when(jnp.logical_not(apart))
    def _():
        my_out[y, x, h] = o_own[...]
        my_out[y, x, 1 - h] = o_core[...]
        local_images.wait()

    forward(in_a, 1, "x", a1)
    forward(in_b, 1, "y", b1)
    fa0 = spread(ff_a, 0, "x")
    fb0 = spread(ff_b, 0, "y")
    for got in (a0, b0, a1, b1):
        settle(got)
    for cp in v:
        cp.wait_recv()

    def row(start, count):
        per = vec_ref.shape[1]
        pieces, at = [], start
        while at < start + count:
            s, r = at // per, at % per
            n = min(per - r, start + count - at)
            xs = s // 2
            pieces.append(vfull[xs // (nx * ny), xs // nx % ny, xs % nx, s % 2][:, r:r + n])
            at += n
        return pieces[0] if len(pieces) == 1 else jnp.concatenate(pieces, axis=1)

    gain, shift_row = row(0, feat), row(feat, feat)
    q_row, v_row = row(2 * feat, feat), row(3 * feat, feat)
    q_row = jnp.where(c == 0, q_row[:, :part], q_row[:, part:])
    v_row = jnp.where(c == 0, v_row[:, :part], v_row[:, part:])
    bias = jnp.concatenate([q_row, jnp.zeros((1, part), F32), v_row], axis=1)

    def project(i, s):
        value = wide_rows(buf, xb[s, i])
        normed = (norm_parts(value)[0] * gain + shift_row).astype(BF)
        h1_ref[i, s] = normed
        qkv_ref[i, s] = (dot(normed, w[...]) + bias).astype(BF)

    near = jnp.where(apart, 1, 0)

    @pl.when(apart)
    def _():
        xl.wait_recv()

    def near_step(i, carry):
        project(i, near)
        return carry

    lax.fori_loop(0, images, near_step, 0)

    @pl.when(apart)
    def _():
        for cp in o_cross:
            cp.wait_recv()

    oa = spread(out_a, 0, "x")
    ob = spread(out_b, 0, "y")
    forward(ff_a, 0, "x", fa0)
    forward(ff_b, 0, "y", fb0)
    x_core = [wires.make(xb.at[0, i], xb.at[1, i], to_core) for i in range(images)]
    for i in range(images):
        @pl.when(apart)
        def _():
            x_cross[i].wait_recv()
            x_core[i].start()

        @pl.when(jnp.logical_not(apart))
        def _():
            x_core[i].wait_recv()

        project(i, 1 - near)
        if i == 0:
            forward(out_a, 0, "x", oa)
            forward(out_b, 0, "y", ob)
        if i == 1 or images == 1:
            settle(oa)
            settle(ob)
            other = wires.send(my_out, other_out, to_core)
    other.wait_recv()
    settle(fa0)
    settle(fb0)

    @pl.when(apart)
    def _():
        for cp in x_cross + o_cross + x_core:
            cp.wait_send()

    @pl.when(jnp.logical_not(apart))
    def _():
        xl.wait_send()

    for cp in keep:
        cp.wait()
    wires.finish()


def head_stage(in_w, out_w, up_w, down_w, vec, images, padded, ny, nx):
    n, half, feat = images.shape
    rows, rows_out, rows_ff = in_w.shape[0], out_w.shape[0], up_w.shape[0]
    width = in_w.shape[1] // 2
    hid = rows_ff // 2
    many = 60 + 24 * ny * nx
    S = jax.ShapeDtypeStruct
    return pl.pallas_call(
        functools.partial(head_kernel, ny, nx),
        in_specs=[VM] * 5 + [ANY],
        out_specs=[VM] * 6 + [ANY] * 3 + [VM],
        out_shape=[
            S((n, 2, padded, feat), BF), S((n, 2, padded, width), BF), S((2, n, half, feat), BF), S((feat, width), BF),
            S((ny, nx, 2, rows_out, feat), BF), S((ny, nx, 2, rows_out, feat), BF),
            S((ny, nx, 2, hid, feat), BF), S((ny, nx, 2, hid, feat), BF), S((2, 2, hid, feat), BF),
            S((2, ny, nx, 2, 1, vec.shape[1]), F32),
        ],
        scratch_shapes=[
            pltpu.VMEM((rows, width), BF), pltpu.VMEM((rows_out, feat), BF), pltpu.VMEM((rows_out, feat), BF),
            pltpu.VMEM((2, 2, hid, feat), BF), pltpu.VMEM((padded, feat), F32),
            pltpu.SemaphoreType.DMA(()), pltpu.SemaphoreType.DMA((3,)),
            pltpu.SemaphoreType.DMA((many,)), pltpu.SemaphoreType.DMA((many,)),
        ],
        name="head_stage",
        compiler_params=pltpu.CompilerParams(collective_id=2, has_side_effects=True, vmem_limit_bytes=60 << 20),
        cost_estimate=pl.CostEstimate(flops=n * 4 * padded * feat * width, bytes_accessed=40 << 20, transcendentals=0),
    )(in_w, out_w, up_w, down_w, vec, images)


def shift(value, axis, up):
    n = lax.axis_size(axis)
    return lax.ppermute(value, axis, [(i, (i + up) % n) for i in range(n)])


def after(value, *others):
    return lax.optimization_barrier((value, others))[0]


def crossing(value):
    return lax.ppermute(value, ("seq", "core"), [(1, 2), (2, 1)])


def pick(own, received):
    return jnp.where(lax.axis_index("seq") == lax.axis_index("core"), own, received)


def crossed(value):
    return pick(value, crossing(value))


def small_sum(value, axes):
    for axis in axes:
        n = lax.axis_size(axis)
        moved, total = value, value
        for _ in range(n - 1):
            moved = shift(moved, axis, 1)
            total = total + moved
        value = total
    return value


def gather_list(piece, axis):
    out = [piece]
    for _ in range(lax.axis_size(axis) - 1):
        out.append(shift(out[-1], axis, -1))
    return out


def gather_plane(piece, first, second, dep=()):
    out = {}
    for i, one in enumerate(gather_list(piece, first)):
        one = after(one, dep) if i else one
        for j, two in enumerate(gather_list(one, second)):
            out[(j, i) if first == "x" else (i, j)] = two
    return out


def reduce_list(pieces, axis, dep):
    total = pieces[-1]
    for piece in pieces[-2::-1]:
        total = (after(shift(total, axis, 1), dep).astype(F32) + piece.astype(F32)).astype(BF)
    return total


def reduce_second(pieces, first, second, dep):
    n_first, n_second = lax.axis_size(first), lax.axis_size(second)
    part = []
    for i in range(n_first):
        row = [pieces[(j, i) if first == "x" else (i, j)] for j in range(n_second)]
        part.append(reduce_list(row, second, dep))
    return part


def adam_update(master, first_moment, second_moment, gradient, step_rate, bias_one, bias_two):
    first_new = 0.5 * first_moment + 0.5 * gradient
    second_new = 0.5 * second_moment + 0.5 * gradient * gradient
    update = first_new / bias_one / (jnp.sqrt(second_new / bias_two) + ADAM_EPS)
    master_new = master - step_rate * (update + WEIGHT_DECAY * master)
    return (master_new, first_new, second_new)


def on_device(images, key_mask, out_grad, step_count, *params):
    masters, firsts, seconds = params[0:5], params[5:10], params[10:15]
    in_weights, out_weights, up_weights, down_weights, vectors = masters
    image_count, half, features = images.shape
    padded = -(-half // PAD_ROWS) * PAD_ROWS
    h, c = lax.axis_index("seq"), lax.axis_index("core")
    y, x = lax.axis_index("y"), lax.axis_index("x")
    ny, nx = lax.axis_size("y"), lax.axis_size("x")
    shards = 4 * ny * nx
    shard = ((h * ny + y) * nx + x) * 2 + c
    at = jnp.stack([h, y, x, c, jnp.int32(ny), jnp.int32(nx), jnp.int32(0), jnp.int32(0)]).astype(jnp.int32)

    h1, qkv, x_both, full_in, my_out, other_out, own_a, own_b, low_ff, full_vec = head_stage(
        in_weights, out_weights, up_weights, down_weights, vectors[None], images, padded, ny, nx
    )
    my_out, other_out = my_out.reshape(HALF_D, D), other_out.reshape(HALF_D, D)
    x_own, x_oth = x_both[0], x_both[1]
    rows_in, rows_out, rows_ff = in_weights.shape[0], out_weights.shape[0], up_weights.shape[0]
    half_ff = rows_ff // 2
    keys = [(ky, kx) for ky in range(ny) for kx in range(nx)]
    full_vec = full_vec.reshape(-1)
    gain_one, shift_one, query_bias, value_bias, out_bias, gain_two, shift_two, down_bias = (
        full_vec[i * D : (i + 1) * D] for i in range(8)
    )
    up_bias = full_vec[8 * D :]

    mask = key_mask.astype(F32)
    mask = jnp.where(h == c, mask, shift(mask, "core", 1)).reshape(image_count, 2, half)
    mask = jnp.where(c == 0, mask, mask[:, ::-1])
    mask = jnp.pad(mask, ((0, 0), (0, 0), (0, padded - half))).reshape(image_count, 2 * padded)
    key_fill = jnp.broadcast_to(jnp.where(mask > 0, 0.0, NEG_FILL)[..., None], mask.shape + (128,)).astype(BF)

    ff_near = lax.ppermute(low_ff, ("seq", "dp"), [(1, 2), (2, 1)])
    g_got = crossing(after(out_grad, ff_near))

    tokens = image_count * 2 * padded
    qkv = qkv.reshape(image_count, 2 * padded, 3 * HALF_D)
    mixed, lse = attend(qkv, key_fill)
    halved = mixed.reshape(image_count, 2, padded, HALF_D)
    mixed_oth = shift(halved, "core", 1)
    ff_near = after(ff_near, mixed)
    ff_far = lax.ppermute(ff_near, ("seq", "dp"), [(1, 0), (2, 3)])
    x2, h2 = middle(x_own, x_oth, halved, mixed_oth, my_out, other_out, out_bias, gain_two, shift_two)

    ff_far, h2 = lax.optimization_barrier((ff_far, h2))
    ff_other = jnp.where(h != lax.axis_index("dp"), ff_near, ff_far)
    ff_a = gather_plane(ff_other[0], "x", "y")
    ff_b = gather_plane(ff_other[1], "y", "x")
    g_own = pick(out_grad, after(g_got, h2))
    g_oth = shift(g_own, "core", 1)
    grad_a, grad_b, y_own, y_oth, dh2, g_bu = mlp(
        at, h2.reshape(tokens, D), g_own, g_oth, up_bias.reshape(shards * 2, half_ff), own_a, own_b, ff_a, ff_b
    )
    result = y_own[:, :half] + shift(y_oth, "core", 1)[:, :half].astype(F32) + x2[:, 0, :half] + down_bias
    result = result.astype(BF)

    dh2 = dh2.reshape(image_count, 2, padded, D)
    dh2_oth = shift(dh2, "core", 1)
    dx2, dattn, g_out, sums_two = middle_back(x2, dh2, dh2_oth, g_own, g_oth, halved, my_out, gain_two)
    result_got = crossing(after(result, dattn))
    dqkv, sums_qkv = attend_back(qkv, key_fill, mixed, dattn.reshape(mixed.shape), lse)
    part_a = reduce_second(grad_a, "x", "y", dqkv)
    part_b = reduce_second(grad_b, "y", "x", dqkv)
    zero = jnp.zeros((D,), F32)
    vec = jnp.concatenate(
        [
            zero,
            zero,
            lax.dynamic_update_slice(zero, sums_qkv[0, :HALF_D], (c * HALF_D,)),
            lax.dynamic_update_slice(zero, sums_qkv[0, 2 * HALF_D :], (c * HALF_D,)),
            sums_two[2],
            sums_two[0],
            sums_two[1],
            sums_two[3],
            g_bu.reshape(-1),
        ]
    ).reshape(-1, 128)
    in_mine, in_theirs, share_out, share_ff, input_grad, vec, norm = tail_stage(
        h1.reshape(tokens, D),
        dqkv.reshape(tokens, 3 * HALF_D),
        g_out.reshape(ny, nx, 2, rows_out, D),
        x_own,
        dx2,
        gain_one,
        vec,
        full_in,
        part_a,
        part_b,
        ny,
        nx,
    )
    activations = pick(result, after(result_got, norm)).astype(F32)
    input_grad = input_grad.astype(F32)
    share_vec = lax.dynamic_slice(vec.reshape(shards, -1), (shard, 0), (1, vec.size // shards)).reshape(-1)
    in_mine, in_theirs = (s.reshape(rows_in, 3, 1, HALF_D) for s in (in_mine, in_theirs))
    share_in = jnp.where(
        c == 0, jnp.concatenate([in_mine, in_theirs], 2), jnp.concatenate([in_theirs, in_mine], 2)
    ).reshape(rows_in, 3 * D)
    share_up, share_down = (share_ff[:, i].reshape(rows_ff, D) for i in range(2))
    shares = tuple(s.astype(F32) for s in (share_in, share_out, share_up, share_down, share_vec))
    grad_norm = norm[0, 0]
    threshold = 0.5 * math.sqrt(4 * D * D + 2 * D * FF + 12 * D)
    clip_factor = jnp.minimum(1.0, threshold / grad_norm)
    bias = 1.0 - jnp.power(F32(0.5), step_count.astype(F32))
    rates = ((D // 2) ** (-0.5), (D // 4) ** (-0.5), D ** (-0.5), FF ** (-0.5), 0.2)
    results = [
        adam_update(masters[i], firsts[i], seconds[i], shares[i] * clip_factor, rates[i], bias, bias) for i in range(5)
    ]
    return (
        grad_norm,
        *(r[0] for r in results),
        *(r[1] for r in results),
        *(r[2] for r in results),
        *(r[0].astype(BF) for r in results),
        activations,
        input_grad,
    )


def solution(mesh):
    seq_n, fsdp_n, dp_n = (mesh.shape[a] for a in ("seq", "fsdp", "dp"))
    nx = math.isqrt(fsdp_n // 2)
    ny = fsdp_n // 2 // nx
    grid = Mesh(np.asarray(mesh.devices).reshape(seq_n, ny, nx, 2, dp_n), AXES)
    tokens = P(("y", "x", "core", "dp"), "seq", None)
    matrix, vector = P(SHARD, None), P(SHARD)
    five = (matrix, matrix, matrix, matrix, vector)
    return jax.shard_map(
        on_device,
        mesh=grid,
        in_specs=(tokens, P(("y", "x", "core", "dp"), None), tokens, P()) + five * 3,
        out_specs=(P(),) + five * 4 + (tokens, tokens),
        check_vma=False,
    )
```

```python
import functools
import math

import jax
import jax.numpy as jnp
import numpy as np
from jax import lax
from jax.experimental import pallas as pl
from jax.experimental.pallas import tpu as pltpu
from jax.sharding import Mesh
from jax.sharding import PartitionSpec as P

D = 1024
FF = 4096
PAD_ROWS = 16

NEG_FILL = -1000000000.0
ADAM_EPS = 1e-08
WEIGHT_DECAY = 0.05
AXES = ("seq", "y", "x", "core", "dp")
SHARD = ("seq", "y", "x", "core")

BF = jnp.bfloat16
F32 = jnp.float32
MESH_ID = pl.DeviceIdType.MESH


class Wires:
    def __init__(self, send_sem, recv_sem):
        self.send_sem, self.recv_sem, self.count, self.sent = send_sem, recv_sem, 0, []

    def make(self, src, dst, to):
        cp = pltpu.make_async_remote_copy(
            src_ref=src, dst_ref=dst, send_sem=self.send_sem.at[self.count], recv_sem=self.recv_sem.at[self.count],
            device_id=to, device_id_type=MESH_ID)
        self.count += 1
        return cp

    def send(self, src, dst, to):
        cp = self.make(src, dst, to)
        cp.start()
        self.sent.append(cp)
        return cp

    def finish(self):
        for cp in self.sent:
            cp.wait_send()


def greet(peers, crossing_peer, apart):
    barrier = pltpu.get_barrier_semaphore()
    for peer in peers:
        pl.semaphore_signal(barrier, inc=1, device_id=peer, device_id_type=MESH_ID)

    @pl.when(apart)
    def _():
        pl.semaphore_signal(barrier, inc=1, device_id=crossing_peer, device_id_type=MESH_ID)

    pl.semaphore_wait(barrier, len(peers) + jnp.where(apart, 1, 0))


def add_all(first, *others):
    total = first.astype(F32)
    for other in others:
        total = total + other.astype(F32)
    return total


def plane_moves(wires, to_x, to_y):
    nx, ny = len(to_x), len(to_y)

    def spread(piece_at, kz, first):
        got = {}
        for k in range(1, nx):
            got[0, k] = wires.send(piece_at(kz, 0, 0), piece_at(kz, 0, 0, k, "x"), to_x[k])
        for k in range(1, ny):
            got[k, 0] = wires.send(piece_at(kz, 0, 0), piece_at(kz, 0, 0, k, "y"), to_y[k])
        return got

    def forward(piece_at, kz, first, got):
        if first == "x":
            for kx in range(1, nx):
                got[0, kx].wait_recv()
                for ky in range(1, ny):
                    got[ky, kx] = wires.send(piece_at(kz, 0, kx), piece_at(kz, 0, kx, ky, "y"), to_y[ky])
            for ky in range(1, ny):
                got[ky, 0].wait_recv()
        else:
            for ky in range(1, ny):
                got[ky, 0].wait_recv()
                for kx in range(1, nx):
                    got[ky, kx] = wires.send(piece_at(kz, ky, 0), piece_at(kz, ky, 0, kx, "x"), to_x[kx])
            for kx in range(1, nx):
                got[0, kx].wait_recv()

    def settle(got):
        for (ky, kx), cp in got.items():
            if ky > 0 and kx > 0:
                cp.wait_recv()

    return spread, forward, settle


def by_offset(store, own):
    def piece_at(kz, ky, kx, k=0, axis=""):
        if k == 0 and ky == 0 and kx == 0:
            return own
        return store.at[ky + (k if axis == "y" else 0), kx + (k if axis == "x" else 0)]

    return piece_at

BF=jnp.bfloat16; F32=jnp.float32
def dot(a, b, dims=(((1,), (0,)), ((), ()))):
    return lax.dot_general(a, b, dims, preferred_element_type=F32)
NT=(((1,),(1,)),((),()))
TN=(((0,),(0,)),((),()))
ANY=pl.BlockSpec(memory_space=pl.ANY)
VM=pl.BlockSpec(memory_space=pltpu.VMEM)
SM=pl.BlockSpec(memory_space=pltpu.SMEM)

def gelu_both(u):
    c0=math.sqrt(2/math.pi)
    sq=u*u
    t=jnp.tanh(u*(c0+(c0*0.044715)*sq))
    half=0.5+0.5*t
    value=u*half
    slope=half+(0.5*u)*(1.0-t*t)*(c0+(3*c0*0.044715)*sq)
    return value,slope

def mlp_kernel(keys,ny,nx,*refs,gtile):
    nk=len(keys)
    h2_ref,go_ref,gt_ref,bu_ref=refs[:4]
    planes=(refs[4:6],refs[6:8])
    o=8
    ga,gb=refs[o:o+nk],refs[o+nk:o+2*nk]
    yown_ref,yoth_ref,dh_ref,gbu_ref,ra_ref,rb_ref=refs[o+2*nk:o+2*nk+6]
    w,dd,a_all,du_all,y_acc,dh_acc,g_out,wsem,gsem,send_sem,recv_sem=refs[o+2*nk+6:]
    h,y,x,c,_=(lax.axis_index(a) for a in AXES)
    to_x=[{"x":lax.rem(x+k,nx)} for k in range(nx)]
    to_y=[{"y":lax.rem(y+k,ny)} for k in range(ny)]
    wires=Wires(send_sem,recv_sem)
    moves=[]
    for ki,(ky,kx) in enumerate(keys):
        cps=[]
        if ky>0: cps.append(wires.make(ga[ki],ra_ref.at[ky-1,kx],to_y[ky]))
        if kx>0: cps.append(wires.make(gb[ki],rb_ref.at[kx-1,ky],to_x[kx]))
        moves.append(cps)
    barrier=pltpu.get_barrier_semaphore()
    for peer in to_x[1:]+to_y[1:]:
        pl.semaphore_signal(barrier,inc=1,device_id=peer,device_id_type=MESH_ID)
    images,half,feat=go_ref.shape
    hid=planes[0][0].shape[3]
    width=4*hid
    padded=h2_ref.shape[0]//(2*images)
    blocks=2*images

    def load(i,slot,go):
        for ki in range(nk):
            @pl.when(i==ki)
            def _():
                for kz in range(2):
                    for ud in range(2):
                        for ab in range(2):
                            cp=pltpu.make_async_copy(planes[kz][ab].at[keys[ki][0],keys[ki][1],ud],w.at[slot,ud,pl.ds((kz*2+ab)*hid,hid)],wsem.at[slot,kz*4+ud*2+ab])
                            cp.start() if go else cp.wait()
    def save(i,go):
        for ki in range(nk):
            @pl.when(i==ki)
            def _():
                for kz in range(2):
                    for ud in range(2):
                        for ab,dst in enumerate((ga[ki],gb[ki])):
                            cp=pltpu.make_async_copy(g_out.at[ud,pl.ds((kz*2+ab)*hid,hid)],dst.at[kz,ud],gsem.at[kz*4+ud*2+ab])
                            cp.start() if go else cp.wait()
    load(0,0,True)
    gbu_ref[...]=jnp.zeros_like(gbu_ref)
    for i in range(images):
        for s,src in enumerate((go_ref,gt_ref)):
            r=(2*i+s)*padded
            tail=padded-16
            dd[r+tail:r+padded,:]=jnp.zeros((16,feat),BF)
            dd[r:r+half,:]=src[i]
    pl.semaphore_wait(barrier,nx+ny-2)
    def step(i,_):
        slot=lax.rem(i,2)
        @pl.when(i>0)
        def _(): save(i-1,False)
        for ki,cps in enumerate(moves):
            if cps:
                @pl.when(i==ki+1)
                def _():
                    for cp in cps: cp.start()
        load(i,slot,False)
        @pl.when(i+1<nk)
        def _(): load(i+1,1-slot,True)
        rows=[]
        for kz in range(2):
            for ab in range(2):
                row=jnp.int32(0)
                for ki,(ky,kx) in enumerate(keys):
                    here=(((lax.rem(h+kz,2)*ny+lax.rem(y+ky,ny))*nx+lax.rem(x+kx,nx))*2+c)*2+ab
                    row=jnp.where(i==ki,here,row)
                rows.append(row)
        bias=jnp.concatenate([bu_ref[pl.ds(r,1),:] for r in rows],axis=1)
        wu=w.at[slot,0]; wd=w.at[slot,1]
        def tokens(b,sums):
            r=pl.ds(pl.multiple_of(b*padded,16),padded)
            u=dot(h2_ref[r,:],wu[...],NT)+bias
            value,slope=gelu_both(u)
            a=value.astype(BF)
            a_all[r,:]=a
            dg=dot(dd[r,:],wd[...],NT)
            du=(dg*slope).astype(BF)
            du_all[r,:]=du
            ynew=dot(a,wd[...]); dnew=dot(du,wu[...])
            @pl.when(i==0)
            def _():
                y_acc[r,:]=ynew; dh_acc[r,:]=dnew
            @pl.when(i>0)
            def _():
                y_acc[r,:]+=ynew; dh_acc[r,:]+=dnew
            return sums+jnp.sum(du.astype(F32),axis=0,keepdims=True)
        sums=lax.fori_loop(0,blocks,tokens,jnp.zeros((1,width),F32))
        for q,row in enumerate(rows):
            gbu_ref[pl.ds(row,1),:]=sums[:,q*hid:(q+1)*hid]
        for t in range(0,width,gtile):
            g_out[1,t:t+gtile,:]=dot(a_all[:,t:t+gtile],dd[...],TN).astype(BF)
            g_out[0,t:t+gtile,:]=dot(du_all[:,t:t+gtile],h2_ref[...],TN).astype(BF)
        save(i,True)
        return 0
    lax.fori_loop(0,nk,step,0)
    for i in range(images):
        r=2*i*padded
        yown_ref[i]=y_acc[r:r+padded,:]
        yoth_ref[i]=y_acc[r+padded:r+2*padded,:].astype(BF)
    dh_ref[...]=dh_acc[...].astype(BF)
    save(nk-1,False)
    for cps in moves:
        for cp in cps:
            cp.wait_recv()
            cp.wait_send()

def mlp(ny,nx,h2,g_own,g_oth,bu_rows,own_a,own_b,oth_a,oth_b,gtile=256):
    keys=sorted(((ky,kx) for ky in range(ny) for kx in range(nx)),reverse=True); nk=len(keys)
    images,half,feat=g_own.shape
    tokens=h2.shape[0]; padded=tokens//(2*images)
    ud,hid=own_a.shape[2:4]
    width=4*hid
    piece=jax.ShapeDtypeStruct((2,ud,hid,feat),BF)
    out=pl.pallas_call(functools.partial(mlp_kernel,keys,ny,nx,gtile=min(gtile,width)),
        in_specs=[VM]*4+[ANY]*4,
        out_specs=[ANY]*(2*nk)+[VM]*4+[ANY]*2,
        out_shape=[piece]*(2*nk)+[jax.ShapeDtypeStruct((images,padded,feat),F32),jax.ShapeDtypeStruct((images,padded,feat),BF),
            jax.ShapeDtypeStruct((tokens,feat),BF),jax.ShapeDtypeStruct(bu_rows.shape,F32),
            jax.ShapeDtypeStruct((ny-1,nx,2,ud,hid,feat),BF),jax.ShapeDtypeStruct((nx-1,ny,2,ud,hid,feat),BF)],
        scratch_shapes=[pltpu.VMEM((2,2,width,feat),BF),pltpu.VMEM((tokens,feat),BF),pltpu.VMEM((tokens,width),BF),pltpu.VMEM((tokens,width),BF),
            pltpu.VMEM((tokens,feat),F32),pltpu.VMEM((tokens,feat),F32),pltpu.VMEM((2,width,feat),BF),
            pltpu.SemaphoreType.DMA((2,8)),pltpu.SemaphoreType.DMA((8,)),pltpu.SemaphoreType.DMA((2*nk,)),pltpu.SemaphoreType.DMA((2*nk,))],
        name="feed_forward",
        compiler_params=pltpu.CompilerParams(collective_id=3,has_side_effects=True,vmem_limit_bytes=60<<20),
        cost_estimate=pl.CostEstimate(flops=nk*6*2*tokens*feat*width,bytes_accessed=40<<20,transcendentals=nk*tokens*width),
    )(h2,g_own,g_oth,bu_rows,own_a,own_b,oth_a,oth_b)
    return dict(zip(keys,out[:nk])),dict(zip(keys,out[nk:2*nk])),out[2*nk:]

HD=64; HALF_D=512

def head_operands(q,k,kb,scale):
    q=q.astype(F32)*scale; k=k.astype(F32); kb=kb.astype(F32)
    lane=lax.broadcasted_iota(jnp.int32,q.shape,1)
    low=lane<HD
    one=jnp.where((lane==0)|(lane==HD),1.0,0.0)
    qs=[jnp.where(low,q,one).astype(BF),jnp.where(low,one,q).astype(BF)]
    ks=[jnp.where(low,k,kb).astype(BF),jnp.where(low,kb,k).astype(BF)]
    return q,k,low,qs,ks

def attend_pair(q,k,v,kb):
    q,k,low,qs,ks=head_operands(q,k,kb,HD**-0.5)
    vt=v.astype(F32).T.astype(BF)
    outs=[]; sums=[]
    for j in range(2):
        s=dot(ks[j],qs[j],NT)
        m=jnp.max(s,axis=0,keepdims=True)
        e=jnp.exp(s-m)
        l=jnp.sum(e,axis=0,keepdims=True)
        o=dot(vt[j*HD:(j+1)*HD],e.astype(BF))
        outs.append(o*(1.0/l))
        sums.append(m+jnp.log(l))
    return jnp.concatenate(outs,axis=0).T.astype(BF),sums

def attend_back_kernel(q_ref,k_ref,v_ref,kb_ref,o_ref,g_ref,lse_ref,keep_ref,give_ref,out_ref,sum_ref,part_ref,land,send_sem,recv_sem,*,pairs,chunk):
    p=pl.program_id(1)
    to_dp={"dp":1-lax.axis_index("dp")}
    cp=pltpu.make_async_remote_copy(src_ref=give_ref,dst_ref=land,send_sem=send_sem,recv_sem=recv_sem,device_id=to_dp,device_id_type=MESH_ID)
    @pl.when((pl.program_id(0)==0)&(p==0))
    def _():
        barrier=pltpu.get_barrier_semaphore()
        pl.semaphore_signal(barrier,inc=1,device_id=to_dp,device_id_type=MESH_ID)
        pl.semaphore_wait(barrier,1)
        cp.start()
    @pl.when((pl.program_id(0)==pl.num_programs(0)-1)&(p==pairs-1))
    def _():
        cp.wait()
        part_ref[...]=add_all(keep_ref[...],land[...]).astype(BF)
    @pl.when((pl.program_id(0)==0)&(p==0))
    def _(): sum_ref[...]=jnp.zeros_like(sum_ref)
    scale=HD**-0.5
    q,k,low,qs,ks=head_operands(q_ref[0],k_ref[0],kb_ref[0],scale)
    qb=q.astype(BF)
    kt=k.T.astype(BF)
    g=g_ref[0]; gf=g.astype(F32)
    prod=(gf*o_ref[0].astype(F32)).T
    v=v_ref[0]
    rows=q.shape[0]
    dqs=[];dks=[];dvs=[]
    for j in range(2):
        gj=(jnp.where(low,gf,0.0) if j==0 else jnp.where(low,0.0,gf)).astype(BF)
        delta=jnp.sum(prod[j*HD:(j+1)*HD],axis=0,keepdims=True)
        lse=lse_ref[0,0,j:j+1,:]
        dq=None; dk=[]; dv=[]
        for r in range(0,rows,chunk):
            s=dot(ks[j][r:r+chunk],qs[j],NT)
            pr=jnp.exp(s-lse)
            dp=dot(v[r:r+chunk],gj,NT)
            ds=(pr*(dp-delta)).astype(BF)
            dv.append(dot(pr.astype(BF),g))
            dk.append(dot(ds,qb))
            t=dot(kt[j*HD:(j+1)*HD,r:r+chunk],ds) if chunk==rows else dot(k[r:r+chunk].astype(BF),ds,TN)[j*HD:(j+1)*HD]
            dq=t if dq is None else dq+t
        dqs.append(dq)
        dks.append(jnp.concatenate(dk,axis=0) if len(dk)>1 else dk[0]); dvs.append(jnp.concatenate(dv,axis=0) if len(dv)>1 else dv[0])
    parts=((jnp.concatenate(dqs,axis=0)*scale).T.astype(BF),jnp.where(low,dks[0],dks[1]).astype(BF),jnp.where(low,dvs[0],dvs[1]).astype(BF))
    for t,part in enumerate(parts):
        at=pl.ds(pl.multiple_of((t*pairs+p)*128,128),128)
        out_ref[0,:,at]=part
        sum_ref[0:1,at]+=jnp.sum(part.astype(F32),axis=0,keepdims=True)

def attend_back(qkv,kbias,mixed,grad,lse,keep,give,chunk=None):
    n,rows,w=qkv.shape; pairs=w//3//128
    chunk=chunk or rows
    blk=lambda off: pl.BlockSpec((1,rows,128),lambda i,p: (i,0,off+p))
    return pl.pallas_call(functools.partial(attend_back_kernel,pairs=pairs,chunk=chunk),grid=(n,pairs),
        in_specs=[blk(0),blk(pairs),blk(2*pairs),pl.BlockSpec((1,rows,128),lambda i,p:(i,0,0)),blk(0),blk(0),pl.BlockSpec((1,1,8,rows),lambda i,p:(i,p,0,0)),VM,VM],
        out_specs=[pl.BlockSpec((1,rows,w),lambda i,p:(i,0,0)),pl.BlockSpec((8,w),lambda i,p:(0,0)),VM],
        out_shape=[jax.ShapeDtypeStruct((n,rows,w),BF),jax.ShapeDtypeStruct((8,w),F32),jax.ShapeDtypeStruct(keep.shape,BF)],
        scratch_shapes=[pltpu.VMEM(keep.shape,BF),pltpu.SemaphoreType.DMA(()),pltpu.SemaphoreType.DMA(())],
        name="attend_back",
        compiler_params=pltpu.CompilerParams(collective_id=4,has_side_effects=True,vmem_limit_bytes=50<<20),
        cost_estimate=pl.CostEstimate(flops=n*pairs*20*rows*rows*128,bytes_accessed=n*rows*w*5,transcendentals=n*pairs*2*rows*rows),
    )(qkv,qkv,qkv,kbias,mixed,grad,lse,keep,give)

NORM_EPS=1e-6
def norm_parts(values):
    center = values - jnp.mean(values, axis=-1, keepdims=True)
    inverse = lax.rsqrt(jnp.mean(center * center, axis=-1, keepdims=True) + NORM_EPS)
    return center * inverse, inverse

def norm_back(values, gain, grad):
    normed, inverse = norm_parts(values)
    scaled = grad * gain
    mean_one = jnp.mean(scaled, axis=-1, keepdims=True)
    mean_two = jnp.mean(scaled * normed, axis=-1, keepdims=True)
    return (scaled - mean_one - normed * mean_two) * inverse, grad * normed

def wide_rows(buf,block):
    n=block.shape[0]; total=buf.shape[0]
    buf[total-16:,:]=jnp.zeros((16,buf.shape[1]),F32)
    buf[0:n,:]=block.astype(F32)
    return buf[...]

def middle_back_kernel(x2_ref,da_ref,db_ref,go_ref,gt_ref,mix_ref,w_ref,gain_ref,dx_ref,dat_ref,gw_ref,sum_ref,buf,acc):
    i=pl.program_id(0)
    @pl.when(i==0)
    def _():
        acc[...]=jnp.zeros_like(acc); sum_ref[...]=jnp.zeros_like(sum_ref)
    for s,src in enumerate((go_ref,gt_ref)):
        dd=wide_rows(buf.at[s],src[0])
        grad=da_ref[0,s].astype(F32)+db_ref[0,1-s].astype(F32)
        dx,gg=norm_back(x2_ref[0,s],gain_ref[...],grad)
        dx=dx+dd
        dob=dx.astype(BF)
        if s==0:
            dx_ref[0]=dx
            for r,t in enumerate((gg,grad,dob.astype(F32),dd)):
                sum_ref[r:r+1,:]+=jnp.sum(t,axis=0,keepdims=True)
        dat_ref[0,s]=dot(dob,w_ref[...],NT).astype(BF)
        acc[...]+=dot(mix_ref[0,s],dob,TN)
    @pl.when(i==pl.num_programs(0)-1)
    def _(): gw_ref[...]=acc[...].astype(BF)

def middle_back(x2,dh_own,dh_oth,g_own,g_oth,mixed,w_own,gain):
    n,half,feat=g_own.shape
    _,_,padded,width=mixed.shape
    tok=pl.BlockSpec((1,half,feat),lambda i:(i,0,0))
    mix=pl.BlockSpec((1,2,padded,width),lambda i:(i,0,0,0))
    big=pl.BlockSpec((1,2,padded,feat),lambda i:(i,0,0,0))
    full=pl.BlockSpec((width,feat),lambda i:(0,0))
    return pl.pallas_call(middle_back_kernel,grid=(n,),
        in_specs=[big,big,big,tok,tok,mix,full,pl.BlockSpec((1,feat),lambda i:(0,0))],
        out_specs=[pl.BlockSpec((1,padded,feat),lambda i:(i,0,0)),mix,full,pl.BlockSpec((8,feat),lambda i:(0,0))],
        out_shape=[jax.ShapeDtypeStruct((n,padded,feat),F32),jax.ShapeDtypeStruct(mixed.shape,BF),jax.ShapeDtypeStruct((width,feat),BF),jax.ShapeDtypeStruct((8,feat),F32)],
        scratch_shapes=[pltpu.VMEM((2,padded,feat),F32),pltpu.VMEM((width,feat),F32)],name="middle_back",
        compiler_params=pltpu.CompilerParams(vmem_limit_bytes=56<<20),
        cost_estimate=pl.CostEstimate(flops=n*8*padded*feat*width,bytes_accessed=30<<20,transcendentals=0),
    )(x2,dh_own,dh_oth,g_own,g_oth,mixed,w_own,gain[None])


def tail_kernel(ny, nx, *refs):
    h1_ref, dqkv_ref, go_ref, x_ref, dx_ref, gain_ref, vec_ref, w = refs[:8]
    fpart = refs[8]
    o = 9
    mine_ref, theirs_ref, so_ref, sf_ref, ig_ref, vout_ref, norm_ref = refs[o:o + 7]
    (grad, ra1, ra2, rb1, rb2, sa, sb, oa1, oa2, ob1, ob2, ta, tb, osum, ocross, ocore, odp, ofin,
     frecv, isum, ipart, irecv, idp, ifin,
     buf, give, got, stage, vrecv, nrecv, nval, send_sem, recv_sem) = refs[o + 7:]
    h, y, x, c, l = (lax.axis_index(a) for a in AXES)
    images, half, feat = x_ref.shape
    padded = dx_ref.shape[1]
    rows = grad.shape[4]
    apart = h != c
    cross = {"seq": 1 - h, "core": 1 - c}
    to_core, to_seq, to_dp = {"core": 1 - c}, {"seq": 1 - h}, {"dp": 1 - l}
    to_x = [{"x": lax.rem(x + k, nx)} for k in range(nx)]
    to_y = [{"y": lax.rem(y + k, ny)} for k in range(ny)]
    yy = [lax.rem(y + k, ny) for k in range(ny)]
    xx = [lax.rem(x + k, nx) for k in range(nx)]
    zz = [h, 1 - h]
    wires = Wires(send_sem, recv_sem)
    greet([to_core, to_seq, to_dp] + to_x[1:] + to_y[1:], cross, apart)

    fs = wires.send(fpart.at[1], frecv, to_seq)
    oa_got = [[wires.send(go_ref.at[yy[ky], xx[kx], h], oa1.at[ky - 1, kx], to_y[ky]) for kx in range(nx)] for ky in range(1, ny)]
    ob_got = [[wires.send(go_ref.at[yy[ky], xx[kx], 1 - h], ob1.at[kx - 1, ky], to_x[kx]) for ky in range(ny)] for kx in range(1, nx)]
    width = nx * 2 * rows
    ia_got, ib_got = [], []
    for ky in range(ny - 1, -1, -1):
        for kz in range(2):
            col = pl.multiple_of((zz[kz] * ny + yy[ky]) * width, 128)
            t = dot(h1_ref[:, pl.ds(col, width)], dqkv_ref[...], TN).astype(BF)
            for q in range(nx):
                for core in range(2):
                    r = (q * 2 + core) * rows
                    grad[zz[kz], yy[ky], q, core] = t[r:r + rows]
            for kx in range(nx):
                if ky > 0:
                    ia_got.append(wires.send(grad.at[zz[kz], yy[ky], xx[kx], c], ra1.at[ky - 1, kz, kx], to_y[ky]))
                if kx > 0:
                    ib_got.append(wires.send(grad.at[zz[kz], yy[ky], xx[kx], 1 - c], rb1.at[kx - 1, kz, ky], to_x[kx]))
    dh_got = []
    for i in range(images):
        r = (2 * i + 1) * padded
        give[i] = dot(dqkv_ref[r:r + padded, :], w[...], NT).astype(BF)
        dh_got.append(wires.send(give.at[i], got.at[i], to_core))
    for row in oa_got + ob_got:
        for cp in row:
            cp.wait_recv()
    o_got = []
    for kx in range(1, nx):
        ta[kx - 1] = add_all(go_ref[y, xx[kx], h], *(oa1[k, kx] for k in range(ny - 1))).astype(BF)
        o_got.append(wires.send(ta.at[kx - 1], oa2.at[kx - 1], to_x[kx]))
    for ky in range(1, ny):
        tb[ky - 1] = add_all(go_ref[yy[ky], x, 1 - h], *(ob1[k, ky] for k in range(nx - 1))).astype(BF)
        o_got.append(wires.send(tb.at[ky - 1], ob2.at[ky - 1], to_y[ky]))

    sum_gain, sum_shift = jnp.zeros((1, feat), F32), jnp.zeros((1, feat), F32)
    crossing_copies = [wires.make(stage.at[i], ig_ref.at[i], cross) for i in range(images)]

    def input_back(i, sum_gain, sum_shift):
        r = 2 * i * padded
        own = dot(dqkv_ref[r:r + padded, :], w[...], NT)
        dh_got[i].wait_recv()
        g = own + got[i].astype(F32)
        dx, gg = norm_back(wide_rows(buf, x_ref[i]), gain_ref[...], g)
        stage[i] = (dx + dx_ref[i]).astype(BF)[:half]

        @pl.when(apart)
        def _():
            crossing_copies[i].start()

        @pl.when(jnp.logical_not(apart))
        def _():
            ig_ref[i] = stage[i]

        return sum_gain + jnp.sum(gg, axis=0, keepdims=True), sum_shift + jnp.sum(g, axis=0, keepdims=True)

    for i in range(min(2, images)):
        sum_gain, sum_shift = input_back(i, sum_gain, sum_shift)
    for cp in ia_got + ib_got:
        cp.wait_recv()
    i_got = []
    for kz in range(2):
        for kx in range(1, nx):
            sa[kx - 1, kz] = add_all(grad[zz[kz], y, xx[kx], c], *(ra1[k, kz, kx] for k in range(ny - 1))).astype(BF)
        for ky in range(1, ny):
            sb[ky - 1, kz] = add_all(grad[zz[kz], yy[ky], x, 1 - c], *(rb1[k, kz, ky] for k in range(nx - 1))).astype(BF)
    for kx in range(1, nx):
        i_got.append(wires.send(sa.at[kx - 1], ra2.at[kx - 1], to_x[kx]))
    for ky in range(1, ny):
        i_got.append(wires.send(sb.at[ky - 1], rb2.at[ky - 1], to_y[ky]))
    for i in range(2, images):
        sum_gain, sum_shift = input_back(i, sum_gain, sum_shift)
    vout_ref[...] = vec_ref[...]
    for q in range(feat // 128):
        vout_ref[q:q + 1, :] = sum_gain[:, q * 128:(q + 1) * 128]
        vout_ref[feat // 128 + q:feat // 128 + q + 1, :] = sum_shift[:, q * 128:(q + 1) * 128]
    rounds = [[to_core], to_x[1:], to_y[1:], [to_seq], [to_dp]]
    slot = [0]

    def start_round(value, landing, peers):
        first = slot[0]
        cps = [wires.send(value, landing.at[first + k], peer) for k, peer in enumerate(peers)]
        slot[0] += len(peers)
        return first, cps

    def end_round(value_ref, landing, started):
        first, cps = started
        for cp in cps:
            cp.wait_recv()
        for cp in cps:
            cp.wait_send()
        wires.sent = [cp for cp in wires.sent if all(cp is not other for other in cps)]
        value_ref[...] = add_all(value_ref[...], *(landing[first + k] for k in range(len(cps))))

    vec_round = start_round(vout_ref, vrecv, rounds[0])
    for cp in i_got:
        cp.wait_recv()
    for kz in range(2):
        isum[0, kz] = add_all(grad[zz[kz], y, x, c], *(ra1[k, kz, 0] for k in range(ny - 1)), *(ra2[k, kz] for k in range(nx - 1))).astype(BF)
        isum[1, kz] = add_all(grad[zz[kz], y, x, 1 - c], *(rb1[k, kz, 0] for k in range(nx - 1)), *(rb2[k, kz] for k in range(ny - 1))).astype(BF)
    idd = wires.send(isum.at[1 - l], idp, to_dp)
    for cp in o_got:
        cp.wait_recv()
    osum[0] = add_all(go_ref[y, x, h], *(oa1[k, 0] for k in range(ny - 1)), *(oa2[k] for k in range(nx - 1))).astype(BF)
    osum[1] = add_all(go_ref[y, x, 1 - h], *(ob1[k, 0] for k in range(nx - 1)), *(ob2[k] for k in range(ny - 1))).astype(BF)
    out_cross = wires.make(osum, ocross, cross)

    @pl.when(apart)
    def _():
        out_cross.start()

    @pl.when(jnp.logical_not(apart))
    def _():
        ocross[...] = osum[...]

    end_round(vout_ref, vrecv, vec_round)
    vec_round = start_round(vout_ref, vrecv, rounds[1])
    idd.wait_recv()
    ipart[...] = add_all(isum[l], idp[...]).astype(BF)
    is_ = wires.send(ipart.at[1], irecv, to_seq)
    end_round(vout_ref, vrecv, vec_round)
    vec_round = start_round(vout_ref, vrecv, rounds[2])

    @pl.when(apart)
    def _():
        out_cross.wait_recv()

    oc = wires.send(ocross.at[1], ocore, to_core)
    fs.wait_recv()
    sf_ref[l] = add_all(fpart[0], frecv[...]).astype(BF)
    ff_last = wires.send(sf_ref.at[l], sf_ref.at[l], to_dp)
    end_round(vout_ref, vrecv, vec_round)
    vec_round = start_round(vout_ref, vrecv, rounds[3])
    oc.wait_recv()
    ofin[...] = add_all(ocross[0], ocore[...]).astype(BF)
    od = wires.send(ofin, odp, to_dp)
    is_.wait_recv()
    ifin[l] = add_all(ipart[0], irecv[...]).astype(BF)
    in_last = wires.send(ifin.at[l], ifin.at[l], to_dp)
    end_round(vout_ref, vrecv, vec_round)
    vec_round = start_round(vout_ref, vrecv, rounds[4])
    in_last.wait_recv()
    ic = wires.send(ifin.at[1], theirs_ref, to_core)
    mine_ref[...] = ifin[0]
    od.wait_recv()
    so_ref[...] = add_all(ofin[...], odp[...]).astype(BF)
    end_round(vout_ref, vrecv, vec_round)
    ff_last.wait_recv()

    def squares(value):
        value = value.astype(F32)
        return jnp.sum(jnp.sum(value * value, axis=0, keepdims=True), axis=1, keepdims=True)

    shard = ((h * ny + y) * nx + x) * 2 + c
    v = vout_ref[...]
    place = lax.broadcasted_iota(jnp.int32, v.shape, 0) * 128 + lax.broadcasted_iota(jnp.int32, v.shape, 1)
    share = v.shape[0] * 128 // (4 * ny * nx)
    v = jnp.where((place >= shard * share) & (place < (shard + 1) * share), v, 0.0)
    total = squares(v) + squares(so_ref[...]) + squares(mine_ref[...])
    for ab in range(2):
        for ud in range(2):
            total = total + squares(sf_ref[ab, ud])
    ic.wait_recv()
    total = total + squares(theirs_ref[...])
    nval[...] = jnp.broadcast_to(total, nval.shape)
    slot[0] = 0
    for peers in rounds[:4]:
        end_round(nval, nrecv, start_round(nval, nrecv, peers))
    norm_ref[...] = jnp.sqrt(nval[...])

    @pl.when(apart)
    def _():
        for cp in crossing_copies:
            cp.wait_recv()
        for cp in crossing_copies:
            cp.wait_send()
        out_cross.wait_send()

    wires.finish()


def tail_stage(h1, dqkv, g_out, x_own, dx2, gain, vec, w, fpart, ny, nx):
    tokens, feat = h1.shape
    width = dqkv.shape[1]
    rows = feat // (4 * ny * nx)
    rows_o = g_out.shape[3]
    images, half, _ = x_own.shape
    padded = dx2.shape[1]
    _, ud, hid, _ = fpart.shape
    ma, mb = max(ny - 1, 1), max(nx - 1, 1)
    piece, out_piece, ff = (rows, width), (rows_o, feat), (ud, hid, feat)
    peers = 4 + nx - 1 + ny - 1
    many = 200 + 32 * ny * nx
    V = lambda *s: pltpu.VMEM(s, BF)
    scratch = [
        V(2, ny, nx, 2, *piece),
        V(ny - 1, 2, nx, *piece), V(nx - 1, 2, *piece), V(nx - 1, 2, ny, *piece), V(ny - 1, 2, *piece),
        V(nx - 1, 2, *piece), V(ny - 1, 2, *piece),
        V(ny - 1, nx, *out_piece), V(nx - 1, *out_piece), V(nx - 1, ny, *out_piece), V(ny - 1, *out_piece),
        V(nx - 1, *out_piece), V(ny - 1, *out_piece),
        V(2, *out_piece), V(2, *out_piece), V(*out_piece), V(*out_piece), V(*out_piece),
        V(*ff),
        V(2, 2, *piece), V(2, *piece), V(*piece), V(2, *piece), V(2, *piece),
        pltpu.VMEM((padded, feat), F32), V(images, padded, feat), V(images, padded, feat), V(images, half, feat),
        pltpu.VMEM((peers,) + vec.shape, F32), pltpu.VMEM((peers, 8, 128), F32), pltpu.VMEM((8, 128), F32),
        pltpu.SemaphoreType.DMA((many,)), pltpu.SemaphoreType.DMA((many,)),
    ]
    return pl.pallas_call(
        functools.partial(tail_kernel, ny, nx),
        in_specs=[VM] * 9,
        out_specs=[VM] * 7,
        out_shape=[
            jax.ShapeDtypeStruct(piece, BF), jax.ShapeDtypeStruct(piece, BF), jax.ShapeDtypeStruct(out_piece, BF),
            jax.ShapeDtypeStruct((2,) + ff, BF), jax.ShapeDtypeStruct(x_own.shape, BF),
            jax.ShapeDtypeStruct(vec.shape, F32), jax.ShapeDtypeStruct((8, 128), F32),
        ],
        scratch_shapes=scratch,
        name="tail_stage",
        compiler_params=pltpu.CompilerParams(collective_id=1, has_side_effects=True, vmem_limit_bytes=62 << 20),
        cost_estimate=pl.CostEstimate(flops=4 * tokens * feat * width, bytes_accessed=40 << 20, transcendentals=0),
    )(h1, dqkv, g_out, x_own, dx2, gain[None], vec, w, fpart)

def head_kernel(ny, nx, *refs):
    (in_ref, out_ref, up_ref, down_ref, vec_ref, img_ref,
     h1_ref, qkv_ref, xb, w, my_out, other_out, fa, fb, cast_ref, vfull,
     theirs, o_own, o_core, tmp, buf, xsem, csem, send_sem, recv_sem) = refs
    h, y, x, c, l = (lax.axis_index(a) for a in AXES)
    images, half, feat = img_ref.shape
    rows = in_ref.shape[0]
    width = w.shape[1]
    part = width // 3
    hid = up_ref.shape[0] // 2
    apart = h != c
    cross = {"seq": 1 - h, "core": 1 - c}
    to_core, to_seq, to_dp = {"core": 1 - c}, {"seq": 1 - h}, {"dp": 1 - l}
    inner, to_near = l != h, {"seq": 1 - h, "dp": 1 - l}
    to_x = [{"x": lax.rem(x + nx - k, nx)} for k in range(nx)]
    to_y = [{"y": lax.rem(y + ny - k, ny)} for k in range(ny)]
    yy = [lax.rem(y + k, ny) for k in range(ny)]
    xx = [lax.rem(x + k, nx) for k in range(nx)]
    zz = [h, 1 - h]
    wires = Wires(send_sem, recv_sem)
    barrier = pltpu.get_barrier_semaphore()
    peers = [to_core, to_seq, to_dp] + to_x[1:] + to_y[1:]
    for peer in peers:
        pl.semaphore_signal(barrier, inc=1, device_id=peer, device_id_type=MESH_ID)

    @pl.when(apart)
    def _():
        pl.semaphore_signal(barrier, inc=1, device_id=cross, device_id_type=MESH_ID)

    @pl.when(inner)
    def _():
        pl.semaphore_signal(barrier, inc=1, device_id=to_near, device_id_type=MESH_ID)

    local_images = pltpu.make_async_copy(img_ref, xb.at[0], xsem)

    @pl.when(jnp.logical_not(apart))
    def _():
        local_images.start()

    def slot(z, yi, xi, core):
        return w.at[pl.ds(pl.multiple_of((((z * ny + yi) * nx + xi) * 2 + core) * rows, 16), rows)]

    mine = slot(h, y, x, c)
    for t in range(3):
        mine[:, t * part:(t + 1) * part] = in_ref[:, pl.ds(pl.multiple_of(t * 2 * part + c * part, 128), part)].astype(BF)
        theirs[:, t * part:(t + 1) * part] = in_ref[:, pl.ds(pl.multiple_of(t * 2 * part + (1 - c) * part, 128), part)].astype(BF)
    vfull[h, y, x, c] = vec_ref[...].astype(BF).astype(F32)
    o_own[...] = out_ref[...].astype(BF)
    pl.semaphore_wait(barrier, len(peers) + jnp.where(apart, 1, 0) + jnp.where(inner, 1, 0))

    spread, forward, settle = plane_moves(wires, to_x, to_y)

    def in_a(kz, ky, kx, *_):
        return slot(zz[kz], yy[ky], xx[kx], c)

    def in_b(kz, ky, kx, *_):
        return slot(zz[kz], yy[ky], xx[kx], 1 - c)

    def out_a(kz, ky, kx, *_):
        return my_out.at[yy[ky], xx[kx], h]

    def out_b(kz, ky, kx, *_):
        return my_out.at[yy[ky], xx[kx], 1 - h]

    ff_a, ff_b = by_offset(fa, tmp.at[0]), by_offset(fb, tmp.at[1])

    b_got = wires.send(theirs, slot(h, y, x, c), to_core)
    def across(core):
        own, other = slot(h, y, x, core), slot(1 - h, y, x, core)
        return wires.make(own, own, to_near), wires.make(other, other, to_dp)

    az, bz = across(c), across(1 - c)

    @pl.when(inner)
    def _():
        az[0].start()

    a0 = spread(in_a, 0, "x")
    vec_peers = [[to_core], to_x[1:], to_y[1:], [to_seq]]
    vec_at = [vfull.at[h, y, x, c], vfull.at[h, y, x], vfull.at[h, y], vfull.at[h]]

    def vec_send(r):
        return [wires.send(vec_at[r], vec_at[r], peer) for peer in vec_peers[r]]

    v = vec_send(0)
    oc = wires.send(o_own, o_core, to_core)
    xl = wires.make(img_ref, xb.at[1], to_core)

    @pl.when(jnp.logical_not(apart))
    def _():
        xl.start()

    b_got.wait_recv()

    @pl.when(inner)
    def _():
        bz[0].start()

    b0 = spread(in_b, 0, "y")
    for cp in v:
        cp.wait_recv()
    v = vec_send(1)
    for ab in range(2):
        tmp[ab, 0] = up_ref[ab * hid:(ab + 1) * hid, :].astype(BF)
        tmp[ab, 1] = down_ref[ab * hid:(ab + 1) * hid, :].astype(BF)
    keep = [
        pltpu.make_async_copy(tmp.at[0], fa.at[0, 0], csem.at[0]),
        pltpu.make_async_copy(tmp.at[1], fb.at[0, 0], csem.at[1]),
        pltpu.make_async_copy(tmp, cast_ref, csem.at[2]),
    ]
    for cp in keep:
        cp.start()
    for cp in v:
        cp.wait_recv()
    v = vec_send(2)
    forward(in_a, 0, "x", a0)
    forward(in_b, 0, "y", b0)
    oc.wait_recv()
    x_cross = [wires.make(img_ref.at[i], xb.at[0, i], cross) for i in range(images)]

    @pl.when(jnp.logical_and(apart, jnp.logical_not(inner)))
    def _():
        x_cross[0].start()

    def arrive(pair):
        @pl.when(inner)
        def _():
            pair[0].wait_recv()
            pair[1].start()

        @pl.when(jnp.logical_not(inner))
        def _():
            pair[1].wait_recv()

    arrive(az)
    a1 = spread(in_a, 1, "x")
    arrive(bz)
    b1 = spread(in_b, 1, "y")
    for cp in v:
        cp.wait_recv()
    v = vec_send(3)
    o_cross = [wires.make(o_own, my_out.at[y, x, 1 - h], cross), wires.make(o_core, my_out.at[y, x, h], cross)]

    @pl.when(jnp.logical_and(apart, inner))
    def _():
        x_cross[0].start()

    @pl.when(apart)
    def _():
        for cp in x_cross[1:] + o_cross:
            cp.start()

    @pl.when(jnp.logical_not(apart))
    def _():
        my_out[y, x, h] = o_own[...]
        my_out[y, x, 1 - h] = o_core[...]
        local_images.wait()

    forward(in_a, 1, "x", a1)
    forward(in_b, 1, "y", b1)
    fa0 = spread(ff_a, 0, "x")
    fb0 = spread(ff_b, 0, "y")
    for got in (a0, b0, a1, b1):
        settle(got)
    for cp in v:
        cp.wait_recv()

    def row(start, count):
        per = vec_ref.shape[1]
        pieces, at = [], start
        while at < start + count:
            s, r = at // per, at % per
            n = min(per - r, start + count - at)
            xs = s // 2
            pieces.append(vfull[xs // (nx * ny), xs // nx % ny, xs % nx, s % 2][:, r:r + n])
            at += n
        return pieces[0] if len(pieces) == 1 else jnp.concatenate(pieces, axis=1)

    gain, shift_row = row(0, feat), row(feat, feat)
    q_row, v_row = row(2 * feat, feat), row(3 * feat, feat)
    q_row = jnp.where(c == 0, q_row[:, :part], q_row[:, part:])
    v_row = jnp.where(c == 0, v_row[:, :part], v_row[:, part:])
    bias = jnp.concatenate([q_row, jnp.zeros((1, part), F32), v_row], axis=1)

    def project(i, s):
        value = wide_rows(buf, xb[s, i])
        normed = (norm_parts(value)[0] * gain + shift_row).astype(BF)
        h1_ref[i, s] = normed
        qkv_ref[i, s] = (dot(normed, w[...]) + bias).astype(BF)

    near = jnp.where(apart, 1, 0)

    @pl.when(apart)
    def _():
        xl.wait_recv()

    def near_step(i, carry):
        project(i, near)
        return carry

    lax.fori_loop(0, images, near_step, 0)

    @pl.when(apart)
    def _():
        for cp in o_cross:
            cp.wait_recv()

    oa = spread(out_a, 0, "x")
    ob = spread(out_b, 0, "y")
    forward(ff_a, 0, "x", fa0)
    forward(ff_b, 0, "y", fb0)
    x_core = [wires.make(xb.at[0, i], xb.at[1, i], to_core) for i in range(images)]
    for i in range(images):
        @pl.when(apart)
        def _():
            x_cross[i].wait_recv()
            x_core[i].start()

        @pl.when(jnp.logical_not(apart))
        def _():
            x_core[i].wait_recv()

        project(i, 1 - near)
        if i == 0:
            forward(out_a, 0, "x", oa)
            forward(out_b, 0, "y", ob)
        if i == 1 or images == 1:
            settle(oa)
            settle(ob)
            other = wires.send(my_out, other_out, to_core)
    other.wait_recv()
    settle(fa0)
    settle(fb0)

    @pl.when(apart)
    def _():
        for cp in x_cross + o_cross + x_core:
            cp.wait_send()

    @pl.when(jnp.logical_not(apart))
    def _():
        xl.wait_send()

    @pl.when(inner)
    def _():
        for cp in az + bz:
            cp.wait_send()

    for cp in keep:
        cp.wait()
    wires.finish()


def head_stage(in_w, out_w, up_w, down_w, vec, images, padded, ny, nx):
    n, half, feat = images.shape
    rows, rows_out, rows_ff = in_w.shape[0], out_w.shape[0], up_w.shape[0]
    width = in_w.shape[1] // 2
    hid = rows_ff // 2
    many = 60 + 24 * ny * nx
    S = jax.ShapeDtypeStruct
    return pl.pallas_call(
        functools.partial(head_kernel, ny, nx),
        in_specs=[VM] * 5 + [ANY],
        out_specs=[VM] * 6 + [ANY] * 3 + [VM],
        out_shape=[
            S((n, 2, padded, feat), BF), S((n, 2, padded, width), BF), S((2, n, half, feat), BF), S((feat, width), BF),
            S((ny, nx, 2, rows_out, feat), BF), S((ny, nx, 2, rows_out, feat), BF),
            S((ny, nx, 2, hid, feat), BF), S((ny, nx, 2, hid, feat), BF), S((2, 2, hid, feat), BF),
            S((2, ny, nx, 2, 1, vec.shape[1]), F32),
        ],
        scratch_shapes=[
            pltpu.VMEM((rows, width), BF), pltpu.VMEM((rows_out, feat), BF), pltpu.VMEM((rows_out, feat), BF),
            pltpu.VMEM((2, 2, hid, feat), BF), pltpu.VMEM((padded, feat), F32),
            pltpu.SemaphoreType.DMA(()), pltpu.SemaphoreType.DMA((3,)),
            pltpu.SemaphoreType.DMA((many,)), pltpu.SemaphoreType.DMA((many,)),
        ],
        name="head_stage",
        compiler_params=pltpu.CompilerParams(collective_id=2, has_side_effects=True, vmem_limit_bytes=60 << 20),
        cost_estimate=pl.CostEstimate(flops=n * 4 * padded * feat * width, bytes_accessed=40 << 20, transcendentals=0),
    )(in_w, out_w, up_w, down_w, vec, images)


def mid_kernel(ny, nx, *refs):
    (qkv_ref, kf_ref, xb, wo_ref, wt_ref, vec_ref, cast_ref, grad_ref,
     mix_ref, lse_ref, x2_ref, h2_ref, g_ref, fa, fb,
     mix_oth, near_land, buf, csem, send_sem, recv_sem) = refs
    h, y, x, c, l = (lax.axis_index(a) for a in AXES)
    images, rows, width = mix_ref.shape
    padded = rows // 2
    pairs = width // 128
    apart, inner = h != c, l != h
    cross, to_near = {"seq": 1 - h, "core": 1 - c}, {"seq": 1 - h, "dp": 1 - l}
    to_core, to_dp = {"core": 1 - c}, {"dp": 1 - l}
    to_x = [{"x": lax.rem(x + nx - k, nx)} for k in range(nx)]
    to_y = [{"y": lax.rem(y + ny - k, ny)} for k in range(ny)]
    wires = Wires(send_sem, recv_sem)
    spread, forward, settle = plane_moves(wires, to_x, to_y)
    barrier = pltpu.get_barrier_semaphore()
    peers = [to_core, to_dp] + to_x[1:] + to_y[1:]
    for peer in peers:
        pl.semaphore_signal(barrier, inc=1, device_id=peer, device_id_type=MESH_ID)

    @pl.when(apart)
    def _():
        pl.semaphore_signal(barrier, inc=1, device_id=cross, device_id_type=MESH_ID)

    @pl.when(inner)
    def _():
        pl.semaphore_signal(barrier, inc=1, device_id=to_near, device_id_type=MESH_ID)

    pl.semaphore_wait(barrier, len(peers) + jnp.where(apart, 1, 0) + jnp.where(inner, 1, 0))
    near_ff = [wires.make(cast_ref.at[ab], near_land.at[ab], to_near) for ab in range(2)]
    far_ff = [wires.make(near_land.at[ab], near_land.at[ab], to_dp) for ab in range(2)]
    local_grad = pltpu.make_async_copy(grad_ref, g_ref.at[0], csem.at[0])
    grad_core = wires.make(grad_ref, g_ref.at[1], to_core)
    g_cross = [wires.make(grad_ref.at[i], g_ref.at[0, i], cross) for i in range(images)]
    g_core = [wires.make(g_ref.at[0, i], g_ref.at[1, i], to_core) for i in range(images)]

    @pl.when(inner)
    def _():
        for cp in near_ff:
            cp.start()

    @pl.when(jnp.logical_not(apart))
    def _():
        local_grad.start()
        grad_core.start()

    @pl.when(apart)
    def _():
        g_cross[0].start()

    mix_got = []
    for i in range(images):
        def pair(p, carry):
            at = [pl.ds(pl.multiple_of((t * pairs + p) * 128, 128), 128) for t in range(3)]
            mixed, sums = attend_pair(qkv_ref[i, :, at[0]], qkv_ref[i, :, at[1]], qkv_ref[i, :, at[2]], kf_ref[i])
            mix_ref[i, :, at[0]] = mixed
            for j in range(2):
                lse_ref[i, p, j:j + 1, :] = sums[j]
            return carry

        lax.fori_loop(0, pairs, pair, 0)
        mix_got.append(wires.send(mix_ref.at[i], mix_oth.at[i], to_core))
        if i + 1 < images:
            @pl.when(apart)
            def _():
                g_cross[i + 1].start()

    gots = []

    def arrive(ab):
        @pl.when(inner)
        def _():
            near_ff[ab].wait_recv()
            far_ff[ab].start()

        @pl.when(jnp.logical_not(inner))
        def _():
            far_ff[ab].wait_recv()

    ff = [by_offset(fa, near_land.at[0]), by_offset(fb, near_land.at[1])]
    order = ("x", "y")

    def middle(i):
        mix_got[i].wait_recv()
        for s in range(2):
            own = slice(s * padded, (s + 1) * padded)
            oth = slice((1 - s) * padded, (2 - s) * padded)
            v = wide_rows(buf, xb[s, i])
            v = v + (dot(mix_ref[i, own, :], wo_ref[...]) + dot(mix_oth[i, oth, :], wt_ref[...])) + vec_ref[0:1, :]
            x2_ref[i, s] = v
            h2_ref[i, s] = (norm_parts(v)[0] * vec_ref[1:2, :] + vec_ref[2:3, :]).astype(BF)

    middle(0)
    arrive(0)
    gots.append(spread(ff[0], 1, "x"))
    for i in range(1, images):
        middle(i)
    arrive(1)
    gots.append(spread(ff[1], 1, "y"))
    keep = [pltpu.make_async_copy(near_land.at[ab], (fa, fb)[ab].at[0, 0], csem.at[1 + ab]) for ab in range(2)]
    for cp in keep:
        cp.start()
    for ab in range(2):
        forward(ff[ab], 1, order[ab], gots[ab])
    for i in range(images):
        @pl.when(apart)
        def _():
            g_cross[i].wait_recv()
            g_core[i].start()

        @pl.when(jnp.logical_not(apart))
        def _():
            g_core[i].wait_recv()

    @pl.when(apart)
    def _():
        grad_core.wait_recv()
        for cp in g_cross + g_core:
            cp.wait_send()

    @pl.when(jnp.logical_not(apart))
    def _():
        local_grad.wait()
        grad_core.wait_send()

    @pl.when(inner)
    def _():
        for cp in near_ff + far_ff:
            cp.wait_send()

    for got in gots:
        settle(got)
    for cp in keep:
        cp.wait()
    wires.finish()


def mid_stage(qkv, key_fill, x_both, w_own, w_oth, vec, low_ff, out_grad, ny, nx):
    n, rows, w3 = qkv.shape
    width, feat = w_own.shape
    half = out_grad.shape[1]
    _, ud, hid, _ = low_ff.shape
    many = 40 + 4 * ny * nx
    S = jax.ShapeDtypeStruct
    return pl.pallas_call(
        functools.partial(mid_kernel, ny, nx),
        in_specs=[VM] * 6 + [ANY] * 2,
        out_specs=[VM] * 5 + [ANY] * 2,
        out_shape=[
            S((n, rows, width), BF), S((n, width // 128, 8, rows), F32), S((n, 2, rows // 2, feat), F32),
            S((n, 2, rows // 2, feat), BF), S((2, n, half, feat), BF),
            S((ny, nx, ud, hid, feat), BF), S((ny, nx, ud, hid, feat), BF),
        ],
        scratch_shapes=[
            pltpu.VMEM((n, rows, width), BF), pltpu.VMEM((2, ud, hid, feat), BF), pltpu.VMEM((rows // 2, feat), F32),
            pltpu.SemaphoreType.DMA((3,)), pltpu.SemaphoreType.DMA((many,)), pltpu.SemaphoreType.DMA((many,)),
        ],
        name="mid_stage",
        compiler_params=pltpu.CompilerParams(collective_id=5, has_side_effects=True, vmem_limit_bytes=60 << 20),
        cost_estimate=pl.CostEstimate(flops=n * 4 * rows * rows * w3, bytes_accessed=50 << 20, transcendentals=n * 8 * rows * rows),
    )(qkv, key_fill, x_both, w_own, w_oth, vec, low_ff, out_grad)


def shift(value, axis, up):
    n = lax.axis_size(axis)
    return lax.ppermute(value, axis, [(i, (i + up) % n) for i in range(n)])


def after(value, *others):
    return lax.optimization_barrier((value, others))[0]


def crossing(value):
    return lax.ppermute(value, ("seq", "core"), [(1, 2), (2, 1)])


def pick(own, received):
    return jnp.where(lax.axis_index("seq") == lax.axis_index("core"), own, received)


def crossed(value):
    return pick(value, crossing(value))


def adam_update(master, first_moment, second_moment, gradient, step_rate, bias_one, bias_two):
    first_new = 0.5 * first_moment + 0.5 * gradient
    second_new = 0.5 * second_moment + 0.5 * gradient * gradient
    update = first_new / bias_one / (jnp.sqrt(second_new / bias_two) + ADAM_EPS)
    master_new = master - step_rate * (update + WEIGHT_DECAY * master)
    return (master_new, first_new, second_new)


def on_device(images, key_mask, out_grad, step_count, *params):
    masters, firsts, seconds = params[0:5], params[5:10], params[10:15]
    in_weights, out_weights, up_weights, down_weights, vectors = masters
    image_count, half, features = images.shape
    padded = -(-half // PAD_ROWS) * PAD_ROWS
    h, c = lax.axis_index("seq"), lax.axis_index("core")
    y, x = lax.axis_index("y"), lax.axis_index("x")
    ny, nx = lax.axis_size("y"), lax.axis_size("x")
    shards = 4 * ny * nx
    shard = ((h * ny + y) * nx + x) * 2 + c

    h1, qkv, x_both, full_in, my_out, other_out, own_a, own_b, low_ff, full_vec = head_stage(
        in_weights, out_weights, up_weights, down_weights, vectors[None], images, padded, ny, nx
    )
    my_out, other_out = my_out.reshape(HALF_D, D), other_out.reshape(HALF_D, D)
    x_own = x_both[0]
    rows_in, rows_out, rows_ff = in_weights.shape[0], out_weights.shape[0], up_weights.shape[0]
    half_ff = rows_ff // 2
    keys = [(ky, kx) for ky in range(ny) for kx in range(nx)]
    full_vec = full_vec.reshape(-1)
    gain_one, shift_one, query_bias, value_bias, out_bias, gain_two, shift_two, down_bias = (
        full_vec[i * D : (i + 1) * D] for i in range(8)
    )
    up_bias = full_vec[8 * D :]

    mask = key_mask.astype(F32)
    mask = jnp.where(h == c, mask, shift(mask, "core", 1)).reshape(image_count, 2, half)
    mask = jnp.where(c == 0, mask, mask[:, ::-1])
    mask = jnp.pad(mask, ((0, 0), (0, 0), (0, padded - half))).reshape(image_count, 2 * padded)
    key_fill = jnp.broadcast_to(jnp.where(mask > 0, 0.0, NEG_FILL)[..., None], mask.shape + (128,)).astype(BF)

    tokens = image_count * 2 * padded
    qkv = qkv.reshape(image_count, 2 * padded, 3 * HALF_D)
    mid_vec = jnp.pad(jnp.stack([out_bias, gain_two, shift_two]), ((0, 5), (0, 0)))
    mixed, lse, x2, h2, g_both, oth_a, oth_b = mid_stage(
        qkv, key_fill, x_both, my_out, other_out, mid_vec, low_ff, out_grad, ny, nx
    )
    g_own, g_oth = g_both[0], g_both[1]
    halved = mixed.reshape(image_count, 2, padded, HALF_D)

    grad_a, grad_b, (y_own, y_oth, dh2, g_bu, first_a, first_b) = mlp(
        ny, nx, h2.reshape(tokens, D), g_own, g_oth, up_bias.reshape(shards * 2, half_ff), own_a, own_b, oth_a, oth_b
    )
    result = y_own[:, :half] + shift(y_oth, "core", 1)[:, :half].astype(F32) + x2[:, 0, :half] + down_bias
    result = result.astype(BF)
    result_got = crossing(result)

    def second_stage(grads, firsts, swap):
        sums = []
        for k in range(firsts.shape[1]):
            sums.append(add_all(grads[(k, 0) if swap else (0, k)], *firsts[:, k]).astype(BF))
        return sums

    sums_a, sums_b = second_stage(grad_a, first_a, False), second_stage(grad_b, first_b, True)
    got_a = [lax.ppermute(s, "x", [(i, (i + k) % nx) for i in range(nx)]) for k, s in enumerate(sums_a) if k]
    got_b = [lax.ppermute(s, "y", [(i, (i + k) % ny) for i in range(ny)]) for k, s in enumerate(sums_b) if k]

    dh2 = dh2.reshape(image_count, 2, padded, D)
    dh2_oth = shift(dh2, "core", 1)
    dx2, dattn, g_out, sums_two = middle_back(x2, dh2, dh2_oth, g_own, g_oth, halved, my_out, gain_two)
    got_a, got_b = after(got_a, dattn), after(got_b, dattn)
    plane_a, plane_b = add_all(sums_a[0], *got_a).astype(BF), add_all(sums_b[0], *got_b).astype(BF)
    l = lax.axis_index("dp")
    half_keep, half_give = jnp.where(l == 0, plane_a, plane_b), jnp.where(l == 0, plane_b, plane_a)
    dqkv, sums_qkv, part_ff = attend_back(
        qkv, key_fill, mixed, dattn.reshape(mixed.shape), lse, half_keep, half_give
    )

    zero = jnp.zeros((D,), F32)
    vec = jnp.concatenate(
        [
            zero,
            zero,
            lax.dynamic_update_slice(zero, sums_qkv[0, :HALF_D], (c * HALF_D,)),
            lax.dynamic_update_slice(zero, sums_qkv[0, 2 * HALF_D :], (c * HALF_D,)),
            sums_two[2],
            sums_two[0],
            sums_two[1],
            sums_two[3],
            g_bu.reshape(-1),
        ]
    ).reshape(-1, 128)
    in_mine, in_theirs, share_out, share_ff, input_grad, vec, norm = tail_stage(
        h1.reshape(tokens, D),
        dqkv.reshape(tokens, 3 * HALF_D),
        g_out.reshape(ny, nx, 2, rows_out, D),
        x_own,
        dx2,
        gain_one,
        vec,
        full_in,
        part_ff,
        ny,
        nx,
    )
    activations = pick(result, after(result_got, norm)).astype(F32)
    input_grad = input_grad.astype(F32)
    share_vec = lax.dynamic_slice(vec.reshape(shards, -1), (shard, 0), (1, vec.size // shards)).reshape(-1)
    in_mine, in_theirs = (s.reshape(rows_in, 3, 1, HALF_D) for s in (in_mine, in_theirs))
    share_in = jnp.where(
        c == 0, jnp.concatenate([in_mine, in_theirs], 2), jnp.concatenate([in_theirs, in_mine], 2)
    ).reshape(rows_in, 3 * D)
    share_up, share_down = (share_ff[:, i].reshape(rows_ff, D) for i in range(2))
    shares = tuple(s.astype(F32) for s in (share_in, share_out, share_up, share_down, share_vec))
    grad_norm = norm[0, 0]
    threshold = 0.5 * math.sqrt(4 * D * D + 2 * D * FF + 12 * D)
    clip_factor = jnp.minimum(1.0, threshold / grad_norm)
    bias = 1.0 - jnp.power(F32(0.5), step_count.astype(F32))
    rates = ((D // 2) ** (-0.5), (D // 4) ** (-0.5), D ** (-0.5), FF ** (-0.5), 0.2)
    results = [
        adam_update(masters[i], firsts[i], seconds[i], shares[i] * clip_factor, rates[i], bias, bias) for i in range(5)
    ]
    return (
        grad_norm,
        *(r[0] for r in results),
        *(r[1] for r in results),
        *(r[2] for r in results),
        *(r[0].astype(BF) for r in results),
        activations,
        input_grad,
    )


def solution(mesh):
    seq_n, fsdp_n, dp_n = (mesh.shape[a] for a in ("seq", "fsdp", "dp"))
    nx = math.isqrt(fsdp_n // 2)
    ny = fsdp_n // 2 // nx
    grid = Mesh(np.asarray(mesh.devices).reshape(seq_n, ny, nx, 2, dp_n), AXES)
    tokens = P(("y", "x", "core", "dp"), "seq", None)
    matrix, vector = P(SHARD, None), P(SHARD)
    five = (matrix, matrix, matrix, matrix, vector)
    return jax.shard_map(
        on_device,
        mesh=grid,
        in_specs=(tokens, P(("y", "x", "core", "dp"), None), tokens, P()) + five * 3,
        out_specs=(P(),) + five * 4 + (tokens, tokens),
        check_vma=False,
    )
```

```python
import functools
import math

import jax
import jax.numpy as jnp
import numpy as np
from jax import lax
from jax.experimental import pallas as pl
from jax.experimental.pallas import tpu as pltpu
from jax.sharding import Mesh
from jax.sharding import PartitionSpec as P

D = 1024
FF = 4096
PAD_ROWS = 16

NEG_FILL = -1000000000.0
ADAM_EPS = 1e-08
WEIGHT_DECAY = 0.05
AXES = ("seq", "y", "x", "core", "dp")
SHARD = ("seq", "y", "x", "core")

BF = jnp.bfloat16
F32 = jnp.float32
MESH_ID = pl.DeviceIdType.MESH


class Wires:
    def __init__(self, send_sem, recv_sem):
        self.send_sem, self.recv_sem, self.count, self.sent = send_sem, recv_sem, 0, []

    def make(self, src, dst, to):
        cp = pltpu.make_async_remote_copy(
            src_ref=src, dst_ref=dst, send_sem=self.send_sem.at[self.count], recv_sem=self.recv_sem.at[self.count],
            device_id=to, device_id_type=MESH_ID)
        self.count += 1
        return cp

    def send(self, src, dst, to):
        cp = self.make(src, dst, to)
        cp.start()
        self.sent.append(cp)
        return cp

    def finish(self):
        for cp in self.sent:
            cp.wait_send()


def greet(peers, crossing_peer, apart):
    barrier = pltpu.get_barrier_semaphore()
    for peer in peers:
        pl.semaphore_signal(barrier, inc=1, device_id=peer, device_id_type=MESH_ID)

    @pl.when(apart)
    def _():
        pl.semaphore_signal(barrier, inc=1, device_id=crossing_peer, device_id_type=MESH_ID)

    pl.semaphore_wait(barrier, len(peers) + jnp.where(apart, 1, 0))


def add_all(first, *others):
    total = first.astype(F32)
    for other in others:
        total = total + other.astype(F32)
    return total


def plane_moves(wires, to_x, to_y):
    nx, ny = len(to_x), len(to_y)

    def spread(piece_at, kz, first):
        got = {}
        for k in range(1, nx):
            got[0, k] = wires.send(piece_at(kz, 0, 0), piece_at(kz, 0, 0, k, "x"), to_x[k])
        for k in range(1, ny):
            got[k, 0] = wires.send(piece_at(kz, 0, 0), piece_at(kz, 0, 0, k, "y"), to_y[k])
        return got

    def forward(piece_at, kz, first, got):
        if first == "x":
            for kx in range(1, nx):
                got[0, kx].wait_recv()
                for ky in range(1, ny):
                    got[ky, kx] = wires.send(piece_at(kz, 0, kx), piece_at(kz, 0, kx, ky, "y"), to_y[ky])
            for ky in range(1, ny):
                got[ky, 0].wait_recv()
        else:
            for ky in range(1, ny):
                got[ky, 0].wait_recv()
                for kx in range(1, nx):
                    got[ky, kx] = wires.send(piece_at(kz, ky, 0), piece_at(kz, ky, 0, kx, "x"), to_x[kx])
            for kx in range(1, nx):
                got[0, kx].wait_recv()

    def settle(got):
        for (ky, kx), cp in got.items():
            if ky > 0 and kx > 0:
                cp.wait_recv()

    return spread, forward, settle


def by_offset(store, own):
    def piece_at(kz, ky, kx, k=0, axis=""):
        if k == 0 and ky == 0 and kx == 0:
            return own
        return store.at[ky + (k if axis == "y" else 0), kx + (k if axis == "x" else 0)]

    return piece_at

BF=jnp.bfloat16; F32=jnp.float32
def dot(a, b, dims=(((1,), (0,)), ((), ()))):
    return lax.dot_general(a, b, dims, preferred_element_type=F32)
NT=(((1,),(1,)),((),()))
TN=(((0,),(0,)),((),()))
ANY=pl.BlockSpec(memory_space=pl.ANY)
VM=pl.BlockSpec(memory_space=pltpu.VMEM)
SM=pl.BlockSpec(memory_space=pltpu.SMEM)

def gelu_both(u):
    c0=math.sqrt(2/math.pi)
    sq=u*u
    t=jnp.tanh(u*(c0+(c0*0.044715)*sq))
    half=0.5+0.5*t
    value=u*half
    slope=half+(0.5*u)*(1.0-t*t)*(c0+(3*c0*0.044715)*sq)
    return value,slope

def mlp_kernel(keys,keys_b,ny,nx,*refs,gtile):
    nk=len(keys)
    h2_ref,g_ref,bu_ref=refs[:3]
    planes=(refs[3:5],refs[5:7])
    o=7
    order=(keys,keys_b)
    ga,gb=refs[o:o+nk],refs[o+nk:o+2*nk]
    yown_ref,yoth_ref,dh_ref,gbu_ref,ra_ref,rb_ref=refs[o+2*nk:o+2*nk+6]
    w,dd,a_all,du_all,y_acc,dh_acc,g_out,wsem,gsem,send_sem,recv_sem=refs[o+2*nk+6:]
    h,y,x,c,_=(lax.axis_index(a) for a in AXES)
    to_x=[{"x":lax.rem(x+k,nx)} for k in range(nx)]
    to_y=[{"y":lax.rem(y+k,ny)} for k in range(ny)]
    wires=Wires(send_sem,recv_sem)
    moves=[]
    for ki,((ky,_),(_,kx)) in enumerate(zip(keys,keys_b)):
        cps=[]
        if ky>0: cps.append(wires.make(ga[ki],ra_ref.at[ky-1,keys[ki][1]],to_y[ky]))
        ky=keys_b[ki][0]
        if kx>0: cps.append(wires.make(gb[ki],rb_ref.at[kx-1,ky],to_x[kx]))
        moves.append(cps)
    barrier=pltpu.get_barrier_semaphore()
    for peer in to_x[1:]+to_y[1:]:
        pl.semaphore_signal(barrier,inc=1,device_id=peer,device_id_type=MESH_ID)
    _,images,half,feat=g_ref.shape
    hid=planes[0][0].shape[3]
    width=4*hid
    padded=h2_ref.shape[0]//(2*images)
    blocks=2*images

    def load(i,slot,go):
        for ki in range(nk):
            @pl.when(i==ki)
            def _():
                for kz in range(2):
                    for ud in range(2):
                        for ab in range(2):
                            cp=pltpu.make_async_copy(planes[kz][ab].at[order[ab][ki][0],order[ab][ki][1],ud],w.at[slot,ud,pl.ds((kz*2+ab)*hid,hid)],wsem.at[slot,kz*4+ud*2+ab])
                            cp.start() if go else cp.wait()
    def save(i,go):
        for ki in range(nk):
            @pl.when(i==ki)
            def _():
                for kz in range(2):
                    for ud in range(2):
                        for ab,dst in enumerate((ga[ki],gb[ki])):
                            cp=pltpu.make_async_copy(g_out.at[ud,pl.ds((kz*2+ab)*hid,hid)],dst.at[kz,ud],gsem.at[kz*4+ud*2+ab])
                            cp.start() if go else cp.wait()
    load(0,0,True)
    gbu_ref[...]=jnp.zeros_like(gbu_ref)
    for i in range(images):
        for s in range(2):
            r=(2*i+s)*padded
            tail=padded-16
            dd[r+tail:r+padded,:]=jnp.zeros((16,feat),BF)
            dd[r:r+half,:]=g_ref[s,i]
    pl.semaphore_wait(barrier,nx+ny-2)
    def step(i,_):
        slot=lax.rem(i,2)
        @pl.when(i>0)
        def _(): save(i-1,False)
        for ki,cps in enumerate(moves):
            if cps:
                @pl.when(i==ki+1)
                def _():
                    for cp in cps: cp.start()
        load(i,slot,False)
        @pl.when(i+1<nk)
        def _(): load(i+1,1-slot,True)
        rows=[]
        for kz in range(2):
            for ab in range(2):
                row=jnp.int32(0)
                for ki,(ky,kx) in enumerate(order[ab]):
                    here=(((lax.rem(h+kz,2)*ny+lax.rem(y+ky,ny))*nx+lax.rem(x+kx,nx))*2+c)*2+ab
                    row=jnp.where(i==ki,here,row)
                rows.append(row)
        bias=jnp.concatenate([bu_ref[pl.ds(r,1),:] for r in rows],axis=1)
        wu=w.at[slot,0]; wd=w.at[slot,1]
        def tokens(b,sums):
            r=pl.ds(pl.multiple_of(b*padded,16),padded)
            u=dot(h2_ref[r,:],wu[...],NT)+bias
            value,slope=gelu_both(u)
            a=value.astype(BF)
            a_all[r,:]=a
            dg=dot(dd[r,:],wd[...],NT)
            du=(dg*slope).astype(BF)
            du_all[r,:]=du
            ynew=dot(a,wd[...]); dnew=dot(du,wu[...])
            @pl.when(i==0)
            def _():
                y_acc[r,:]=ynew; dh_acc[r,:]=dnew
            @pl.when(i>0)
            def _():
                y_acc[r,:]+=ynew; dh_acc[r,:]+=dnew
            return sums+jnp.sum(du.astype(F32),axis=0,keepdims=True)
        sums=lax.fori_loop(0,blocks,tokens,jnp.zeros((1,width),F32))
        for q,row in enumerate(rows):
            gbu_ref[pl.ds(row,1),:]=sums[:,q*hid:(q+1)*hid]
        for t in range(0,width,gtile):
            g_out[1,t:t+gtile,:]=dot(a_all[:,t:t+gtile],dd[...],TN).astype(BF)
            g_out[0,t:t+gtile,:]=dot(du_all[:,t:t+gtile],h2_ref[...],TN).astype(BF)
        save(i,True)
        return 0
    lax.fori_loop(0,nk,step,0)
    for i in range(images):
        r=2*i*padded
        yown_ref[i]=y_acc[r:r+padded,:]
        yoth_ref[i]=y_acc[r+padded:r+2*padded,:].astype(BF)
    dh_ref[...]=dh_acc[...].astype(BF)
    save(nk-1,False)
    for cps in moves:
        for cp in cps:
            cp.wait_recv()
            cp.wait_send()

def mlp(ny,nx,h2,g_both,bu_rows,own_a,own_b,oth_a,oth_b,gtile=256):
    keys=sorted(((ky,kx) for ky in range(ny) for kx in range(nx)),reverse=True); nk=len(keys)
    _,images,half,feat=g_both.shape
    keys_b=sorted(keys,key=lambda k:(k[1],k[0]),reverse=True)
    tokens=h2.shape[0]; padded=tokens//(2*images)
    ud,hid=own_a.shape[2:4]
    width=4*hid
    piece=jax.ShapeDtypeStruct((2,ud,hid,feat),BF)
    out=pl.pallas_call(functools.partial(mlp_kernel,keys,keys_b,ny,nx,gtile=min(gtile,width)),
        in_specs=[VM]*3+[ANY]*4,
        out_specs=[ANY]*(2*nk)+[VM]*4+[ANY]*2,
        out_shape=[piece]*(2*nk)+[jax.ShapeDtypeStruct((images,padded,feat),F32),jax.ShapeDtypeStruct((images,padded,feat),BF),
            jax.ShapeDtypeStruct((tokens,feat),BF),jax.ShapeDtypeStruct(bu_rows.shape,F32),
            jax.ShapeDtypeStruct((ny-1,nx,2,ud,hid,feat),BF),jax.ShapeDtypeStruct((nx-1,ny,2,ud,hid,feat),BF)],
        scratch_shapes=[pltpu.VMEM((2,2,width,feat),BF),pltpu.VMEM((tokens,feat),BF),pltpu.VMEM((tokens,width),BF),pltpu.VMEM((tokens,width),BF),
            pltpu.VMEM((tokens,feat),F32),pltpu.VMEM((tokens,feat),F32),pltpu.VMEM((2,width,feat),BF),
            pltpu.SemaphoreType.DMA((2,8)),pltpu.SemaphoreType.DMA((8,)),pltpu.SemaphoreType.DMA((2*nk,)),pltpu.SemaphoreType.DMA((2*nk,))],
        name="feed_forward",
        compiler_params=pltpu.CompilerParams(collective_id=3,has_side_effects=True,vmem_limit_bytes=60<<20),
        cost_estimate=pl.CostEstimate(flops=nk*6*2*tokens*feat*width,bytes_accessed=40<<20,transcendentals=nk*tokens*width),
    )(h2,g_both,bu_rows,own_a,own_b,oth_a,oth_b)
    return dict(zip(keys,out[:nk])),dict(zip(keys_b,out[nk:2*nk])),out[2*nk:]

HD=64; HALF_D=512

def head_operands(q,k,kb,scale):
    q=q.astype(F32)*scale; k=k.astype(F32); kb=kb.astype(F32)
    lane=lax.broadcasted_iota(jnp.int32,q.shape,1)
    low=lane<HD
    one=jnp.where((lane==0)|(lane==HD),1.0,0.0)
    qs=[jnp.where(low,q,one).astype(BF),jnp.where(low,one,q).astype(BF)]
    ks=[jnp.where(low,k,kb).astype(BF),jnp.where(low,kb,k).astype(BF)]
    return q,k,low,qs,ks

def attend_pair(q,k,v,kb):
    q,k,low,qs,ks=head_operands(q,k,kb,HD**-0.5)
    vt=v.astype(F32).T.astype(BF)
    outs=[]; sums=[]
    for j in range(2):
        s=dot(ks[j],qs[j],NT)
        m=jnp.max(s,axis=0,keepdims=True)
        e=jnp.exp(s-m)
        l=jnp.sum(e,axis=0,keepdims=True)
        o=dot(vt[j*HD:(j+1)*HD],e.astype(BF))
        outs.append(o*(1.0/l))
        sums.append(m+jnp.log(l))
    return jnp.concatenate(outs,axis=0).T.astype(BF),sums

def attend_back_kernel(q_ref,k_ref,v_ref,kb_ref,o_ref,g_ref,lse_ref,out_ref,sum_ref,*,pairs,chunk):
    p=pl.program_id(1)
    @pl.when((pl.program_id(0)==0)&(p==0))
    def _(): sum_ref[...]=jnp.zeros_like(sum_ref)
    scale=HD**-0.5
    q,k,low,qs,ks=head_operands(q_ref[0],k_ref[0],kb_ref[0],scale)
    qb=q.astype(BF)
    kt=k.T.astype(BF)
    g=g_ref[0]; gf=g.astype(F32)
    prod=(gf*o_ref[0].astype(F32)).T
    v=v_ref[0]
    rows=q.shape[0]
    dqs=[];dks=[];dvs=[]
    for j in range(2):
        gj=(jnp.where(low,gf,0.0) if j==0 else jnp.where(low,0.0,gf)).astype(BF)
        delta=jnp.sum(prod[j*HD:(j+1)*HD],axis=0,keepdims=True)
        lse=lse_ref[0,0,j:j+1,:]
        dq=None; dk=[]; dv=[]
        for r in range(0,rows,chunk):
            s=dot(ks[j][r:r+chunk],qs[j],NT)
            pr=jnp.exp(s-lse)
            dp=dot(v[r:r+chunk],gj,NT)
            ds=(pr*(dp-delta)).astype(BF)
            dv.append(dot(pr.astype(BF),g))
            dk.append(dot(ds,qb))
            t=dot(kt[j*HD:(j+1)*HD,r:r+chunk],ds) if chunk==rows else dot(k[r:r+chunk].astype(BF),ds,TN)[j*HD:(j+1)*HD]
            dq=t if dq is None else dq+t
        dqs.append(dq)
        dks.append(jnp.concatenate(dk,axis=0) if len(dk)>1 else dk[0]); dvs.append(jnp.concatenate(dv,axis=0) if len(dv)>1 else dv[0])
    parts=((jnp.concatenate(dqs,axis=0)*scale).T.astype(BF),jnp.where(low,dks[0],dks[1]).astype(BF),jnp.where(low,dvs[0],dvs[1]).astype(BF))
    for t,part in enumerate(parts):
        at=pl.ds(pl.multiple_of((t*pairs+p)*128,128),128)
        out_ref[0,:,at]=part
        sum_ref[0:1,at]+=jnp.sum(part.astype(F32),axis=0,keepdims=True)

def attend_back(qkv,kbias,mixed,grad,lse,chunk=None):
    n,rows,w=qkv.shape; pairs=w//3//128
    chunk=chunk or rows
    blk=lambda off: pl.BlockSpec((1,rows,128),lambda i,p: (i,0,off+p))
    return pl.pallas_call(functools.partial(attend_back_kernel,pairs=pairs,chunk=chunk),grid=(n,pairs),
        in_specs=[blk(0),blk(pairs),blk(2*pairs),pl.BlockSpec((1,rows,128),lambda i,p:(i,0,0)),blk(0),blk(0),pl.BlockSpec((1,1,8,rows),lambda i,p:(i,p,0,0))],
        out_specs=[pl.BlockSpec((1,rows,w),lambda i,p:(i,0,0)),pl.BlockSpec((8,w),lambda i,p:(0,0))],
        out_shape=[jax.ShapeDtypeStruct((n,rows,w),BF),jax.ShapeDtypeStruct((8,w),F32)],
        name="attend_back",
        compiler_params=pltpu.CompilerParams(vmem_limit_bytes=50<<20),
        cost_estimate=pl.CostEstimate(flops=n*pairs*20*rows*rows*128,bytes_accessed=n*rows*w*5,transcendentals=n*pairs*2*rows*rows),
    )(qkv,qkv,qkv,kbias,mixed,grad,lse)

NORM_EPS=1e-6
def norm_parts(values):
    center = values - jnp.mean(values, axis=-1, keepdims=True)
    inverse = lax.rsqrt(jnp.mean(center * center, axis=-1, keepdims=True) + NORM_EPS)
    return center * inverse, inverse

def norm_back(values, gain, grad):
    normed, inverse = norm_parts(values)
    scaled = grad * gain
    mean_one = jnp.mean(scaled, axis=-1, keepdims=True)
    mean_two = jnp.mean(scaled * normed, axis=-1, keepdims=True)
    return (scaled - mean_one - normed * mean_two) * inverse, grad * normed

def wide_rows(buf,block):
    n=block.shape[0]; total=buf.shape[0]
    buf[total-16:,:]=jnp.zeros((16,buf.shape[1]),F32)
    buf[0:n,:]=block.astype(F32)
    return buf[...]

def middle_back_kernel(x2_ref,da_ref,db_ref,go_ref,gt_ref,mix_ref,w_ref,gain_ref,dx_ref,dat_ref,gw_ref,sum_ref,buf,acc):
    i=pl.program_id(0)
    @pl.when(i==0)
    def _():
        acc[...]=jnp.zeros_like(acc); sum_ref[...]=jnp.zeros_like(sum_ref)
    for s,src in enumerate((go_ref,gt_ref)):
        dd=wide_rows(buf.at[s],src[0,0])
        grad=da_ref[0,s].astype(F32)+db_ref[0,1-s].astype(F32)
        dx,gg=norm_back(x2_ref[0,s],gain_ref[...],grad)
        dx=dx+dd
        dob=dx.astype(BF)
        if s==0:
            dx_ref[0]=dx
            for r,t in enumerate((gg,grad,dob.astype(F32),dd)):
                sum_ref[r:r+1,:]+=jnp.sum(t,axis=0,keepdims=True)
        dat_ref[0,s]=dot(dob,w_ref[...],NT).astype(BF)
        acc[...]+=dot(mix_ref[0,s],dob,TN)
    @pl.when(i==pl.num_programs(0)-1)
    def _(): gw_ref[...]=acc[...].astype(BF)

def middle_back(x2,dh_own,dh_oth,g_both,mixed,w_own,gain):
    _,n,half,feat=g_both.shape
    _,_,padded,width=mixed.shape
    tok=lambda s: pl.BlockSpec((1,1,half,feat),lambda i:(s,i,0,0))
    mix=pl.BlockSpec((1,2,padded,width),lambda i:(i,0,0,0))
    big=pl.BlockSpec((1,2,padded,feat),lambda i:(i,0,0,0))
    full=pl.BlockSpec((width,feat),lambda i:(0,0))
    return pl.pallas_call(middle_back_kernel,grid=(n,),
        in_specs=[big,big,big,tok(0),tok(1),mix,full,pl.BlockSpec((1,feat),lambda i:(0,0))],
        out_specs=[pl.BlockSpec((1,padded,feat),lambda i:(i,0,0)),mix,full,pl.BlockSpec((8,feat),lambda i:(0,0))],
        out_shape=[jax.ShapeDtypeStruct((n,padded,feat),F32),jax.ShapeDtypeStruct(mixed.shape,BF),jax.ShapeDtypeStruct((width,feat),BF),jax.ShapeDtypeStruct((8,feat),F32)],
        scratch_shapes=[pltpu.VMEM((2,padded,feat),F32),pltpu.VMEM((width,feat),F32)],name="middle_back",
        compiler_params=pltpu.CompilerParams(vmem_limit_bytes=56<<20),
        cost_estimate=pl.CostEstimate(flops=n*8*padded*feat*width,bytes_accessed=30<<20,transcendentals=0),
    )(x2,dh_own,dh_oth,g_both,g_both,mixed,w_own,gain[None])


def tail_kernel(ny, nx, *refs):
    h1_ref, dqkv_ref, go_ref, x_ref, dx_ref, gain_ref, vec_ref, w = refs[:8]
    keep_ref, pass_ref = refs[8:10]
    o = 10
    mine_ref, theirs_ref, so_ref, sf_ref, ig_ref, vout_ref, norm_ref = refs[o:o + 7]
    (grad, ra1, ra2, rb1, rb2, sa, sb, oa1, oa2, ob1, ob2, ta, tb, osum, ocross, ocore, odp, ofin,
     fpart, fdp, frecv, isum, ipart, irecv, idp, ifin,
     buf, give, got, stage, vrecv, nrecv, nval, send_sem, recv_sem) = refs[o + 7:]
    h, y, x, c, l = (lax.axis_index(a) for a in AXES)
    _, images, half, feat = x_ref.shape
    padded = dx_ref.shape[1]
    rows = grad.shape[4]
    apart = h != c
    cross = {"seq": 1 - h, "core": 1 - c}
    to_core, to_seq, to_dp = {"core": 1 - c}, {"seq": 1 - h}, {"dp": 1 - l}
    to_x = [{"x": lax.rem(x + k, nx)} for k in range(nx)]
    to_y = [{"y": lax.rem(y + k, ny)} for k in range(ny)]
    yy = [lax.rem(y + k, ny) for k in range(ny)]
    xx = [lax.rem(x + k, nx) for k in range(nx)]
    zz = [h, 1 - h]
    wires = Wires(send_sem, recv_sem)
    greet([to_core, to_seq, to_dp] + to_x[1:] + to_y[1:], cross, apart)

    fd = wires.send(pass_ref, fdp, to_dp)
    oa_got = [[wires.send(go_ref.at[yy[ky], xx[kx], h], oa1.at[ky - 1, kx], to_y[ky]) for kx in range(nx)] for ky in range(1, ny)]
    ob_got = [[wires.send(go_ref.at[yy[ky], xx[kx], 1 - h], ob1.at[kx - 1, ky], to_x[kx]) for ky in range(ny)] for kx in range(1, nx)]
    width = nx * 2 * rows
    ia_got, ib_got = [], []
    for ky in range(ny - 1, -1, -1):
        for kz in range(2):
            col = pl.multiple_of((zz[kz] * ny + yy[ky]) * width, 128)
            t = dot(h1_ref[:, pl.ds(col, width)], dqkv_ref[...], TN).astype(BF)
            for q in range(nx):
                for core in range(2):
                    r = (q * 2 + core) * rows
                    grad[zz[kz], yy[ky], q, core] = t[r:r + rows]
            for kx in range(nx):
                if ky > 0:
                    ia_got.append(wires.send(grad.at[zz[kz], yy[ky], xx[kx], c], ra1.at[ky - 1, kz, kx], to_y[ky]))
                if kx > 0:
                    ib_got.append(wires.send(grad.at[zz[kz], yy[ky], xx[kx], 1 - c], rb1.at[kx - 1, kz, ky], to_x[kx]))
    dh_got = []
    for i in range(images):
        r = (2 * i + 1) * padded
        give[i] = dot(dqkv_ref[r:r + padded, :], w[...], NT).astype(BF)
        dh_got.append(wires.send(give.at[i], got.at[i], to_core))
    sum_gain, sum_shift = jnp.zeros((1, feat), F32), jnp.zeros((1, feat), F32)
    crossing_copies = [wires.make(stage.at[i], ig_ref.at[i], cross) for i in range(images)]

    def input_back(i, sum_gain, sum_shift):
        r = 2 * i * padded
        own = dot(dqkv_ref[r:r + padded, :], w[...], NT)
        dh_got[i].wait_recv()
        g = own + got[i].astype(F32)
        dx, gg = norm_back(wide_rows(buf, x_ref[0, i]), gain_ref[...], g)
        stage[i] = (dx + dx_ref[i]).astype(BF)[:half]

        @pl.when(apart)
        def _():
            crossing_copies[i].start()

        @pl.when(jnp.logical_not(apart))
        def _():
            ig_ref[i] = stage[i]

        return sum_gain + jnp.sum(gg, axis=0, keepdims=True), sum_shift + jnp.sum(g, axis=0, keepdims=True)

    for i in range(images):
        sum_gain, sum_shift = input_back(i, sum_gain, sum_shift)
    fd.wait_recv()
    fpart[...] = add_all(keep_ref[...], fdp[...]).astype(BF)
    fs = wires.send(fpart.at[1], frecv, to_seq)
    for row in oa_got + ob_got:
        for cp in row:
            cp.wait_recv()
    o_got = []
    for kx in range(1, nx):
        ta[kx - 1] = add_all(go_ref[y, xx[kx], h], *(oa1[k, kx] for k in range(ny - 1))).astype(BF)
        o_got.append(wires.send(ta.at[kx - 1], oa2.at[kx - 1], to_x[kx]))
    for ky in range(1, ny):
        tb[ky - 1] = add_all(go_ref[yy[ky], x, 1 - h], *(ob1[k, ky] for k in range(nx - 1))).astype(BF)
        o_got.append(wires.send(tb.at[ky - 1], ob2.at[ky - 1], to_y[ky]))

    for cp in ia_got + ib_got:
        cp.wait_recv()
    i_got = []
    for kz in range(2):
        for kx in range(1, nx):
            sa[kx - 1, kz] = add_all(grad[zz[kz], y, xx[kx], c], *(ra1[k, kz, kx] for k in range(ny - 1))).astype(BF)
        for ky in range(1, ny):
            sb[ky - 1, kz] = add_all(grad[zz[kz], yy[ky], x, 1 - c], *(rb1[k, kz, ky] for k in range(nx - 1))).astype(BF)
    for kx in range(1, nx):
        i_got.append(wires.send(sa.at[kx - 1], ra2.at[kx - 1], to_x[kx]))
    for ky in range(1, ny):
        i_got.append(wires.send(sb.at[ky - 1], rb2.at[ky - 1], to_y[ky]))
    vout_ref[...] = vec_ref[...]
    for q in range(feat // 128):
        vout_ref[q:q + 1, :] = sum_gain[:, q * 128:(q + 1) * 128]
        vout_ref[feat // 128 + q:feat // 128 + q + 1, :] = sum_shift[:, q * 128:(q + 1) * 128]
    rounds = [[to_core], to_x[1:], to_y[1:], [to_seq], [to_dp]]
    slot = [0]

    def start_round(value, landing, peers):
        first = slot[0]
        cps = [wires.send(value, landing.at[first + k], peer) for k, peer in enumerate(peers)]
        slot[0] += len(peers)
        return first, cps

    def end_round(value_ref, landing, started):
        first, cps = started
        for cp in cps:
            cp.wait_recv()
        for cp in cps:
            cp.wait_send()
        wires.sent = [cp for cp in wires.sent if all(cp is not other for other in cps)]
        value_ref[...] = add_all(value_ref[...], *(landing[first + k] for k in range(len(cps))))

    vec_round = start_round(vout_ref, vrecv, rounds[0])
    for cp in i_got:
        cp.wait_recv()
    for kz in range(2):
        isum[0, kz] = add_all(grad[zz[kz], y, x, c], *(ra1[k, kz, 0] for k in range(ny - 1)), *(ra2[k, kz] for k in range(nx - 1))).astype(BF)
        isum[1, kz] = add_all(grad[zz[kz], y, x, 1 - c], *(rb1[k, kz, 0] for k in range(nx - 1)), *(rb2[k, kz] for k in range(ny - 1))).astype(BF)
    idd = wires.send(isum.at[1 - l], idp, to_dp)
    for cp in o_got:
        cp.wait_recv()
    osum[0] = add_all(go_ref[y, x, h], *(oa1[k, 0] for k in range(ny - 1)), *(oa2[k] for k in range(nx - 1))).astype(BF)
    osum[1] = add_all(go_ref[y, x, 1 - h], *(ob1[k, 0] for k in range(nx - 1)), *(ob2[k] for k in range(ny - 1))).astype(BF)
    out_cross = wires.make(osum, ocross, cross)

    @pl.when(apart)
    def _():
        out_cross.start()

    @pl.when(jnp.logical_not(apart))
    def _():
        ocross[...] = osum[...]

    end_round(vout_ref, vrecv, vec_round)
    vec_round = start_round(vout_ref, vrecv, rounds[1])
    idd.wait_recv()
    ipart[...] = add_all(isum[l], idp[...]).astype(BF)
    is_ = wires.send(ipart.at[1], irecv, to_seq)
    end_round(vout_ref, vrecv, vec_round)
    vec_round = start_round(vout_ref, vrecv, rounds[2])

    @pl.when(apart)
    def _():
        out_cross.wait_recv()

    oc = wires.send(ocross.at[1], ocore, to_core)
    fs.wait_recv()
    sf_ref[l] = add_all(fpart[0], frecv[...]).astype(BF)
    ff_last = wires.send(sf_ref.at[l], sf_ref.at[l], to_dp)
    end_round(vout_ref, vrecv, vec_round)
    vec_round = start_round(vout_ref, vrecv, rounds[3])
    oc.wait_recv()
    ofin[...] = add_all(ocross[0], ocore[...]).astype(BF)
    od = wires.send(ofin, odp, to_dp)
    is_.wait_recv()
    ifin[l] = add_all(ipart[0], irecv[...]).astype(BF)
    in_last = wires.send(ifin.at[l], ifin.at[l], to_dp)
    end_round(vout_ref, vrecv, vec_round)
    vec_round = start_round(vout_ref, vrecv, rounds[4])
    in_last.wait_recv()
    ic = wires.send(ifin.at[1], theirs_ref, to_core)
    mine_ref[...] = ifin[0]
    od.wait_recv()
    so_ref[...] = add_all(ofin[...], odp[...]).astype(BF)
    end_round(vout_ref, vrecv, vec_round)
    ff_last.wait_recv()

    def squares(value):
        value = value.astype(F32)
        return jnp.sum(jnp.sum(value * value, axis=0, keepdims=True), axis=1, keepdims=True)

    shard = ((h * ny + y) * nx + x) * 2 + c
    v = vout_ref[...]
    place = lax.broadcasted_iota(jnp.int32, v.shape, 0) * 128 + lax.broadcasted_iota(jnp.int32, v.shape, 1)
    share = v.shape[0] * 128 // (4 * ny * nx)
    v = jnp.where((place >= shard * share) & (place < (shard + 1) * share), v, 0.0)
    total = squares(v) + squares(so_ref[...]) + squares(mine_ref[...])
    for ab in range(2):
        for ud in range(2):
            total = total + squares(sf_ref[ab, ud])
    ic.wait_recv()
    total = total + squares(theirs_ref[...])
    nval[...] = jnp.broadcast_to(total, nval.shape)
    slot[0] = 0
    for peers in rounds[:4]:
        end_round(nval, nrecv, start_round(nval, nrecv, peers))
    norm_ref[...] = jnp.sqrt(nval[...])

    @pl.when(apart)
    def _():
        for cp in crossing_copies:
            cp.wait_recv()
        for cp in crossing_copies:
            cp.wait_send()
        out_cross.wait_send()

    wires.finish()


def tail_stage(h1, dqkv, g_out, x_own, dx2, gain, vec, w, keep, give, ny, nx):
    tokens, feat = h1.shape
    width = dqkv.shape[1]
    rows = feat // (4 * ny * nx)
    rows_o = g_out.shape[3]
    _, images, half, _ = x_own.shape
    padded = dx2.shape[1]
    _, ud, hid, _ = keep.shape
    ma, mb = max(ny - 1, 1), max(nx - 1, 1)
    piece, out_piece, ff = (rows, width), (rows_o, feat), (ud, hid, feat)
    peers = 4 + nx - 1 + ny - 1
    many = 200 + 32 * ny * nx
    V = lambda *s: pltpu.VMEM(s, BF)
    scratch = [
        V(2, ny, nx, 2, *piece),
        V(ny - 1, 2, nx, *piece), V(nx - 1, 2, *piece), V(nx - 1, 2, ny, *piece), V(ny - 1, 2, *piece),
        V(nx - 1, 2, *piece), V(ny - 1, 2, *piece),
        V(ny - 1, nx, *out_piece), V(nx - 1, *out_piece), V(nx - 1, ny, *out_piece), V(ny - 1, *out_piece),
        V(nx - 1, *out_piece), V(ny - 1, *out_piece),
        V(2, *out_piece), V(2, *out_piece), V(*out_piece), V(*out_piece), V(*out_piece),
        V(2, *ff), V(2, *ff), V(*ff),
        V(2, 2, *piece), V(2, *piece), V(*piece), V(2, *piece), V(2, *piece),
        pltpu.VMEM((padded, feat), F32), V(images, padded, feat), V(images, padded, feat), V(images, half, feat),
        pltpu.VMEM((peers,) + vec.shape, F32), pltpu.VMEM((peers, 8, 128), F32), pltpu.VMEM((8, 128), F32),
        pltpu.SemaphoreType.DMA((many,)), pltpu.SemaphoreType.DMA((many,)),
    ]
    return pl.pallas_call(
        functools.partial(tail_kernel, ny, nx),
        in_specs=[VM] * 10,
        out_specs=[VM] * 7,
        out_shape=[
            jax.ShapeDtypeStruct(piece, BF), jax.ShapeDtypeStruct(piece, BF), jax.ShapeDtypeStruct(out_piece, BF),
            jax.ShapeDtypeStruct((2,) + ff, BF), jax.ShapeDtypeStruct(x_own.shape[1:], BF),
            jax.ShapeDtypeStruct(vec.shape, F32), jax.ShapeDtypeStruct((8, 128), F32),
        ],
        scratch_shapes=scratch,
        name="tail_stage",
        compiler_params=pltpu.CompilerParams(collective_id=1, has_side_effects=True, vmem_limit_bytes=62 << 20),
        cost_estimate=pl.CostEstimate(flops=4 * tokens * feat * width, bytes_accessed=40 << 20, transcendentals=0),
    )(h1, dqkv, g_out, x_own, dx2, gain[None], vec, w, keep, give)

def head_kernel(ny, nx, *refs):
    (in_ref, out_ref, up_ref, down_ref, vec_ref, img_ref,
     h1_ref, qkv_ref, xb, w, my_out, other_out, fa, fb, cast_ref, vfull,
     theirs, o_own, o_core, tmp, buf, xsem, csem, send_sem, recv_sem) = refs
    h, y, x, c, l = (lax.axis_index(a) for a in AXES)
    images, half, feat = img_ref.shape
    rows = in_ref.shape[0]
    width = w.shape[1]
    part = width // 3
    hid = up_ref.shape[0] // 2
    apart = h != c
    cross = {"seq": 1 - h, "core": 1 - c}
    to_core, to_seq, to_dp = {"core": 1 - c}, {"seq": 1 - h}, {"dp": 1 - l}
    inner, to_near = l != h, {"seq": 1 - h, "dp": 1 - l}
    to_x = [{"x": lax.rem(x + nx - k, nx)} for k in range(nx)]
    to_y = [{"y": lax.rem(y + ny - k, ny)} for k in range(ny)]
    yy = [lax.rem(y + k, ny) for k in range(ny)]
    xx = [lax.rem(x + k, nx) for k in range(nx)]
    zz = [h, 1 - h]
    wires = Wires(send_sem, recv_sem)
    barrier = pltpu.get_barrier_semaphore()
    peers = [to_core, to_seq, to_dp] + to_x[1:] + to_y[1:]
    for peer in peers:
        pl.semaphore_signal(barrier, inc=1, device_id=peer, device_id_type=MESH_ID)

    @pl.when(apart)
    def _():
        pl.semaphore_signal(barrier, inc=1, device_id=cross, device_id_type=MESH_ID)

    @pl.when(inner)
    def _():
        pl.semaphore_signal(barrier, inc=1, device_id=to_near, device_id_type=MESH_ID)

    local_images = pltpu.make_async_copy(img_ref, xb.at[0], xsem)

    @pl.when(jnp.logical_not(apart))
    def _():
        local_images.start()

    def slot(z, yi, xi, core):
        return w.at[pl.ds(pl.multiple_of((((z * ny + yi) * nx + xi) * 2 + core) * rows, 16), rows)]

    mine = slot(h, y, x, c)
    for t in range(3):
        mine[:, t * part:(t + 1) * part] = in_ref[:, pl.ds(pl.multiple_of(t * 2 * part + c * part, 128), part)].astype(BF)
        theirs[:, t * part:(t + 1) * part] = in_ref[:, pl.ds(pl.multiple_of(t * 2 * part + (1 - c) * part, 128), part)].astype(BF)
    vfull[h, y, x, c] = vec_ref[...].astype(BF).astype(F32)
    o_own[...] = out_ref[...].astype(BF)
    pl.semaphore_wait(barrier, len(peers) + jnp.where(apart, 1, 0) + jnp.where(inner, 1, 0))

    spread, forward, settle = plane_moves(wires, to_x, to_y)

    def in_a(kz, ky, kx, *_):
        return slot(zz[kz], yy[ky], xx[kx], c)

    def in_b(kz, ky, kx, *_):
        return slot(zz[kz], yy[ky], xx[kx], 1 - c)

    def out_a(kz, ky, kx, *_):
        return my_out.at[yy[ky], xx[kx], h]

    def out_b(kz, ky, kx, *_):
        return my_out.at[yy[ky], xx[kx], 1 - h]

    ff_a, ff_b = by_offset(fa, tmp.at[0]), by_offset(fb, tmp.at[1])

    b_got = wires.send(theirs, slot(h, y, x, c), to_core)
    def across(core):
        own, other = slot(h, y, x, core), slot(1 - h, y, x, core)
        return wires.make(own, own, to_near), wires.make(other, other, to_dp)

    az, bz = across(c), across(1 - c)

    @pl.when(inner)
    def _():
        az[0].start()

    a0 = spread(in_a, 0, "x")
    vec_peers = [[to_core], to_x[1:], to_y[1:], [to_seq]]
    vec_at = [vfull.at[h, y, x, c], vfull.at[h, y, x], vfull.at[h, y], vfull.at[h]]

    def vec_send(r):
        return [wires.send(vec_at[r], vec_at[r], peer) for peer in vec_peers[r]]

    v = vec_send(0)
    oc = wires.send(o_own, o_core, to_core)
    xl = wires.make(img_ref, xb.at[1], to_core)

    @pl.when(jnp.logical_not(apart))
    def _():
        xl.start()

    b_got.wait_recv()

    @pl.when(inner)
    def _():
        bz[0].start()

    b0 = spread(in_b, 0, "y")
    for cp in v:
        cp.wait_recv()
    v = vec_send(1)
    for ab in range(2):
        tmp[ab, 0] = up_ref[ab * hid:(ab + 1) * hid, :].astype(BF)
        tmp[ab, 1] = down_ref[ab * hid:(ab + 1) * hid, :].astype(BF)
    keep = [
        pltpu.make_async_copy(tmp.at[0], fa.at[0, 0], csem.at[0]),
        pltpu.make_async_copy(tmp.at[1], fb.at[0, 0], csem.at[1]),
        pltpu.make_async_copy(tmp, cast_ref, csem.at[2]),
    ]
    for cp in keep:
        cp.start()
    for cp in v:
        cp.wait_recv()
    v = vec_send(2)
    forward(in_a, 0, "x", a0)
    forward(in_b, 0, "y", b0)
    oc.wait_recv()
    x_cross = [wires.make(img_ref.at[i], xb.at[0, i], cross) for i in range(images)]
    o_cross = [wires.make(o_own, my_out.at[y, x, 1 - h], cross), wires.make(o_core, my_out.at[y, x, h], cross)]

    @pl.when(apart)
    def _():
        for cp in o_cross:
            cp.start()

    @pl.when(jnp.logical_and(apart, jnp.logical_not(inner)))
    def _():
        x_cross[0].start()

    def arrive(pair):
        @pl.when(inner)
        def _():
            pair[0].wait_recv()
            pair[1].start()

        @pl.when(jnp.logical_not(inner))
        def _():
            pair[1].wait_recv()

    arrive(az)
    a1 = spread(in_a, 1, "x")
    arrive(bz)
    b1 = spread(in_b, 1, "y")
    for cp in v:
        cp.wait_recv()
    v = vec_send(3)

    @pl.when(jnp.logical_and(apart, inner))
    def _():
        x_cross[0].start()

    @pl.when(apart)
    def _():
        for cp in x_cross[1:]:
            cp.start()

    @pl.when(jnp.logical_not(apart))
    def _():
        my_out[y, x, h] = o_own[...]
        my_out[y, x, 1 - h] = o_core[...]
        local_images.wait()

    @pl.when(apart)
    def _():
        for cp in o_cross:
            cp.wait_recv()

    oa = spread(out_a, 0, "x")
    ob = spread(out_b, 0, "y")
    forward(in_a, 1, "x", a1)
    forward(in_b, 1, "y", b1)
    forward(out_a, 0, "x", oa)
    forward(out_b, 0, "y", ob)
    fa0 = spread(ff_a, 0, "x")
    fb0 = spread(ff_b, 0, "y")
    for got in (a0, b0, a1, b1):
        settle(got)
    for cp in v:
        cp.wait_recv()

    def row(start, count):
        per = vec_ref.shape[1]
        pieces, at = [], start
        while at < start + count:
            s, r = at // per, at % per
            n = min(per - r, start + count - at)
            xs = s // 2
            pieces.append(vfull[xs // (nx * ny), xs // nx % ny, xs % nx, s % 2][:, r:r + n])
            at += n
        return pieces[0] if len(pieces) == 1 else jnp.concatenate(pieces, axis=1)

    gain, shift_row = row(0, feat), row(feat, feat)
    q_row, v_row = row(2 * feat, feat), row(3 * feat, feat)
    q_row = jnp.where(c == 0, q_row[:, :part], q_row[:, part:])
    v_row = jnp.where(c == 0, v_row[:, :part], v_row[:, part:])
    bias = jnp.concatenate([q_row, jnp.zeros((1, part), F32), v_row], axis=1)

    def project(i, s):
        value = wide_rows(buf, xb[s, i])
        normed = (norm_parts(value)[0] * gain + shift_row).astype(BF)
        h1_ref[i, s] = normed
        qkv_ref[i, s] = (dot(normed, w[...]) + bias).astype(BF)

    near = jnp.where(apart, 1, 0)

    @pl.when(apart)
    def _():
        xl.wait_recv()

    def near_step(i, carry):
        project(i, near)
        return carry

    lax.fori_loop(0, images, near_step, 0)

    forward(ff_a, 0, "x", fa0)
    forward(ff_b, 0, "y", fb0)
    x_core = [wires.make(xb.at[0, i], xb.at[1, i], to_core) for i in range(images)]
    for i in range(images):
        @pl.when(apart)
        def _():
            x_cross[i].wait_recv()
            x_core[i].start()

        @pl.when(jnp.logical_not(apart))
        def _():
            x_core[i].wait_recv()

        project(i, 1 - near)
        if i == 0:
            settle(oa)
            settle(ob)
            other = wires.send(my_out, other_out, to_core)
    other.wait_recv()
    settle(fa0)
    settle(fb0)

    @pl.when(apart)
    def _():
        for cp in x_cross + o_cross + x_core:
            cp.wait_send()

    @pl.when(jnp.logical_not(apart))
    def _():
        xl.wait_send()

    @pl.when(inner)
    def _():
        for cp in az + bz:
            cp.wait_send()

    for cp in keep:
        cp.wait()
    wires.finish()


def head_stage(in_w, out_w, up_w, down_w, vec, images, padded, ny, nx):
    n, half, feat = images.shape
    rows, rows_out, rows_ff = in_w.shape[0], out_w.shape[0], up_w.shape[0]
    width = in_w.shape[1] // 2
    hid = rows_ff // 2
    many = 60 + 24 * ny * nx
    S = jax.ShapeDtypeStruct
    return pl.pallas_call(
        functools.partial(head_kernel, ny, nx),
        in_specs=[VM] * 5 + [ANY],
        out_specs=[VM] * 6 + [ANY] * 3 + [VM],
        out_shape=[
            S((n, 2, padded, feat), BF), S((n, 2, padded, width), BF), S((2, n, half, feat), BF), S((feat, width), BF),
            S((ny, nx, 2, rows_out, feat), BF), S((ny, nx, 2, rows_out, feat), BF),
            S((ny, nx, 2, hid, feat), BF), S((ny, nx, 2, hid, feat), BF), S((2, 2, hid, feat), BF),
            S((2, ny, nx, 2, 1, vec.shape[1]), F32),
        ],
        scratch_shapes=[
            pltpu.VMEM((rows, width), BF), pltpu.VMEM((rows_out, feat), BF), pltpu.VMEM((rows_out, feat), BF),
            pltpu.VMEM((2, 2, hid, feat), BF), pltpu.VMEM((padded, feat), F32),
            pltpu.SemaphoreType.DMA(()), pltpu.SemaphoreType.DMA((3,)),
            pltpu.SemaphoreType.DMA((many,)), pltpu.SemaphoreType.DMA((many,)),
        ],
        name="head_stage",
        compiler_params=pltpu.CompilerParams(collective_id=2, has_side_effects=True, vmem_limit_bytes=60 << 20),
        cost_estimate=pl.CostEstimate(flops=n * 4 * padded * feat * width, bytes_accessed=40 << 20, transcendentals=0),
    )(in_w, out_w, up_w, down_w, vec, images)


def mid_kernel(ny, nx, *refs):
    (qkv_ref, kf_ref, xb, wo_ref, wt_ref, vec_ref, cast_ref, grad_ref,
     mix_ref, lse_ref, x2_ref, h2_ref, g_ref, fa, fb,
     mix_oth, near_land, buf, csem, send_sem, recv_sem) = refs
    h, y, x, c, l = (lax.axis_index(a) for a in AXES)
    images, rows, width = mix_ref.shape
    padded = rows // 2
    pairs = width // 128
    apart, inner = h != c, l != h
    cross, to_near = {"seq": 1 - h, "core": 1 - c}, {"seq": 1 - h, "dp": 1 - l}
    to_core, to_dp = {"core": 1 - c}, {"dp": 1 - l}
    to_x = [{"x": lax.rem(x + nx - k, nx)} for k in range(nx)]
    to_y = [{"y": lax.rem(y + ny - k, ny)} for k in range(ny)]
    wires = Wires(send_sem, recv_sem)
    spread, forward, settle = plane_moves(wires, to_x, to_y)
    barrier = pltpu.get_barrier_semaphore()
    peers = [to_core, to_dp] + to_x[1:] + to_y[1:]
    for peer in peers:
        pl.semaphore_signal(barrier, inc=1, device_id=peer, device_id_type=MESH_ID)

    @pl.when(apart)
    def _():
        pl.semaphore_signal(barrier, inc=1, device_id=cross, device_id_type=MESH_ID)

    @pl.when(inner)
    def _():
        pl.semaphore_signal(barrier, inc=1, device_id=to_near, device_id_type=MESH_ID)

    pl.semaphore_wait(barrier, len(peers) + jnp.where(apart, 1, 0) + jnp.where(inner, 1, 0))
    near_ff = [wires.make(cast_ref.at[ab], near_land.at[ab], to_near) for ab in range(2)]
    far_ff = [wires.make(near_land.at[ab], near_land.at[ab], to_dp) for ab in range(2)]
    local_grad = pltpu.make_async_copy(grad_ref, g_ref.at[0], csem.at[0])
    grad_core = wires.make(grad_ref, g_ref.at[1], to_core)
    g_cross = [wires.make(grad_ref.at[i], g_ref.at[0, i], cross) for i in range(images)]
    g_core = [wires.make(g_ref.at[0, i], g_ref.at[1, i], to_core) for i in range(images)]

    @pl.when(inner)
    def _():
        near_ff[0].start()

    @pl.when(jnp.logical_not(apart))
    def _():
        local_grad.start()
        grad_core.start()

    def relay(ab):
        @pl.when(inner)
        def _():
            near_ff[ab].wait_recv()
            far_ff[ab].start()

    def arrive(ab):
        @pl.when(jnp.logical_not(inner))
        def _():
            far_ff[ab].wait_recv()

    mix_got = []
    for i in range(images):
        def pair(p, carry):
            at = [pl.ds(pl.multiple_of((t * pairs + p) * 128, 128), 128) for t in range(3)]
            mixed, sums = attend_pair(qkv_ref[i, :, at[0]], qkv_ref[i, :, at[1]], qkv_ref[i, :, at[2]], kf_ref[i])
            mix_ref[i, :, at[0]] = mixed
            for j in range(2):
                lse_ref[i, p, j:j + 1, :] = sums[j]
            return carry

        lax.fori_loop(0, pairs, pair, 0)
        mix_got.append(wires.send(mix_ref.at[i], mix_oth.at[i], to_core))
        if i == 0:
            @pl.when(inner)
            def _():
                near_ff[1].start()

        if i == max(images - 2, 0):
            relay(0)
        if i == images - 1:
            relay(1)
            @pl.when(apart)
            def _():
                for cp in g_cross:
                    cp.start()

    gots = []

    ff = [by_offset(fa, near_land.at[0]), by_offset(fb, near_land.at[1])]
    order = ("x", "y")

    def middle(i):
        mix_got[i].wait_recv()
        for s in range(2):
            own = slice(s * padded, (s + 1) * padded)
            oth = slice((1 - s) * padded, (2 - s) * padded)
            v = wide_rows(buf, xb[s, i])
            v = v + (dot(mix_ref[i, own, :], wo_ref[...]) + dot(mix_oth[i, oth, :], wt_ref[...])) + vec_ref[0:1, :]
            x2_ref[i, s] = v
            h2_ref[i, s] = (norm_parts(v)[0] * vec_ref[1:2, :] + vec_ref[2:3, :]).astype(BF)

    middle(0)
    arrive(0)
    gots.append(spread(ff[0], 1, "x"))
    for i in range(1, images):
        middle(i)
    arrive(1)
    gots.append(spread(ff[1], 1, "y"))
    keep = [pltpu.make_async_copy(near_land.at[ab], (fa, fb)[ab].at[0, 0], csem.at[1 + ab]) for ab in range(2)]
    for cp in keep:
        cp.start()
    for ab in range(2):
        forward(ff[ab], 1, order[ab], gots[ab])
    for i in range(images):
        @pl.when(apart)
        def _():
            g_cross[i].wait_recv()
            g_core[i].start()

        @pl.when(jnp.logical_not(apart))
        def _():
            g_core[i].wait_recv()

    @pl.when(apart)
    def _():
        grad_core.wait_recv()
        for cp in g_cross + g_core:
            cp.wait_send()

    @pl.when(jnp.logical_not(apart))
    def _():
        local_grad.wait()
        grad_core.wait_send()

    @pl.when(inner)
    def _():
        for cp in near_ff + far_ff:
            cp.wait_send()

    for got in gots:
        settle(got)
    for cp in keep:
        cp.wait()
    wires.finish()


def mid_stage(qkv, key_fill, x_both, w_own, w_oth, vec, low_ff, out_grad, ny, nx):
    n, rows, w3 = qkv.shape
    width, feat = w_own.shape
    half = out_grad.shape[1]
    _, ud, hid, _ = low_ff.shape
    many = 40 + 4 * ny * nx
    S = jax.ShapeDtypeStruct
    return pl.pallas_call(
        functools.partial(mid_kernel, ny, nx),
        in_specs=[VM] * 6 + [ANY] * 2,
        out_specs=[VM] * 5 + [ANY] * 2,
        out_shape=[
            S((n, rows, width), BF), S((n, width // 128, 8, rows), F32), S((n, 2, rows // 2, feat), F32),
            S((n, 2, rows // 2, feat), BF), S((2, n, half, feat), BF),
            S((ny, nx, ud, hid, feat), BF), S((ny, nx, ud, hid, feat), BF),
        ],
        scratch_shapes=[
            pltpu.VMEM((n, rows, width), BF), pltpu.VMEM((2, ud, hid, feat), BF), pltpu.VMEM((rows // 2, feat), F32),
            pltpu.SemaphoreType.DMA((3,)), pltpu.SemaphoreType.DMA((many,)), pltpu.SemaphoreType.DMA((many,)),
        ],
        name="mid_stage",
        compiler_params=pltpu.CompilerParams(collective_id=5, has_side_effects=True, vmem_limit_bytes=60 << 20),
        cost_estimate=pl.CostEstimate(flops=n * 4 * rows * rows * w3, bytes_accessed=50 << 20, transcendentals=n * 8 * rows * rows),
    )(qkv, key_fill, x_both, w_own, w_oth, vec, low_ff, out_grad)


def shift(value, axis, up):
    n = lax.axis_size(axis)
    return lax.ppermute(value, axis, [(i, (i + up) % n) for i in range(n)])


def after(value, *others):
    return lax.optimization_barrier((value, others))[0]


def crossing(value):
    return lax.ppermute(value, ("seq", "core"), [(1, 2), (2, 1)])


def pick(own, received):
    return jnp.where(lax.axis_index("seq") == lax.axis_index("core"), own, received)


def crossed(value):
    return pick(value, crossing(value))


def adam_update(master, first_moment, second_moment, gradient, step_rate, bias_one, bias_two):
    first_new = 0.5 * first_moment + 0.5 * gradient
    second_new = 0.5 * second_moment + 0.5 * gradient * gradient
    update = first_new / bias_one / (jnp.sqrt(second_new / bias_two) + ADAM_EPS)
    master_new = master - step_rate * (update + WEIGHT_DECAY * master)
    return (master_new, first_new, second_new)


def on_device(images, key_mask, out_grad, step_count, *params):
    masters, firsts, seconds = params[0:5], params[5:10], params[10:15]
    in_weights, out_weights, up_weights, down_weights, vectors = masters
    image_count, half, features = images.shape
    padded = -(-half // PAD_ROWS) * PAD_ROWS
    h, c = lax.axis_index("seq"), lax.axis_index("core")
    y, x = lax.axis_index("y"), lax.axis_index("x")
    ny, nx = lax.axis_size("y"), lax.axis_size("x")
    shards = 4 * ny * nx
    shard = ((h * ny + y) * nx + x) * 2 + c

    h1, qkv, x_both, full_in, my_out, other_out, own_a, own_b, low_ff, full_vec = head_stage(
        in_weights, out_weights, up_weights, down_weights, vectors[None], images, padded, ny, nx
    )
    my_out, other_out = my_out.reshape(HALF_D, D), other_out.reshape(HALF_D, D)
    rows_in, rows_out, rows_ff = in_weights.shape[0], out_weights.shape[0], up_weights.shape[0]
    half_ff = rows_ff // 2
    keys = [(ky, kx) for ky in range(ny) for kx in range(nx)]
    full_vec = full_vec.reshape(-1)
    gain_one, shift_one, query_bias, value_bias, out_bias, gain_two, shift_two, down_bias = (
        full_vec[i * D : (i + 1) * D] for i in range(8)
    )
    up_bias = full_vec[8 * D :]

    mask = key_mask.astype(F32)
    mask = jnp.where(h == c, mask, shift(mask, "core", 1)).reshape(image_count, 2, half)
    mask = jnp.where(c == 0, mask, mask[:, ::-1])
    mask = jnp.pad(mask, ((0, 0), (0, 0), (0, padded - half))).reshape(image_count, 2 * padded)
    key_fill = jnp.broadcast_to(jnp.where(mask > 0, 0.0, NEG_FILL)[..., None], mask.shape + (128,)).astype(BF)

    tokens = image_count * 2 * padded
    qkv = qkv.reshape(image_count, 2 * padded, 3 * HALF_D)
    mid_vec = jnp.pad(jnp.stack([out_bias, gain_two, shift_two]), ((0, 5), (0, 0)))
    mixed, lse, x2, h2, g_both, oth_a, oth_b = mid_stage(
        qkv, key_fill, x_both, my_out, other_out, mid_vec, low_ff, out_grad, ny, nx
    )
    halved = mixed.reshape(image_count, 2, padded, HALF_D)

    grad_a, grad_b, (y_own, y_oth, dh2, g_bu, first_a, first_b) = mlp(
        ny, nx, h2.reshape(tokens, D), g_both, up_bias.reshape(shards * 2, half_ff), own_a, own_b, oth_a, oth_b
    )
    result = y_own[:, :half] + shift(y_oth, "core", 1)[:, :half].astype(F32) + x2[:, 0, :half] + down_bias
    result = result.astype(BF)
    result_got = crossing(result)

    def second_stage(grads, firsts, swap):
        sums = []
        for k in range(firsts.shape[1]):
            sums.append(add_all(grads[(k, 0) if swap else (0, k)], *firsts[:, k]).astype(BF))
        return sums

    sums_a, sums_b = second_stage(grad_a, first_a, False), second_stage(grad_b, first_b, True)
    got_a = [lax.ppermute(s, "x", [(i, (i + k) % nx) for i in range(nx)]) for k, s in enumerate(sums_a) if k]
    got_b = [lax.ppermute(s, "y", [(i, (i + k) % ny) for i in range(ny)]) for k, s in enumerate(sums_b) if k]

    dh2 = dh2.reshape(image_count, 2, padded, D)
    dh2_oth = shift(dh2, "core", 1)
    dx2, dattn, g_out, sums_two = middle_back(x2, dh2, dh2_oth, g_both, halved, my_out, gain_two)
    dqkv, sums_qkv = attend_back(qkv, key_fill, mixed, dattn.reshape(mixed.shape), lse)
    got_a, got_b = after(got_a, dqkv), after(got_b, dqkv)
    plane_a, plane_b = add_all(sums_a[0], *got_a).astype(BF), add_all(sums_b[0], *got_b).astype(BF)
    l = lax.axis_index("dp")
    half_keep, half_give = jnp.where(l == 0, plane_a, plane_b), jnp.where(l == 0, plane_b, plane_a)

    zero = jnp.zeros((D,), F32)
    vec = jnp.concatenate(
        [
            zero,
            zero,
            lax.dynamic_update_slice(zero, sums_qkv[0, :HALF_D], (c * HALF_D,)),
            lax.dynamic_update_slice(zero, sums_qkv[0, 2 * HALF_D :], (c * HALF_D,)),
            sums_two[2],
            sums_two[0],
            sums_two[1],
            sums_two[3],
            g_bu.reshape(-1),
        ]
    ).reshape(-1, 128)
    in_mine, in_theirs, share_out, share_ff, input_grad, vec, norm = tail_stage(
        h1.reshape(tokens, D),
        dqkv.reshape(tokens, 3 * HALF_D),
        g_out.reshape(ny, nx, 2, rows_out, D),
        x_both,
        dx2,
        gain_one,
        vec,
        full_in,
        half_keep,
        half_give,
        ny,
        nx,
    )
    activations = pick(result, after(result_got, norm)).astype(F32)
    input_grad = input_grad.astype(F32)
    share_vec = lax.dynamic_slice(vec.reshape(shards, -1), (shard, 0), (1, vec.size // shards)).reshape(-1)
    in_mine, in_theirs = (s.reshape(rows_in, 3, 1, HALF_D) for s in (in_mine, in_theirs))
    share_in = jnp.where(
        c == 0, jnp.concatenate([in_mine, in_theirs], 2), jnp.concatenate([in_theirs, in_mine], 2)
    ).reshape(rows_in, 3 * D)
    share_up, share_down = (share_ff[:, i].reshape(rows_ff, D) for i in range(2))
    shares = tuple(s.astype(F32) for s in (share_in, share_out, share_up, share_down, share_vec))
    grad_norm = norm[0, 0]
    threshold = 0.5 * math.sqrt(4 * D * D + 2 * D * FF + 12 * D)
    clip_factor = jnp.minimum(1.0, threshold / grad_norm)
    bias = 1.0 - jnp.power(F32(0.5), step_count.astype(F32))
    rates = ((D // 2) ** (-0.5), (D // 4) ** (-0.5), D ** (-0.5), FF ** (-0.5), 0.2)
    results = [
        adam_update(masters[i], firsts[i], seconds[i], shares[i] * clip_factor, rates[i], bias, bias) for i in range(5)
    ]
    return (
        grad_norm,
        *(r[0] for r in results),
        *(r[1] for r in results),
        *(r[2] for r in results),
        *(r[0].astype(BF) for r in results),
        activations,
        input_grad,
    )


def solution(mesh):
    seq_n, fsdp_n, dp_n = (mesh.shape[a] for a in ("seq", "fsdp", "dp"))
    nx = math.isqrt(fsdp_n // 2)
    ny = fsdp_n // 2 // nx
    grid = Mesh(np.asarray(mesh.devices).reshape(seq_n, ny, nx, 2, dp_n), AXES)
    tokens = P(("y", "x", "core", "dp"), "seq", None)
    matrix, vector = P(SHARD, None), P(SHARD)
    five = (matrix, matrix, matrix, matrix, vector)
    return jax.shard_map(
        on_device,
        mesh=grid,
        in_specs=(tokens, P(("y", "x", "core", "dp"), None), tokens, P()) + five * 3,
        out_specs=(P(),) + five * 4 + (tokens, tokens),
        check_vma=False,
    )
```

```python
import functools
import math

import jax
import jax.numpy as jnp
import numpy as np
from jax import lax
from jax.experimental import pallas as pl
from jax.experimental.pallas import tpu as pltpu
from jax.sharding import Mesh
from jax.sharding import PartitionSpec as P

D = 1024
FF = 4096
PAD_ROWS = 16

NEG_FILL = -1000000000.0
ADAM_EPS = 1e-08
WEIGHT_DECAY = 0.05
AXES = ("seq", "y", "x", "core", "dp")
SHARD = ("seq", "y", "x", "core")

BF = jnp.bfloat16
F32 = jnp.float32
MESH_ID = pl.DeviceIdType.MESH


class Wires:
    def __init__(self, send_sem, recv_sem):
        self.send_sem, self.recv_sem, self.count, self.sent = send_sem, recv_sem, 0, []

    def make(self, src, dst, to):
        cp = pltpu.make_async_remote_copy(
            src_ref=src, dst_ref=dst, send_sem=self.send_sem.at[self.count], recv_sem=self.recv_sem.at[self.count],
            device_id=to, device_id_type=MESH_ID)
        self.count += 1
        return cp

    def send(self, src, dst, to):
        cp = self.make(src, dst, to)
        cp.start()
        self.sent.append(cp)
        return cp

    def finish(self):
        for cp in self.sent:
            cp.wait_send()


def greet(peers, crossing_peer, apart):
    barrier = pltpu.get_barrier_semaphore()
    for peer in peers:
        pl.semaphore_signal(barrier, inc=1, device_id=peer, device_id_type=MESH_ID)

    @pl.when(apart)
    def _():
        pl.semaphore_signal(barrier, inc=1, device_id=crossing_peer, device_id_type=MESH_ID)

    pl.semaphore_wait(barrier, len(peers) + jnp.where(apart, 1, 0))


def add_all(first, *others):
    total = first.astype(F32)
    for other in others:
        total = total + other.astype(F32)
    return total


def plane_moves(wires, to_x, to_y):
    nx, ny = len(to_x), len(to_y)

    def spread(piece_at, kz, first):
        got = {}
        for k in range(1, nx):
            got[0, k] = wires.send(piece_at(kz, 0, 0), piece_at(kz, 0, 0, k, "x"), to_x[k])
        for k in range(1, ny):
            got[k, 0] = wires.send(piece_at(kz, 0, 0), piece_at(kz, 0, 0, k, "y"), to_y[k])
        return got

    def forward(piece_at, kz, first, got):
        if first == "x":
            for kx in range(1, nx):
                got[0, kx].wait_recv()
                for ky in range(1, ny):
                    got[ky, kx] = wires.send(piece_at(kz, 0, kx), piece_at(kz, 0, kx, ky, "y"), to_y[ky])
            for ky in range(1, ny):
                got[ky, 0].wait_recv()
        else:
            for ky in range(1, ny):
                got[ky, 0].wait_recv()
                for kx in range(1, nx):
                    got[ky, kx] = wires.send(piece_at(kz, ky, 0), piece_at(kz, ky, 0, kx, "x"), to_x[kx])
            for kx in range(1, nx):
                got[0, kx].wait_recv()

    def settle(got):
        for (ky, kx), cp in got.items():
            if ky > 0 and kx > 0:
                cp.wait_recv()

    return spread, forward, settle


def by_offset(store, own):
    def piece_at(kz, ky, kx, k=0, axis=""):
        if k == 0 and ky == 0 and kx == 0:
            return own
        return store.at[ky + (k if axis == "y" else 0), kx + (k if axis == "x" else 0)]

    return piece_at

BF=jnp.bfloat16; F32=jnp.float32
def dot(a, b, dims=(((1,), (0,)), ((), ()))):
    return lax.dot_general(a, b, dims, preferred_element_type=F32)
NT=(((1,),(1,)),((),()))
TN=(((0,),(0,)),((),()))
ANY=pl.BlockSpec(memory_space=pl.ANY)
VM=pl.BlockSpec(memory_space=pltpu.VMEM)
SM=pl.BlockSpec(memory_space=pltpu.SMEM)

def gelu_both(u):
    c0=math.sqrt(2/math.pi)
    sq=u*u
    t=jnp.tanh(u*(c0+(c0*0.044715)*sq))
    half=0.5+0.5*t
    value=u*half
    slope=half+(0.5*u)*(1.0-t*t)*(c0+(3*c0*0.044715)*sq)
    return value,slope

def mlp_kernel(keys,keys_b,ny,nx,*refs,gtile):
    nk=len(keys)
    h2_ref,g_ref,bu_ref=refs[:3]
    planes=(refs[3:5],refs[5:7])
    o=7
    order=(keys,keys_b)
    ga,gb=refs[o:o+nk],refs[o+nk:o+2*nk]
    yown_ref,yoth_ref,dh_ref,gbu_ref,ra_ref,rb_ref=refs[o+2*nk:o+2*nk+6]
    w,dd,a_all,du_all,y_acc,dh_acc,g_out,wsem,gsem,send_sem,recv_sem=refs[o+2*nk+6:]
    h,y,x,c,_=(lax.axis_index(a) for a in AXES)
    to_x=[{"x":lax.rem(x+k,nx)} for k in range(nx)]
    to_y=[{"y":lax.rem(y+k,ny)} for k in range(ny)]
    wires=Wires(send_sem,recv_sem)
    moves=[]
    for ki,((ky,_),(_,kx)) in enumerate(zip(keys,keys_b)):
        cps=[]
        if ky>0: cps.append(wires.make(ga[ki],ra_ref.at[ky-1,keys[ki][1]],to_y[ky]))
        ky=keys_b[ki][0]
        if kx>0: cps.append(wires.make(gb[ki],rb_ref.at[kx-1,ky],to_x[kx]))
        moves.append(cps)
    barrier=pltpu.get_barrier_semaphore()
    for peer in to_x[1:]+to_y[1:]:
        pl.semaphore_signal(barrier,inc=1,device_id=peer,device_id_type=MESH_ID)
    _,images,half,feat=g_ref.shape
    hid=planes[0][0].shape[3]
    width=4*hid
    padded=h2_ref.shape[0]//(2*images)
    blocks=2*images

    def load(i,slot,go):
        for ki in range(nk):
            @pl.when(i==ki)
            def _():
                for kz in range(2):
                    for ud in range(2):
                        for ab in range(2):
                            cp=pltpu.make_async_copy(planes[kz][ab].at[order[ab][ki][0],order[ab][ki][1],ud],w.at[slot,ud,pl.ds((kz*2+ab)*hid,hid)],wsem.at[slot,kz*4+ud*2+ab])
                            cp.start() if go else cp.wait()
    def save(i,go):
        for ki in range(nk):
            @pl.when(i==ki)
            def _():
                for kz in range(2):
                    for ud in range(2):
                        for ab,dst in enumerate((ga[ki],gb[ki])):
                            cp=pltpu.make_async_copy(g_out.at[ud,pl.ds((kz*2+ab)*hid,hid)],dst.at[kz,ud],gsem.at[kz*4+ud*2+ab])
                            cp.start() if go else cp.wait()
    load(0,0,True)
    gbu_ref[...]=jnp.zeros_like(gbu_ref)
    for i in range(images):
        for s in range(2):
            r=(2*i+s)*padded
            tail=padded-16
            dd[r+tail:r+padded,:]=jnp.zeros((16,feat),BF)
            dd[r:r+half,:]=g_ref[s,i]
    pl.semaphore_wait(barrier,nx+ny-2)
    def step(i,_):
        slot=lax.rem(i,2)
        @pl.when(i>0)
        def _(): save(i-1,False)
        for ki,cps in enumerate(moves):
            if cps:
                @pl.when(i==ki+1)
                def _():
                    for cp in cps: cp.start()
        load(i,slot,False)
        @pl.when(i+1<nk)
        def _(): load(i+1,1-slot,True)
        rows=[]
        for kz in range(2):
            for ab in range(2):
                row=jnp.int32(0)
                for ki,(ky,kx) in enumerate(order[ab]):
                    here=(((lax.rem(h+kz,2)*ny+lax.rem(y+ky,ny))*nx+lax.rem(x+kx,nx))*2+c)*2+ab
                    row=jnp.where(i==ki,here,row)
                rows.append(row)
        bias=jnp.concatenate([bu_ref[pl.ds(r,1),:] for r in rows],axis=1)
        wu=w.at[slot,0]; wd=w.at[slot,1]
        def tokens(b,sums):
            r=pl.ds(pl.multiple_of(b*padded,16),padded)
            u=dot(h2_ref[r,:],wu[...],NT)+bias
            value,slope=gelu_both(u)
            a=value.astype(BF)
            a_all[r,:]=a
            dg=dot(dd[r,:],wd[...],NT)
            du=(dg*slope).astype(BF)
            du_all[r,:]=du
            ynew=dot(a,wd[...]); dnew=dot(du,wu[...])
            @pl.when(i==0)
            def _():
                y_acc[r,:]=ynew; dh_acc[r,:]=dnew
            @pl.when(i>0)
            def _():
                y_acc[r,:]+=ynew; dh_acc[r,:]+=dnew
            return sums+jnp.sum(du.astype(F32),axis=0,keepdims=True)
        sums=lax.fori_loop(0,blocks,tokens,jnp.zeros((1,width),F32))
        for q,row in enumerate(rows):
            gbu_ref[pl.ds(row,1),:]=sums[:,q*hid:(q+1)*hid]
        for t in range(0,width,gtile):
            g_out[1,t:t+gtile,:]=dot(a_all[:,t:t+gtile],dd[...],TN).astype(BF)
            g_out[0,t:t+gtile,:]=dot(du_all[:,t:t+gtile],h2_ref[...],TN).astype(BF)
        save(i,True)
        return 0
    lax.fori_loop(0,nk,step,0)
    for i in range(images):
        r=2*i*padded
        yown_ref[i]=y_acc[r:r+padded,:]
        yoth_ref[i]=y_acc[r+padded:r+2*padded,:].astype(BF)
    dh_ref[...]=dh_acc[...].astype(BF)
    save(nk-1,False)
    for cps in moves:
        for cp in cps:
            cp.wait_recv()
            cp.wait_send()

def mlp(ny,nx,h2,g_both,bu_rows,own_a,own_b,oth_a,oth_b,gtile=256):
    keys=sorted(((ky,kx) for ky in range(ny) for kx in range(nx)),reverse=True); nk=len(keys)
    _,images,half,feat=g_both.shape
    keys_b=sorted(keys,key=lambda k:(k[1],k[0]),reverse=True)
    tokens=h2.shape[0]; padded=tokens//(2*images)
    ud,hid=own_a.shape[2:4]
    width=4*hid
    piece=jax.ShapeDtypeStruct((2,ud,hid,feat),BF)
    out=pl.pallas_call(functools.partial(mlp_kernel,keys,keys_b,ny,nx,gtile=min(gtile,width)),
        in_specs=[VM]*3+[ANY]*4,
        out_specs=[ANY]*(2*nk)+[VM]*4+[ANY]*2,
        out_shape=[piece]*(2*nk)+[jax.ShapeDtypeStruct((images,padded,feat),F32),jax.ShapeDtypeStruct((images,padded,feat),BF),
            jax.ShapeDtypeStruct((tokens,feat),BF),jax.ShapeDtypeStruct(bu_rows.shape,F32),
            jax.ShapeDtypeStruct((ny-1,nx,2,ud,hid,feat),BF),jax.ShapeDtypeStruct((nx-1,ny,2,ud,hid,feat),BF)],
        scratch_shapes=[pltpu.VMEM((2,2,width,feat),BF),pltpu.VMEM((tokens,feat),BF),pltpu.VMEM((tokens,width),BF),pltpu.VMEM((tokens,width),BF),
            pltpu.VMEM((tokens,feat),F32),pltpu.VMEM((tokens,feat),F32),pltpu.VMEM((2,width,feat),BF),
            pltpu.SemaphoreType.DMA((2,8)),pltpu.SemaphoreType.DMA((8,)),pltpu.SemaphoreType.DMA((2*nk,)),pltpu.SemaphoreType.DMA((2*nk,))],
        name="feed_forward",
        compiler_params=pltpu.CompilerParams(collective_id=3,has_side_effects=True,vmem_limit_bytes=60<<20),
        cost_estimate=pl.CostEstimate(flops=nk*6*2*tokens*feat*width,bytes_accessed=40<<20,transcendentals=nk*tokens*width),
    )(h2,g_both,bu_rows,own_a,own_b,oth_a,oth_b)
    return dict(zip(keys,out[:nk])),dict(zip(keys_b,out[nk:2*nk])),out[2*nk:]

HD=64; HALF_D=512

def head_operands(q,k,kb,scale):
    q=q.astype(F32)*scale; k=k.astype(F32); kb=kb.astype(F32)
    lane=lax.broadcasted_iota(jnp.int32,q.shape,1)
    low=lane<HD
    one=jnp.where((lane==0)|(lane==HD),1.0,0.0)
    qs=[jnp.where(low,q,one).astype(BF),jnp.where(low,one,q).astype(BF)]
    ks=[jnp.where(low,k,kb).astype(BF),jnp.where(low,kb,k).astype(BF)]
    return q,k,low,qs,ks

def attend_pair(q,k,v,kb):
    q,k,low,qs,ks=head_operands(q,k,kb,HD**-0.5)
    vt=v.astype(F32).T.astype(BF)
    outs=[]; sums=[]
    for j in range(2):
        s=dot(ks[j],qs[j],NT)
        m=jnp.max(s,axis=0,keepdims=True)
        e=jnp.exp(s-m)
        l=jnp.sum(e,axis=0,keepdims=True)
        o=dot(vt[j*HD:(j+1)*HD],e.astype(BF))
        outs.append(o*(1.0/l))
        sums.append(m+jnp.log(l))
    return jnp.concatenate(outs,axis=0).T.astype(BF),sums

def attend_back_kernel(q_ref,k_ref,v_ref,kb_ref,o_ref,g_ref,lse_ref,out_ref,sum_ref,*,pairs,chunk):
    p=pl.program_id(1)
    @pl.when((pl.program_id(0)==0)&(p==0))
    def _(): sum_ref[...]=jnp.zeros_like(sum_ref)
    scale=HD**-0.5
    q,k,low,qs,ks=head_operands(q_ref[0],k_ref[0],kb_ref[0],scale)
    qb=q.astype(BF)
    kt=k.T.astype(BF)
    g=g_ref[0]; gf=g.astype(F32)
    prod=(gf*o_ref[0].astype(F32)).T
    v=v_ref[0]
    rows=q.shape[0]
    dqs=[];dks=[];dvs=[]
    for j in range(2):
        gj=(jnp.where(low,gf,0.0) if j==0 else jnp.where(low,0.0,gf)).astype(BF)
        delta=jnp.sum(prod[j*HD:(j+1)*HD],axis=0,keepdims=True)
        lse=lse_ref[0,0,j:j+1,:]
        dq=None; dk=[]; dv=[]
        for r in range(0,rows,chunk):
            s=dot(ks[j][r:r+chunk],qs[j],NT)
            pr=jnp.exp(s-lse)
            dp=dot(v[r:r+chunk],gj,NT)
            ds=(pr*(dp-delta)).astype(BF)
            dv.append(dot(pr.astype(BF),g))
            dk.append(dot(ds,qb))
            t=dot(kt[j*HD:(j+1)*HD,r:r+chunk],ds) if chunk==rows else dot(k[r:r+chunk].astype(BF),ds,TN)[j*HD:(j+1)*HD]
            dq=t if dq is None else dq+t
        dqs.append(dq)
        dks.append(jnp.concatenate(dk,axis=0) if len(dk)>1 else dk[0]); dvs.append(jnp.concatenate(dv,axis=0) if len(dv)>1 else dv[0])
    parts=((jnp.concatenate(dqs,axis=0)*scale).T.astype(BF),jnp.where(low,dks[0],dks[1]).astype(BF),jnp.where(low,dvs[0],dvs[1]).astype(BF))
    for t,part in enumerate(parts):
        at=pl.ds(pl.multiple_of((t*pairs+p)*128,128),128)
        out_ref[0,:,at]=part
        sum_ref[0:1,at]+=jnp.sum(part.astype(F32),axis=0,keepdims=True)

def attend_back(qkv,kbias,mixed,grad,lse,chunk=None):
    n,rows,w=qkv.shape; pairs=w//3//128
    chunk=chunk or rows
    blk=lambda off: pl.BlockSpec((1,rows,128),lambda i,p: (i,0,off+p))
    return pl.pallas_call(functools.partial(attend_back_kernel,pairs=pairs,chunk=chunk),grid=(n,pairs),
        in_specs=[blk(0),blk(pairs),blk(2*pairs),pl.BlockSpec((1,rows,128),lambda i,p:(i,0,0)),blk(0),blk(0),pl.BlockSpec((1,1,8,rows),lambda i,p:(i,p,0,0))],
        out_specs=[pl.BlockSpec((1,rows,w),lambda i,p:(i,0,0)),pl.BlockSpec((8,w),lambda i,p:(0,0))],
        out_shape=[jax.ShapeDtypeStruct((n,rows,w),BF),jax.ShapeDtypeStruct((8,w),F32)],
        name="attend_back",
        compiler_params=pltpu.CompilerParams(vmem_limit_bytes=50<<20),
        cost_estimate=pl.CostEstimate(flops=n*pairs*20*rows*rows*128,bytes_accessed=n*rows*w*5,transcendentals=n*pairs*2*rows*rows),
    )(qkv,qkv,qkv,kbias,mixed,grad,lse)

NORM_EPS=1e-6
def norm_parts(values):
    center = values - jnp.mean(values, axis=-1, keepdims=True)
    inverse = lax.rsqrt(jnp.mean(center * center, axis=-1, keepdims=True) + NORM_EPS)
    return center * inverse, inverse

def norm_back(values, gain, grad):
    normed, inverse = norm_parts(values)
    scaled = grad * gain
    mean_one = jnp.mean(scaled, axis=-1, keepdims=True)
    mean_two = jnp.mean(scaled * normed, axis=-1, keepdims=True)
    return (scaled - mean_one - normed * mean_two) * inverse, grad * normed

def wide_rows(buf,block):
    n=block.shape[0]; total=buf.shape[0]
    buf[total-16:,:]=jnp.zeros((16,buf.shape[1]),F32)
    buf[0:n,:]=block.astype(F32)
    return buf[...]

def middle_back_kernel(x2_ref,da_ref,db_ref,go_ref,gt_ref,mix_ref,w_ref,gain_ref,dx_ref,dat_ref,gw_ref,sum_ref,buf,acc):
    i=pl.program_id(0)
    @pl.when(i==0)
    def _():
        acc[...]=jnp.zeros_like(acc); sum_ref[...]=jnp.zeros_like(sum_ref)
    for s,src in enumerate((go_ref,gt_ref)):
        dd=wide_rows(buf.at[s],src[0,0])
        grad=da_ref[0,s].astype(F32)+db_ref[0,1-s].astype(F32)
        dx,gg=norm_back(x2_ref[0,s],gain_ref[...],grad)
        dx=dx+dd
        dob=dx.astype(BF)
        if s==0:
            dx_ref[0]=dx
            for r,t in enumerate((gg,grad,dob.astype(F32),dd)):
                sum_ref[r:r+1,:]+=jnp.sum(t,axis=0,keepdims=True)
        dat_ref[0,s]=dot(dob,w_ref[...],NT).astype(BF)
        acc[...]+=dot(mix_ref[0,s],dob,TN)
    @pl.when(i==pl.num_programs(0)-1)
    def _(): gw_ref[...]=acc[...].astype(BF)

def middle_back(x2,dh_own,dh_oth,g_both,mixed,w_own,gain):
    _,n,half,feat=g_both.shape
    _,_,padded,width=mixed.shape
    tok=lambda s: pl.BlockSpec((1,1,half,feat),lambda i:(s,i,0,0))
    mix=pl.BlockSpec((1,2,padded,width),lambda i:(i,0,0,0))
    big=pl.BlockSpec((1,2,padded,feat),lambda i:(i,0,0,0))
    full=pl.BlockSpec((width,feat),lambda i:(0,0))
    return pl.pallas_call(middle_back_kernel,grid=(n,),
        in_specs=[big,big,big,tok(0),tok(1),mix,full,pl.BlockSpec((1,feat),lambda i:(0,0))],
        out_specs=[pl.BlockSpec((1,padded,feat),lambda i:(i,0,0)),mix,full,pl.BlockSpec((8,feat),lambda i:(0,0))],
        out_shape=[jax.ShapeDtypeStruct((n,padded,feat),F32),jax.ShapeDtypeStruct(mixed.shape,BF),jax.ShapeDtypeStruct((width,feat),BF),jax.ShapeDtypeStruct((8,feat),F32)],
        scratch_shapes=[pltpu.VMEM((2,padded,feat),F32),pltpu.VMEM((width,feat),F32)],name="middle_back",
        compiler_params=pltpu.CompilerParams(vmem_limit_bytes=56<<20),
        cost_estimate=pl.CostEstimate(flops=n*8*padded*feat*width,bytes_accessed=30<<20,transcendentals=0),
    )(x2,dh_own,dh_oth,g_both,g_both,mixed,w_own,gain[None])


def tail_kernel(ny, nx, *refs):
    h1_ref, dqkv_ref, go_ref, x_ref, dx_ref, gain_ref, vec_ref, w = refs[:8]
    keep_ref, pass_ref = refs[8:10]
    o = 10
    mine_ref, theirs_ref, so_ref, sf_ref, ig_ref, vout_ref, norm_ref = refs[o:o + 7]
    (grad, ra1, ra2, rb1, rb2, sa, sb, oa1, oa2, ob1, ob2, ta, tb, osum, ocross, ocore, odp, ofin,
     fpart, fdp, frecv, isum, ipart, irecv, idp, ifin,
     buf, give, got, stage, vrecv, nrecv, nval, send_sem, recv_sem) = refs[o + 7:]
    h, y, x, c, l = (lax.axis_index(a) for a in AXES)
    _, images, half, feat = x_ref.shape
    padded = dx_ref.shape[1]
    rows = grad.shape[4]
    apart = h != c
    cross = {"seq": 1 - h, "core": 1 - c}
    to_core, to_seq, to_dp = {"core": 1 - c}, {"seq": 1 - h}, {"dp": 1 - l}
    to_x = [{"x": lax.rem(x + k, nx)} for k in range(nx)]
    to_y = [{"y": lax.rem(y + k, ny)} for k in range(ny)]
    yy = [lax.rem(y + k, ny) for k in range(ny)]
    xx = [lax.rem(x + k, nx) for k in range(nx)]
    zz = [h, 1 - h]
    wires = Wires(send_sem, recv_sem)
    greet([to_core, to_seq, to_dp] + to_x[1:] + to_y[1:], cross, apart)

    fd = wires.send(pass_ref, fdp, to_dp)
    oa_got = [[wires.send(go_ref.at[yy[ky], xx[kx], h], oa1.at[ky - 1, kx], to_y[ky]) for kx in range(nx)] for ky in range(1, ny)]
    ob_got = [[wires.send(go_ref.at[yy[ky], xx[kx], 1 - h], ob1.at[kx - 1, ky], to_x[kx]) for ky in range(ny)] for kx in range(1, nx)]
    width = nx * 2 * rows
    ia_got, ib_got = [], []
    for ky in range(ny - 1, -1, -1):
        for kz in range(2):
            col = pl.multiple_of((zz[kz] * ny + yy[ky]) * width, 128)
            t = dot(h1_ref[:, pl.ds(col, width)], dqkv_ref[...], TN).astype(BF)
            for q in range(nx):
                for core in range(2):
                    r = (q * 2 + core) * rows
                    grad[zz[kz], yy[ky], q, core] = t[r:r + rows]
            for kx in range(nx):
                if ky > 0:
                    ia_got.append(wires.send(grad.at[zz[kz], yy[ky], xx[kx], c], ra1.at[ky - 1, kz, kx], to_y[ky]))
                if kx > 0:
                    ib_got.append(wires.send(grad.at[zz[kz], yy[ky], xx[kx], 1 - c], rb1.at[kx - 1, kz, ky], to_x[kx]))
    dh_got = []
    for i in range(images):
        r = (2 * i + 1) * padded
        give[i] = dot(dqkv_ref[r:r + padded, :], w[...], NT).astype(BF)
        dh_got.append(wires.send(give.at[i], got.at[i], to_core))
    sum_gain, sum_shift = jnp.zeros((1, feat), F32), jnp.zeros((1, feat), F32)
    crossing_copies = [wires.make(stage.at[i], ig_ref.at[i], cross) for i in range(images)]

    def input_back(i, sum_gain, sum_shift):
        r = 2 * i * padded
        own = dot(dqkv_ref[r:r + padded, :], w[...], NT)
        dh_got[i].wait_recv()
        g = own + got[i].astype(F32)
        dx, gg = norm_back(wide_rows(buf, x_ref[0, i]), gain_ref[...], g)
        stage[i] = (dx + dx_ref[i]).astype(BF)[:half]

        @pl.when(apart)
        def _():
            crossing_copies[i].start()

        @pl.when(jnp.logical_not(apart))
        def _():
            ig_ref[i] = stage[i]

        return sum_gain + jnp.sum(gg, axis=0, keepdims=True), sum_shift + jnp.sum(g, axis=0, keepdims=True)

    for i in range(images):
        sum_gain, sum_shift = input_back(i, sum_gain, sum_shift)
    fd.wait_recv()
    fpart[...] = add_all(keep_ref[...], fdp[...]).astype(BF)
    fs = wires.send(fpart.at[1], frecv, to_seq)
    for row in oa_got + ob_got:
        for cp in row:
            cp.wait_recv()
    o_got = []
    for kx in range(1, nx):
        ta[kx - 1] = add_all(go_ref[y, xx[kx], h], *(oa1[k, kx] for k in range(ny - 1))).astype(BF)
        o_got.append(wires.send(ta.at[kx - 1], oa2.at[kx - 1], to_x[kx]))
    for ky in range(1, ny):
        tb[ky - 1] = add_all(go_ref[yy[ky], x, 1 - h], *(ob1[k, ky] for k in range(nx - 1))).astype(BF)
        o_got.append(wires.send(tb.at[ky - 1], ob2.at[ky - 1], to_y[ky]))

    for cp in ia_got + ib_got:
        cp.wait_recv()
    i_got = []
    for kz in range(2):
        for kx in range(1, nx):
            sa[kx - 1, kz] = add_all(grad[zz[kz], y, xx[kx], c], *(ra1[k, kz, kx] for k in range(ny - 1))).astype(BF)
        for ky in range(1, ny):
            sb[ky - 1, kz] = add_all(grad[zz[kz], yy[ky], x, 1 - c], *(rb1[k, kz, ky] for k in range(nx - 1))).astype(BF)
    for kx in range(1, nx):
        i_got.append(wires.send(sa.at[kx - 1], ra2.at[kx - 1], to_x[kx]))
    for ky in range(1, ny):
        i_got.append(wires.send(sb.at[ky - 1], rb2.at[ky - 1], to_y[ky]))
    vout_ref[...] = vec_ref[...]
    for q in range(feat // 128):
        vout_ref[q:q + 1, :] = sum_gain[:, q * 128:(q + 1) * 128]
        vout_ref[feat // 128 + q:feat // 128 + q + 1, :] = sum_shift[:, q * 128:(q + 1) * 128]
    rounds = [[to_core], to_x[1:], to_y[1:], [to_seq], [to_dp]]
    slot = [0]

    def start_round(value, landing, peers):
        first = slot[0]
        cps = [wires.send(value, landing.at[first + k], peer) for k, peer in enumerate(peers)]
        slot[0] += len(peers)
        return first, cps

    def end_round(value_ref, landing, started):
        first, cps = started
        for cp in cps:
            cp.wait_recv()
        for cp in cps:
            cp.wait_send()
        wires.sent = [cp for cp in wires.sent if all(cp is not other for other in cps)]
        value_ref[...] = add_all(value_ref[...], *(landing[first + k] for k in range(len(cps))))

    vec_round = start_round(vout_ref, vrecv, rounds[0])
    for cp in i_got:
        cp.wait_recv()
    for kz in range(2):
        isum[0, kz] = add_all(grad[zz[kz], y, x, c], *(ra1[k, kz, 0] for k in range(ny - 1)), *(ra2[k, kz] for k in range(nx - 1))).astype(BF)
        isum[1, kz] = add_all(grad[zz[kz], y, x, 1 - c], *(rb1[k, kz, 0] for k in range(nx - 1)), *(rb2[k, kz] for k in range(ny - 1))).astype(BF)
    idd = wires.send(isum.at[1 - l], idp, to_dp)
    for cp in o_got:
        cp.wait_recv()
    osum[0] = add_all(go_ref[y, x, h], *(oa1[k, 0] for k in range(ny - 1)), *(oa2[k] for k in range(nx - 1))).astype(BF)
    osum[1] = add_all(go_ref[y, x, 1 - h], *(ob1[k, 0] for k in range(nx - 1)), *(ob2[k] for k in range(ny - 1))).astype(BF)
    out_cross = wires.make(osum, ocross, cross)

    @pl.when(apart)
    def _():
        out_cross.start()

    @pl.when(jnp.logical_not(apart))
    def _():
        ocross[...] = osum[...]

    end_round(vout_ref, vrecv, vec_round)
    vec_round = start_round(vout_ref, vrecv, rounds[1])
    idd.wait_recv()
    ipart[...] = add_all(isum[l], idp[...]).astype(BF)
    is_ = wires.send(ipart.at[1], irecv, to_seq)
    end_round(vout_ref, vrecv, vec_round)
    vec_round = start_round(vout_ref, vrecv, rounds[2])

    @pl.when(apart)
    def _():
        out_cross.wait_recv()

    oc = wires.send(ocross.at[1], ocore, to_core)
    fs.wait_recv()
    sf_ref[l] = add_all(fpart[0], frecv[...]).astype(BF)
    ff_last = wires.send(sf_ref.at[l], sf_ref.at[l], to_dp)
    end_round(vout_ref, vrecv, vec_round)
    vec_round = start_round(vout_ref, vrecv, rounds[3])
    oc.wait_recv()
    ofin[...] = add_all(ocross[0], ocore[...]).astype(BF)
    od = wires.send(ofin, odp, to_dp)
    is_.wait_recv()
    ifin[l] = add_all(ipart[0], irecv[...]).astype(BF)
    in_last = wires.send(ifin.at[l], ifin.at[l], to_dp)
    end_round(vout_ref, vrecv, vec_round)
    vec_round = start_round(vout_ref, vrecv, rounds[4])
    in_last.wait_recv()
    ic = wires.send(ifin.at[1], theirs_ref, to_core)
    mine_ref[...] = ifin[0]
    od.wait_recv()
    so_ref[...] = add_all(ofin[...], odp[...]).astype(BF)
    end_round(vout_ref, vrecv, vec_round)
    ff_last.wait_recv()

    def squares(value):
        value = value.astype(F32)
        return jnp.sum(jnp.sum(value * value, axis=0, keepdims=True), axis=1, keepdims=True)

    shard = ((h * ny + y) * nx + x) * 2 + c
    v = vout_ref[...]
    place = lax.broadcasted_iota(jnp.int32, v.shape, 0) * 128 + lax.broadcasted_iota(jnp.int32, v.shape, 1)
    share = v.shape[0] * 128 // (4 * ny * nx)
    v = jnp.where((place >= shard * share) & (place < (shard + 1) * share), v, 0.0)
    total = squares(v) + squares(so_ref[...]) + squares(mine_ref[...])
    for ab in range(2):
        for ud in range(2):
            total = total + squares(sf_ref[ab, ud])
    ic.wait_recv()
    total = total + squares(theirs_ref[...])
    nval[...] = jnp.broadcast_to(total, nval.shape)
    slot[0] = 0
    for peers in rounds[:4]:
        end_round(nval, nrecv, start_round(nval, nrecv, peers))
    norm_ref[...] = jnp.sqrt(nval[...])

    @pl.when(apart)
    def _():
        for cp in crossing_copies:
            cp.wait_recv()
        for cp in crossing_copies:
            cp.wait_send()
        out_cross.wait_send()

    wires.finish()


def tail_stage(h1, dqkv, g_out, x_own, dx2, gain, vec, w, keep, give, ny, nx):
    tokens, feat = h1.shape
    width = dqkv.shape[1]
    rows = feat // (4 * ny * nx)
    rows_o = g_out.shape[3]
    _, images, half, _ = x_own.shape
    padded = dx2.shape[1]
    _, ud, hid, _ = keep.shape
    ma, mb = max(ny - 1, 1), max(nx - 1, 1)
    piece, out_piece, ff = (rows, width), (rows_o, feat), (ud, hid, feat)
    peers = 4 + nx - 1 + ny - 1
    many = 200 + 32 * ny * nx
    V = lambda *s: pltpu.VMEM(s, BF)
    scratch = [
        V(2, ny, nx, 2, *piece),
        V(ny - 1, 2, nx, *piece), V(nx - 1, 2, *piece), V(nx - 1, 2, ny, *piece), V(ny - 1, 2, *piece),
        V(nx - 1, 2, *piece), V(ny - 1, 2, *piece),
        V(ny - 1, nx, *out_piece), V(nx - 1, *out_piece), V(nx - 1, ny, *out_piece), V(ny - 1, *out_piece),
        V(nx - 1, *out_piece), V(ny - 1, *out_piece),
        V(2, *out_piece), V(2, *out_piece), V(*out_piece), V(*out_piece), V(*out_piece),
        V(2, *ff), V(2, *ff), V(*ff),
        V(2, 2, *piece), V(2, *piece), V(*piece), V(2, *piece), V(2, *piece),
        pltpu.VMEM((padded, feat), F32), V(images, padded, feat), V(images, padded, feat), V(images, half, feat),
        pltpu.VMEM((peers,) + vec.shape, F32), pltpu.VMEM((peers, 8, 128), F32), pltpu.VMEM((8, 128), F32),
        pltpu.SemaphoreType.DMA((many,)), pltpu.SemaphoreType.DMA((many,)),
    ]
    return pl.pallas_call(
        functools.partial(tail_kernel, ny, nx),
        in_specs=[VM] * 10,
        out_specs=[VM] * 7,
        out_shape=[
            jax.ShapeDtypeStruct(piece, BF), jax.ShapeDtypeStruct(piece, BF), jax.ShapeDtypeStruct(out_piece, BF),
            jax.ShapeDtypeStruct((2,) + ff, BF), jax.ShapeDtypeStruct(x_own.shape[1:], BF),
            jax.ShapeDtypeStruct(vec.shape, F32), jax.ShapeDtypeStruct((8, 128), F32),
        ],
        scratch_shapes=scratch,
        name="tail_stage",
        compiler_params=pltpu.CompilerParams(collective_id=1, has_side_effects=True, vmem_limit_bytes=62 << 20),
        cost_estimate=pl.CostEstimate(flops=4 * tokens * feat * width, bytes_accessed=40 << 20, transcendentals=0),
    )(h1, dqkv, g_out, x_own, dx2, gain[None], vec, w, keep, give)

def head_kernel(ny, nx, *refs):
    (in_ref, out_ref, up_ref, down_ref, vec_ref, img_ref,
     h1_ref, qkv_ref, xb, w, my_out, other_out, fa, fb, near_ref, vfull,
     theirs, o_own, o_core, tmp, buf, xsem, csem, send_sem, recv_sem) = refs
    h, y, x, c, l = (lax.axis_index(a) for a in AXES)
    images, half, feat = img_ref.shape
    rows = in_ref.shape[0]
    width = w.shape[1]
    part = width // 3
    hid = up_ref.shape[0] // 2
    apart = h != c
    cross = {"seq": 1 - h, "core": 1 - c}
    to_core, to_seq, to_dp = {"core": 1 - c}, {"seq": 1 - h}, {"dp": 1 - l}
    inner, to_near = l != h, {"seq": 1 - h, "dp": 1 - l}
    to_x = [{"x": lax.rem(x + nx - k, nx)} for k in range(nx)]
    to_y = [{"y": lax.rem(y + ny - k, ny)} for k in range(ny)]
    yy = [lax.rem(y + k, ny) for k in range(ny)]
    xx = [lax.rem(x + k, nx) for k in range(nx)]
    zz = [h, 1 - h]
    wires = Wires(send_sem, recv_sem)
    barrier = pltpu.get_barrier_semaphore()
    peers = [to_core, to_seq, to_dp] + to_x[1:] + to_y[1:]
    for peer in peers:
        pl.semaphore_signal(barrier, inc=1, device_id=peer, device_id_type=MESH_ID)

    @pl.when(apart)
    def _():
        pl.semaphore_signal(barrier, inc=1, device_id=cross, device_id_type=MESH_ID)

    @pl.when(inner)
    def _():
        pl.semaphore_signal(barrier, inc=1, device_id=to_near, device_id_type=MESH_ID)

    local_images = pltpu.make_async_copy(img_ref, xb.at[0], xsem)

    @pl.when(jnp.logical_not(apart))
    def _():
        local_images.start()

    def slot(z, yi, xi, core):
        return w.at[pl.ds(pl.multiple_of((((z * ny + yi) * nx + xi) * 2 + core) * rows, 16), rows)]

    mine = slot(h, y, x, c)
    for t in range(3):
        mine[:, t * part:(t + 1) * part] = in_ref[:, pl.ds(pl.multiple_of(t * 2 * part + c * part, 128), part)].astype(BF)
        theirs[:, t * part:(t + 1) * part] = in_ref[:, pl.ds(pl.multiple_of(t * 2 * part + (1 - c) * part, 128), part)].astype(BF)
    vfull[h, y, x, c] = vec_ref[...].astype(BF).astype(F32)
    o_own[...] = out_ref[...].astype(BF)
    pl.semaphore_wait(barrier, len(peers) + jnp.where(apart, 1, 0) + jnp.where(inner, 1, 0))

    spread, forward, settle = plane_moves(wires, to_x, to_y)

    def in_a(kz, ky, kx, *_):
        return slot(zz[kz], yy[ky], xx[kx], c)

    def in_b(kz, ky, kx, *_):
        return slot(zz[kz], yy[ky], xx[kx], 1 - c)

    def out_a(kz, ky, kx, *_):
        return my_out.at[yy[ky], xx[kx], h]

    def out_b(kz, ky, kx, *_):
        return my_out.at[yy[ky], xx[kx], 1 - h]

    ff_a, ff_b = by_offset(fa, tmp.at[0]), by_offset(fb, tmp.at[1])

    b_got = wires.send(theirs, slot(h, y, x, c), to_core)
    def across(core):
        own, other = slot(h, y, x, core), slot(1 - h, y, x, core)
        return wires.make(own, own, to_near), wires.make(other, other, to_dp)

    az, bz = across(c), across(1 - c)

    @pl.when(inner)
    def _():
        az[0].start()

    a0 = spread(in_a, 0, "x")
    vec_peers = [[to_core], to_x[1:], to_y[1:], [to_seq]]
    vec_at = [vfull.at[h, y, x, c], vfull.at[h, y, x], vfull.at[h, y], vfull.at[h]]

    def vec_send(r):
        return [wires.send(vec_at[r], vec_at[r], peer) for peer in vec_peers[r]]

    v = vec_send(0)
    oc = wires.send(o_own, o_core, to_core)
    xl = wires.make(img_ref, xb.at[1], to_core)

    @pl.when(jnp.logical_not(apart))
    def _():
        xl.start()

    b_got.wait_recv()

    @pl.when(inner)
    def _():
        bz[0].start()

    b0 = spread(in_b, 0, "y")
    for cp in v:
        cp.wait_recv()
    v = vec_send(1)
    for ab in range(2):
        tmp[ab, 0] = up_ref[ab * hid:(ab + 1) * hid, :].astype(BF)
        tmp[ab, 1] = down_ref[ab * hid:(ab + 1) * hid, :].astype(BF)
    keep = [
        pltpu.make_async_copy(tmp.at[0], fa.at[0, 0], csem.at[0]),
        pltpu.make_async_copy(tmp.at[1], fb.at[0, 0], csem.at[1]),
    ]
    for cp in keep:
        cp.start()
    for cp in v:
        cp.wait_recv()
    v = vec_send(2)
    forward(in_a, 0, "x", a0)
    forward(in_b, 0, "y", b0)
    oc.wait_recv()
    x_cross = [wires.make(img_ref.at[i], xb.at[0, i], cross) for i in range(images)]
    o_cross = [wires.make(o_own, my_out.at[y, x, 1 - h], cross), wires.make(o_core, my_out.at[y, x, h], cross)]

    @pl.when(apart)
    def _():
        for cp in o_cross:
            cp.start()

    @pl.when(jnp.logical_and(apart, jnp.logical_not(inner)))
    def _():
        x_cross[0].start()

    def arrive(pair):
        @pl.when(inner)
        def _():
            pair[0].wait_recv()
            pair[1].start()

        @pl.when(jnp.logical_not(inner))
        def _():
            pair[1].wait_recv()

    arrive(az)
    a1 = spread(in_a, 1, "x")
    arrive(bz)
    b1 = spread(in_b, 1, "y")
    for cp in v:
        cp.wait_recv()
    v = vec_send(3)

    @pl.when(jnp.logical_and(apart, inner))
    def _():
        x_cross[0].start()

    @pl.when(apart)
    def _():
        for cp in x_cross[1:]:
            cp.start()

    @pl.when(jnp.logical_not(apart))
    def _():
        my_out[y, x, h] = o_own[...]
        my_out[y, x, 1 - h] = o_core[...]
        local_images.wait()

    @pl.when(apart)
    def _():
        for cp in o_cross:
            cp.wait_recv()

    oa = spread(out_a, 0, "x")
    ob = spread(out_b, 0, "y")
    forward(in_a, 1, "x", a1)
    forward(in_b, 1, "y", b1)
    forward(out_a, 0, "x", oa)
    forward(out_b, 0, "y", ob)
    fa0 = spread(ff_a, 0, "x")
    fb0 = spread(ff_b, 0, "y")
    for got in (a0, b0, a1, b1):
        settle(got)
    for cp in v:
        cp.wait_recv()

    def row(start, count):
        per = vec_ref.shape[1]
        pieces, at = [], start
        while at < start + count:
            s, r = at // per, at % per
            n = min(per - r, start + count - at)
            xs = s // 2
            pieces.append(vfull[xs // (nx * ny), xs // nx % ny, xs % nx, s % 2][:, r:r + n])
            at += n
        return pieces[0] if len(pieces) == 1 else jnp.concatenate(pieces, axis=1)

    gain, shift_row = row(0, feat), row(feat, feat)
    q_row, v_row = row(2 * feat, feat), row(3 * feat, feat)
    q_row = jnp.where(c == 0, q_row[:, :part], q_row[:, part:])
    v_row = jnp.where(c == 0, v_row[:, :part], v_row[:, part:])
    bias = jnp.concatenate([q_row, jnp.zeros((1, part), F32), v_row], axis=1)

    def project(i, s):
        value = wide_rows(buf, xb[s, i])
        normed = (norm_parts(value)[0] * gain + shift_row).astype(BF)
        h1_ref[i, s] = normed
        qkv_ref[i, s] = (dot(normed, w[...]) + bias).astype(BF)

    near = jnp.where(apart, 1, 0)

    @pl.when(apart)
    def _():
        xl.wait_recv()

    def near_step(i, carry):
        project(i, near)
        return carry

    lax.fori_loop(0, images, near_step, 0)

    forward(ff_a, 0, "x", fa0)
    forward(ff_b, 0, "y", fb0)
    near_ff = [wires.make(tmp.at[ab], near_ref.at[ab], to_near) for ab in range(2)]
    x_core = [wires.make(xb.at[0, i], xb.at[1, i], to_core) for i in range(images)]
    for i in range(images):
        @pl.when(apart)
        def _():
            x_cross[i].wait_recv()
            x_core[i].start()

        @pl.when(jnp.logical_not(apart))
        def _():
            x_core[i].wait_recv()

        if i == images - 1:
            @pl.when(inner)
            def _():
                for cp in near_ff:
                    cp.start()

        project(i, 1 - near)
        if i == 0:
            settle(oa)
            settle(ob)
            other = wires.send(my_out, other_out, to_core)
    other.wait_recv()
    settle(fa0)
    settle(fb0)

    @pl.when(apart)
    def _():
        for cp in x_cross + o_cross + x_core:
            cp.wait_send()

    @pl.when(jnp.logical_not(apart))
    def _():
        xl.wait_send()

    @pl.when(inner)
    def _():
        for cp in near_ff:
            cp.wait_recv()
        for cp in (*az, *bz, *near_ff):
            cp.wait_send()

    for cp in keep:
        cp.wait()
    wires.finish()


def head_stage(in_w, out_w, up_w, down_w, vec, images, padded, ny, nx):
    n, half, feat = images.shape
    rows, rows_out, rows_ff = in_w.shape[0], out_w.shape[0], up_w.shape[0]
    width = in_w.shape[1] // 2
    hid = rows_ff // 2
    many = 60 + 24 * ny * nx
    S = jax.ShapeDtypeStruct
    return pl.pallas_call(
        functools.partial(head_kernel, ny, nx),
        in_specs=[VM] * 5 + [ANY],
        out_specs=[VM] * 6 + [ANY] * 3 + [VM],
        out_shape=[
            S((n, 2, padded, feat), BF), S((n, 2, padded, width), BF), S((2, n, half, feat), BF), S((feat, width), BF),
            S((ny, nx, 2, rows_out, feat), BF), S((ny, nx, 2, rows_out, feat), BF),
            S((ny, nx, 2, hid, feat), BF), S((ny, nx, 2, hid, feat), BF), S((2, 2, hid, feat), BF),
            S((2, ny, nx, 2, 1, vec.shape[1]), F32),
        ],
        scratch_shapes=[
            pltpu.VMEM((rows, width), BF), pltpu.VMEM((rows_out, feat), BF), pltpu.VMEM((rows_out, feat), BF),
            pltpu.VMEM((2, 2, hid, feat), BF), pltpu.VMEM((padded, feat), F32),
            pltpu.SemaphoreType.DMA(()), pltpu.SemaphoreType.DMA((3,)),
            pltpu.SemaphoreType.DMA((many,)), pltpu.SemaphoreType.DMA((many,)),
        ],
        name="head_stage",
        compiler_params=pltpu.CompilerParams(collective_id=2, has_side_effects=True, vmem_limit_bytes=60 << 20),
        cost_estimate=pl.CostEstimate(flops=n * 4 * padded * feat * width, bytes_accessed=40 << 20, transcendentals=0),
    )(in_w, out_w, up_w, down_w, vec, images)


def mid_kernel(ny, nx, *refs):
    (qkv_ref, kf_ref, xb, wo_ref, wt_ref, vec_ref, near_ref, grad_ref,
     mix_ref, lse_ref, x2_ref, h2_ref, g_ref, fa, fb,
     mix_oth, land, buf, csem, send_sem, recv_sem) = refs
    h, y, x, c, l = (lax.axis_index(a) for a in AXES)
    images, rows, width = mix_ref.shape
    padded = rows // 2
    pairs = width // 128
    apart, inner = h != c, l != h
    cross = {"seq": 1 - h, "core": 1 - c}
    to_core, to_dp = {"core": 1 - c}, {"dp": 1 - l}
    to_x = [{"x": lax.rem(x + nx - k, nx)} for k in range(nx)]
    to_y = [{"y": lax.rem(y + ny - k, ny)} for k in range(ny)]
    wires = Wires(send_sem, recv_sem)
    spread, forward, settle = plane_moves(wires, to_x, to_y)
    barrier = pltpu.get_barrier_semaphore()
    peers = [to_core, to_dp] + to_x[1:] + to_y[1:]
    for peer in peers:
        pl.semaphore_signal(barrier, inc=1, device_id=peer, device_id_type=MESH_ID)

    @pl.when(apart)
    def _():
        pl.semaphore_signal(barrier, inc=1, device_id=cross, device_id_type=MESH_ID)

    pl.semaphore_wait(barrier, len(peers) + jnp.where(apart, 1, 0))
    here_ff = [pltpu.make_async_copy(near_ref.at[ab], land.at[ab], csem.at[3 + ab]) for ab in range(2)]
    far_ff = [wires.make(near_ref.at[ab], land.at[ab], to_dp) for ab in range(2)]
    local_grad = pltpu.make_async_copy(grad_ref, g_ref.at[0], csem.at[0])
    grad_core = wires.make(grad_ref, g_ref.at[1], to_core)
    g_cross = [wires.make(grad_ref.at[i], g_ref.at[0, i], cross) for i in range(images)]
    g_core = [wires.make(g_ref.at[0, i], g_ref.at[1, i], to_core) for i in range(images)]

    @pl.when(inner)
    def _():
        for cp in far_ff + here_ff:
            cp.start()

    @pl.when(jnp.logical_not(apart))
    def _():
        local_grad.start()
        grad_core.start()

    def arrive(ab):
        @pl.when(inner)
        def _():
            here_ff[ab].wait()

        @pl.when(jnp.logical_not(inner))
        def _():
            far_ff[ab].wait_recv()

        return spread(ff[ab], 1, order[ab])

    ff = [by_offset(fa, land.at[0]), by_offset(fb, land.at[1])]
    order = ("x", "y")
    gots = []

    @pl.when(apart)
    def _():
        for cp in g_cross:
            cp.start()

    mix_got = []
    for i in range(images):
        def pair(p, carry):
            at = [pl.ds(pl.multiple_of((t * pairs + p) * 128, 128), 128) for t in range(3)]
            mixed, sums = attend_pair(qkv_ref[i, :, at[0]], qkv_ref[i, :, at[1]], qkv_ref[i, :, at[2]], kf_ref[i])
            mix_ref[i, :, at[0]] = mixed
            for j in range(2):
                lse_ref[i, p, j:j + 1, :] = sums[j]
            return carry

        lax.fori_loop(0, pairs, pair, 0)
        mix_got.append(wires.send(mix_ref.at[i], mix_oth.at[i], to_core))
        if i == max(images - 2, 0):
            gots.append(arrive(0))
        if i == images - 1:
            gots.append(arrive(1))

    def middle(i):
        mix_got[i].wait_recv()
        for s in range(2):
            own = slice(s * padded, (s + 1) * padded)
            oth = slice((1 - s) * padded, (2 - s) * padded)
            v = wide_rows(buf, xb[s, i])
            v = v + (dot(mix_ref[i, own, :], wo_ref[...]) + dot(mix_oth[i, oth, :], wt_ref[...])) + vec_ref[0:1, :]
            x2_ref[i, s] = v
            h2_ref[i, s] = (norm_parts(v)[0] * vec_ref[1:2, :] + vec_ref[2:3, :]).astype(BF)

    for i in range(images):
        middle(i)
        if i == 0:
            forward(ff[0], 1, order[0], gots[0])
    keep = [pltpu.make_async_copy(land.at[ab], (fa, fb)[ab].at[0, 0], csem.at[1 + ab]) for ab in range(2)]
    for cp in keep:
        cp.start()
    forward(ff[1], 1, order[1], gots[1])
    for i in range(images):
        @pl.when(apart)
        def _():
            g_cross[i].wait_recv()
            g_core[i].start()

        @pl.when(jnp.logical_not(apart))
        def _():
            g_core[i].wait_recv()

    @pl.when(apart)
    def _():
        grad_core.wait_recv()
        for cp in g_cross + g_core:
            cp.wait_send()

    @pl.when(jnp.logical_not(apart))
    def _():
        local_grad.wait()
        grad_core.wait_send()

    @pl.when(inner)
    def _():
        for cp in far_ff:
            cp.wait_send()

    for got in gots:
        settle(got)
    for cp in keep:
        cp.wait()
    wires.finish()


def mid_stage(qkv, key_fill, x_both, w_own, w_oth, vec, low_ff, out_grad, ny, nx):
    n, rows, w3 = qkv.shape
    width, feat = w_own.shape
    half = out_grad.shape[1]
    _, ud, hid, _ = low_ff.shape
    many = 40 + 4 * ny * nx
    S = jax.ShapeDtypeStruct
    return pl.pallas_call(
        functools.partial(mid_kernel, ny, nx),
        in_specs=[VM] * 6 + [ANY] * 2,
        out_specs=[VM] * 5 + [ANY] * 2,
        out_shape=[
            S((n, rows, width), BF), S((n, width // 128, 8, rows), F32), S((n, 2, rows // 2, feat), F32),
            S((n, 2, rows // 2, feat), BF), S((2, n, half, feat), BF),
            S((ny, nx, ud, hid, feat), BF), S((ny, nx, ud, hid, feat), BF),
        ],
        scratch_shapes=[
            pltpu.VMEM((n, rows, width), BF), pltpu.VMEM((2, ud, hid, feat), BF), pltpu.VMEM((rows // 2, feat), F32),
            pltpu.SemaphoreType.DMA((5,)), pltpu.SemaphoreType.DMA((many,)), pltpu.SemaphoreType.DMA((many,)),
        ],
        name="mid_stage",
        compiler_params=pltpu.CompilerParams(collective_id=5, has_side_effects=True, vmem_limit_bytes=60 << 20),
        cost_estimate=pl.CostEstimate(flops=n * 4 * rows * rows * w3, bytes_accessed=50 << 20, transcendentals=n * 8 * rows * rows),
    )(qkv, key_fill, x_both, w_own, w_oth, vec, low_ff, out_grad)


def shift(value, axis, up):
    n = lax.axis_size(axis)
    return lax.ppermute(value, axis, [(i, (i + up) % n) for i in range(n)])


def after(value, *others):
    return lax.optimization_barrier((value, others))[0]


def crossing(value):
    return lax.ppermute(value, ("seq", "core"), [(1, 2), (2, 1)])


def pick(own, received):
    return jnp.where(lax.axis_index("seq") == lax.axis_index("core"), own, received)


def crossed(value):
    return pick(value, crossing(value))


def adam_update(master, first_moment, second_moment, gradient, step_rate, bias_one, bias_two):
    first_new = 0.5 * first_moment + 0.5 * gradient
    second_new = 0.5 * second_moment + 0.5 * gradient * gradient
    update = first_new / bias_one / (jnp.sqrt(second_new / bias_two) + ADAM_EPS)
    master_new = master - step_rate * (update + WEIGHT_DECAY * master)
    return (master_new, first_new, second_new)


def on_device(images, key_mask, out_grad, step_count, *params):
    masters, firsts, seconds = params[0:5], params[5:10], params[10:15]
    in_weights, out_weights, up_weights, down_weights, vectors = masters
    image_count, half, features = images.shape
    padded = -(-half // PAD_ROWS) * PAD_ROWS
    h, c = lax.axis_index("seq"), lax.axis_index("core")
    y, x = lax.axis_index("y"), lax.axis_index("x")
    ny, nx = lax.axis_size("y"), lax.axis_size("x")
    shards = 4 * ny * nx
    shard = ((h * ny + y) * nx + x) * 2 + c

    h1, qkv, x_both, full_in, my_out, other_out, own_a, own_b, low_ff, full_vec = head_stage(
        in_weights, out_weights, up_weights, down_weights, vectors[None], images, padded, ny, nx
    )
    my_out, other_out = my_out.reshape(HALF_D, D), other_out.reshape(HALF_D, D)
    rows_in, rows_out, rows_ff = in_weights.shape[0], out_weights.shape[0], up_weights.shape[0]
    half_ff = rows_ff // 2
    keys = [(ky, kx) for ky in range(ny) for kx in range(nx)]
    full_vec = full_vec.reshape(-1)
    gain_one, shift_one, query_bias, value_bias, out_bias, gain_two, shift_two, down_bias = (
        full_vec[i * D : (i + 1) * D] for i in range(8)
    )
    up_bias = full_vec[8 * D :]

    mask = key_mask.astype(F32)
    mask = jnp.where(h == c, mask, shift(mask, "core", 1)).reshape(image_count, 2, half)
    mask = jnp.where(c == 0, mask, mask[:, ::-1])
    mask = jnp.pad(mask, ((0, 0), (0, 0), (0, padded - half))).reshape(image_count, 2 * padded)
    key_fill = jnp.broadcast_to(jnp.where(mask > 0, 0.0, NEG_FILL)[..., None], mask.shape + (128,)).astype(BF)

    tokens = image_count * 2 * padded
    qkv = qkv.reshape(image_count, 2 * padded, 3 * HALF_D)
    mid_vec = jnp.pad(jnp.stack([out_bias, gain_two, shift_two]), ((0, 5), (0, 0)))
    mixed, lse, x2, h2, g_both, oth_a, oth_b = mid_stage(
        qkv, key_fill, x_both, my_out, other_out, mid_vec, low_ff, out_grad, ny, nx
    )
    halved = mixed.reshape(image_count, 2, padded, HALF_D)

    grad_a, grad_b, (y_own, y_oth, dh2, g_bu, first_a, first_b) = mlp(
        ny, nx, h2.reshape(tokens, D), g_both, up_bias.reshape(shards * 2, half_ff), own_a, own_b, oth_a, oth_b
    )
    result = y_own[:, :half] + shift(y_oth, "core", 1)[:, :half].astype(F32) + x2[:, 0, :half] + down_bias
    result = result.astype(BF)
    result_got = crossing(result)

    def second_stage(grads, firsts, swap):
        sums = []
        for k in range(firsts.shape[1]):
            sums.append(add_all(grads[(k, 0) if swap else (0, k)], *firsts[:, k]).astype(BF))
        return sums

    sums_a, sums_b = second_stage(grad_a, first_a, False), second_stage(grad_b, first_b, True)
    got_a = [lax.ppermute(s, "x", [(i, (i + k) % nx) for i in range(nx)]) for k, s in enumerate(sums_a) if k]
    got_b = [lax.ppermute(s, "y", [(i, (i + k) % ny) for i in range(ny)]) for k, s in enumerate(sums_b) if k]

    dh2 = dh2.reshape(image_count, 2, padded, D)
    dh2_oth = shift(dh2, "core", 1)
    dx2, dattn, g_out, sums_two = middle_back(x2, dh2, dh2_oth, g_both, halved, my_out, gain_two)
    dqkv, sums_qkv = attend_back(qkv, key_fill, mixed, dattn.reshape(mixed.shape), lse)
    got_a, got_b = after(got_a, dqkv), after(got_b, dqkv)
    plane_a, plane_b = add_all(sums_a[0], *got_a).astype(BF), add_all(sums_b[0], *got_b).astype(BF)
    l = lax.axis_index("dp")
    half_keep, half_give = jnp.where(l == 0, plane_a, plane_b), jnp.where(l == 0, plane_b, plane_a)

    zero = jnp.zeros((D,), F32)
    vec = jnp.concatenate(
        [
            zero,
            zero,
            lax.dynamic_update_slice(zero, sums_qkv[0, :HALF_D], (c * HALF_D,)),
            lax.dynamic_update_slice(zero, sums_qkv[0, 2 * HALF_D :], (c * HALF_D,)),
            sums_two[2],
            sums_two[0],
            sums_two[1],
            sums_two[3],
            g_bu.reshape(-1),
        ]
    ).reshape(-1, 128)
    in_mine, in_theirs, share_out, share_ff, input_grad, vec, norm = tail_stage(
        h1.reshape(tokens, D),
        dqkv.reshape(tokens, 3 * HALF_D),
        g_out.reshape(ny, nx, 2, rows_out, D),
        x_both,
        dx2,
        gain_one,
        vec,
        full_in,
        half_keep,
        half_give,
        ny,
        nx,
    )
    activations = pick(result, after(result_got, norm)).astype(F32)
    input_grad = input_grad.astype(F32)
    share_vec = lax.dynamic_slice(vec.reshape(shards, -1), (shard, 0), (1, vec.size // shards)).reshape(-1)
    in_mine, in_theirs = (s.reshape(rows_in, 3, 1, HALF_D) for s in (in_mine, in_theirs))
    share_in = jnp.where(
        c == 0, jnp.concatenate([in_mine, in_theirs], 2), jnp.concatenate([in_theirs, in_mine], 2)
    ).reshape(rows_in, 3 * D)
    share_up, share_down = (share_ff[:, i].reshape(rows_ff, D) for i in range(2))
    shares = tuple(s.astype(F32) for s in (share_in, share_out, share_up, share_down, share_vec))
    grad_norm = norm[0, 0]
    threshold = 0.5 * math.sqrt(4 * D * D + 2 * D * FF + 12 * D)
    clip_factor = jnp.minimum(1.0, threshold / grad_norm)
    bias = 1.0 - jnp.power(F32(0.5), step_count.astype(F32))
    rates = ((D // 2) ** (-0.5), (D // 4) ** (-0.5), D ** (-0.5), FF ** (-0.5), 0.2)
    results = [
        adam_update(masters[i], firsts[i], seconds[i], shares[i] * clip_factor, rates[i], bias, bias) for i in range(5)
    ]
    return (
        grad_norm,
        *(r[0] for r in results),
        *(r[1] for r in results),
        *(r[2] for r in results),
        *(r[0].astype(BF) for r in results),
        activations,
        input_grad,
    )


def solution(mesh):
    seq_n, fsdp_n, dp_n = (mesh.shape[a] for a in ("seq", "fsdp", "dp"))
    nx = math.isqrt(fsdp_n // 2)
    ny = fsdp_n // 2 // nx
    grid = Mesh(np.asarray(mesh.devices).reshape(seq_n, ny, nx, 2, dp_n), AXES)
    tokens = P(("y", "x", "core", "dp"), "seq", None)
    matrix, vector = P(SHARD, None), P(SHARD)
    five = (matrix, matrix, matrix, matrix, vector)
    return jax.shard_map(
        on_device,
        mesh=grid,
        in_specs=(tokens, P(("y", "x", "core", "dp"), None), tokens, P()) + five * 3,
        out_specs=(P(),) + five * 4 + (tokens, tokens),
        check_vma=False,
    )
```

```python
import functools
import math

import jax
import jax.numpy as jnp
import numpy as np
from jax import lax
from jax.experimental import pallas as pl
from jax.experimental.pallas import tpu as pltpu
from jax.sharding import Mesh
from jax.sharding import PartitionSpec as P

D = 1024
FF = 4096
PAD_ROWS = 16

NEG_FILL = -1000000000.0
ADAM_EPS = 1e-08
WEIGHT_DECAY = 0.05
AXES = ("seq", "y", "x", "core", "dp")
SHARD = ("seq", "y", "x", "core")

BF = jnp.bfloat16
F32 = jnp.float32
MESH_ID = pl.DeviceIdType.MESH


class Wires:
    def __init__(self, send_sem, recv_sem):
        self.send_sem, self.recv_sem, self.count, self.sent = send_sem, recv_sem, 0, []

    def make(self, src, dst, to):
        cp = pltpu.make_async_remote_copy(
            src_ref=src, dst_ref=dst, send_sem=self.send_sem.at[self.count], recv_sem=self.recv_sem.at[self.count],
            device_id=to, device_id_type=MESH_ID)
        self.count += 1
        return cp

    def send(self, src, dst, to):
        cp = self.make(src, dst, to)
        cp.start()
        self.sent.append(cp)
        return cp

    def finish(self):
        for cp in self.sent:
            cp.wait_send()


def greet(peers, crossing_peer, apart):
    barrier = pltpu.get_barrier_semaphore()
    for peer in peers:
        pl.semaphore_signal(barrier, inc=1, device_id=peer, device_id_type=MESH_ID)

    @pl.when(apart)
    def _():
        pl.semaphore_signal(barrier, inc=1, device_id=crossing_peer, device_id_type=MESH_ID)

    pl.semaphore_wait(barrier, len(peers) + jnp.where(apart, 1, 0))


def add_all(first, *others):
    total = first.astype(F32)
    for other in others:
        total = total + other.astype(F32)
    return total


def plane_moves(wires, to_x, to_y):
    nx, ny = len(to_x), len(to_y)

    def spread(piece_at, kz, first):
        got = {}
        for k in range(1, nx):
            got[0, k] = wires.send(piece_at(kz, 0, 0), piece_at(kz, 0, 0, k, "x"), to_x[k])
        for k in range(1, ny):
            got[k, 0] = wires.send(piece_at(kz, 0, 0), piece_at(kz, 0, 0, k, "y"), to_y[k])
        return got

    def forward(piece_at, kz, first, got):
        if first == "x":
            for kx in range(1, nx):
                got[0, kx].wait_recv()
                for ky in range(1, ny):
                    got[ky, kx] = wires.send(piece_at(kz, 0, kx), piece_at(kz, 0, kx, ky, "y"), to_y[ky])
            for ky in range(1, ny):
                got[ky, 0].wait_recv()
        else:
            for ky in range(1, ny):
                got[ky, 0].wait_recv()
                for kx in range(1, nx):
                    got[ky, kx] = wires.send(piece_at(kz, ky, 0), piece_at(kz, ky, 0, kx, "x"), to_x[kx])
            for kx in range(1, nx):
                got[0, kx].wait_recv()

    def settle(got):
        for (ky, kx), cp in got.items():
            if ky > 0 and kx > 0:
                cp.wait_recv()

    return spread, forward, settle


def by_offset(store, own):
    def piece_at(kz, ky, kx, k=0, axis=""):
        if k == 0 and ky == 0 and kx == 0:
            return own
        return store.at[ky + (k if axis == "y" else 0), kx + (k if axis == "x" else 0)]

    return piece_at

BF=jnp.bfloat16; F32=jnp.float32
def dot(a, b, dims=(((1,), (0,)), ((), ()))):
    return lax.dot_general(a, b, dims, preferred_element_type=F32)
NT=(((1,),(1,)),((),()))
TN=(((0,),(0,)),((),()))
ANY=pl.BlockSpec(memory_space=pl.ANY)
VM=pl.BlockSpec(memory_space=pltpu.VMEM)
SM=pl.BlockSpec(memory_space=pltpu.SMEM)

def gelu_both(u):
    c0=math.sqrt(2/math.pi)
    sq=u*u
    t=jnp.tanh(u*(c0+(c0*0.044715)*sq))
    half=0.5+0.5*t
    value=u*half
    slope=half+(0.5*u)*(1.0-t*t)*(c0+(3*c0*0.044715)*sq)
    return value,slope

def mlp_kernel(keys,keys_b,ny,nx,*refs,gtile):
    nk=len(keys)
    h2_ref,g_ref,bu_ref=refs[:3]
    planes=(refs[3:5],refs[5:7])
    o=7
    order=(keys,keys_b)
    ga,gb=refs[o:o+nk],refs[o+nk:o+2*nk]
    yown_ref,yoth_ref,dh_ref,gbu_ref,ra_ref,rb_ref=refs[o+2*nk:o+2*nk+6]
    w,dd,a_all,du_all,y_acc,dh_acc,g_out,wsem,gsem,send_sem,recv_sem=refs[o+2*nk+6:]
    h,y,x,c,_=(lax.axis_index(a) for a in AXES)
    to_x=[{"x":lax.rem(x+k,nx)} for k in range(nx)]
    to_y=[{"y":lax.rem(y+k,ny)} for k in range(ny)]
    wires=Wires(send_sem,recv_sem)
    moves=[]
    for ki,((ky,_),(_,kx)) in enumerate(zip(keys,keys_b)):
        cps=[]
        if ky>0: cps.append(wires.make(ga[ki],ra_ref.at[ky-1,keys[ki][1]],to_y[ky]))
        ky=keys_b[ki][0]
        if kx>0: cps.append(wires.make(gb[ki],rb_ref.at[kx-1,ky],to_x[kx]))
        moves.append(cps)
    barrier=pltpu.get_barrier_semaphore()
    for peer in to_x[1:]+to_y[1:]:
        pl.semaphore_signal(barrier,inc=1,device_id=peer,device_id_type=MESH_ID)
    _,images,half,feat=g_ref.shape
    hid=planes[0][0].shape[3]
    width=4*hid
    padded=h2_ref.shape[0]//(2*images)
    blocks=2*images

    def load(i,slot,go):
        for ki in range(nk):
            @pl.when(i==ki)
            def _():
                for kz in range(2):
                    for ud in range(2):
                        for ab in range(2):
                            cp=pltpu.make_async_copy(planes[kz][ab].at[order[ab][ki][0],order[ab][ki][1],ud],w.at[slot,ud,pl.ds((kz*2+ab)*hid,hid)],wsem.at[slot,kz*4+ud*2+ab])
                            cp.start() if go else cp.wait()
    def save(i,go):
        for ki in range(nk):
            @pl.when(i==ki)
            def _():
                for kz in range(2):
                    for ud in range(2):
                        for ab,dst in enumerate((ga[ki],gb[ki])):
                            cp=pltpu.make_async_copy(g_out.at[ud,pl.ds((kz*2+ab)*hid,hid)],dst.at[kz,ud],gsem.at[kz*4+ud*2+ab])
                            cp.start() if go else cp.wait()
    load(0,0,True)
    gbu_ref[...]=jnp.zeros_like(gbu_ref)
    for i in range(images):
        for s in range(2):
            r=(2*i+s)*padded
            tail=padded-16
            dd[r+tail:r+padded,:]=jnp.zeros((16,feat),BF)
            dd[r:r+half,:]=g_ref[s,i]
    pl.semaphore_wait(barrier,nx+ny-2)
    def step(i,_):
        slot=lax.rem(i,2)
        @pl.when(i>0)
        def _(): save(i-1,False)
        for ki,cps in enumerate(moves):
            if cps:
                @pl.when(i==ki+1)
                def _():
                    for cp in cps: cp.start()
        load(i,slot,False)
        @pl.when(i+1<nk)
        def _(): load(i+1,1-slot,True)
        rows=[]
        for kz in range(2):
            for ab in range(2):
                row=jnp.int32(0)
                for ki,(ky,kx) in enumerate(order[ab]):
                    here=(((lax.rem(h+kz,2)*ny+lax.rem(y+ky,ny))*nx+lax.rem(x+kx,nx))*2+c)*2+ab
                    row=jnp.where(i==ki,here,row)
                rows.append(row)
        bias=jnp.concatenate([bu_ref[pl.ds(r,1),:] for r in rows],axis=1)
        wu=w.at[slot,0]; wd=w.at[slot,1]
        def tokens(b,sums):
            r=pl.ds(pl.multiple_of(b*padded,16),padded)
            u=dot(h2_ref[r,:],wu[...],NT)+bias
            value,slope=gelu_both(u)
            a=value.astype(BF)
            a_all[r,:]=a
            dg=dot(dd[r,:],wd[...],NT)
            du=(dg*slope).astype(BF)
            du_all[r,:]=du
            ynew=dot(a,wd[...]); dnew=dot(du,wu[...])
            @pl.when(i==0)
            def _():
                y_acc[r,:]=ynew; dh_acc[r,:]=dnew
            @pl.when(i>0)
            def _():
                y_acc[r,:]+=ynew; dh_acc[r,:]+=dnew
            return sums+jnp.sum(du.astype(F32),axis=0,keepdims=True)
        sums=lax.fori_loop(0,blocks,tokens,jnp.zeros((1,width),F32))
        for q,row in enumerate(rows):
            gbu_ref[pl.ds(row,1),:]=sums[:,q*hid:(q+1)*hid]
        for t in range(0,width,gtile):
            g_out[1,t:t+gtile,:]=dot(a_all[:,t:t+gtile],dd[...],TN).astype(BF)
            g_out[0,t:t+gtile,:]=dot(du_all[:,t:t+gtile],h2_ref[...],TN).astype(BF)
        save(i,True)
        return 0
    lax.fori_loop(0,nk,step,0)
    for i in range(images):
        r=2*i*padded
        yown_ref[i]=y_acc[r:r+padded,:]
        yoth_ref[i]=y_acc[r+padded:r+2*padded,:].astype(BF)
    dh_ref[...]=dh_acc[...].astype(BF)
    save(nk-1,False)
    for cps in moves:
        for cp in cps:
            cp.wait_recv()
            cp.wait_send()

def mlp(ny,nx,h2,g_both,bu_rows,own_a,own_b,oth_a,oth_b,gtile=256):
    keys=sorted(((ky,kx) for ky in range(ny) for kx in range(nx)),reverse=True); nk=len(keys)
    _,images,half,feat=g_both.shape
    keys_b=sorted(keys,key=lambda k:(k[1],k[0]),reverse=True)
    tokens=h2.shape[0]; padded=tokens//(2*images)
    ud,hid=own_a.shape[2:4]
    width=4*hid
    piece=jax.ShapeDtypeStruct((2,ud,hid,feat),BF)
    out=pl.pallas_call(functools.partial(mlp_kernel,keys,keys_b,ny,nx,gtile=min(gtile,width)),
        in_specs=[VM]*3+[ANY]*4,
        out_specs=[ANY]*(2*nk)+[VM]*4+[ANY]*2,
        out_shape=[piece]*(2*nk)+[jax.ShapeDtypeStruct((images,padded,feat),F32),jax.ShapeDtypeStruct((images,padded,feat),BF),
            jax.ShapeDtypeStruct((tokens,feat),BF),jax.ShapeDtypeStruct(bu_rows.shape,F32),
            jax.ShapeDtypeStruct((ny-1,nx,2,ud,hid,feat),BF),jax.ShapeDtypeStruct((nx-1,ny,2,ud,hid,feat),BF)],
        scratch_shapes=[pltpu.VMEM((2,2,width,feat),BF),pltpu.VMEM((tokens,feat),BF),pltpu.VMEM((tokens,width),BF),pltpu.VMEM((tokens,width),BF),
            pltpu.VMEM((tokens,feat),F32),pltpu.VMEM((tokens,feat),F32),pltpu.VMEM((2,width,feat),BF),
            pltpu.SemaphoreType.DMA((2,8)),pltpu.SemaphoreType.DMA((8,)),pltpu.SemaphoreType.DMA((2*nk,)),pltpu.SemaphoreType.DMA((2*nk,))],
        name="feed_forward",
        compiler_params=pltpu.CompilerParams(collective_id=3,has_side_effects=True,vmem_limit_bytes=60<<20),
        cost_estimate=pl.CostEstimate(flops=nk*6*2*tokens*feat*width,bytes_accessed=40<<20,transcendentals=nk*tokens*width),
    )(h2,g_both,bu_rows,own_a,own_b,oth_a,oth_b)
    return dict(zip(keys,out[:nk])),dict(zip(keys_b,out[nk:2*nk])),out[2*nk:]

HD=64; HALF_D=512

def head_operands(q,k,kb,scale):
    q=q.astype(F32)*scale; k=k.astype(F32); kb=kb.astype(F32)
    lane=lax.broadcasted_iota(jnp.int32,q.shape,1)
    low=lane<HD
    one=jnp.where((lane==0)|(lane==HD),1.0,0.0)
    qs=[jnp.where(low,q,one).astype(BF),jnp.where(low,one,q).astype(BF)]
    ks=[jnp.where(low,k,kb).astype(BF),jnp.where(low,kb,k).astype(BF)]
    return q,k,low,qs,ks

def attend_pair(q,k,v,kb):
    q,k,low,qs,ks=head_operands(q,k,kb,HD**-0.5)
    vt=v.astype(F32).T.astype(BF)
    outs=[]; sums=[]
    for j in range(2):
        s=dot(ks[j],qs[j],NT)
        m=jnp.max(s,axis=0,keepdims=True)
        e=jnp.exp(s-m)
        l=jnp.sum(e,axis=0,keepdims=True)
        o=dot(vt[j*HD:(j+1)*HD],e.astype(BF))
        outs.append(o*(1.0/l))
        sums.append(m+jnp.log(l))
    return jnp.concatenate(outs,axis=0).T.astype(BF),sums

def attend_back_kernel(q_ref,k_ref,v_ref,kb_ref,o_ref,g_ref,lse_ref,out_ref,sum_ref,*,pairs,chunk):
    p=pl.program_id(1)
    @pl.when((pl.program_id(0)==0)&(p==0))
    def _(): sum_ref[...]=jnp.zeros_like(sum_ref)
    scale=HD**-0.5
    q,k,low,qs,ks=head_operands(q_ref[0],k_ref[0],kb_ref[0],scale)
    qb=q.astype(BF)
    kt=k.T.astype(BF)
    g=g_ref[0]; gf=g.astype(F32)
    prod=(gf*o_ref[0].astype(F32)).T
    v=v_ref[0]
    rows=q.shape[0]
    dqs=[];dks=[];dvs=[]
    for j in range(2):
        gj=(jnp.where(low,gf,0.0) if j==0 else jnp.where(low,0.0,gf)).astype(BF)
        delta=jnp.sum(prod[j*HD:(j+1)*HD],axis=0,keepdims=True)
        lse=lse_ref[0,0,j:j+1,:]
        dq=None; dk=[]; dv=[]
        for r in range(0,rows,chunk):
            s=dot(ks[j][r:r+chunk],qs[j],NT)
            pr=jnp.exp(s-lse)
            dp=dot(v[r:r+chunk],gj,NT)
            ds=(pr*(dp-delta)).astype(BF)
            dv.append(dot(pr.astype(BF),g))
            dk.append(dot(ds,qb))
            t=dot(kt[j*HD:(j+1)*HD,r:r+chunk],ds) if chunk==rows else dot(k[r:r+chunk].astype(BF),ds,TN)[j*HD:(j+1)*HD]
            dq=t if dq is None else dq+t
        dqs.append(dq)
        dks.append(jnp.concatenate(dk,axis=0) if len(dk)>1 else dk[0]); dvs.append(jnp.concatenate(dv,axis=0) if len(dv)>1 else dv[0])
    parts=((jnp.concatenate(dqs,axis=0)*scale).T.astype(BF),jnp.where(low,dks[0],dks[1]).astype(BF),jnp.where(low,dvs[0],dvs[1]).astype(BF))
    for t,part in enumerate(parts):
        at=pl.ds(pl.multiple_of((t*pairs+p)*128,128),128)
        out_ref[0,:,at]=part
        sum_ref[0:1,at]+=jnp.sum(part.astype(F32),axis=0,keepdims=True)

def attend_back(qkv,kbias,mixed,grad,lse,chunk=None):
    n,rows,w=qkv.shape; pairs=w//3//128
    chunk=chunk or rows
    blk=lambda off: pl.BlockSpec((1,rows,128),lambda i,p: (i,0,off+p))
    return pl.pallas_call(functools.partial(attend_back_kernel,pairs=pairs,chunk=chunk),grid=(n,pairs),
        in_specs=[blk(0),blk(pairs),blk(2*pairs),pl.BlockSpec((1,rows,128),lambda i,p:(i,0,0)),blk(0),blk(0),pl.BlockSpec((1,1,8,rows),lambda i,p:(i,p,0,0))],
        out_specs=[pl.BlockSpec((1,rows,w),lambda i,p:(i,0,0)),pl.BlockSpec((8,w),lambda i,p:(0,0))],
        out_shape=[jax.ShapeDtypeStruct((n,rows,w),BF),jax.ShapeDtypeStruct((8,w),F32)],
        name="attend_back",
        compiler_params=pltpu.CompilerParams(vmem_limit_bytes=50<<20),
        cost_estimate=pl.CostEstimate(flops=n*pairs*20*rows*rows*128,bytes_accessed=n*rows*w*5,transcendentals=n*pairs*2*rows*rows),
    )(qkv,qkv,qkv,kbias,mixed,grad,lse)

NORM_EPS=1e-6
def norm_parts(values):
    center = values - jnp.mean(values, axis=-1, keepdims=True)
    inverse = lax.rsqrt(jnp.mean(center * center, axis=-1, keepdims=True) + NORM_EPS)
    return center * inverse, inverse

def norm_back(values, gain, grad):
    normed, inverse = norm_parts(values)
    scaled = grad * gain
    mean_one = jnp.mean(scaled, axis=-1, keepdims=True)
    mean_two = jnp.mean(scaled * normed, axis=-1, keepdims=True)
    return (scaled - mean_one - normed * mean_two) * inverse, grad * normed

def wide_rows(buf,block):
    n=block.shape[0]; total=buf.shape[0]
    buf[total-16:,:]=jnp.zeros((16,buf.shape[1]),F32)
    buf[0:n,:]=block.astype(F32)
    return buf[...]

def middle_back_kernel(x2_ref,da_ref,db_ref,go_ref,gt_ref,mix_ref,w_ref,gain_ref,dx_ref,dat_ref,gw_ref,sum_ref,buf,acc):
    i=pl.program_id(0)
    @pl.when(i==0)
    def _():
        acc[...]=jnp.zeros_like(acc); sum_ref[...]=jnp.zeros_like(sum_ref)
    for s,src in enumerate((go_ref,gt_ref)):
        dd=wide_rows(buf.at[s],src[0,0])
        grad=da_ref[0,s].astype(F32)+db_ref[0,1-s].astype(F32)
        dx,gg=norm_back(x2_ref[0,s],gain_ref[...],grad)
        dx=dx+dd
        dob=dx.astype(BF)
        if s==0:
            dx_ref[0]=dx
            for r,t in enumerate((gg,grad,dob.astype(F32),dd)):
                sum_ref[r:r+1,:]+=jnp.sum(t,axis=0,keepdims=True)
        dat_ref[0,s]=dot(dob,w_ref[...],NT).astype(BF)
        acc[...]+=dot(mix_ref[0,s],dob,TN)
    @pl.when(i==pl.num_programs(0)-1)
    def _(): gw_ref[...]=acc[...].astype(BF)

def middle_back(x2,dh_own,dh_oth,g_both,mixed,w_own,gain):
    _,n,half,feat=g_both.shape
    _,_,padded,width=mixed.shape
    tok=lambda s: pl.BlockSpec((1,1,half,feat),lambda i:(s,i,0,0))
    mix=pl.BlockSpec((1,2,padded,width),lambda i:(i,0,0,0))
    big=pl.BlockSpec((1,2,padded,feat),lambda i:(i,0,0,0))
    full=pl.BlockSpec((width,feat),lambda i:(0,0))
    return pl.pallas_call(middle_back_kernel,grid=(n,),
        in_specs=[big,big,big,tok(0),tok(1),mix,full,pl.BlockSpec((1,feat),lambda i:(0,0))],
        out_specs=[pl.BlockSpec((1,padded,feat),lambda i:(i,0,0)),mix,full,pl.BlockSpec((8,feat),lambda i:(0,0))],
        out_shape=[jax.ShapeDtypeStruct((n,padded,feat),F32),jax.ShapeDtypeStruct(mixed.shape,BF),jax.ShapeDtypeStruct((width,feat),BF),jax.ShapeDtypeStruct((8,feat),F32)],
        scratch_shapes=[pltpu.VMEM((2,padded,feat),F32),pltpu.VMEM((width,feat),F32)],name="middle_back",
        compiler_params=pltpu.CompilerParams(vmem_limit_bytes=56<<20),
        cost_estimate=pl.CostEstimate(flops=n*8*padded*feat*width,bytes_accessed=30<<20,transcendentals=0),
    )(x2,dh_own,dh_oth,g_both,g_both,mixed,w_own,gain[None])


def tail_kernel(ny, nx, *refs):
    h1_ref, dqkv_ref, go_ref, x_ref, dx_ref, gain_ref, vec_ref, w = refs[:8]
    keep_ref, pass_ref = refs[8:10]
    o = 10
    mine_ref, theirs_ref, so_ref, sf_ref, ig_ref, vout_ref, norm_ref = refs[o:o + 7]
    (grad, ra1, ra2, rb1, rb2, sa, sb, oa1, oa2, ob1, ob2, ta, tb, osum, ocross, ocore, odp, ofin,
     fpart, fdp, frecv, isum, ipart, irecv, idp, ifin,
     buf, give, got, stage, vrecv, nrecv, nval, send_sem, recv_sem) = refs[o + 7:]
    h, y, x, c, l = (lax.axis_index(a) for a in AXES)
    _, images, half, feat = x_ref.shape
    padded = dx_ref.shape[1]
    rows = grad.shape[4]
    apart = h != c
    cross = {"seq": 1 - h, "core": 1 - c}
    to_core, to_seq, to_dp = {"core": 1 - c}, {"seq": 1 - h}, {"dp": 1 - l}
    to_x = [{"x": lax.rem(x + k, nx)} for k in range(nx)]
    to_y = [{"y": lax.rem(y + k, ny)} for k in range(ny)]
    yy = [lax.rem(y + k, ny) for k in range(ny)]
    xx = [lax.rem(x + k, nx) for k in range(nx)]
    zz = [h, 1 - h]
    wires = Wires(send_sem, recv_sem)
    greet([to_core, to_seq, to_dp] + to_x[1:] + to_y[1:], cross, apart)

    fd = wires.send(pass_ref, fdp, to_dp)
    oa_got = [[wires.send(go_ref.at[yy[ky], xx[kx], h], oa1.at[ky - 1, kx], to_y[ky]) for kx in range(nx)] for ky in range(1, ny)]
    ob_got = [[wires.send(go_ref.at[yy[ky], xx[kx], 1 - h], ob1.at[kx - 1, ky], to_x[kx]) for ky in range(ny)] for kx in range(1, nx)]
    width = nx * 2 * rows
    ia_got, ib_got = [], []
    for ky in range(ny - 1, -1, -1):
        for kz in range(2):
            col = pl.multiple_of((zz[kz] * ny + yy[ky]) * width, 128)
            t = dot(h1_ref[:, pl.ds(col, width)], dqkv_ref[...], TN).astype(BF)
            for q in range(nx):
                for core in range(2):
                    r = (q * 2 + core) * rows
                    grad[zz[kz], yy[ky], q, core] = t[r:r + rows]
            for kx in range(nx):
                if ky > 0:
                    ia_got.append(wires.send(grad.at[zz[kz], yy[ky], xx[kx], c], ra1.at[ky - 1, kz, kx], to_y[ky]))
                if kx > 0:
                    ib_got.append(wires.send(grad.at[zz[kz], yy[ky], xx[kx], 1 - c], rb1.at[kx - 1, kz, ky], to_x[kx]))
    dh_got = []
    for i in range(images):
        r = (2 * i + 1) * padded
        give[i] = dot(dqkv_ref[r:r + padded, :], w[...], NT).astype(BF)
        dh_got.append(wires.send(give.at[i], got.at[i], to_core))
    sum_gain, sum_shift = jnp.zeros((1, feat), F32), jnp.zeros((1, feat), F32)
    crossing_copies = [wires.make(stage.at[i], ig_ref.at[i], cross) for i in range(images)]

    def input_back(i, sum_gain, sum_shift):
        r = 2 * i * padded
        own = dot(dqkv_ref[r:r + padded, :], w[...], NT)
        dh_got[i].wait_recv()
        g = own + got[i].astype(F32)
        dx, gg = norm_back(wide_rows(buf, x_ref[0, i]), gain_ref[...], g)
        stage[i] = (dx + dx_ref[i]).astype(BF)[:half]

        if i == 0:
            @pl.when(apart)
            def _():
                crossing_copies[i].start()

        @pl.when(jnp.logical_not(apart))
        def _():
            ig_ref[i] = stage[i]

        return sum_gain + jnp.sum(gg, axis=0, keepdims=True), sum_shift + jnp.sum(g, axis=0, keepdims=True)

    for i in range(images):
        sum_gain, sum_shift = input_back(i, sum_gain, sum_shift)
    fd.wait_recv()
    fpart[...] = add_all(keep_ref[...], fdp[...]).astype(BF)
    fs = wires.send(fpart.at[1], frecv, to_seq)
    for row in oa_got + ob_got:
        for cp in row:
            cp.wait_recv()
    o_got = []
    for kx in range(1, nx):
        ta[kx - 1] = add_all(go_ref[y, xx[kx], h], *(oa1[k, kx] for k in range(ny - 1))).astype(BF)
        o_got.append(wires.send(ta.at[kx - 1], oa2.at[kx - 1], to_x[kx]))
    for ky in range(1, ny):
        tb[ky - 1] = add_all(go_ref[yy[ky], x, 1 - h], *(ob1[k, ky] for k in range(nx - 1))).astype(BF)
        o_got.append(wires.send(tb.at[ky - 1], ob2.at[ky - 1], to_y[ky]))

    for cp in ia_got + ib_got:
        cp.wait_recv()
    i_got = []
    for kz in range(2):
        for kx in range(1, nx):
            sa[kx - 1, kz] = add_all(grad[zz[kz], y, xx[kx], c], *(ra1[k, kz, kx] for k in range(ny - 1))).astype(BF)
        for ky in range(1, ny):
            sb[ky - 1, kz] = add_all(grad[zz[kz], yy[ky], x, 1 - c], *(rb1[k, kz, ky] for k in range(nx - 1))).astype(BF)
    for kx in range(1, nx):
        i_got.append(wires.send(sa.at[kx - 1], ra2.at[kx - 1], to_x[kx]))
    for ky in range(1, ny):
        i_got.append(wires.send(sb.at[ky - 1], rb2.at[ky - 1], to_y[ky]))
    vout_ref[...] = vec_ref[...]
    for q in range(feat // 128):
        vout_ref[q:q + 1, :] = sum_gain[:, q * 128:(q + 1) * 128]
        vout_ref[feat // 128 + q:feat // 128 + q + 1, :] = sum_shift[:, q * 128:(q + 1) * 128]
    rounds = [[to_core], to_x[1:], to_y[1:], [to_seq], [to_dp]]
    slot = [0]

    def start_round(value, landing, peers):
        first = slot[0]
        cps = [wires.send(value, landing.at[first + k], peer) for k, peer in enumerate(peers)]
        slot[0] += len(peers)
        return first, cps

    def end_round(value_ref, landing, started):
        first, cps = started
        for cp in cps:
            cp.wait_recv()
        for cp in cps:
            cp.wait_send()
        wires.sent = [cp for cp in wires.sent if all(cp is not other for other in cps)]
        value_ref[...] = add_all(value_ref[...], *(landing[first + k] for k in range(len(cps))))

    vec_round = start_round(vout_ref, vrecv, rounds[0])
    for cp in i_got:
        cp.wait_recv()
    for kz in range(2):
        isum[0, kz] = add_all(grad[zz[kz], y, x, c], *(ra1[k, kz, 0] for k in range(ny - 1)), *(ra2[k, kz] for k in range(nx - 1))).astype(BF)
        isum[1, kz] = add_all(grad[zz[kz], y, x, 1 - c], *(rb1[k, kz, 0] for k in range(nx - 1)), *(rb2[k, kz] for k in range(ny - 1))).astype(BF)
    idd = wires.send(isum.at[1 - l], idp, to_dp)
    for cp in o_got:
        cp.wait_recv()
    osum[0] = add_all(go_ref[y, x, h], *(oa1[k, 0] for k in range(ny - 1)), *(oa2[k] for k in range(nx - 1))).astype(BF)
    osum[1] = add_all(go_ref[y, x, 1 - h], *(ob1[k, 0] for k in range(nx - 1)), *(ob2[k] for k in range(ny - 1))).astype(BF)
    out_cross = wires.make(osum, ocross, cross)

    @pl.when(apart)
    def _():
        out_cross.start()

    @pl.when(jnp.logical_not(apart))
    def _():
        ocross[...] = osum[...]

    end_round(vout_ref, vrecv, vec_round)
    vec_round = start_round(vout_ref, vrecv, rounds[1])
    idd.wait_recv()
    ipart[...] = add_all(isum[l], idp[...]).astype(BF)
    is_ = wires.send(ipart.at[1], irecv, to_seq)

    @pl.when(apart)
    def _():
        for cp in crossing_copies[1:]:
            cp.start()

    end_round(vout_ref, vrecv, vec_round)
    vec_round = start_round(vout_ref, vrecv, rounds[2])

    @pl.when(apart)
    def _():
        out_cross.wait_recv()

    oc = wires.send(ocross.at[1], ocore, to_core)
    fs.wait_recv()
    sf_ref[l] = add_all(fpart[0], frecv[...]).astype(BF)
    ff_last = wires.send(sf_ref.at[l], sf_ref.at[l], to_dp)
    end_round(vout_ref, vrecv, vec_round)
    vec_round = start_round(vout_ref, vrecv, rounds[3])
    oc.wait_recv()
    ofin[...] = add_all(ocross[0], ocore[...]).astype(BF)
    od = wires.send(ofin, odp, to_dp)
    is_.wait_recv()
    ifin[l] = add_all(ipart[0], irecv[...]).astype(BF)
    in_last = wires.send(ifin.at[l], ifin.at[l], to_dp)
    end_round(vout_ref, vrecv, vec_round)
    vec_round = start_round(vout_ref, vrecv, rounds[4])
    in_last.wait_recv()
    ic = wires.send(ifin.at[1], theirs_ref, to_core)
    mine_ref[...] = ifin[0]
    od.wait_recv()
    so_ref[...] = add_all(ofin[...], odp[...]).astype(BF)
    end_round(vout_ref, vrecv, vec_round)
    ff_last.wait_recv()

    def squares(value):
        value = value.astype(F32)
        return jnp.sum(jnp.sum(value * value, axis=0, keepdims=True), axis=1, keepdims=True)

    shard = ((h * ny + y) * nx + x) * 2 + c
    v = vout_ref[...]
    place = lax.broadcasted_iota(jnp.int32, v.shape, 0) * 128 + lax.broadcasted_iota(jnp.int32, v.shape, 1)
    share = v.shape[0] * 128 // (4 * ny * nx)
    v = jnp.where((place >= shard * share) & (place < (shard + 1) * share), v, 0.0)
    total = squares(v) + squares(so_ref[...]) + squares(mine_ref[...])
    for ab in range(2):
        for ud in range(2):
            total = total + squares(sf_ref[ab, ud])
    ic.wait_recv()
    total = total + squares(theirs_ref[...])
    nval[...] = jnp.broadcast_to(total, nval.shape)
    slot[0] = 0
    for peers in rounds[:4]:
        end_round(nval, nrecv, start_round(nval, nrecv, peers))
    norm_ref[...] = jnp.sqrt(nval[...])

    @pl.when(apart)
    def _():
        for cp in crossing_copies:
            cp.wait_recv()
        for cp in crossing_copies:
            cp.wait_send()
        out_cross.wait_send()

    wires.finish()


def tail_stage(h1, dqkv, g_out, x_own, dx2, gain, vec, w, keep, give, ny, nx):
    tokens, feat = h1.shape
    width = dqkv.shape[1]
    rows = feat // (4 * ny * nx)
    rows_o = g_out.shape[3]
    _, images, half, _ = x_own.shape
    padded = dx2.shape[1]
    _, ud, hid, _ = keep.shape
    ma, mb = max(ny - 1, 1), max(nx - 1, 1)
    piece, out_piece, ff = (rows, width), (rows_o, feat), (ud, hid, feat)
    peers = 4 + nx - 1 + ny - 1
    many = 200 + 32 * ny * nx
    V = lambda *s: pltpu.VMEM(s, BF)
    scratch = [
        V(2, ny, nx, 2, *piece),
        V(ny - 1, 2, nx, *piece), V(nx - 1, 2, *piece), V(nx - 1, 2, ny, *piece), V(ny - 1, 2, *piece),
        V(nx - 1, 2, *piece), V(ny - 1, 2, *piece),
        V(ny - 1, nx, *out_piece), V(nx - 1, *out_piece), V(nx - 1, ny, *out_piece), V(ny - 1, *out_piece),
        V(nx - 1, *out_piece), V(ny - 1, *out_piece),
        V(2, *out_piece), V(2, *out_piece), V(*out_piece), V(*out_piece), V(*out_piece),
        V(2, *ff), V(2, *ff), V(*ff),
        V(2, 2, *piece), V(2, *piece), V(*piece), V(2, *piece), V(2, *piece),
        pltpu.VMEM((padded, feat), F32), V(images, padded, feat), V(images, padded, feat), V(images, half, feat),
        pltpu.VMEM((peers,) + vec.shape, F32), pltpu.VMEM((peers, 8, 128), F32), pltpu.VMEM((8, 128), F32),
        pltpu.SemaphoreType.DMA((many,)), pltpu.SemaphoreType.DMA((many,)),
    ]
    return pl.pallas_call(
        functools.partial(tail_kernel, ny, nx),
        in_specs=[VM] * 10,
        out_specs=[VM] * 7,
        out_shape=[
            jax.ShapeDtypeStruct(piece, BF), jax.ShapeDtypeStruct(piece, BF), jax.ShapeDtypeStruct(out_piece, BF),
            jax.ShapeDtypeStruct((2,) + ff, BF), jax.ShapeDtypeStruct(x_own.shape[1:], BF),
            jax.ShapeDtypeStruct(vec.shape, F32), jax.ShapeDtypeStruct((8, 128), F32),
        ],
        scratch_shapes=scratch,
        name="tail_stage",
        compiler_params=pltpu.CompilerParams(collective_id=1, has_side_effects=True, vmem_limit_bytes=62 << 20),
        cost_estimate=pl.CostEstimate(flops=4 * tokens * feat * width, bytes_accessed=40 << 20, transcendentals=0),
    )(h1, dqkv, g_out, x_own, dx2, gain[None], vec, w, keep, give)

def head_kernel(ny, nx, *refs):
    (in_ref, out_ref, up_ref, down_ref, vec_ref, img_ref,
     h1_ref, qkv_ref, xb, w, my_out, other_out, fa, fb, near_ref, vfull,
     theirs, o_own, o_core, tmp, buf, xsem, csem, send_sem, recv_sem) = refs
    h, y, x, c, l = (lax.axis_index(a) for a in AXES)
    images, half, feat = img_ref.shape
    rows = in_ref.shape[0]
    width = w.shape[1]
    part = width // 3
    hid = up_ref.shape[0] // 2
    apart = h != c
    cross = {"seq": 1 - h, "core": 1 - c}
    to_core, to_seq, to_dp = {"core": 1 - c}, {"seq": 1 - h}, {"dp": 1 - l}
    inner, to_near = l != h, {"seq": 1 - h, "dp": 1 - l}
    to_x = [{"x": lax.rem(x + nx - k, nx)} for k in range(nx)]
    to_y = [{"y": lax.rem(y + ny - k, ny)} for k in range(ny)]
    yy = [lax.rem(y + k, ny) for k in range(ny)]
    xx = [lax.rem(x + k, nx) for k in range(nx)]
    zz = [h, 1 - h]
    wires = Wires(send_sem, recv_sem)
    barrier = pltpu.get_barrier_semaphore()
    peers = [to_core, to_seq, to_dp] + to_x[1:] + to_y[1:]
    for peer in peers:
        pl.semaphore_signal(barrier, inc=1, device_id=peer, device_id_type=MESH_ID)

    @pl.when(apart)
    def _():
        pl.semaphore_signal(barrier, inc=1, device_id=cross, device_id_type=MESH_ID)

    @pl.when(inner)
    def _():
        pl.semaphore_signal(barrier, inc=1, device_id=to_near, device_id_type=MESH_ID)

    local_images = pltpu.make_async_copy(img_ref, xb.at[0], xsem)

    @pl.when(jnp.logical_not(apart))
    def _():
        local_images.start()

    def slot(z, yi, xi, core):
        return w.at[pl.ds(pl.multiple_of((((z * ny + yi) * nx + xi) * 2 + core) * rows, 16), rows)]

    mine = slot(h, y, x, c)
    for t in range(3):
        mine[:, t * part:(t + 1) * part] = in_ref[:, pl.ds(pl.multiple_of(t * 2 * part + c * part, 128), part)].astype(BF)
        theirs[:, t * part:(t + 1) * part] = in_ref[:, pl.ds(pl.multiple_of(t * 2 * part + (1 - c) * part, 128), part)].astype(BF)
    vfull[h, y, x, c] = vec_ref[...].astype(BF).astype(F32)
    o_own[...] = out_ref[...].astype(BF)
    pl.semaphore_wait(barrier, len(peers) + jnp.where(apart, 1, 0) + jnp.where(inner, 1, 0))

    spread, forward, settle = plane_moves(wires, to_x, to_y)

    def in_a(kz, ky, kx, *_):
        return slot(zz[kz], yy[ky], xx[kx], c)

    def in_b(kz, ky, kx, *_):
        return slot(zz[kz], yy[ky], xx[kx], 1 - c)

    def out_a(kz, ky, kx, *_):
        return my_out.at[yy[ky], xx[kx], h]

    def out_b(kz, ky, kx, *_):
        return my_out.at[yy[ky], xx[kx], 1 - h]

    ff_a, ff_b = by_offset(fa, tmp.at[0]), by_offset(fb, tmp.at[1])

    b_got = wires.send(theirs, slot(h, y, x, c), to_core)
    def across(core):
        own, other = slot(h, y, x, core), slot(1 - h, y, x, core)
        return wires.make(own, own, to_near), wires.make(other, other, to_dp)

    az, bz = across(c), across(1 - c)

    @pl.when(inner)
    def _():
        az[0].start()

    a0 = spread(in_a, 0, "x")
    vec_peers = [[to_core], to_x[1:], to_y[1:], [to_seq]]
    vec_at = [vfull.at[h, y, x, c], vfull.at[h, y, x], vfull.at[h, y], vfull.at[h]]

    def vec_send(r):
        return [wires.send(vec_at[r], vec_at[r], peer) for peer in vec_peers[r]]

    v = vec_send(0)
    oc = wires.send(o_own, o_core, to_core)
    xl = wires.make(img_ref, xb.at[1], to_core)

    @pl.when(jnp.logical_not(apart))
    def _():
        xl.start()

    b_got.wait_recv()

    @pl.when(inner)
    def _():
        bz[0].start()

    b0 = spread(in_b, 0, "y")
    for cp in v:
        cp.wait_recv()
    v = vec_send(1)
    for ab in range(2):
        tmp[ab, 0] = up_ref[ab * hid:(ab + 1) * hid, :].astype(BF)
        tmp[ab, 1] = down_ref[ab * hid:(ab + 1) * hid, :].astype(BF)
    keep = [
        pltpu.make_async_copy(tmp.at[0], fa.at[0, 0], csem.at[0]),
        pltpu.make_async_copy(tmp.at[1], fb.at[0, 0], csem.at[1]),
    ]
    for cp in keep:
        cp.start()
    for cp in v:
        cp.wait_recv()
    v = vec_send(2)
    forward(in_a, 0, "x", a0)
    forward(in_b, 0, "y", b0)
    oc.wait_recv()
    x_cross = [wires.make(img_ref.at[i], xb.at[0, i], cross) for i in range(images)]
    o_cross = [wires.make(o_own, my_out.at[y, x, 1 - h], cross), wires.make(o_core, my_out.at[y, x, h], cross)]

    @pl.when(apart)
    def _():
        for cp in o_cross:
            cp.start()

    @pl.when(jnp.logical_and(apart, jnp.logical_not(inner)))
    def _():
        x_cross[0].start()

    def arrive(pair):
        @pl.when(inner)
        def _():
            pair[0].wait_recv()
            pair[1].start()

        @pl.when(jnp.logical_not(inner))
        def _():
            pair[1].wait_recv()

    arrive(az)
    a1 = spread(in_a, 1, "x")
    arrive(bz)
    b1 = spread(in_b, 1, "y")
    for cp in v:
        cp.wait_recv()
    v = vec_send(3)

    @pl.when(jnp.logical_and(apart, inner))
    def _():
        x_cross[0].start()

    @pl.when(apart)
    def _():
        for cp in x_cross[1:]:
            cp.start()

    @pl.when(jnp.logical_not(apart))
    def _():
        my_out[y, x, h] = o_own[...]
        my_out[y, x, 1 - h] = o_core[...]
        local_images.wait()

    @pl.when(apart)
    def _():
        for cp in o_cross:
            cp.wait_recv()

    oa = spread(out_a, 0, "x")
    ob = spread(out_b, 0, "y")
    forward(in_a, 1, "x", a1)
    forward(in_b, 1, "y", b1)
    forward(out_a, 0, "x", oa)
    forward(out_b, 0, "y", ob)
    fa0 = spread(ff_a, 0, "x")
    fb0 = spread(ff_b, 0, "y")
    for got in (a0, b0, a1, b1):
        settle(got)
    for cp in v:
        cp.wait_recv()

    def row(start, count):
        per = vec_ref.shape[1]
        pieces, at = [], start
        while at < start + count:
            s, r = at // per, at % per
            n = min(per - r, start + count - at)
            xs = s // 2
            pieces.append(vfull[xs // (nx * ny), xs // nx % ny, xs % nx, s % 2][:, r:r + n])
            at += n
        return pieces[0] if len(pieces) == 1 else jnp.concatenate(pieces, axis=1)

    gain, shift_row = row(0, feat), row(feat, feat)
    q_row, v_row = row(2 * feat, feat), row(3 * feat, feat)
    q_row = jnp.where(c == 0, q_row[:, :part], q_row[:, part:])
    v_row = jnp.where(c == 0, v_row[:, :part], v_row[:, part:])
    bias = jnp.concatenate([q_row, jnp.zeros((1, part), F32), v_row], axis=1)

    def project(i, s):
        value = wide_rows(buf, xb[s, i])
        normed = (norm_parts(value)[0] * gain + shift_row).astype(BF)
        h1_ref[i, s] = normed
        qkv_ref[i, s] = (dot(normed, w[...]) + bias).astype(BF)

    near = jnp.where(apart, 1, 0)

    @pl.when(apart)
    def _():
        xl.wait_recv()

    def near_step(i, carry):
        project(i, near)
        return carry

    lax.fori_loop(0, images, near_step, 0)

    forward(ff_a, 0, "x", fa0)
    forward(ff_b, 0, "y", fb0)
    near_ff = [wires.make(tmp.at[ab], near_ref.at[ab], to_near) for ab in range(2)]
    x_core = [wires.make(xb.at[0, i], xb.at[1, i], to_core) for i in range(images)]
    for i in range(images):
        @pl.when(apart)
        def _():
            x_cross[i].wait_recv()
            x_core[i].start()

        @pl.when(jnp.logical_not(apart))
        def _():
            x_core[i].wait_recv()

        if i == images - 1:
            @pl.when(inner)
            def _():
                for cp in near_ff:
                    cp.start()

        project(i, 1 - near)
        if i == 0:
            settle(oa)
            settle(ob)
            other = wires.send(my_out, other_out, to_core)
    other.wait_recv()
    settle(fa0)
    settle(fb0)

    @pl.when(apart)
    def _():
        for cp in x_cross + o_cross + x_core:
            cp.wait_send()

    @pl.when(jnp.logical_not(apart))
    def _():
        xl.wait_send()

    @pl.when(inner)
    def _():
        for cp in near_ff:
            cp.wait_recv()
        for cp in (*az, *bz, *near_ff):
            cp.wait_send()

    for cp in keep:
        cp.wait()
    wires.finish()


def head_stage(in_w, out_w, up_w, down_w, vec, images, padded, ny, nx):
    n, half, feat = images.shape
    rows, rows_out, rows_ff = in_w.shape[0], out_w.shape[0], up_w.shape[0]
    width = in_w.shape[1] // 2
    hid = rows_ff // 2
    many = 60 + 24 * ny * nx
    S = jax.ShapeDtypeStruct
    return pl.pallas_call(
        functools.partial(head_kernel, ny, nx),
        in_specs=[VM] * 5 + [ANY],
        out_specs=[VM] * 6 + [ANY] * 3 + [VM],
        out_shape=[
            S((n, 2, padded, feat), BF), S((n, 2, padded, width), BF), S((2, n, half, feat), BF), S((feat, width), BF),
            S((ny, nx, 2, rows_out, feat), BF), S((ny, nx, 2, rows_out, feat), BF),
            S((ny, nx, 2, hid, feat), BF), S((ny, nx, 2, hid, feat), BF), S((2, 2, hid, feat), BF),
            S((2, ny, nx, 2, 1, vec.shape[1]), F32),
        ],
        scratch_shapes=[
            pltpu.VMEM((rows, width), BF), pltpu.VMEM((rows_out, feat), BF), pltpu.VMEM((rows_out, feat), BF),
            pltpu.VMEM((2, 2, hid, feat), BF), pltpu.VMEM((padded, feat), F32),
            pltpu.SemaphoreType.DMA(()), pltpu.SemaphoreType.DMA((3,)),
            pltpu.SemaphoreType.DMA((many,)), pltpu.SemaphoreType.DMA((many,)),
        ],
        name="head_stage",
        compiler_params=pltpu.CompilerParams(collective_id=2, has_side_effects=True, vmem_limit_bytes=60 << 20),
        cost_estimate=pl.CostEstimate(flops=n * 4 * padded * feat * width, bytes_accessed=40 << 20, transcendentals=0),
    )(in_w, out_w, up_w, down_w, vec, images)


def mid_kernel(ny, nx, *refs):
    (qkv_ref, kf_ref, xb, wo_ref, wt_ref, vec_ref, near_ref, grad_ref,
     mix_ref, lse_ref, x2_ref, h2_ref, g_ref, fa, fb,
     mix_oth, land, buf, csem, send_sem, recv_sem) = refs
    h, y, x, c, l = (lax.axis_index(a) for a in AXES)
    images, rows, width = mix_ref.shape
    padded = rows // 2
    pairs = width // 128
    apart, inner = h != c, l != h
    cross = {"seq": 1 - h, "core": 1 - c}
    to_core, to_dp = {"core": 1 - c}, {"dp": 1 - l}
    to_x = [{"x": lax.rem(x + nx - k, nx)} for k in range(nx)]
    to_y = [{"y": lax.rem(y + ny - k, ny)} for k in range(ny)]
    wires = Wires(send_sem, recv_sem)
    spread, forward, settle = plane_moves(wires, to_x, to_y)
    barrier = pltpu.get_barrier_semaphore()
    peers = [to_core, to_dp] + to_x[1:] + to_y[1:]
    for peer in peers:
        pl.semaphore_signal(barrier, inc=1, device_id=peer, device_id_type=MESH_ID)

    @pl.when(apart)
    def _():
        pl.semaphore_signal(barrier, inc=1, device_id=cross, device_id_type=MESH_ID)

    pl.semaphore_wait(barrier, len(peers) + jnp.where(apart, 1, 0))
    here_ff = [pltpu.make_async_copy(near_ref.at[ab], land.at[ab], csem.at[3 + ab]) for ab in range(2)]
    far_ff = [wires.make(near_ref.at[ab], land.at[ab], to_dp) for ab in range(2)]
    local_grad = pltpu.make_async_copy(grad_ref, g_ref.at[0], csem.at[0])
    grad_core = wires.make(grad_ref, g_ref.at[1], to_core)
    g_cross = [wires.make(grad_ref.at[i], g_ref.at[0, i], cross) for i in range(images)]
    g_core = [wires.make(g_ref.at[0, i], g_ref.at[1, i], to_core) for i in range(images)]

    @pl.when(inner)
    def _():
        for cp in far_ff + here_ff:
            cp.start()

    @pl.when(jnp.logical_not(apart))
    def _():
        local_grad.start()
        grad_core.start()

    def arrive(ab):
        @pl.when(inner)
        def _():
            here_ff[ab].wait()

        @pl.when(jnp.logical_not(inner))
        def _():
            far_ff[ab].wait_recv()

        return spread(ff[ab], 1, order[ab])

    ff = [by_offset(fa, land.at[0]), by_offset(fb, land.at[1])]
    order = ("x", "y")
    gots = []

    @pl.when(apart)
    def _():
        for cp in g_cross:
            cp.start()

    mix_got = []
    for i in range(images):
        def pair(p, carry):
            at = [pl.ds(pl.multiple_of((t * pairs + p) * 128, 128), 128) for t in range(3)]
            mixed, sums = attend_pair(qkv_ref[i, :, at[0]], qkv_ref[i, :, at[1]], qkv_ref[i, :, at[2]], kf_ref[i])
            mix_ref[i, :, at[0]] = mixed
            for j in range(2):
                lse_ref[i, p, j:j + 1, :] = sums[j]
            return carry

        lax.fori_loop(0, pairs, pair, 0)
        mix_got.append(wires.send(mix_ref.at[i], mix_oth.at[i], to_core))
        if i == max(images - 2, 0):
            gots.append(arrive(0))
        if i == images - 1:
            gots.append(arrive(1))

    def middle(i):
        mix_got[i].wait_recv()
        for s in range(2):
            own = slice(s * padded, (s + 1) * padded)
            oth = slice((1 - s) * padded, (2 - s) * padded)
            v = wide_rows(buf, xb[s, i])
            v = v + (dot(mix_ref[i, own, :], wo_ref[...]) + dot(mix_oth[i, oth, :], wt_ref[...])) + vec_ref[0:1, :]
            x2_ref[i, s] = v
            h2_ref[i, s] = (norm_parts(v)[0] * vec_ref[1:2, :] + vec_ref[2:3, :]).astype(BF)

    for i in range(images):
        middle(i)
        if i == 0:
            forward(ff[0], 1, order[0], gots[0])
    keep = [pltpu.make_async_copy(land.at[ab], (fa, fb)[ab].at[0, 0], csem.at[1 + ab]) for ab in range(2)]
    for cp in keep:
        cp.start()
    forward(ff[1], 1, order[1], gots[1])
    for i in range(images):
        @pl.when(apart)
        def _():
            g_cross[i].wait_recv()
            g_core[i].start()

        @pl.when(jnp.logical_not(apart))
        def _():
            g_core[i].wait_recv()

    @pl.when(apart)
    def _():
        grad_core.wait_recv()
        for cp in g_cross + g_core:
            cp.wait_send()

    @pl.when(jnp.logical_not(apart))
    def _():
        local_grad.wait()
        grad_core.wait_send()

    @pl.when(inner)
    def _():
        for cp in far_ff:
            cp.wait_send()

    for got in gots:
        settle(got)
    for cp in keep:
        cp.wait()
    wires.finish()


def mid_stage(qkv, key_fill, x_both, w_own, w_oth, vec, low_ff, out_grad, ny, nx):
    n, rows, w3 = qkv.shape
    width, feat = w_own.shape
    half = out_grad.shape[1]
    _, ud, hid, _ = low_ff.shape
    many = 40 + 4 * ny * nx
    S = jax.ShapeDtypeStruct
    return pl.pallas_call(
        functools.partial(mid_kernel, ny, nx),
        in_specs=[VM] * 6 + [ANY] * 2,
        out_specs=[VM] * 5 + [ANY] * 2,
        out_shape=[
            S((n, rows, width), BF), S((n, width // 128, 8, rows), F32), S((n, 2, rows // 2, feat), F32),
            S((n, 2, rows // 2, feat), BF), S((2, n, half, feat), BF),
            S((ny, nx, ud, hid, feat), BF), S((ny, nx, ud, hid, feat), BF),
        ],
        scratch_shapes=[
            pltpu.VMEM((n, rows, width), BF), pltpu.VMEM((2, ud, hid, feat), BF), pltpu.VMEM((rows // 2, feat), F32),
            pltpu.SemaphoreType.DMA((5,)), pltpu.SemaphoreType.DMA((many,)), pltpu.SemaphoreType.DMA((many,)),
        ],
        name="mid_stage",
        compiler_params=pltpu.CompilerParams(collective_id=5, has_side_effects=True, vmem_limit_bytes=60 << 20),
        cost_estimate=pl.CostEstimate(flops=n * 4 * rows * rows * w3, bytes_accessed=50 << 20, transcendentals=n * 8 * rows * rows),
    )(qkv, key_fill, x_both, w_own, w_oth, vec, low_ff, out_grad)


def shift(value, axis, up):
    n = lax.axis_size(axis)
    return lax.ppermute(value, axis, [(i, (i + up) % n) for i in range(n)])


def after(value, *others):
    return lax.optimization_barrier((value, others))[0]


def crossing(value):
    return lax.ppermute(value, ("seq", "core"), [(1, 2), (2, 1)])


def pick(own, received):
    return jnp.where(lax.axis_index("seq") == lax.axis_index("core"), own, received)


def crossed(value):
    return pick(value, crossing(value))


def adam_update(master, first_moment, second_moment, gradient, step_rate, bias_one, bias_two):
    first_new = 0.5 * first_moment + 0.5 * gradient
    second_new = 0.5 * second_moment + 0.5 * gradient * gradient
    update = first_new / bias_one / (jnp.sqrt(second_new / bias_two) + ADAM_EPS)
    master_new = master - step_rate * (update + WEIGHT_DECAY * master)
    return (master_new, first_new, second_new)


def on_device(images, key_mask, out_grad, step_count, *params):
    masters, firsts, seconds = params[0:5], params[5:10], params[10:15]
    in_weights, out_weights, up_weights, down_weights, vectors = masters
    image_count, half, features = images.shape
    padded = -(-half // PAD_ROWS) * PAD_ROWS
    h, c = lax.axis_index("seq"), lax.axis_index("core")
    y, x = lax.axis_index("y"), lax.axis_index("x")
    ny, nx = lax.axis_size("y"), lax.axis_size("x")
    shards = 4 * ny * nx
    shard = ((h * ny + y) * nx + x) * 2 + c

    h1, qkv, x_both, full_in, my_out, other_out, own_a, own_b, low_ff, full_vec = head_stage(
        in_weights, out_weights, up_weights, down_weights, vectors[None], images, padded, ny, nx
    )
    my_out, other_out = my_out.reshape(HALF_D, D), other_out.reshape(HALF_D, D)
    rows_in, rows_out, rows_ff = in_weights.shape[0], out_weights.shape[0], up_weights.shape[0]
    half_ff = rows_ff // 2
    keys = [(ky, kx) for ky in range(ny) for kx in range(nx)]
    full_vec = full_vec.reshape(-1)
    gain_one, shift_one, query_bias, value_bias, out_bias, gain_two, shift_two, down_bias = (
        full_vec[i * D : (i + 1) * D] for i in range(8)
    )
    up_bias = full_vec[8 * D :]

    mask = key_mask.astype(F32)
    mask = jnp.where(h == c, mask, shift(mask, "core", 1)).reshape(image_count, 2, half)
    mask = jnp.where(c == 0, mask, mask[:, ::-1])
    mask = jnp.pad(mask, ((0, 0), (0, 0), (0, padded - half))).reshape(image_count, 2 * padded)
    key_fill = jnp.broadcast_to(jnp.where(mask > 0, 0.0, NEG_FILL)[..., None], mask.shape + (128,)).astype(BF)

    tokens = image_count * 2 * padded
    qkv = qkv.reshape(image_count, 2 * padded, 3 * HALF_D)
    mid_vec = jnp.pad(jnp.stack([out_bias, gain_two, shift_two]), ((0, 5), (0, 0)))
    mixed, lse, x2, h2, g_both, oth_a, oth_b = mid_stage(
        qkv, key_fill, x_both, my_out, other_out, mid_vec, low_ff, out_grad, ny, nx
    )
    halved = mixed.reshape(image_count, 2, padded, HALF_D)

    grad_a, grad_b, (y_own, y_oth, dh2, g_bu, first_a, first_b) = mlp(
        ny, nx, h2.reshape(tokens, D), g_both, up_bias.reshape(shards * 2, half_ff), own_a, own_b, oth_a, oth_b
    )
    result = y_own[:, :half] + shift(y_oth, "core", 1)[:, :half].astype(F32) + x2[:, 0, :half] + down_bias
    result = result.astype(BF)
    result_got = crossing(result)

    def second_stage(grads, firsts, swap):
        sums = []
        for k in range(firsts.shape[1]):
            sums.append(add_all(grads[(k, 0) if swap else (0, k)], *firsts[:, k]).astype(BF))
        return sums

    sums_a, sums_b = second_stage(grad_a, first_a, False), second_stage(grad_b, first_b, True)
    got_a = [lax.ppermute(s, "x", [(i, (i + k) % nx) for i in range(nx)]) for k, s in enumerate(sums_a) if k]
    got_b = [lax.ppermute(s, "y", [(i, (i + k) % ny) for i in range(ny)]) for k, s in enumerate(sums_b) if k]

    dh2 = dh2.reshape(image_count, 2, padded, D)
    dh2_oth = shift(dh2, "core", 1)
    dx2, dattn, g_out, sums_two = middle_back(x2, dh2, dh2_oth, g_both, halved, my_out, gain_two)
    dqkv, sums_qkv = attend_back(qkv, key_fill, mixed, dattn.reshape(mixed.shape), lse)
    got_a, got_b = after(got_a, dqkv), after(got_b, dqkv)
    plane_a, plane_b = add_all(sums_a[0], *got_a).astype(BF), add_all(sums_b[0], *got_b).astype(BF)
    l = lax.axis_index("dp")
    half_keep, half_give = jnp.where(l == 0, plane_a, plane_b), jnp.where(l == 0, plane_b, plane_a)

    zero = jnp.zeros((D,), F32)
    vec = jnp.concatenate(
        [
            zero,
            zero,
            lax.dynamic_update_slice(zero, sums_qkv[0, :HALF_D], (c * HALF_D,)),
            lax.dynamic_update_slice(zero, sums_qkv[0, 2 * HALF_D :], (c * HALF_D,)),
            sums_two[2],
            sums_two[0],
            sums_two[1],
            sums_two[3],
            g_bu.reshape(-1),
        ]
    ).reshape(-1, 128)
    in_mine, in_theirs, share_out, share_ff, input_grad, vec, norm = tail_stage(
        h1.reshape(tokens, D),
        dqkv.reshape(tokens, 3 * HALF_D),
        g_out.reshape(ny, nx, 2, rows_out, D),
        x_both,
        dx2,
        gain_one,
        vec,
        full_in,
        half_keep,
        half_give,
        ny,
        nx,
    )
    activations = pick(result, after(result_got, norm)).astype(F32)
    input_grad = input_grad.astype(F32)
    share_vec = lax.dynamic_slice(vec.reshape(shards, -1), (shard, 0), (1, vec.size // shards)).reshape(-1)
    in_mine, in_theirs = (s.reshape(rows_in, 3, 1, HALF_D) for s in (in_mine, in_theirs))
    share_in = jnp.where(
        c == 0, jnp.concatenate([in_mine, in_theirs], 2), jnp.concatenate([in_theirs, in_mine], 2)
    ).reshape(rows_in, 3 * D)
    share_up, share_down = (share_ff[:, i].reshape(rows_ff, D) for i in range(2))
    shares = tuple(s.astype(F32) for s in (share_in, share_out, share_up, share_down, share_vec))
    grad_norm = norm[0, 0]
    threshold = 0.5 * math.sqrt(4 * D * D + 2 * D * FF + 12 * D)
    clip_factor = jnp.minimum(1.0, threshold / grad_norm)
    bias = 1.0 - jnp.power(F32(0.5), step_count.astype(F32))
    rates = ((D // 2) ** (-0.5), (D // 4) ** (-0.5), D ** (-0.5), FF ** (-0.5), 0.2)
    results = [
        adam_update(masters[i], firsts[i], seconds[i], shares[i] * clip_factor, rates[i], bias, bias) for i in range(5)
    ]
    return (
        grad_norm,
        *(r[0] for r in results),
        *(r[1] for r in results),
        *(r[2] for r in results),
        *(r[0].astype(BF) for r in results),
        activations,
        input_grad,
    )


def solution(mesh):
    seq_n, fsdp_n, dp_n = (mesh.shape[a] for a in ("seq", "fsdp", "dp"))
    nx = math.isqrt(fsdp_n // 2)
    ny = fsdp_n // 2 // nx
    grid = Mesh(np.asarray(mesh.devices).reshape(seq_n, ny, nx, 2, dp_n), AXES)
    tokens = P(("y", "x", "core", "dp"), "seq", None)
    matrix, vector = P(SHARD, None), P(SHARD)
    five = (matrix, matrix, matrix, matrix, vector)
    return jax.shard_map(
        on_device,
        mesh=grid,
        in_specs=(tokens, P(("y", "x", "core", "dp"), None), tokens, P()) + five * 3,
        out_specs=(P(),) + five * 4 + (tokens, tokens),
        check_vma=False,
    )
```

```python
import functools
import math

import jax
import jax.numpy as jnp
import numpy as np
from jax import lax
from jax.experimental import pallas as pl
from jax.experimental.pallas import tpu as pltpu
from jax.sharding import Mesh
from jax.sharding import PartitionSpec as P

D = 1024
FF = 4096
PAD_ROWS = 16

NEG_FILL = -1000000000.0
ADAM_EPS = 1e-08
WEIGHT_DECAY = 0.05
AXES = ("seq", "y", "x", "core", "dp")
SHARD = ("seq", "y", "x", "core")

BF = jnp.bfloat16
F32 = jnp.float32
MESH_ID = pl.DeviceIdType.MESH


class Wires:
    def __init__(self, send_sem, recv_sem):
        self.send_sem, self.recv_sem, self.count, self.sent = send_sem, recv_sem, 0, []

    def make(self, src, dst, to):
        cp = pltpu.make_async_remote_copy(
            src_ref=src, dst_ref=dst, send_sem=self.send_sem.at[self.count], recv_sem=self.recv_sem.at[self.count],
            device_id=to, device_id_type=MESH_ID)
        self.count += 1
        return cp

    def send(self, src, dst, to):
        cp = self.make(src, dst, to)
        cp.start()
        self.sent.append(cp)
        return cp

    def finish(self):
        for cp in self.sent:
            cp.wait_send()


def greet(peers, crossing_peer, apart):
    barrier = pltpu.get_barrier_semaphore()
    for peer in peers:
        pl.semaphore_signal(barrier, inc=1, device_id=peer, device_id_type=MESH_ID)

    @pl.when(apart)
    def _():
        pl.semaphore_signal(barrier, inc=1, device_id=crossing_peer, device_id_type=MESH_ID)

    pl.semaphore_wait(barrier, len(peers) + jnp.where(apart, 1, 0))


def add_all(first, *others):
    total = first.astype(F32)
    for other in others:
        total = total + other.astype(F32)
    return total


def plane_moves(wires, to_x, to_y):
    nx, ny = len(to_x), len(to_y)

    def spread(piece_at, kz, first):
        got = {}
        for k in range(1, nx):
            got[0, k] = wires.send(piece_at(kz, 0, 0), piece_at(kz, 0, 0, k, "x"), to_x[k])
        for k in range(1, ny):
            got[k, 0] = wires.send(piece_at(kz, 0, 0), piece_at(kz, 0, 0, k, "y"), to_y[k])
        return got

    def forward(piece_at, kz, first, got):
        if first == "x":
            for kx in range(1, nx):
                got[0, kx].wait_recv()
                for ky in range(1, ny):
                    got[ky, kx] = wires.send(piece_at(kz, 0, kx), piece_at(kz, 0, kx, ky, "y"), to_y[ky])
            for ky in range(1, ny):
                got[ky, 0].wait_recv()
        else:
            for ky in range(1, ny):
                got[ky, 0].wait_recv()
                for kx in range(1, nx):
                    got[ky, kx] = wires.send(piece_at(kz, ky, 0), piece_at(kz, ky, 0, kx, "x"), to_x[kx])
            for kx in range(1, nx):
                got[0, kx].wait_recv()

    def settle(got):
        for (ky, kx), cp in got.items():
            if ky > 0 and kx > 0:
                cp.wait_recv()

    return spread, forward, settle


def by_offset(store, own):
    def piece_at(kz, ky, kx, k=0, axis=""):
        if k == 0 and ky == 0 and kx == 0:
            return own
        return store.at[ky + (k if axis == "y" else 0), kx + (k if axis == "x" else 0)]

    return piece_at

BF=jnp.bfloat16; F32=jnp.float32
def dot(a, b, dims=(((1,), (0,)), ((), ()))):
    return lax.dot_general(a, b, dims, preferred_element_type=F32)
NT=(((1,),(1,)),((),()))
TN=(((0,),(0,)),((),()))
ANY=pl.BlockSpec(memory_space=pl.ANY)
VM=pl.BlockSpec(memory_space=pltpu.VMEM)
SM=pl.BlockSpec(memory_space=pltpu.SMEM)

def gelu_both(u):
    c0=math.sqrt(2/math.pi)
    sq=u*u
    t=jnp.tanh(u*(c0+(c0*0.044715)*sq))
    half=0.5+0.5*t
    value=u*half
    slope=half+(0.5*u)*(1.0-t*t)*(c0+(3*c0*0.044715)*sq)
    return value,slope

def mlp_kernel(keys,keys_b,ny,nx,*refs,gtile):
    nk=len(keys)
    h2_ref,g_ref,bu_ref=refs[:3]
    planes=(refs[3:5],refs[5:7])
    o=7
    order=(keys,keys_b)
    ga,gb=refs[o:o+nk],refs[o+nk:o+2*nk]
    yown_ref,yoth_ref,dh_ref,gbu_ref,ra_ref,rb_ref=refs[o+2*nk:o+2*nk+6]
    w,dd,a_all,du_all,y_acc,dh_acc,g_out,wsem,gsem,send_sem,recv_sem=refs[o+2*nk+6:]
    h,y,x,c,_=(lax.axis_index(a) for a in AXES)
    to_x=[{"x":lax.rem(x+k,nx)} for k in range(nx)]
    to_y=[{"y":lax.rem(y+k,ny)} for k in range(ny)]
    wires=Wires(send_sem,recv_sem)
    moves=[]
    for ki,((ky,_),(_,kx)) in enumerate(zip(keys,keys_b)):
        cps=[]
        if ky>0: cps.append(wires.make(ga[ki],ra_ref.at[ky-1,keys[ki][1]],to_y[ky]))
        ky=keys_b[ki][0]
        if kx>0: cps.append(wires.make(gb[ki],rb_ref.at[kx-1,ky],to_x[kx]))
        moves.append(cps)
    barrier=pltpu.get_barrier_semaphore()
    for peer in to_x[1:]+to_y[1:]:
        pl.semaphore_signal(barrier,inc=1,device_id=peer,device_id_type=MESH_ID)
    _,images,half,feat=g_ref.shape
    hid=planes[0][0].shape[3]
    width=4*hid
    padded=h2_ref.shape[0]//(2*images)
    blocks=2*images

    def load(i,slot,go):
        for ki in range(nk):
            @pl.when(i==ki)
            def _():
                for kz in range(2):
                    for ud in range(2):
                        for ab in range(2):
                            cp=pltpu.make_async_copy(planes[kz][ab].at[order[ab][ki][0],order[ab][ki][1],ud],w.at[slot,ud,pl.ds((kz*2+ab)*hid,hid)],wsem.at[slot,kz*4+ud*2+ab])
                            cp.start() if go else cp.wait()
    def save(i,go):
        for ki in range(nk):
            @pl.when(i==ki)
            def _():
                for kz in range(2):
                    for ud in range(2):
                        for ab,dst in enumerate((ga[ki],gb[ki])):
                            cp=pltpu.make_async_copy(g_out.at[ud,pl.ds((kz*2+ab)*hid,hid)],dst.at[kz,ud],gsem.at[kz*4+ud*2+ab])
                            cp.start() if go else cp.wait()
    load(0,0,True)
    gbu_ref[...]=jnp.zeros_like(gbu_ref)
    for i in range(images):
        for s in range(2):
            r=(2*i+s)*padded
            tail=padded-16
            dd[r+tail:r+padded,:]=jnp.zeros((16,feat),BF)
            dd[r:r+half,:]=g_ref[s,i]
    pl.semaphore_wait(barrier,nx+ny-2)
    def step(i,_):
        slot=lax.rem(i,2)
        @pl.when(i>0)
        def _(): save(i-1,False)
        for ki,cps in enumerate(moves):
            if cps:
                @pl.when(i==ki+1)
                def _():
                    for cp in cps: cp.start()
        load(i,slot,False)
        @pl.when(i+1<nk)
        def _(): load(i+1,1-slot,True)
        rows=[]
        for kz in range(2):
            for ab in range(2):
                row=jnp.int32(0)
                for ki,(ky,kx) in enumerate(order[ab]):
                    here=(((lax.rem(h+kz,2)*ny+lax.rem(y+ky,ny))*nx+lax.rem(x+kx,nx))*2+c)*2+ab
                    row=jnp.where(i==ki,here,row)
                rows.append(row)
        bias=jnp.concatenate([bu_ref[pl.ds(r,1),:] for r in rows],axis=1)
        wu=w.at[slot,0]; wd=w.at[slot,1]
        def tokens(b,sums):
            r=pl.ds(pl.multiple_of(b*padded,16),padded)
            u=dot(h2_ref[r,:],wu[...],NT)+bias
            value,slope=gelu_both(u)
            a=value.astype(BF)
            a_all[r,:]=a
            dg=dot(dd[r,:],wd[...],NT)
            du=(dg*slope).astype(BF)
            du_all[r,:]=du
            ynew=dot(a,wd[...]); dnew=dot(du,wu[...])
            @pl.when(i==0)
            def _():
                y_acc[r,:]=ynew; dh_acc[r,:]=dnew
            @pl.when(i>0)
            def _():
                y_acc[r,:]+=ynew; dh_acc[r,:]+=dnew
            return sums+jnp.sum(du.astype(F32),axis=0,keepdims=True)
        sums=lax.fori_loop(0,blocks,tokens,jnp.zeros((1,width),F32))
        for q,row in enumerate(rows):
            gbu_ref[pl.ds(row,1),:]=sums[:,q*hid:(q+1)*hid]
        for t in range(0,width,gtile):
            g_out[1,t:t+gtile,:]=dot(a_all[:,t:t+gtile],dd[...],TN).astype(BF)
            g_out[0,t:t+gtile,:]=dot(du_all[:,t:t+gtile],h2_ref[...],TN).astype(BF)
        save(i,True)
        return 0
    lax.fori_loop(0,nk,step,0)
    for i in range(images):
        r=2*i*padded
        yown_ref[i]=y_acc[r:r+padded,:]
        yoth_ref[i]=y_acc[r+padded:r+2*padded,:].astype(BF)
    dh_ref[...]=dh_acc[...].astype(BF)
    save(nk-1,False)
    for cps in moves:
        for cp in cps:
            cp.wait_recv()
            cp.wait_send()

def mlp(ny,nx,h2,g_both,bu_rows,own_a,own_b,oth_a,oth_b,gtile=256):
    keys=sorted(((ky,kx) for ky in range(ny) for kx in range(nx)),reverse=True); nk=len(keys)
    _,images,half,feat=g_both.shape
    keys_b=sorted(keys,key=lambda k:(k[1],k[0]),reverse=True)
    tokens=h2.shape[0]; padded=tokens//(2*images)
    ud,hid=own_a.shape[2:4]
    width=4*hid
    piece=jax.ShapeDtypeStruct((2,ud,hid,feat),BF)
    out=pl.pallas_call(functools.partial(mlp_kernel,keys,keys_b,ny,nx,gtile=min(gtile,width)),
        in_specs=[VM]*3+[ANY]*4,
        out_specs=[ANY]*(2*nk)+[VM]*4+[ANY]*2,
        out_shape=[piece]*(2*nk)+[jax.ShapeDtypeStruct((images,padded,feat),F32),jax.ShapeDtypeStruct((images,padded,feat),BF),
            jax.ShapeDtypeStruct((tokens,feat),BF),jax.ShapeDtypeStruct(bu_rows.shape,F32),
            jax.ShapeDtypeStruct((ny-1,nx,2,ud,hid,feat),BF),jax.ShapeDtypeStruct((nx-1,ny,2,ud,hid,feat),BF)],
        scratch_shapes=[pltpu.VMEM((2,2,width,feat),BF),pltpu.VMEM((tokens,feat),BF),pltpu.VMEM((tokens,width),BF),pltpu.VMEM((tokens,width),BF),
            pltpu.VMEM((tokens,feat),F32),pltpu.VMEM((tokens,feat),F32),pltpu.VMEM((2,width,feat),BF),
            pltpu.SemaphoreType.DMA((2,8)),pltpu.SemaphoreType.DMA((8,)),pltpu.SemaphoreType.DMA((2*nk,)),pltpu.SemaphoreType.DMA((2*nk,))],
        name="feed_forward",
        compiler_params=pltpu.CompilerParams(collective_id=3,has_side_effects=True,vmem_limit_bytes=60<<20),
        cost_estimate=pl.CostEstimate(flops=nk*6*2*tokens*feat*width,bytes_accessed=40<<20,transcendentals=nk*tokens*width),
    )(h2,g_both,bu_rows,own_a,own_b,oth_a,oth_b)
    return dict(zip(keys,out[:nk])),dict(zip(keys_b,out[nk:2*nk])),out[2*nk:]

HD=64; HALF_D=512

def head_operands(q,k,kb,scale):
    q=q.astype(F32)*scale; k=k.astype(F32); kb=kb.astype(F32)
    lane=lax.broadcasted_iota(jnp.int32,q.shape,1)
    low=lane<HD
    one=jnp.where((lane==0)|(lane==HD),1.0,0.0)
    qs=[jnp.where(low,q,one).astype(BF),jnp.where(low,one,q).astype(BF)]
    ks=[jnp.where(low,k,kb).astype(BF),jnp.where(low,kb,k).astype(BF)]
    return q,k,low,qs,ks

def attend_pair(q,k,v,kb):
    q,k,low,qs,ks=head_operands(q,k,kb,HD**-0.5)
    vt=v.astype(F32).T.astype(BF)
    outs=[]; sums=[]
    for j in range(2):
        s=dot(ks[j],qs[j],NT)
        m=jnp.max(s,axis=0,keepdims=True)
        e=jnp.exp(s-m)
        l=jnp.sum(e,axis=0,keepdims=True)
        o=dot(vt[j*HD:(j+1)*HD],e.astype(BF))
        outs.append(o*(1.0/l))
        sums.append(m+jnp.log(l))
    return jnp.concatenate(outs,axis=0).T.astype(BF),sums

def attend_back_kernel(q_ref,k_ref,v_ref,kb_ref,o_ref,g_ref,lse_ref,out_ref,sum_ref,*,pairs,chunk):
    p=pl.program_id(1)
    @pl.when((pl.program_id(0)==0)&(p==0))
    def _(): sum_ref[...]=jnp.zeros_like(sum_ref)
    scale=HD**-0.5
    q,k,low,qs,ks=head_operands(q_ref[0],k_ref[0],kb_ref[0],scale)
    qb=q.astype(BF)
    kt=k.T.astype(BF)
    g=g_ref[0]; gf=g.astype(F32)
    prod=(gf*o_ref[0].astype(F32)).T
    v=v_ref[0]
    rows=q.shape[0]
    dqs=[];dks=[];dvs=[]
    for j in range(2):
        gj=(jnp.where(low,gf,0.0) if j==0 else jnp.where(low,0.0,gf)).astype(BF)
        delta=jnp.sum(prod[j*HD:(j+1)*HD],axis=0,keepdims=True)
        lse=lse_ref[0,0,j:j+1,:]
        dq=None; dk=[]; dv=[]
        for r in range(0,rows,chunk):
            s=dot(ks[j][r:r+chunk],qs[j],NT)
            pr=jnp.exp(s-lse)
            dp=dot(v[r:r+chunk],gj,NT)
            ds=(pr*(dp-delta)).astype(BF)
            dv.append(dot(pr.astype(BF),g))
            dk.append(dot(ds,qb))
            t=dot(kt[j*HD:(j+1)*HD,r:r+chunk],ds) if chunk==rows else dot(k[r:r+chunk].astype(BF),ds,TN)[j*HD:(j+1)*HD]
            dq=t if dq is None else dq+t
        dqs.append(dq)
        dks.append(jnp.concatenate(dk,axis=0) if len(dk)>1 else dk[0]); dvs.append(jnp.concatenate(dv,axis=0) if len(dv)>1 else dv[0])
    parts=((jnp.concatenate(dqs,axis=0)*scale).T.astype(BF),jnp.where(low,dks[0],dks[1]).astype(BF),jnp.where(low,dvs[0],dvs[1]).astype(BF))
    for t,part in enumerate(parts):
        at=pl.ds(pl.multiple_of((t*pairs+p)*128,128),128)
        out_ref[0,:,at]=part
        sum_ref[0:1,at]+=jnp.sum(part.astype(F32),axis=0,keepdims=True)

def attend_back(qkv,kbias,mixed,grad,lse,chunk=None):
    n,rows,w=qkv.shape; pairs=w//3//128
    chunk=chunk or rows
    blk=lambda off: pl.BlockSpec((1,rows,128),lambda i,p: (i,0,off+p))
    return pl.pallas_call(functools.partial(attend_back_kernel,pairs=pairs,chunk=chunk),grid=(n,pairs),
        in_specs=[blk(0),blk(pairs),blk(2*pairs),pl.BlockSpec((1,rows,128),lambda i,p:(i,0,0)),blk(0),blk(0),pl.BlockSpec((1,1,8,rows),lambda i,p:(i,p,0,0))],
        out_specs=[pl.BlockSpec((1,rows,w),lambda i,p:(i,0,0)),pl.BlockSpec((8,w),lambda i,p:(0,0))],
        out_shape=[jax.ShapeDtypeStruct((n,rows,w),BF),jax.ShapeDtypeStruct((8,w),F32)],
        name="attend_back",
        compiler_params=pltpu.CompilerParams(vmem_limit_bytes=50<<20),
        cost_estimate=pl.CostEstimate(flops=n*pairs*20*rows*rows*128,bytes_accessed=n*rows*w*5,transcendentals=n*pairs*2*rows*rows),
    )(qkv,qkv,qkv,kbias,mixed,grad,lse)

NORM_EPS=1e-6
def norm_parts(values):
    center = values - jnp.mean(values, axis=-1, keepdims=True)
    inverse = lax.rsqrt(jnp.mean(center * center, axis=-1, keepdims=True) + NORM_EPS)
    return center * inverse, inverse

def norm_back(values, gain, grad):
    normed, inverse = norm_parts(values)
    scaled = grad * gain
    mean_one = jnp.mean(scaled, axis=-1, keepdims=True)
    mean_two = jnp.mean(scaled * normed, axis=-1, keepdims=True)
    return (scaled - mean_one - normed * mean_two) * inverse, grad * normed

def wide_rows(buf,block):
    n=block.shape[0]; total=buf.shape[0]
    buf[total-16:,:]=jnp.zeros((16,buf.shape[1]),F32)
    buf[0:n,:]=block.astype(F32)
    return buf[...]

def middle_back_kernel(x2_ref,da_ref,db_ref,go_ref,gt_ref,mix_ref,w_ref,gain_ref,dx_ref,dat_ref,gw_ref,sum_ref,buf,acc):
    i=pl.program_id(0)
    @pl.when(i==0)
    def _():
        acc[...]=jnp.zeros_like(acc); sum_ref[...]=jnp.zeros_like(sum_ref)
    for s,src in enumerate((go_ref,gt_ref)):
        dd=wide_rows(buf.at[s],src[0,0])
        grad=da_ref[0,s].astype(F32)+db_ref[0,1-s].astype(F32)
        dx,gg=norm_back(x2_ref[0,s],gain_ref[...],grad)
        dx=dx+dd
        dob=dx.astype(BF)
        if s==0:
            dx_ref[0]=dx
            for r,t in enumerate((gg,grad,dob.astype(F32),dd)):
                sum_ref[r:r+1,:]+=jnp.sum(t,axis=0,keepdims=True)
        dat_ref[0,s]=dot(dob,w_ref[...],NT).astype(BF)
        acc[...]+=dot(mix_ref[0,s],dob,TN)
    @pl.when(i==pl.num_programs(0)-1)
    def _(): gw_ref[...]=acc[...].astype(BF)

def middle_back(x2,dh_own,dh_oth,g_both,mixed,w_own,gain):
    _,n,half,feat=g_both.shape
    _,_,padded,width=mixed.shape
    tok=lambda s: pl.BlockSpec((1,1,half,feat),lambda i:(s,i,0,0))
    mix=pl.BlockSpec((1,2,padded,width),lambda i:(i,0,0,0))
    big=pl.BlockSpec((1,2,padded,feat),lambda i:(i,0,0,0))
    full=pl.BlockSpec((width,feat),lambda i:(0,0))
    return pl.pallas_call(middle_back_kernel,grid=(n,),
        in_specs=[big,big,big,tok(0),tok(1),mix,full,pl.BlockSpec((1,feat),lambda i:(0,0))],
        out_specs=[pl.BlockSpec((1,padded,feat),lambda i:(i,0,0)),mix,full,pl.BlockSpec((8,feat),lambda i:(0,0))],
        out_shape=[jax.ShapeDtypeStruct((n,padded,feat),F32),jax.ShapeDtypeStruct(mixed.shape,BF),jax.ShapeDtypeStruct((width,feat),BF),jax.ShapeDtypeStruct((8,feat),F32)],
        scratch_shapes=[pltpu.VMEM((2,padded,feat),F32),pltpu.VMEM((width,feat),F32)],name="middle_back",
        compiler_params=pltpu.CompilerParams(vmem_limit_bytes=56<<20),
        cost_estimate=pl.CostEstimate(flops=n*8*padded*feat*width,bytes_accessed=30<<20,transcendentals=0),
    )(x2,dh_own,dh_oth,g_both,g_both,mixed,w_own,gain[None])


def tail_kernel(ny, nx, *refs):
    h1_ref, dqkv_ref, go_ref, x_ref, dx_ref, gain_ref, vec_ref, w = refs[:8]
    keep_ref, pass_ref = refs[8:10]
    o = 10
    mine_ref, theirs_ref, so_ref, sf_ref, ig_ref, vout_ref, norm_ref = refs[o:o + 7]
    (grad, ra1, ra2, rb1, rb2, sa, sb, oa1, oa2, ob1, ob2, ta, tb, osum, ocross, ocore, odp, ofin,
     fpart, fdp, frecv, isum, ipart, irecv, idp, ifin,
     buf, give, got, stage, vrecv, nrecv, nval, send_sem, recv_sem) = refs[o + 7:]
    h, y, x, c, l = (lax.axis_index(a) for a in AXES)
    _, images, half, feat = x_ref.shape
    padded = dx_ref.shape[1]
    rows = grad.shape[4]
    apart = h != c
    cross = {"seq": 1 - h, "core": 1 - c}
    to_core, to_seq, to_dp = {"core": 1 - c}, {"seq": 1 - h}, {"dp": 1 - l}
    to_x = [{"x": lax.rem(x + k, nx)} for k in range(nx)]
    to_y = [{"y": lax.rem(y + k, ny)} for k in range(ny)]
    yy = [lax.rem(y + k, ny) for k in range(ny)]
    xx = [lax.rem(x + k, nx) for k in range(nx)]
    zz = [h, 1 - h]
    wires = Wires(send_sem, recv_sem)
    greet([to_core, to_seq, to_dp] + to_x[1:] + to_y[1:], cross, apart)

    fd = wires.send(pass_ref, fdp, to_dp)
    oa_got = [[wires.send(go_ref.at[yy[ky], xx[kx], h], oa1.at[ky - 1, kx], to_y[ky]) for kx in range(nx)] for ky in range(1, ny)]
    ob_got = [[wires.send(go_ref.at[yy[ky], xx[kx], 1 - h], ob1.at[kx - 1, ky], to_x[kx]) for ky in range(ny)] for kx in range(1, nx)]
    width = nx * 2 * rows
    ia_got, ib_got = [], []
    for ky in range(ny - 1, -1, -1):
        for kz in range(2):
            col = pl.multiple_of((zz[kz] * ny + yy[ky]) * width, 128)
            t = dot(h1_ref[:, pl.ds(col, width)], dqkv_ref[...], TN).astype(BF)
            for q in range(nx):
                for core in range(2):
                    r = (q * 2 + core) * rows
                    grad[zz[kz], yy[ky], q, core] = t[r:r + rows]
            for kx in range(nx):
                if ky > 0:
                    ia_got.append(wires.send(grad.at[zz[kz], yy[ky], xx[kx], c], ra1.at[ky - 1, kz, kx], to_y[ky]))
                if kx > 0:
                    ib_got.append(wires.send(grad.at[zz[kz], yy[ky], xx[kx], 1 - c], rb1.at[kx - 1, kz, ky], to_x[kx]))
    dh_got = []
    for i in range(images):
        r = (2 * i + 1) * padded
        give[i] = dot(dqkv_ref[r:r + padded, :], w[...], NT).astype(BF)
        dh_got.append(wires.send(give.at[i], got.at[i], to_core))
    sum_gain, sum_shift = jnp.zeros((1, feat), F32), jnp.zeros((1, feat), F32)
    crossing_copies = [wires.make(stage.at[i], ig_ref.at[i], cross) for i in range(images)]

    def input_back(i, sum_gain, sum_shift):
        r = 2 * i * padded
        own = dot(dqkv_ref[r:r + padded, :], w[...], NT)
        dh_got[i].wait_recv()
        g = own + got[i].astype(F32)
        dx, gg = norm_back(wide_rows(buf, x_ref[0, i]), gain_ref[...], g)
        stage[i] = (dx + dx_ref[i]).astype(BF)[:half]

        if i == 0:
            @pl.when(apart)
            def _():
                crossing_copies[i].start()

        @pl.when(jnp.logical_not(apart))
        def _():
            ig_ref[i] = stage[i]

        return sum_gain + jnp.sum(gg, axis=0, keepdims=True), sum_shift + jnp.sum(g, axis=0, keepdims=True)

    for i in range(images):
        sum_gain, sum_shift = input_back(i, sum_gain, sum_shift)
    fd.wait_recv()
    fpart[...] = add_all(keep_ref[...], fdp[...]).astype(BF)
    fs = wires.send(fpart.at[1], frecv, to_seq)
    for row in oa_got + ob_got:
        for cp in row:
            cp.wait_recv()
    o_got = []
    for kx in range(1, nx):
        ta[kx - 1] = add_all(go_ref[y, xx[kx], h], *(oa1[k, kx] for k in range(ny - 1))).astype(BF)
        o_got.append(wires.send(ta.at[kx - 1], oa2.at[kx - 1], to_x[kx]))
    for ky in range(1, ny):
        tb[ky - 1] = add_all(go_ref[yy[ky], x, 1 - h], *(ob1[k, ky] for k in range(nx - 1))).astype(BF)
        o_got.append(wires.send(tb.at[ky - 1], ob2.at[ky - 1], to_y[ky]))

    for cp in ia_got + ib_got:
        cp.wait_recv()
    i_got = []
    for kz in range(2):
        for kx in range(1, nx):
            sa[kx - 1, kz] = add_all(grad[zz[kz], y, xx[kx], c], *(ra1[k, kz, kx] for k in range(ny - 1))).astype(BF)
        for ky in range(1, ny):
            sb[ky - 1, kz] = add_all(grad[zz[kz], yy[ky], x, 1 - c], *(rb1[k, kz, ky] for k in range(nx - 1))).astype(BF)
    for kx in range(1, nx):
        i_got.append(wires.send(sa.at[kx - 1], ra2.at[kx - 1], to_x[kx]))
    for ky in range(1, ny):
        i_got.append(wires.send(sb.at[ky - 1], rb2.at[ky - 1], to_y[ky]))
    vout_ref[...] = vec_ref[...]
    for q in range(feat // 128):
        vout_ref[q:q + 1, :] = sum_gain[:, q * 128:(q + 1) * 128]
        vout_ref[feat // 128 + q:feat // 128 + q + 1, :] = sum_shift[:, q * 128:(q + 1) * 128]
    rounds = [[to_core], to_x[1:], to_y[1:], [to_seq], [to_dp]]
    slot = [0]

    def start_round(value, landing, peers):
        first = slot[0]
        cps = [wires.send(value, landing.at[first + k], peer) for k, peer in enumerate(peers)]
        slot[0] += len(peers)
        return first, cps

    def end_round(value_ref, landing, started):
        first, cps = started
        for cp in cps:
            cp.wait_recv()
        for cp in cps:
            cp.wait_send()
        wires.sent = [cp for cp in wires.sent if all(cp is not other for other in cps)]
        value_ref[...] = add_all(value_ref[...], *(landing[first + k] for k in range(len(cps))))

    vec_round = start_round(vout_ref, vrecv, rounds[0])
    for cp in i_got:
        cp.wait_recv()
    for kz in range(2):
        isum[0, kz] = add_all(grad[zz[kz], y, x, c], *(ra1[k, kz, 0] for k in range(ny - 1)), *(ra2[k, kz] for k in range(nx - 1))).astype(BF)
        isum[1, kz] = add_all(grad[zz[kz], y, x, 1 - c], *(rb1[k, kz, 0] for k in range(nx - 1)), *(rb2[k, kz] for k in range(ny - 1))).astype(BF)
    idd = wires.send(isum.at[1 - l], idp, to_dp)
    for cp in o_got:
        cp.wait_recv()
    osum[0] = add_all(go_ref[y, x, h], *(oa1[k, 0] for k in range(ny - 1)), *(oa2[k] for k in range(nx - 1))).astype(BF)
    osum[1] = add_all(go_ref[y, x, 1 - h], *(ob1[k, 0] for k in range(nx - 1)), *(ob2[k] for k in range(ny - 1))).astype(BF)
    out_cross = wires.make(osum, ocross, cross)

    @pl.when(apart)
    def _():
        out_cross.start()

    @pl.when(jnp.logical_not(apart))
    def _():
        ocross[...] = osum[...]

    end_round(vout_ref, vrecv, vec_round)
    vec_round = start_round(vout_ref, vrecv, rounds[1])
    idd.wait_recv()
    ipart[...] = add_all(isum[l], idp[...]).astype(BF)
    is_ = wires.send(ipart.at[1], irecv, to_seq)

    @pl.when(apart)
    def _():
        for cp in crossing_copies[1:]:
            cp.start()

    end_round(vout_ref, vrecv, vec_round)
    vec_round = start_round(vout_ref, vrecv, rounds[2])

    @pl.when(apart)
    def _():
        out_cross.wait_recv()

    oc = wires.send(ocross.at[1], ocore, to_core)
    fs.wait_recv()
    sf_ref[l] = add_all(fpart[0], frecv[...]).astype(BF)
    ff_last = wires.send(sf_ref.at[l], sf_ref.at[l], to_dp)
    end_round(vout_ref, vrecv, vec_round)
    vec_round = start_round(vout_ref, vrecv, rounds[3])
    oc.wait_recv()
    ofin[...] = add_all(ocross[0], ocore[...]).astype(BF)
    od = wires.send(ofin, odp, to_dp)
    is_.wait_recv()
    ifin[l] = add_all(ipart[0], irecv[...]).astype(BF)
    in_last = wires.send(ifin.at[l], ifin.at[l], to_dp)
    end_round(vout_ref, vrecv, vec_round)
    vec_round = start_round(vout_ref, vrecv, rounds[4])
    in_last.wait_recv()
    ic = wires.send(ifin.at[1], theirs_ref, to_core)
    mine_ref[...] = ifin[0]
    od.wait_recv()
    so_ref[...] = add_all(ofin[...], odp[...]).astype(BF)
    end_round(vout_ref, vrecv, vec_round)
    ff_last.wait_recv()

    def squares(value):
        value = value.astype(F32)
        return jnp.sum(jnp.sum(value * value, axis=0, keepdims=True), axis=1, keepdims=True)

    shard = ((h * ny + y) * nx + x) * 2 + c
    v = vout_ref[...]
    place = lax.broadcasted_iota(jnp.int32, v.shape, 0) * 128 + lax.broadcasted_iota(jnp.int32, v.shape, 1)
    share = v.shape[0] * 128 // (4 * ny * nx)
    v = jnp.where((place >= shard * share) & (place < (shard + 1) * share), v, 0.0)
    total = squares(v) + squares(so_ref[...]) + squares(mine_ref[...])
    for ab in range(2):
        for ud in range(2):
            total = total + squares(sf_ref[ab, ud])
    ic.wait_recv()
    total = total + squares(theirs_ref[...])
    nval[...] = jnp.broadcast_to(total, nval.shape)
    slot[0] = 0
    for peers in rounds[:4]:
        end_round(nval, nrecv, start_round(nval, nrecv, peers))
    norm_ref[...] = jnp.sqrt(nval[...])

    @pl.when(apart)
    def _():
        for cp in crossing_copies:
            cp.wait_recv()
        for cp in crossing_copies:
            cp.wait_send()
        out_cross.wait_send()

    wires.finish()


def tail_stage(h1, dqkv, g_out, x_own, dx2, gain, vec, w, keep, give, ny, nx):
    tokens, feat = h1.shape
    width = dqkv.shape[1]
    rows = feat // (4 * ny * nx)
    rows_o = g_out.shape[3]
    _, images, half, _ = x_own.shape
    padded = dx2.shape[1]
    _, ud, hid, _ = keep.shape
    ma, mb = max(ny - 1, 1), max(nx - 1, 1)
    piece, out_piece, ff = (rows, width), (rows_o, feat), (ud, hid, feat)
    peers = 4 + nx - 1 + ny - 1
    many = 200 + 32 * ny * nx
    V = lambda *s: pltpu.VMEM(s, BF)
    scratch = [
        V(2, ny, nx, 2, *piece),
        V(ny - 1, 2, nx, *piece), V(nx - 1, 2, *piece), V(nx - 1, 2, ny, *piece), V(ny - 1, 2, *piece),
        V(nx - 1, 2, *piece), V(ny - 1, 2, *piece),
        V(ny - 1, nx, *out_piece), V(nx - 1, *out_piece), V(nx - 1, ny, *out_piece), V(ny - 1, *out_piece),
        V(nx - 1, *out_piece), V(ny - 1, *out_piece),
        V(2, *out_piece), V(2, *out_piece), V(*out_piece), V(*out_piece), V(*out_piece),
        V(2, *ff), V(2, *ff), V(*ff),
        V(2, 2, *piece), V(2, *piece), V(*piece), V(2, *piece), V(2, *piece),
        pltpu.VMEM((padded, feat), F32), V(images, padded, feat), V(images, padded, feat), V(images, half, feat),
        pltpu.VMEM((peers,) + vec.shape, F32), pltpu.VMEM((peers, 8, 128), F32), pltpu.VMEM((8, 128), F32),
        pltpu.SemaphoreType.DMA((many,)), pltpu.SemaphoreType.DMA((many,)),
    ]
    return pl.pallas_call(
        functools.partial(tail_kernel, ny, nx),
        in_specs=[VM] * 10,
        out_specs=[VM] * 7,
        out_shape=[
            jax.ShapeDtypeStruct(piece, BF), jax.ShapeDtypeStruct(piece, BF), jax.ShapeDtypeStruct(out_piece, BF),
            jax.ShapeDtypeStruct((2,) + ff, BF), jax.ShapeDtypeStruct(x_own.shape[1:], BF),
            jax.ShapeDtypeStruct(vec.shape, F32), jax.ShapeDtypeStruct((8, 128), F32),
        ],
        scratch_shapes=scratch,
        name="tail_stage",
        compiler_params=pltpu.CompilerParams(collective_id=1, has_side_effects=True, vmem_limit_bytes=62 << 20),
        cost_estimate=pl.CostEstimate(flops=4 * tokens * feat * width, bytes_accessed=40 << 20, transcendentals=0),
    )(h1, dqkv, g_out, x_own, dx2, gain[None], vec, w, keep, give)

def head_kernel(ny, nx, *refs):
    (in_ref, out_ref, up_ref, down_ref, vec_ref, img_ref,
     h1_ref, qkv_ref, xb, w, my_out, other_out, fa, fb, near_ref, vfull,
     theirs, o_own, o_core, tmp, buf, xsem, csem, send_sem, recv_sem) = refs
    h, y, x, c, l = (lax.axis_index(a) for a in AXES)
    images, half, feat = img_ref.shape
    rows = in_ref.shape[0]
    width = w.shape[1]
    part = width // 3
    hid = up_ref.shape[0] // 2
    apart = h != c
    cross = {"seq": 1 - h, "core": 1 - c}
    to_core, to_seq, to_dp = {"core": 1 - c}, {"seq": 1 - h}, {"dp": 1 - l}
    inner, to_near = l != h, {"seq": 1 - h, "dp": 1 - l}
    to_x = [{"x": lax.rem(x + nx - k, nx)} for k in range(nx)]
    to_y = [{"y": lax.rem(y + ny - k, ny)} for k in range(ny)]
    yy = [lax.rem(y + k, ny) for k in range(ny)]
    xx = [lax.rem(x + k, nx) for k in range(nx)]
    zz = [h, 1 - h]
    wires = Wires(send_sem, recv_sem)
    barrier = pltpu.get_barrier_semaphore()
    peers = [to_core, to_seq, to_dp] + to_x[1:] + to_y[1:]
    for peer in peers:
        pl.semaphore_signal(barrier, inc=1, device_id=peer, device_id_type=MESH_ID)

    @pl.when(apart)
    def _():
        pl.semaphore_signal(barrier, inc=1, device_id=cross, device_id_type=MESH_ID)

    @pl.when(inner)
    def _():
        pl.semaphore_signal(barrier, inc=1, device_id=to_near, device_id_type=MESH_ID)

    local_images = pltpu.make_async_copy(img_ref, xb.at[0], xsem)

    @pl.when(jnp.logical_not(apart))
    def _():
        local_images.start()

    def slot(z, yi, xi, core):
        return w.at[pl.ds(pl.multiple_of((((z * ny + yi) * nx + xi) * 2 + core) * rows, 16), rows)]

    mine = slot(h, y, x, c)
    for t in range(3):
        mine[:, t * part:(t + 1) * part] = in_ref[:, pl.ds(pl.multiple_of(t * 2 * part + c * part, 128), part)].astype(BF)
        theirs[:, t * part:(t + 1) * part] = in_ref[:, pl.ds(pl.multiple_of(t * 2 * part + (1 - c) * part, 128), part)].astype(BF)
    vfull[h, y, x, c] = vec_ref[...].astype(BF).astype(F32)
    o_own[...] = out_ref[...].astype(BF)
    pl.semaphore_wait(barrier, len(peers) + jnp.where(apart, 1, 0) + jnp.where(inner, 1, 0))

    spread, forward, settle = plane_moves(wires, to_x, to_y)

    def in_a(kz, ky, kx, *_):
        return slot(zz[kz], yy[ky], xx[kx], c)

    def in_b(kz, ky, kx, *_):
        return slot(zz[kz], yy[ky], xx[kx], 1 - c)

    def out_a(kz, ky, kx, *_):
        return my_out.at[yy[ky], xx[kx], h]

    def out_b(kz, ky, kx, *_):
        return my_out.at[yy[ky], xx[kx], 1 - h]

    ff_a, ff_b = by_offset(fa, tmp.at[0]), by_offset(fb, tmp.at[1])

    b_got = wires.send(theirs, slot(h, y, x, c), to_core)
    def across(core):
        own, other = slot(h, y, x, core), slot(1 - h, y, x, core)
        return wires.make(own, own, to_near), wires.make(other, other, to_dp)

    az, bz = across(c), across(1 - c)

    @pl.when(inner)
    def _():
        az[0].start()

    a0 = spread(in_a, 0, "x")
    vec_peers = [[to_core], to_x[1:], to_y[1:], [to_seq]]
    vec_at = [vfull.at[h, y, x, c], vfull.at[h, y, x], vfull.at[h, y], vfull.at[h]]

    def vec_send(r):
        return [wires.send(vec_at[r], vec_at[r], peer) for peer in vec_peers[r]]

    v = vec_send(0)
    oc = wires.send(o_own, o_core, to_core)
    xl = wires.make(img_ref, xb.at[1], to_core)

    @pl.when(jnp.logical_not(apart))
    def _():
        xl.start()

    b_got.wait_recv()

    @pl.when(inner)
    def _():
        bz[0].start()

    b0 = spread(in_b, 0, "y")
    for cp in v:
        cp.wait_recv()
    v = vec_send(1)
    for ab in range(2):
        tmp[ab, 0] = up_ref[ab * hid:(ab + 1) * hid, :].astype(BF)
        tmp[ab, 1] = down_ref[ab * hid:(ab + 1) * hid, :].astype(BF)
    keep = [
        pltpu.make_async_copy(tmp.at[0], fa.at[0, 0], csem.at[0]),
        pltpu.make_async_copy(tmp.at[1], fb.at[0, 0], csem.at[1]),
    ]
    for cp in keep:
        cp.start()
    for cp in v:
        cp.wait_recv()
    v = vec_send(2)
    forward(in_a, 0, "x", a0)
    forward(in_b, 0, "y", b0)
    oc.wait_recv()
    x_cross = [wires.make(img_ref.at[i], xb.at[0, i], cross) for i in range(images)]
    o_cross = [wires.make(o_own, my_out.at[y, x, 1 - h], cross), wires.make(o_core, my_out.at[y, x, h], cross)]

    @pl.when(apart)
    def _():
        for cp in o_cross:
            cp.start()

    @pl.when(jnp.logical_and(apart, jnp.logical_not(inner)))
    def _():
        x_cross[0].start()

    def arrive(pair):
        @pl.when(inner)
        def _():
            pair[0].wait_recv()
            pair[1].start()

        @pl.when(jnp.logical_not(inner))
        def _():
            pair[1].wait_recv()

    arrive(az)
    a1 = spread(in_a, 1, "x")
    arrive(bz)
    b1 = spread(in_b, 1, "y")
    for cp in v:
        cp.wait_recv()
    v = vec_send(3)

    @pl.when(jnp.logical_and(apart, inner))
    def _():
        x_cross[0].start()

    @pl.when(apart)
    def _():
        for cp in x_cross[1:]:
            cp.start()

    @pl.when(jnp.logical_not(apart))
    def _():
        my_out[y, x, h] = o_own[...]
        my_out[y, x, 1 - h] = o_core[...]
        local_images.wait()

    @pl.when(apart)
    def _():
        for cp in o_cross:
            cp.wait_recv()

    oa = spread(out_a, 0, "x")
    ob = spread(out_b, 0, "y")
    forward(in_a, 1, "x", a1)
    forward(in_b, 1, "y", b1)
    forward(out_a, 0, "x", oa)
    forward(out_b, 0, "y", ob)
    fa0 = spread(ff_a, 0, "x")
    fb0 = spread(ff_b, 0, "y")
    for got in (a0, b0, a1, b1):
        settle(got)
    for cp in v:
        cp.wait_recv()

    def row(start, count):
        per = vec_ref.shape[1]
        pieces, at = [], start
        while at < start + count:
            s, r = at // per, at % per
            n = min(per - r, start + count - at)
            xs = s // 2
            pieces.append(vfull[xs // (nx * ny), xs // nx % ny, xs % nx, s % 2][:, r:r + n])
            at += n
        return pieces[0] if len(pieces) == 1 else jnp.concatenate(pieces, axis=1)

    gain, shift_row = row(0, feat), row(feat, feat)
    q_row, v_row = row(2 * feat, feat), row(3 * feat, feat)
    q_row = jnp.where(c == 0, q_row[:, :part], q_row[:, part:])
    v_row = jnp.where(c == 0, v_row[:, :part], v_row[:, part:])
    bias = jnp.concatenate([q_row, jnp.zeros((1, part), F32), v_row], axis=1)

    def project(i, s):
        value = wide_rows(buf, xb[s, i])
        normed = (norm_parts(value)[0] * gain + shift_row).astype(BF)
        h1_ref[i, s] = normed
        qkv_ref[i, s] = (dot(normed, w[...]) + bias).astype(BF)

    near = jnp.where(apart, 1, 0)

    @pl.when(apart)
    def _():
        xl.wait_recv()

    def near_step(i, carry):
        project(i, near)
        return carry

    lax.fori_loop(0, images, near_step, 0)

    forward(ff_a, 0, "x", fa0)
    forward(ff_b, 0, "y", fb0)
    near_ff = [wires.make(tmp.at[ab], near_ref.at[ab], to_near) for ab in range(2)]
    x_core = [wires.make(xb.at[0, i], xb.at[1, i], to_core) for i in range(images)]
    for i in range(images):
        @pl.when(apart)
        def _():
            x_cross[i].wait_recv()
            x_core[i].start()

        @pl.when(jnp.logical_not(apart))
        def _():
            x_core[i].wait_recv()

        if i == max(images - 2, 0):
            @pl.when(inner)
            def _():
                near_ff[0].start()

        if i == images - 1:
            @pl.when(inner)
            def _():
                near_ff[1].start()

        project(i, 1 - near)
        if i == 0:
            settle(oa)
            settle(ob)
            other = wires.send(my_out, other_out, to_core)
    other.wait_recv()
    settle(fa0)
    settle(fb0)

    @pl.when(apart)
    def _():
        for cp in x_cross + o_cross + x_core:
            cp.wait_send()

    @pl.when(jnp.logical_not(apart))
    def _():
        xl.wait_send()

    @pl.when(inner)
    def _():
        for cp in near_ff:
            cp.wait_recv()
        for cp in (*az, *bz, *near_ff):
            cp.wait_send()

    for cp in keep:
        cp.wait()
    wires.finish()


def head_stage(in_w, out_w, up_w, down_w, vec, images, padded, ny, nx):
    n, half, feat = images.shape
    rows, rows_out, rows_ff = in_w.shape[0], out_w.shape[0], up_w.shape[0]
    width = in_w.shape[1] // 2
    hid = rows_ff // 2
    many = 60 + 24 * ny * nx
    S = jax.ShapeDtypeStruct
    return pl.pallas_call(
        functools.partial(head_kernel, ny, nx),
        in_specs=[VM] * 5 + [ANY],
        out_specs=[VM] * 6 + [ANY] * 3 + [VM],
        out_shape=[
            S((n, 2, padded, feat), BF), S((n, 2, padded, width), BF), S((2, n, half, feat), BF), S((feat, width), BF),
            S((ny, nx, 2, rows_out, feat), BF), S((ny, nx, 2, rows_out, feat), BF),
            S((ny, nx, 2, hid, feat), BF), S((ny, nx, 2, hid, feat), BF), S((2, 2, hid, feat), BF),
            S((2, ny, nx, 2, 1, vec.shape[1]), F32),
        ],
        scratch_shapes=[
            pltpu.VMEM((rows, width), BF), pltpu.VMEM((rows_out, feat), BF), pltpu.VMEM((rows_out, feat), BF),
            pltpu.VMEM((2, 2, hid, feat), BF), pltpu.VMEM((padded, feat), F32),
            pltpu.SemaphoreType.DMA(()), pltpu.SemaphoreType.DMA((3,)),
            pltpu.SemaphoreType.DMA((many,)), pltpu.SemaphoreType.DMA((many,)),
        ],
        name="head_stage",
        compiler_params=pltpu.CompilerParams(collective_id=2, has_side_effects=True, vmem_limit_bytes=60 << 20),
        cost_estimate=pl.CostEstimate(flops=n * 4 * padded * feat * width, bytes_accessed=40 << 20, transcendentals=0),
    )(in_w, out_w, up_w, down_w, vec, images)


def mid_kernel(ny, nx, *refs):
    (qkv_ref, kf_ref, xb, wo_ref, wt_ref, vec_ref, near_ref, grad_ref,
     mix_ref, lse_ref, x2_ref, h2_ref, g_ref, fa, fb,
     mix_oth, land, buf, csem, send_sem, recv_sem) = refs
    h, y, x, c, l = (lax.axis_index(a) for a in AXES)
    images, rows, width = mix_ref.shape
    padded = rows // 2
    pairs = width // 128
    apart, inner = h != c, l != h
    cross = {"seq": 1 - h, "core": 1 - c}
    to_core, to_dp = {"core": 1 - c}, {"dp": 1 - l}
    to_x = [{"x": lax.rem(x + nx - k, nx)} for k in range(nx)]
    to_y = [{"y": lax.rem(y + ny - k, ny)} for k in range(ny)]
    wires = Wires(send_sem, recv_sem)
    spread, forward, settle = plane_moves(wires, to_x, to_y)
    barrier = pltpu.get_barrier_semaphore()
    peers = [to_core, to_dp] + to_x[1:] + to_y[1:]
    for peer in peers:
        pl.semaphore_signal(barrier, inc=1, device_id=peer, device_id_type=MESH_ID)

    @pl.when(apart)
    def _():
        pl.semaphore_signal(barrier, inc=1, device_id=cross, device_id_type=MESH_ID)

    pl.semaphore_wait(barrier, len(peers) + jnp.where(apart, 1, 0))
    here_ff = [pltpu.make_async_copy(near_ref.at[ab], land.at[ab], csem.at[3 + ab]) for ab in range(2)]
    far_ff = [wires.make(near_ref.at[ab], land.at[ab], to_dp) for ab in range(2)]
    local_grad = pltpu.make_async_copy(grad_ref, g_ref.at[0], csem.at[0])
    grad_core = wires.make(grad_ref, g_ref.at[1], to_core)
    g_cross = [wires.make(grad_ref.at[i], g_ref.at[0, i], cross) for i in range(images)]
    g_core = [wires.make(g_ref.at[0, i], g_ref.at[1, i], to_core) for i in range(images)]

    @pl.when(inner)
    def _():
        for cp in far_ff + here_ff:
            cp.start()

    @pl.when(jnp.logical_not(apart))
    def _():
        local_grad.start()
        grad_core.start()

    def arrive(ab):
        @pl.when(inner)
        def _():
            here_ff[ab].wait()

        @pl.when(jnp.logical_not(inner))
        def _():
            far_ff[ab].wait_recv()

        return spread(ff[ab], 1, order[ab])

    ff = [by_offset(fa, land.at[0]), by_offset(fb, land.at[1])]
    order = ("x", "y")
    gots = []

    @pl.when(apart)
    def _():
        for cp in g_cross:
            cp.start()

    mix_got = []
    for i in range(images):
        def pair(p, carry):
            at = [pl.ds(pl.multiple_of((t * pairs + p) * 128, 128), 128) for t in range(3)]
            mixed, sums = attend_pair(qkv_ref[i, :, at[0]], qkv_ref[i, :, at[1]], qkv_ref[i, :, at[2]], kf_ref[i])
            mix_ref[i, :, at[0]] = mixed
            for j in range(2):
                lse_ref[i, p, j:j + 1, :] = sums[j]
            return carry

        lax.fori_loop(0, pairs, pair, 0)
        mix_got.append(wires.send(mix_ref.at[i], mix_oth.at[i], to_core))
        if i == max(images - 2, 0):
            gots.append(arrive(0))
        if i == images - 1:
            gots.append(arrive(1))

    def middle(i):
        mix_got[i].wait_recv()
        for s in range(2):
            own = slice(s * padded, (s + 1) * padded)
            oth = slice((1 - s) * padded, (2 - s) * padded)
            v = wide_rows(buf, xb[s, i])
            v = v + (dot(mix_ref[i, own, :], wo_ref[...]) + dot(mix_oth[i, oth, :], wt_ref[...])) + vec_ref[0:1, :]
            x2_ref[i, s] = v
            h2_ref[i, s] = (norm_parts(v)[0] * vec_ref[1:2, :] + vec_ref[2:3, :]).astype(BF)

    for i in range(images):
        middle(i)
        if i == 0:
            forward(ff[0], 1, order[0], gots[0])
    keep = [pltpu.make_async_copy(land.at[ab], (fa, fb)[ab].at[0, 0], csem.at[1 + ab]) for ab in range(2)]
    for cp in keep:
        cp.start()
    forward(ff[1], 1, order[1], gots[1])
    for i in range(images):
        @pl.when(apart)
        def _():
            g_cross[i].wait_recv()
            g_core[i].start()

        @pl.when(jnp.logical_not(apart))
        def _():
            g_core[i].wait_recv()

    @pl.when(apart)
    def _():
        grad_core.wait_recv()
        for cp in g_cross + g_core:
            cp.wait_send()

    @pl.when(jnp.logical_not(apart))
    def _():
        local_grad.wait()
        grad_core.wait_send()

    @pl.when(inner)
    def _():
        for cp in far_ff:
            cp.wait_send()

    for got in gots:
        settle(got)
    for cp in keep:
        cp.wait()
    wires.finish()


def mid_stage(qkv, key_fill, x_both, w_own, w_oth, vec, low_ff, out_grad, ny, nx):
    n, rows, w3 = qkv.shape
    width, feat = w_own.shape
    half = out_grad.shape[1]
    _, ud, hid, _ = low_ff.shape
    many = 40 + 4 * ny * nx
    S = jax.ShapeDtypeStruct
    return pl.pallas_call(
        functools.partial(mid_kernel, ny, nx),
        in_specs=[VM] * 6 + [ANY] * 2,
        out_specs=[VM] * 5 + [ANY] * 2,
        out_shape=[
            S((n, rows, width), BF), S((n, width // 128, 8, rows), F32), S((n, 2, rows // 2, feat), F32),
            S((n, 2, rows // 2, feat), BF), S((2, n, half, feat), BF),
            S((ny, nx, ud, hid, feat), BF), S((ny, nx, ud, hid, feat), BF),
        ],
        scratch_shapes=[
            pltpu.VMEM((n, rows, width), BF), pltpu.VMEM((2, ud, hid, feat), BF), pltpu.VMEM((rows // 2, feat), F32),
            pltpu.SemaphoreType.DMA((5,)), pltpu.SemaphoreType.DMA((many,)), pltpu.SemaphoreType.DMA((many,)),
        ],
        name="mid_stage",
        compiler_params=pltpu.CompilerParams(collective_id=5, has_side_effects=True, vmem_limit_bytes=60 << 20),
        cost_estimate=pl.CostEstimate(flops=n * 4 * rows * rows * w3, bytes_accessed=50 << 20, transcendentals=n * 8 * rows * rows),
    )(qkv, key_fill, x_both, w_own, w_oth, vec, low_ff, out_grad)


def shift(value, axis, up):
    n = lax.axis_size(axis)
    return lax.ppermute(value, axis, [(i, (i + up) % n) for i in range(n)])


def after(value, *others):
    return lax.optimization_barrier((value, others))[0]


def crossing(value):
    return lax.ppermute(value, ("seq", "core"), [(1, 2), (2, 1)])


def pick(own, received):
    return jnp.where(lax.axis_index("seq") == lax.axis_index("core"), own, received)


def crossed(value):
    return pick(value, crossing(value))


def adam_update(master, first_moment, second_moment, gradient, step_rate, bias_one, bias_two):
    first_new = 0.5 * first_moment + 0.5 * gradient
    second_new = 0.5 * second_moment + 0.5 * gradient * gradient
    update = first_new / bias_one / (jnp.sqrt(second_new / bias_two) + ADAM_EPS)
    master_new = master - step_rate * (update + WEIGHT_DECAY * master)
    return (master_new, first_new, second_new)


def on_device(images, key_mask, out_grad, step_count, *params):
    masters, firsts, seconds = params[0:5], params[5:10], params[10:15]
    in_weights, out_weights, up_weights, down_weights, vectors = masters
    image_count, half, features = images.shape
    padded = -(-half // PAD_ROWS) * PAD_ROWS
    h, c = lax.axis_index("seq"), lax.axis_index("core")
    y, x = lax.axis_index("y"), lax.axis_index("x")
    ny, nx = lax.axis_size("y"), lax.axis_size("x")
    shards = 4 * ny * nx
    shard = ((h * ny + y) * nx + x) * 2 + c

    h1, qkv, x_both, full_in, my_out, other_out, own_a, own_b, low_ff, full_vec = head_stage(
        in_weights, out_weights, up_weights, down_weights, vectors[None], images, padded, ny, nx
    )
    my_out, other_out = my_out.reshape(HALF_D, D), other_out.reshape(HALF_D, D)
    rows_in, rows_out, rows_ff = in_weights.shape[0], out_weights.shape[0], up_weights.shape[0]
    half_ff = rows_ff // 2
    keys = [(ky, kx) for ky in range(ny) for kx in range(nx)]
    full_vec = full_vec.reshape(-1)
    gain_one, shift_one, query_bias, value_bias, out_bias, gain_two, shift_two, down_bias = (
        full_vec[i * D : (i + 1) * D] for i in range(8)
    )
    up_bias = full_vec[8 * D :]

    mask = key_mask.astype(F32)
    mask = jnp.where(h == c, mask, shift(mask, "core", 1)).reshape(image_count, 2, half)
    mask = jnp.where(c == 0, mask, mask[:, ::-1])
    mask = jnp.pad(mask, ((0, 0), (0, 0), (0, padded - half))).reshape(image_count, 2 * padded)
    key_fill = jnp.broadcast_to(jnp.where(mask > 0, 0.0, NEG_FILL)[..., None], mask.shape + (128,)).astype(BF)

    tokens = image_count * 2 * padded
    qkv = qkv.reshape(image_count, 2 * padded, 3 * HALF_D)
    mid_vec = jnp.pad(jnp.stack([out_bias, gain_two, shift_two]), ((0, 5), (0, 0)))
    mixed, lse, x2, h2, g_both, oth_a, oth_b = mid_stage(
        qkv, key_fill, x_both, my_out, other_out, mid_vec, low_ff, out_grad, ny, nx
    )
    halved = mixed.reshape(image_count, 2, padded, HALF_D)

    grad_a, grad_b, (y_own, y_oth, dh2, g_bu, first_a, first_b) = mlp(
        ny, nx, h2.reshape(tokens, D), g_both, up_bias.reshape(shards * 2, half_ff), own_a, own_b, oth_a, oth_b
    )
    result = y_own[:, :half] + shift(y_oth, "core", 1)[:, :half].astype(F32) + x2[:, 0, :half] + down_bias
    result = result.astype(BF)
    result_got = crossing(result)

    def second_stage(grads, firsts, swap):
        sums = []
        for k in range(firsts.shape[1]):
            sums.append(add_all(grads[(k, 0) if swap else (0, k)], *firsts[:, k]).astype(BF))
        return sums

    sums_a, sums_b = second_stage(grad_a, first_a, False), second_stage(grad_b, first_b, True)
    got_a = [lax.ppermute(s, "x", [(i, (i + k) % nx) for i in range(nx)]) for k, s in enumerate(sums_a) if k]
    got_b = [lax.ppermute(s, "y", [(i, (i + k) % ny) for i in range(ny)]) for k, s in enumerate(sums_b) if k]

    dh2 = dh2.reshape(image_count, 2, padded, D)
    dh2_oth = shift(dh2, "core", 1)
    dx2, dattn, g_out, sums_two = middle_back(x2, dh2, dh2_oth, g_both, halved, my_out, gain_two)
    dqkv, sums_qkv = attend_back(qkv, key_fill, mixed, dattn.reshape(mixed.shape), lse)
    got_a, got_b = after(got_a, dqkv), after(got_b, dqkv)
    plane_a, plane_b = add_all(sums_a[0], *got_a).astype(BF), add_all(sums_b[0], *got_b).astype(BF)
    l = lax.axis_index("dp")
    half_keep, half_give = jnp.where(l == 0, plane_a, plane_b), jnp.where(l == 0, plane_b, plane_a)

    zero = jnp.zeros((D,), F32)
    vec = jnp.concatenate(
        [
            zero,
            zero,
            lax.dynamic_update_slice(zero, sums_qkv[0, :HALF_D], (c * HALF_D,)),
            lax.dynamic_update_slice(zero, sums_qkv[0, 2 * HALF_D :], (c * HALF_D,)),
            sums_two[2],
            sums_two[0],
            sums_two[1],
            sums_two[3],
            g_bu.reshape(-1),
        ]
    ).reshape(-1, 128)
    in_mine, in_theirs, share_out, share_ff, input_grad, vec, norm = tail_stage(
        h1.reshape(tokens, D),
        dqkv.reshape(tokens, 3 * HALF_D),
        g_out.reshape(ny, nx, 2, rows_out, D),
        x_both,
        dx2,
        gain_one,
        vec,
        full_in,
        half_keep,
        half_give,
        ny,
        nx,
    )
    activations = pick(result, after(result_got, norm)).astype(F32)
    input_grad = input_grad.astype(F32)
    share_vec = lax.dynamic_slice(vec.reshape(shards, -1), (shard, 0), (1, vec.size // shards)).reshape(-1)
    in_mine, in_theirs = (s.reshape(rows_in, 3, 1, HALF_D) for s in (in_mine, in_theirs))
    share_in = jnp.where(
        c == 0, jnp.concatenate([in_mine, in_theirs], 2), jnp.concatenate([in_theirs, in_mine], 2)
    ).reshape(rows_in, 3 * D)
    share_up, share_down = (share_ff[:, i].reshape(rows_ff, D) for i in range(2))
    shares = tuple(s.astype(F32) for s in (share_in, share_out, share_up, share_down, share_vec))
    grad_norm = norm[0, 0]
    threshold = 0.5 * math.sqrt(4 * D * D + 2 * D * FF + 12 * D)
    clip_factor = jnp.minimum(1.0, threshold / grad_norm)
    bias = 1.0 - jnp.power(F32(0.5), step_count.astype(F32))
    rates = ((D // 2) ** (-0.5), (D // 4) ** (-0.5), D ** (-0.5), FF ** (-0.5), 0.2)
    results = [
        adam_update(masters[i], firsts[i], seconds[i], shares[i] * clip_factor, rates[i], bias, bias) for i in range(5)
    ]
    return (
        grad_norm,
        *(r[0] for r in results),
        *(r[1] for r in results),
        *(r[2] for r in results),
        *(r[0].astype(BF) for r in results),
        activations,
        input_grad,
    )


def solution(mesh):
    seq_n, fsdp_n, dp_n = (mesh.shape[a] for a in ("seq", "fsdp", "dp"))
    nx = math.isqrt(fsdp_n // 2)
    ny = fsdp_n // 2 // nx
    grid = Mesh(np.asarray(mesh.devices).reshape(seq_n, ny, nx, 2, dp_n), AXES)
    tokens = P(("y", "x", "core", "dp"), "seq", None)
    matrix, vector = P(SHARD, None), P(SHARD)
    five = (matrix, matrix, matrix, matrix, vector)
    return jax.shard_map(
        on_device,
        mesh=grid,
        in_specs=(tokens, P(("y", "x", "core", "dp"), None), tokens, P()) + five * 3,
        out_specs=(P(),) + five * 4 + (tokens, tokens),
        check_vma=False,
    )
```
